32 devices in a mesh: dp: 8 (over y, x, core), seq: 4 (over z).
Axes of the slice: x: 2, y: 2, z: 4, core: 2. Of those that a mesh axis runs over, the one named last changes fastest.
Arguments:
- tokens: bfloat16 [32, 640, 1024], P('dp', 'seq'), may hold values from -6 to 6
- filled: int32 [32, 640], P('dp', 'seq'), may hold values from 0 to 1, as said below
- out_grad: bfloat16 [32, 640, 1024], P('dp', 'seq'), may hold values from -6 to 6
- norm1_gain: bfloat16 [1024], P('dp'), may hold values from 0.25 to 1.75
- norm1_bias: bfloat16 [1024], P('dp'), may hold values from -3 to 3
- qkv_weight: bfloat16 [1024, 3072], P('dp'), may hold values from -1 to 1
- qv_bias: bfloat16 [2048], P('dp'), may hold values from -3 to 3
- out_weight: bfloat16 [1024, 1024], P('dp'), may hold values from -1 to 1
- out_bias: bfloat16 [1024], P('dp'), may hold values from -3 to 3
- norm2_gain: bfloat16 [1024], P('dp'), may hold values from 0.25 to 1.75
- norm2_bias: bfloat16 [1024], P('dp'), may hold values from -3 to 3
- up_weight: bfloat16 [1024, 4096], P('dp'), may hold values from -0.1875 to 0.1875
- up_bias: bfloat16 [4096], P('dp'), may hold values from -3 to 3
- down_weight: bfloat16 [4096, 1024], P('dp'), may hold values from -0.1875 to 0.1875
- down_bias: bfloat16 [1024], P('dp'), may hold values from -3 to 3
- clip_threshold: int32 [], replicated, may hold values from 8 to 12
Outputs:
- block_out: bfloat16 [32, 640, 1024], P('dp', 'seq')
- tokens_grad: bfloat16 [32, 640, 1024], P('dp', 'seq')
- norm1_gain_grad: float32 [1024], P('dp')
- norm1_bias_grad: float32 [1024], P('dp')
- qkv_weight_grad: float32 [1024, 3072], P('dp')
- qv_bias_grad: float32 [2048], P('dp')
- out_weight_grad: float32 [1024, 1024], P('dp')
- out_bias_grad: float32 [1024], P('dp')
- norm2_gain_grad: float32 [1024], P('dp')
- norm2_bias_grad: float32 [1024], P('dp')
- up_weight_grad: float32 [1024, 4096], P('dp')
- up_bias_grad: float32 [4096], P('dp')
- down_weight_grad: float32 [4096, 1024], P('dp')
- down_bias_grad: float32 [1024], P('dp')
- clipped_qkv_weight: bfloat16 [1024, 3072], P('dp')
- clipped_qv_bias: bfloat16 [2048], P('dp')
- head_max: float32 [16], replicated
The draws below stay inside these ranges and needn't reach their ends.
Inputs may be any that keep to these rules, and one draw needn't show every extreme that they name: `filled`: each image's flags are 1 on a leading run of at least 320 slots and 0 after it.
All inputs are finite; a program needn't handle non-finite values.
Results may differ from the reference program's by a relative error of at most 0.018.
Values may be sent and summed in bfloat16 or wider, within the bound.
A program may use at most 192 MiB of HBM per device.

```python
import math
import jax
import jax.numpy as jnp
from jax import lax

D = 1024
H = 16
HD = 64
FF = 4096
LENGTH = 640
IMG_DEV = 4
IMAGES = 32
N_DP = 8


def draw_filled(key, part):
    lengths = jax.random.randint(key, (IMAGES,), LENGTH // 2, LENGTH + 1)
    positions = jnp.arange(LENGTH)
    return (positions[None, :] < lengths[:, None]).astype(jnp.int32)


def draw_qkv_weight(key, part):
    key_base, key_heads = jax.random.split(key)
    base = jnp.clip(jax.random.normal(key_base, (D, 3 * D), jnp.float32), -6.0, 6.0) * D ** (-0.5)
    head_scale = jnp.exp(jax.random.uniform(key_heads, (H,), jnp.float32, math.log(0.85), math.log(1.45)))
    head_cols = jnp.repeat(head_scale, HD)
    column_scale = jnp.concatenate([head_cols, head_cols, jnp.ones((D,), jnp.float32)])
    return (base * column_scale[None, :]).astype(jnp.bfloat16)


def steps_of(rng, dims, pieces, least, largest):
    loudness, own = 1.0, jax.random.fold_in(rng, 6)
    for dim, shards_of in pieces:
        draws = jnp.exp(jax.random.uniform(jax.random.fold_in(own, dim), (shards_of,), jnp.float32, least / len(pieces), largest / len(pieces)))
        loudness = loudness * jnp.repeat(draws, dims[dim] // shards_of).reshape([-1 if axis == dim else 1 for axis in range(len(dims))])
    return loudness


def noise(key, dims, scale, most, pieces=(), held_as=jnp.bfloat16):
    array = scale * jax.random.normal(key, dims, jnp.float32)
    if pieces:
        array = array * steps_of(key, dims, pieces, -0.22, 0.18)
    return jnp.clip(array, -most, most).astype(held_as)


def setup_inputs(seed: int = 0) -> dict:
    arg_keys = jax.random.split(jax.random.key(seed), 17)
    return {
        "tokens": noise(arg_keys[0], (IMAGES, LENGTH, D), 1.0, 6.0, ((0, 8), (1, 4))),
        "filled": draw_filled(jax.random.fold_in(arg_keys[16], 71), 0),
        "out_grad": noise(arg_keys[2], (IMAGES, LENGTH, D), 1.0, 6.0, ((0, 8), (1, 4))),
        "norm1_gain": jnp.clip(1.0 + 0.15 * jax.random.normal(arg_keys[3], (D,), jnp.float32), 0.25, 1.75).astype(jnp.bfloat16),
        "norm1_bias": noise(arg_keys[4], (D,), 0.5, 3.0, ((0, 8),)),
        "qkv_weight": draw_qkv_weight(jax.random.fold_in(arg_keys[16], 71), 0),
        "qv_bias": noise(arg_keys[6], (2 * D,), 0.5, 3.0, ((0, 8),)),
        "out_weight": noise(arg_keys[7], (D, D), (D // 32) ** -0.5, 1.0, ((0, 8),)),
        "out_bias": noise(arg_keys[8], (D,), 0.5, 3.0, ((0, 8),)),
        "norm2_gain": jnp.clip(1.0 + 0.15 * jax.random.normal(arg_keys[9], (D,), jnp.float32), 0.25, 1.75).astype(jnp.bfloat16),
        "norm2_bias": noise(arg_keys[10], (D,), 0.5, 3.0, ((0, 8),)),
        "up_weight": noise(arg_keys[11], (D, FF), D ** -0.5, 0.1875, ((0, 8),)),
        "up_bias": noise(arg_keys[12], (FF,), 0.5, 3.0, ((0, 8),)),
        "down_weight": noise(arg_keys[13], (FF, D), (FF // 4) ** -0.5, 0.1875, ((0, 8),)),
        "down_bias": noise(arg_keys[14], (D,), 0.5, 3.0, ((0, 8),)),
        "clip_threshold": jax.random.randint(arg_keys[15], (), 8, 13).astype(jnp.int32),
    }


@jax.custom_vjp
def low(v):
    return lax.optimization_barrier(v.astype(jnp.bfloat16)).astype(jnp.float32)

@jax.custom_vjp
def low_back(v):
    return v

def low_keep(v):
    return (low(v), None)

def low_pass(kept, grad):
    return (grad,)

def back_keep(v):
    return (v, None)

def back_low(kept, grad):
    return (low(grad),)
low.defvjp(low_keep, low_pass)
low_back.defvjp(back_keep, back_low)
epsilon = 1e-06
very_negative = -1e+30

def norm_apply(values, gain_vec, shift_vec):
    center = lax.optimization_barrier(jnp.mean(values, axis=-1, keepdims=True))
    centered = values - center
    spread = lax.optimization_barrier(jnp.mean(centered * centered, axis=-1, keepdims=True))
    return centered * lax.rsqrt(spread + epsilon) * gain_vec + shift_vec

def matmul(left_op, right_op):
    return jnp.dot(left_op, right_op, precision=lax.Precision.HIGHEST, preferred_element_type=jnp.float32)

def attend_image(inputs):
    queries, keys_in, values_in, key_keep = inputs
    raw_scores = jnp.einsum('qhd,khd->hqk', queries, keys_in, precision=lax.Precision.HIGHEST) * HD ** (-0.5)
    raw_scores = low_back(raw_scores)
    masked = jnp.where(key_keep[None, None, :], raw_scores, very_negative)
    row_peak = lax.optimization_barrier(jnp.max(masked, axis=-1, keepdims=True))
    exp_scores = jnp.exp(masked - row_peak)
    soft_probs = exp_scores / lax.optimization_barrier(jnp.sum(exp_scores, axis=-1, keepdims=True))
    mixed_rows = jnp.einsum('hqk,khd->qhd', low(soft_probs), values_in, precision=lax.Precision.HIGHEST)
    pair_keep = key_keep[:, None] & key_keep[None, :]
    head_top = lax.optimization_barrier(jnp.max(jnp.where(pair_keep[None], raw_scores, very_negative), axis=(1, 2)))
    return (mixed_rows, head_top)

def layer(tokens_in, gain_one, shift_one, w_qkv, b_qv, w_out, b_out, gain_two, shift_two, w_up, b_up, w_down, b_down, key_keep):
    images = tokens_in.shape[0]
    row_values = tokens_in.reshape(-1, D)
    hidden_one = low(norm_apply(row_values, gain_one, shift_one))
    qkv_bias = jnp.concatenate([b_qv[:D], jnp.zeros((D,), jnp.float32), b_qv[D:]])
    projected = low(low_back(matmul(hidden_one, w_qkv) + qkv_bias)).reshape(images, LENGTH, 3, H, HD)
    mixed_rows, head_top = lax.map(jax.checkpoint(attend_image), (projected[:, :, 0], projected[:, :, 1], projected[:, :, 2], key_keep))
    attended = low(low_back(mixed_rows.reshape(-1, D)))
    branch = low_back(matmul(attended, w_out) + b_out)
    middle = row_values + branch
    hidden_two = low(norm_apply(middle, gain_two, shift_two))
    pre_act = low_back(matmul(hidden_two, w_up) + b_up)
    activated = low(jax.nn.gelu(pre_act, approximate=False))
    result = middle + (matmul(activated, w_down) + b_down)
    return (result.reshape(images, LENGTH, D), lax.optimization_barrier(jnp.max(head_top, axis=0)))

def reference(tokens, filled, out_grad, norm1_gain, norm1_bias, qkv_weight, qv_bias, out_weight, out_bias, norm2_gain, norm2_bias, up_weight, up_bias, down_weight, down_bias, clip_threshold):
    params = tuple((p.astype(jnp.float32) for p in (norm1_gain, norm1_bias, qkv_weight, qv_bias, out_weight, out_bias, norm2_gain, norm2_bias, up_weight, up_bias, down_weight, down_bias)))
    token_groups = tokens.astype(jnp.float32).reshape(N_DP, IMG_DEV, LENGTH, D)
    grad_groups = out_grad.astype(jnp.float32).reshape(N_DP, IMG_DEV, LENGTH, D)
    keep_groups = (filled > 0).reshape(N_DP, IMG_DEV, LENGTH)

    def group_step(totals, group):
        group_tokens, group_grad, group_keep = group

        def forward(tokens_in, *param_list):
            return layer(tokens_in, *param_list, group_keep)
        outputs, pull_back, head_top = jax.vjp(forward, group_tokens, *params, has_aux=True)
        cotangents = pull_back(group_grad)
        new_totals = tuple((t_old + t_new for t_old, t_new in zip(totals, cotangents[1:])))
        return (new_totals, (outputs.astype(jnp.bfloat16), cotangents[0].astype(jnp.bfloat16), head_top))
    start = tuple((jnp.zeros_like(p) for p in params))
    totals, (outputs, input_grads, tops) = lax.scan(group_step, start, (token_groups, grad_groups, keep_groups))
    head_max = lax.optimization_barrier(jnp.max(tops, axis=0))
    limit = clip_threshold.astype(jnp.float32)
    root_factor = jnp.sqrt(limit / jnp.maximum(head_max, limit))
    head_cols = jnp.repeat(root_factor, HD)
    weight_scale = jnp.concatenate([head_cols, head_cols, jnp.ones((D,), jnp.float32)])
    bias_scale = jnp.concatenate([head_cols, jnp.ones((D,), jnp.float32)])
    clipped_weight = (params[2] * weight_scale[None, :]).astype(jnp.bfloat16)
    clipped_bias = (params[3] * bias_scale).astype(jnp.bfloat16)
    return (outputs.reshape(IMAGES, LENGTH, D), input_grads.reshape(IMAGES, LENGTH, D), totals[0], totals[1], totals[2], totals[3], totals[4], totals[5], totals[6], totals[7], totals[8], totals[9], totals[10], totals[11], clipped_weight, clipped_bias, head_max)
```

```python
import jax
import jax.numpy as jnp
from jax import lax
from jax.sharding import PartitionSpec as P

H = 16
HD = 64


epsilon = 1e-06
very_negative = -1e30


def norm_apply(values, gain_vec, shift_vec):
    center = jnp.mean(values, axis=-1, keepdims=True)
    centered = values - center
    spread = jnp.mean(centered * centered, axis=-1, keepdims=True)
    return centered * lax.rsqrt(spread + epsilon) * gain_vec + shift_vec


def exact_gelu(values):
    return jax.nn.gelu(values, approximate=False)


def last_dot(left_op, right_op):
    return lax.dot_general(
        left_op, right_op, (((1,), (1,)), ((), ())), preferred_element_type=jnp.float32
    )


def first_dot(left_op, right_op):
    return lax.dot_general(
        left_op, right_op, (((0,), (0,)), ((), ())), preferred_element_type=jnp.float32
    )


def column_sum(values):
    return jnp.sum(values.astype(jnp.float32), axis=0)


def score_block(queries, keys_in, key_keep):
    raw_scores = jnp.einsum(
        "qhd,khd->hqk", queries, keys_in, preferred_element_type=jnp.float32
    ) * HD ** (-0.5)
    masked = jnp.where(key_keep[None, None, :], raw_scores, very_negative)
    return (raw_scores, masked)


def attend_forward(inputs):
    queries, keys_in, values_in, key_keep = inputs
    raw_scores, masked = score_block(queries, keys_in, key_keep)
    row_peak = jnp.max(masked, axis=-1, keepdims=True)
    exp_scores = jnp.exp(masked - row_peak)
    row_total = jnp.sum(exp_scores, axis=-1, keepdims=True)
    soft_probs = (exp_scores / row_total).astype(jnp.bfloat16)
    mixed_rows = jnp.einsum(
        "hqk,khd->qhd", soft_probs, values_in, preferred_element_type=jnp.float32
    )
    logsum = row_peak + jnp.log(row_total)
    pair_keep = key_keep[:, None] & key_keep[None, :]
    head_top = jnp.max(jnp.where(pair_keep[None], raw_scores, very_negative), axis=(1, 2))
    flat_rows = mixed_rows.astype(jnp.bfloat16).reshape(mixed_rows.shape[0], -1)
    return (flat_rows, logsum, head_top)


def attend_backward(inputs):
    queries, keys_in, values_in, key_keep, logsum, upstream = inputs
    raw_scores, masked = score_block(queries, keys_in, key_keep)
    soft_probs = jnp.exp(masked - logsum)
    probs_low = soft_probs.astype(jnp.bfloat16)
    value_grad = jnp.einsum("hqk,qhd->khd", probs_low, upstream, preferred_element_type=jnp.float32)
    prob_grad = jnp.einsum("qhd,khd->hqk", upstream, values_in, preferred_element_type=jnp.float32)
    inner_sum = jnp.sum(soft_probs * prob_grad, axis=-1, keepdims=True)
    score_grad = (soft_probs * (prob_grad - inner_sum)).astype(jnp.bfloat16)
    score_scale = HD ** (-0.5)
    query_grad = (
        jnp.einsum("hqk,khd->qhd", score_grad, keys_in, preferred_element_type=jnp.float32)
        * score_scale
    )
    key_grad = (
        jnp.einsum("hqk,qhd->khd", score_grad, queries, preferred_element_type=jnp.float32)
        * score_scale
    )
    stacked = jnp.stack([query_grad, key_grad, value_grad], axis=1)
    return stacked.astype(jnp.bfloat16).reshape(stacked.shape[0], 3, -1)


def by_head_local(
    tokens,
    filled,
    out_grad,
    norm1_gain,
    norm1_bias,
    qkv_weight,
    qv_bias,
    out_weight,
    out_bias,
    norm2_gain,
    norm2_bias,
    up_weight,
    up_bias,
    down_weight,
    down_bias,
    clip_threshold,
):
    gathered = (
        lax.all_gather(norm1_gain, "dp", axis=0, tiled=True),
        lax.all_gather(norm1_bias, "dp", axis=0, tiled=True),
        lax.all_gather(qkv_weight, "dp", axis=0, tiled=True),
        lax.all_gather(qv_bias, "dp", axis=0, tiled=True),
        lax.all_gather(out_weight, "dp", axis=0, tiled=True),
        lax.all_gather(out_bias, "dp", axis=0, tiled=True),
        lax.all_gather(norm2_gain, "dp", axis=0, tiled=True),
        lax.all_gather(norm2_bias, "dp", axis=0, tiled=True),
        lax.all_gather(up_weight, "dp", axis=0, tiled=True),
        lax.all_gather(up_bias, "dp", axis=0, tiled=True),
        lax.all_gather(down_weight, "dp", axis=0, tiled=True),
        lax.all_gather(down_bias, "dp", axis=0, tiled=True),
    )
    (
        gain_one,
        shift_one,
        w_qkv,
        b_qv,
        w_out,
        b_out,
        gain_two,
        shift_two,
        w_up,
        b_up,
        w_down,
        b_down,
    ) = gathered
    images, local_rows, model_width = tokens.shape
    groups = lax.axis_size("seq")
    group_width = model_width // groups
    local_heads = group_width // HD
    length = local_rows * groups
    row_count = images * local_rows
    tokens_flat = tokens.astype(jnp.float32).reshape(row_count, model_width)
    gain_one_f = gain_one.astype(jnp.float32)
    shift_one_f = shift_one.astype(jnp.float32)
    gain_two_f = gain_two.astype(jnp.float32)
    shift_two_f = shift_two.astype(jnp.float32)
    hidden_one = norm_apply(tokens_flat, gain_one_f, shift_one_f).astype(jnp.bfloat16)
    bias_float = b_qv.astype(jnp.float32)
    qkv_bias = jnp.concatenate(
        [bias_float[:model_width], jnp.zeros((model_width,), jnp.float32), bias_float[model_width:]]
    )
    projected = (jnp.dot(hidden_one, w_qkv, preferred_element_type=jnp.float32) + qkv_bias).astype(
        jnp.bfloat16
    )
    key_flags = lax.all_gather(filled, "seq", axis=1, tiled=True)
    keep_all = key_flags > 0
    by_heads = lax.all_to_all(
        projected.reshape(images, local_rows, 3, groups, group_width),
        "seq",
        split_axis=3,
        concat_axis=1,
        tiled=True,
    )
    by_heads = by_heads.reshape(images, length, 3, local_heads, HD)
    queries = by_heads[:, :, 0]
    keys_all = by_heads[:, :, 1]
    values_all = by_heads[:, :, 2]
    attended, logsums, tops = lax.map(attend_forward, (queries, keys_all, values_all, keep_all))
    local_peak = jnp.max(tops, axis=0)
    peak_vector = lax.dynamic_update_slice(
        jnp.full((H,), very_negative, jnp.float32),
        local_peak,
        (lax.axis_index("seq") * local_heads,),
    )
    head_max = lax.pmax(peak_vector, ("dp", "seq"))
    back_rows = lax.all_to_all(
        attended.reshape(images, groups, local_rows, group_width),
        "seq",
        split_axis=1,
        concat_axis=3,
        tiled=True,
    )
    attn_rows = back_rows.reshape(row_count, model_width)
    branch = jnp.dot(attn_rows, w_out, preferred_element_type=jnp.float32) + b_out.astype(
        jnp.float32
    )
    middle = tokens_flat + branch
    hidden_two = norm_apply(middle, gain_two_f, shift_two_f).astype(jnp.bfloat16)
    pre_act = jnp.dot(hidden_two, w_up, preferred_element_type=jnp.float32) + b_up.astype(
        jnp.float32
    )
    activated = exact_gelu(pre_act).astype(jnp.bfloat16)
    block_rows = middle + (
        jnp.dot(activated, w_down, preferred_element_type=jnp.float32) + b_down.astype(jnp.float32)
    )
    block_out = block_rows.astype(jnp.bfloat16).reshape(tokens.shape)
    gain_one_b, w_qkv_b, w_out_b, gain_two_b, w_up_b, w_down_b = (
        lax.all_gather(norm1_gain, "dp", axis=0, tiled=True),
        lax.all_gather(qkv_weight, "dp", axis=0, tiled=True),
        lax.all_gather(out_weight, "dp", axis=0, tiled=True),
        lax.all_gather(norm2_gain, "dp", axis=0, tiled=True),
        lax.all_gather(up_weight, "dp", axis=0, tiled=True),
        lax.all_gather(down_weight, "dp", axis=0, tiled=True),
    )
    upstream = out_grad.reshape(row_count, model_width)
    upstream_f = upstream.astype(jnp.float32)
    d_bias_down = jnp.sum(upstream_f, axis=0)
    d_down = first_dot(activated, upstream)
    act_grad = last_dot(upstream, w_down_b)
    gelu_out, gelu_pull = jax.vjp(exact_gelu, pre_act)
    pre_grad = gelu_pull(act_grad)[0].astype(jnp.bfloat16)
    d_bias_up = column_sum(pre_grad)
    d_up = first_dot(hidden_two, pre_grad)
    hidden_two_grad = last_dot(pre_grad, w_up_b)
    norm_out_two, pull_two = jax.vjp(
        norm_apply, middle, gain_two_b.astype(jnp.float32), shift_two_f
    )
    mid_norm_grad, d_gain_two, d_shift_two = pull_two(hidden_two_grad)
    middle_grad = upstream_f + mid_norm_grad
    branch_grad = middle_grad.astype(jnp.bfloat16)
    d_bias_out = column_sum(branch_grad)
    d_out = first_dot(attn_rows, branch_grad)
    attn_grad = last_dot(branch_grad, w_out_b).astype(jnp.bfloat16)
    grad_heads = lax.all_to_all(
        attn_grad.reshape(images, local_rows, groups, group_width),
        "seq",
        split_axis=2,
        concat_axis=1,
        tiled=True,
    )
    grad_heads = grad_heads.reshape(images, length, local_heads, HD)
    head_grads = lax.map(
        attend_backward, (queries, keys_all, values_all, keep_all, logsums, grad_heads)
    )
    token_grads = lax.all_to_all(
        head_grads.reshape(images, groups, local_rows, 3, group_width),
        "seq",
        split_axis=1,
        concat_axis=4,
        tiled=True,
    )
    token_grads = token_grads.reshape(row_count, 3 * model_width)
    d_qkv = first_dot(hidden_one, token_grads)
    bias_sums = column_sum(token_grads)
    d_bias_qv = jnp.concatenate([bias_sums[:model_width], bias_sums[2 * model_width :]])
    first_grad = last_dot(token_grads, w_qkv_b)
    norm_out_one, pull_one = jax.vjp(
        norm_apply, tokens_flat, gain_one_b.astype(jnp.float32), shift_one_f
    )
    in_norm_grad, d_gain_one, d_shift_one = pull_one(first_grad)
    tokens_grad = (middle_grad + in_norm_grad).astype(jnp.bfloat16).reshape(tokens.shape)
    terms = (
        d_gain_one,
        d_shift_one,
        d_qkv,
        d_bias_qv,
        d_out,
        d_bias_out,
        d_gain_two,
        d_shift_two,
        d_up,
        d_bias_up,
        d_down,
        d_bias_down,
    )
    data_shards = (
        lax.psum_scatter(
            terms[0].astype(jnp.bfloat16), "dp", scatter_dimension=0, tiled=True
        ).astype(jnp.float32),
        lax.psum_scatter(
            terms[1].astype(jnp.bfloat16), "dp", scatter_dimension=0, tiled=True
        ).astype(jnp.float32),
        lax.psum_scatter(
            terms[2].astype(jnp.bfloat16), "dp", scatter_dimension=0, tiled=True
        ).astype(jnp.float32),
        lax.psum_scatter(
            terms[3].astype(jnp.bfloat16), "dp", scatter_dimension=0, tiled=True
        ).astype(jnp.float32),
        lax.psum_scatter(
            terms[4].astype(jnp.bfloat16), "dp", scatter_dimension=0, tiled=True
        ).astype(jnp.float32),
        lax.psum_scatter(
            terms[5].astype(jnp.bfloat16), "dp", scatter_dimension=0, tiled=True
        ).astype(jnp.float32),
        lax.psum_scatter(
            terms[6].astype(jnp.bfloat16), "dp", scatter_dimension=0, tiled=True
        ).astype(jnp.float32),
        lax.psum_scatter(
            terms[7].astype(jnp.bfloat16), "dp", scatter_dimension=0, tiled=True
        ).astype(jnp.float32),
        lax.psum_scatter(
            terms[8].astype(jnp.bfloat16), "dp", scatter_dimension=0, tiled=True
        ).astype(jnp.float32),
        lax.psum_scatter(
            terms[9].astype(jnp.bfloat16), "dp", scatter_dimension=0, tiled=True
        ).astype(jnp.float32),
        lax.psum_scatter(
            terms[10].astype(jnp.bfloat16), "dp", scatter_dimension=0, tiled=True
        ).astype(jnp.float32),
        lax.psum_scatter(
            terms[11].astype(jnp.bfloat16), "dp", scatter_dimension=0, tiled=True
        ).astype(jnp.float32),
    )
    shards = (
        lax.psum(data_shards[0].astype(jnp.bfloat16), "seq").astype(jnp.float32),
        lax.psum(data_shards[1].astype(jnp.bfloat16), "seq").astype(jnp.float32),
        lax.psum(data_shards[2].astype(jnp.bfloat16), "seq").astype(jnp.float32),
        lax.psum(data_shards[3].astype(jnp.bfloat16), "seq").astype(jnp.float32),
        lax.psum(data_shards[4].astype(jnp.bfloat16), "seq").astype(jnp.float32),
        lax.psum(data_shards[5].astype(jnp.bfloat16), "seq").astype(jnp.float32),
        lax.psum(data_shards[6].astype(jnp.bfloat16), "seq").astype(jnp.float32),
        lax.psum(data_shards[7].astype(jnp.bfloat16), "seq").astype(jnp.float32),
        lax.psum(data_shards[8].astype(jnp.bfloat16), "seq").astype(jnp.float32),
        lax.psum(data_shards[9].astype(jnp.bfloat16), "seq").astype(jnp.float32),
        lax.psum(data_shards[10].astype(jnp.bfloat16), "seq").astype(jnp.float32),
        lax.psum(data_shards[11].astype(jnp.bfloat16), "seq").astype(jnp.float32),
    )
    limit = clip_threshold.astype(jnp.float32)
    root_factor = jnp.sqrt(limit / jnp.maximum(head_max, limit))
    head_cols = jnp.repeat(root_factor, HD)
    weight_scale = jnp.concatenate([head_cols, head_cols, jnp.ones((model_width,), jnp.float32)])
    clipped_weight = (qkv_weight.astype(jnp.float32) * weight_scale[None, :]).astype(jnp.bfloat16)
    bias_count = qv_bias.shape[0]
    bias_scale = jnp.concatenate([head_cols, jnp.ones((model_width,), jnp.float32)])
    shard_scale = lax.dynamic_slice_in_dim(
        bias_scale, lax.axis_index("dp") * bias_count, bias_count
    )
    clipped_bias = (qv_bias.astype(jnp.float32) * shard_scale).astype(jnp.bfloat16)
    return (
        block_out,
        tokens_grad,
        shards[0],
        shards[1],
        shards[2],
        shards[3],
        shards[4],
        shards[5],
        shards[6],
        shards[7],
        shards[8],
        shards[9],
        shards[10],
        shards[11],
        clipped_weight,
        clipped_bias,
        head_max,
    )


def gather_small(pieces):
    sizes = [piece.shape[0] for piece in pieces]
    packed = jnp.concatenate(pieces)
    everyone = lax.all_gather(packed, "dp", axis=0, tiled=False)
    outs, start = [], 0
    for size in sizes:
        outs.append(everyone[:, start : start + size].reshape(-1))
        start += size
    return outs


def by_image_local(
    tokens,
    filled,
    out_grad,
    norm1_gain,
    norm1_bias,
    qkv_weight,
    qv_bias,
    out_weight,
    out_bias,
    norm2_gain,
    norm2_bias,
    up_weight,
    up_bias,
    down_weight,
    down_bias,
    clip_threshold,
):
    images, local_rows, model_width = tokens.shape
    length = local_rows * images
    w_qkv = lax.all_gather(qkv_weight, "dp", axis=0, tiled=True)
    small = gather_small(
        [norm1_gain, norm1_bias, qv_bias, out_bias, norm2_gain, norm2_bias, up_bias, down_bias]
    )
    gain_one, shift_one, b_qv, b_out, gain_two, shift_two, b_up, b_down = [
        piece.astype(jnp.float32) for piece in small
    ]
    w_out = lax.all_gather(out_weight, "dp", axis=0, tiled=True)
    w_up = lax.all_gather(up_weight, "dp", axis=0, tiled=True)
    w_down = lax.all_gather(down_weight, "dp", axis=0, tiled=True)

    def to_image(rows):
        return lax.all_to_all(rows, "seq", split_axis=0, concat_axis=1, tiled=True)

    def from_image(rows):
        return lax.all_to_all(
            rows.reshape(1, length, -1), "seq", split_axis=1, concat_axis=0, tiled=True
        )

    tokens_low = to_image(tokens).reshape(length, model_width)
    upstream = to_image(out_grad).reshape(length, model_width)
    keep = to_image(filled).reshape(length) > 0
    tokens_flat = tokens_low.astype(jnp.float32)
    hidden_one = norm_apply(tokens_flat, gain_one, shift_one).astype(jnp.bfloat16)
    qkv_bias = jnp.concatenate(
        [b_qv[:model_width], jnp.zeros((model_width,), jnp.float32), b_qv[model_width:]]
    )
    projected = (jnp.dot(hidden_one, w_qkv, preferred_element_type=jnp.float32) + qkv_bias).astype(
        jnp.bfloat16
    )
    heads_view = projected.reshape(length, 3, H, HD)
    queries, keys_all, values_all = heads_view[:, 0], heads_view[:, 1], heads_view[:, 2]
    attn_rows, logsum, top = attend_forward((queries, keys_all, values_all, keep))
    head_max = lax.pmax(top, ("dp", "seq"))
    middle = tokens_flat + (jnp.dot(attn_rows, w_out, preferred_element_type=jnp.float32) + b_out)
    hidden_two = norm_apply(middle, gain_two, shift_two).astype(jnp.bfloat16)
    pre_act = jnp.dot(hidden_two, w_up, preferred_element_type=jnp.float32) + b_up
    activated = exact_gelu(pre_act).astype(jnp.bfloat16)
    block_rows = middle + (jnp.dot(activated, w_down, preferred_element_type=jnp.float32) + b_down)
    block_out = from_image(block_rows.astype(jnp.bfloat16)).reshape(tokens.shape)
    upstream_f = upstream.astype(jnp.float32)
    d_bias_down = jnp.sum(upstream_f, axis=0)
    d_down = first_dot(activated, upstream)
    act_grad = last_dot(upstream, w_down)
    gelu_out, gelu_pull = jax.vjp(exact_gelu, pre_act)
    pre_grad = gelu_pull(act_grad)[0].astype(jnp.bfloat16)
    d_bias_up = column_sum(pre_grad)
    d_up = first_dot(hidden_two, pre_grad)
    hidden_two_grad = last_dot(pre_grad, w_up)
    norm_out_two, pull_two = jax.vjp(norm_apply, middle, gain_two, shift_two)
    mid_norm_grad, d_gain_two, d_shift_two = pull_two(hidden_two_grad)
    middle_grad = upstream_f + mid_norm_grad
    branch_grad = middle_grad.astype(jnp.bfloat16)
    d_bias_out = column_sum(branch_grad)
    d_out = first_dot(attn_rows, branch_grad)
    attn_grad = last_dot(branch_grad, w_out).astype(jnp.bfloat16)
    token_grads = attend_backward(
        (queries, keys_all, values_all, keep, logsum, attn_grad.reshape(length, H, HD))
    ).reshape(length, 3 * model_width)
    d_qkv = first_dot(hidden_one, token_grads)
    bias_sums = column_sum(token_grads)
    d_bias_qv = jnp.concatenate([bias_sums[:model_width], bias_sums[2 * model_width :]])
    first_grad = last_dot(token_grads, w_qkv)
    norm_out_one, pull_one = jax.vjp(norm_apply, tokens_flat, gain_one, shift_one)
    in_norm_grad, d_gain_one, d_shift_one = pull_one(first_grad)
    tokens_grad = from_image((middle_grad + in_norm_grad).astype(jnp.bfloat16)).reshape(
        tokens.shape
    )

    def reduce_matrix(term):
        part = lax.psum_scatter(
            term.astype(jnp.bfloat16), "dp", scatter_dimension=0, tiled=True
        )
        return lax.psum(part, "seq").astype(jnp.float32)

    small_terms = [
        d_gain_one,
        d_shift_one,
        d_bias_qv,
        d_bias_out,
        d_gain_two,
        d_shift_two,
        d_bias_up,
        d_bias_down,
    ]
    shards = lax.axis_size("dp")
    packed = jnp.concatenate([term.reshape(shards, -1) for term in small_terms], axis=1)
    mine = lax.psum(
        lax.psum_scatter(packed, "dp", scatter_dimension=0, tiled=True), "seq"
    ).reshape(-1)
    small_out, start = [], 0
    for term in small_terms:
        size = term.shape[0] // shards
        small_out.append(mine[start : start + size])
        start += size
    s_gain_one, s_shift_one, s_qv, s_out, s_gain_two, s_shift_two, s_up, s_down = small_out
    limit = clip_threshold.astype(jnp.float32)
    root_factor = jnp.sqrt(limit / jnp.maximum(head_max, limit))
    head_cols = jnp.repeat(root_factor, HD)
    weight_scale = jnp.concatenate([head_cols, head_cols, jnp.ones((model_width,), jnp.float32)])
    clipped_weight = (qkv_weight.astype(jnp.float32) * weight_scale[None, :]).astype(jnp.bfloat16)
    bias_count = qv_bias.shape[0]
    bias_scale = jnp.concatenate([head_cols, jnp.ones((model_width,), jnp.float32)])
    shard_scale = lax.dynamic_slice_in_dim(
        bias_scale, lax.axis_index("dp") * bias_count, bias_count
    )
    clipped_bias = (qv_bias.astype(jnp.float32) * shard_scale).astype(jnp.bfloat16)
    return (
        block_out,
        tokens_grad,
        s_gain_one,
        s_shift_one,
        reduce_matrix(d_qkv),
        s_qv,
        reduce_matrix(d_out),
        s_out,
        s_gain_two,
        s_shift_two,
        reduce_matrix(d_up),
        s_up,
        reduce_matrix(d_down),
        s_down,
        clipped_weight,
        clipped_bias,
        head_max,
    )


def local(*args):
    if args[0].shape[0] == lax.axis_size("seq"):
        return by_image_local(*args)
    return by_head_local(*args)


def solution(mesh):
    return jax.shard_map(
        local,
        mesh=mesh,
        in_specs=(
            P("dp", "seq", None),
            P("dp", "seq"),
            P("dp", "seq", None),
            P("dp"),
            P("dp"),
            P("dp", None),
            P("dp"),
            P("dp", None),
            P("dp"),
            P("dp"),
            P("dp"),
            P("dp", None),
            P("dp"),
            P("dp", None),
            P("dp"),
            P(),
        ),
        out_specs=(
            P("dp", "seq", None),
            P("dp", "seq", None),
            P("dp"),
            P("dp"),
            P("dp", None),
            P("dp"),
            P("dp", None),
            P("dp"),
            P("dp"),
            P("dp"),
            P("dp", None),
            P("dp"),
            P("dp", None),
            P("dp"),
            P("dp", None),
            P("dp"),
            P(),
        ),
        check_vma=False,
    )
```

```python
import math

import jax
import jax.numpy as jnp
from jax import lax
from jax.experimental import pallas as pl
from jax.experimental.pallas import tpu as pltpu
from jax.sharding import PartitionSpec as P

H = 16
HD = 64


epsilon = 1e-06
very_negative = -1e30


def norm_apply(values, gain_vec, shift_vec):
    center = jnp.mean(values, axis=-1, keepdims=True)
    centered = values - center
    spread = jnp.mean(centered * centered, axis=-1, keepdims=True)
    return centered * lax.rsqrt(spread + epsilon) * gain_vec + shift_vec


def exact_gelu(values):
    return jax.nn.gelu(values, approximate=False)


def last_dot(left_op, right_op):
    return lax.dot_general(
        left_op, right_op, (((1,), (1,)), ((), ())), preferred_element_type=jnp.float32
    )


def first_dot(left_op, right_op):
    return lax.dot_general(
        left_op, right_op, (((0,), (0,)), ((), ())), preferred_element_type=jnp.float32
    )


def column_sum(values):
    return jnp.sum(values.astype(jnp.float32), axis=0)


def score_block(queries, keys_in, key_keep):
    raw_scores = jnp.einsum(
        "qhd,khd->hqk", queries, keys_in, preferred_element_type=jnp.float32
    ) * HD ** (-0.5)
    masked = jnp.where(key_keep[None, None, :], raw_scores, very_negative)
    return (raw_scores, masked)


def attend_forward(inputs):
    queries, keys_in, values_in, key_keep = inputs
    raw_scores, masked = score_block(queries, keys_in, key_keep)
    row_peak = jnp.max(masked, axis=-1, keepdims=True)
    exp_scores = jnp.exp(masked - row_peak)
    row_total = jnp.sum(exp_scores, axis=-1, keepdims=True)
    soft_probs = (exp_scores / row_total).astype(jnp.bfloat16)
    mixed_rows = jnp.einsum(
        "hqk,khd->qhd", soft_probs, values_in, preferred_element_type=jnp.float32
    )
    logsum = row_peak + jnp.log(row_total)
    pair_keep = key_keep[:, None] & key_keep[None, :]
    head_top = jnp.max(jnp.where(pair_keep[None], raw_scores, very_negative), axis=(1, 2))
    flat_rows = mixed_rows.astype(jnp.bfloat16).reshape(mixed_rows.shape[0], -1)
    return (flat_rows, logsum, head_top)


def attend_backward(inputs):
    queries, keys_in, values_in, key_keep, logsum, upstream = inputs
    raw_scores, masked = score_block(queries, keys_in, key_keep)
    soft_probs = jnp.exp(masked - logsum)
    probs_low = soft_probs.astype(jnp.bfloat16)
    value_grad = jnp.einsum("hqk,qhd->khd", probs_low, upstream, preferred_element_type=jnp.float32)
    prob_grad = jnp.einsum("qhd,khd->hqk", upstream, values_in, preferred_element_type=jnp.float32)
    inner_sum = jnp.sum(soft_probs * prob_grad, axis=-1, keepdims=True)
    score_grad = (soft_probs * (prob_grad - inner_sum)).astype(jnp.bfloat16)
    score_scale = HD ** (-0.5)
    query_grad = (
        jnp.einsum("hqk,khd->qhd", score_grad, keys_in, preferred_element_type=jnp.float32)
        * score_scale
    )
    key_grad = (
        jnp.einsum("hqk,qhd->khd", score_grad, queries, preferred_element_type=jnp.float32)
        * score_scale
    )
    stacked = jnp.stack([query_grad, key_grad, value_grad], axis=1)
    return stacked.astype(jnp.bfloat16).reshape(stacked.shape[0], 3, -1)


def by_head_local(
    tokens,
    filled,
    out_grad,
    norm1_gain,
    norm1_bias,
    qkv_weight,
    qv_bias,
    out_weight,
    out_bias,
    norm2_gain,
    norm2_bias,
    up_weight,
    up_bias,
    down_weight,
    down_bias,
    clip_threshold,
):
    gathered = (
        lax.all_gather(norm1_gain, "dp", axis=0, tiled=True),
        lax.all_gather(norm1_bias, "dp", axis=0, tiled=True),
        lax.all_gather(qkv_weight, "dp", axis=0, tiled=True),
        lax.all_gather(qv_bias, "dp", axis=0, tiled=True),
        lax.all_gather(out_weight, "dp", axis=0, tiled=True),
        lax.all_gather(out_bias, "dp", axis=0, tiled=True),
        lax.all_gather(norm2_gain, "dp", axis=0, tiled=True),
        lax.all_gather(norm2_bias, "dp", axis=0, tiled=True),
        lax.all_gather(up_weight, "dp", axis=0, tiled=True),
        lax.all_gather(up_bias, "dp", axis=0, tiled=True),
        lax.all_gather(down_weight, "dp", axis=0, tiled=True),
        lax.all_gather(down_bias, "dp", axis=0, tiled=True),
    )
    (
        gain_one,
        shift_one,
        w_qkv,
        b_qv,
        w_out,
        b_out,
        gain_two,
        shift_two,
        w_up,
        b_up,
        w_down,
        b_down,
    ) = gathered
    images, local_rows, model_width = tokens.shape
    groups = lax.axis_size("seq")
    group_width = model_width // groups
    local_heads = group_width // HD
    length = local_rows * groups
    row_count = images * local_rows
    tokens_flat = tokens.astype(jnp.float32).reshape(row_count, model_width)
    gain_one_f = gain_one.astype(jnp.float32)
    shift_one_f = shift_one.astype(jnp.float32)
    gain_two_f = gain_two.astype(jnp.float32)
    shift_two_f = shift_two.astype(jnp.float32)
    hidden_one = norm_apply(tokens_flat, gain_one_f, shift_one_f).astype(jnp.bfloat16)
    bias_float = b_qv.astype(jnp.float32)
    qkv_bias = jnp.concatenate(
        [bias_float[:model_width], jnp.zeros((model_width,), jnp.float32), bias_float[model_width:]]
    )
    projected = (jnp.dot(hidden_one, w_qkv, preferred_element_type=jnp.float32) + qkv_bias).astype(
        jnp.bfloat16
    )
    key_flags = lax.all_gather(filled, "seq", axis=1, tiled=True)
    keep_all = key_flags > 0
    by_heads = lax.all_to_all(
        projected.reshape(images, local_rows, 3, groups, group_width),
        "seq",
        split_axis=3,
        concat_axis=1,
        tiled=True,
    )
    by_heads = by_heads.reshape(images, length, 3, local_heads, HD)
    queries = by_heads[:, :, 0]
    keys_all = by_heads[:, :, 1]
    values_all = by_heads[:, :, 2]
    attended, logsums, tops = lax.map(attend_forward, (queries, keys_all, values_all, keep_all))
    local_peak = jnp.max(tops, axis=0)
    peak_vector = lax.dynamic_update_slice(
        jnp.full((H,), very_negative, jnp.float32),
        local_peak,
        (lax.axis_index("seq") * local_heads,),
    )
    head_max = lax.pmax(peak_vector, ("dp", "seq"))
    back_rows = lax.all_to_all(
        attended.reshape(images, groups, local_rows, group_width),
        "seq",
        split_axis=1,
        concat_axis=3,
        tiled=True,
    )
    attn_rows = back_rows.reshape(row_count, model_width)
    branch = jnp.dot(attn_rows, w_out, preferred_element_type=jnp.float32) + b_out.astype(
        jnp.float32
    )
    middle = tokens_flat + branch
    hidden_two = norm_apply(middle, gain_two_f, shift_two_f).astype(jnp.bfloat16)
    pre_act = jnp.dot(hidden_two, w_up, preferred_element_type=jnp.float32) + b_up.astype(
        jnp.float32
    )
    activated = exact_gelu(pre_act).astype(jnp.bfloat16)
    block_rows = middle + (
        jnp.dot(activated, w_down, preferred_element_type=jnp.float32) + b_down.astype(jnp.float32)
    )
    block_out = block_rows.astype(jnp.bfloat16).reshape(tokens.shape)
    gain_one_b, w_qkv_b, w_out_b, gain_two_b, w_up_b, w_down_b = (
        lax.all_gather(norm1_gain, "dp", axis=0, tiled=True),
        lax.all_gather(qkv_weight, "dp", axis=0, tiled=True),
        lax.all_gather(out_weight, "dp", axis=0, tiled=True),
        lax.all_gather(norm2_gain, "dp", axis=0, tiled=True),
        lax.all_gather(up_weight, "dp", axis=0, tiled=True),
        lax.all_gather(down_weight, "dp", axis=0, tiled=True),
    )
    upstream = out_grad.reshape(row_count, model_width)
    upstream_f = upstream.astype(jnp.float32)
    d_bias_down = jnp.sum(upstream_f, axis=0)
    d_down = first_dot(activated, upstream)
    act_grad = last_dot(upstream, w_down_b)
    gelu_out, gelu_pull = jax.vjp(exact_gelu, pre_act)
    pre_grad = gelu_pull(act_grad)[0].astype(jnp.bfloat16)
    d_bias_up = column_sum(pre_grad)
    d_up = first_dot(hidden_two, pre_grad)
    hidden_two_grad = last_dot(pre_grad, w_up_b)
    norm_out_two, pull_two = jax.vjp(
        norm_apply, middle, gain_two_b.astype(jnp.float32), shift_two_f
    )
    mid_norm_grad, d_gain_two, d_shift_two = pull_two(hidden_two_grad)
    middle_grad = upstream_f + mid_norm_grad
    branch_grad = middle_grad.astype(jnp.bfloat16)
    d_bias_out = column_sum(branch_grad)
    d_out = first_dot(attn_rows, branch_grad)
    attn_grad = last_dot(branch_grad, w_out_b).astype(jnp.bfloat16)
    grad_heads = lax.all_to_all(
        attn_grad.reshape(images, local_rows, groups, group_width),
        "seq",
        split_axis=2,
        concat_axis=1,
        tiled=True,
    )
    grad_heads = grad_heads.reshape(images, length, local_heads, HD)
    head_grads = lax.map(
        attend_backward, (queries, keys_all, values_all, keep_all, logsums, grad_heads)
    )
    token_grads = lax.all_to_all(
        head_grads.reshape(images, groups, local_rows, 3, group_width),
        "seq",
        split_axis=1,
        concat_axis=4,
        tiled=True,
    )
    token_grads = token_grads.reshape(row_count, 3 * model_width)
    d_qkv = first_dot(hidden_one, token_grads)
    bias_sums = column_sum(token_grads)
    d_bias_qv = jnp.concatenate([bias_sums[:model_width], bias_sums[2 * model_width :]])
    first_grad = last_dot(token_grads, w_qkv_b)
    norm_out_one, pull_one = jax.vjp(
        norm_apply, tokens_flat, gain_one_b.astype(jnp.float32), shift_one_f
    )
    in_norm_grad, d_gain_one, d_shift_one = pull_one(first_grad)
    tokens_grad = (middle_grad + in_norm_grad).astype(jnp.bfloat16).reshape(tokens.shape)
    terms = (
        d_gain_one,
        d_shift_one,
        d_qkv,
        d_bias_qv,
        d_out,
        d_bias_out,
        d_gain_two,
        d_shift_two,
        d_up,
        d_bias_up,
        d_down,
        d_bias_down,
    )
    data_shards = (
        lax.psum_scatter(
            terms[0].astype(jnp.bfloat16), "dp", scatter_dimension=0, tiled=True
        ).astype(jnp.float32),
        lax.psum_scatter(
            terms[1].astype(jnp.bfloat16), "dp", scatter_dimension=0, tiled=True
        ).astype(jnp.float32),
        lax.psum_scatter(
            terms[2].astype(jnp.bfloat16), "dp", scatter_dimension=0, tiled=True
        ).astype(jnp.float32),
        lax.psum_scatter(
            terms[3].astype(jnp.bfloat16), "dp", scatter_dimension=0, tiled=True
        ).astype(jnp.float32),
        lax.psum_scatter(
            terms[4].astype(jnp.bfloat16), "dp", scatter_dimension=0, tiled=True
        ).astype(jnp.float32),
        lax.psum_scatter(
            terms[5].astype(jnp.bfloat16), "dp", scatter_dimension=0, tiled=True
        ).astype(jnp.float32),
        lax.psum_scatter(
            terms[6].astype(jnp.bfloat16), "dp", scatter_dimension=0, tiled=True
        ).astype(jnp.float32),
        lax.psum_scatter(
            terms[7].astype(jnp.bfloat16), "dp", scatter_dimension=0, tiled=True
        ).astype(jnp.float32),
        lax.psum_scatter(
            terms[8].astype(jnp.bfloat16), "dp", scatter_dimension=0, tiled=True
        ).astype(jnp.float32),
        lax.psum_scatter(
            terms[9].astype(jnp.bfloat16), "dp", scatter_dimension=0, tiled=True
        ).astype(jnp.float32),
        lax.psum_scatter(
            terms[10].astype(jnp.bfloat16), "dp", scatter_dimension=0, tiled=True
        ).astype(jnp.float32),
        lax.psum_scatter(
            terms[11].astype(jnp.bfloat16), "dp", scatter_dimension=0, tiled=True
        ).astype(jnp.float32),
    )
    shards = (
        lax.psum(data_shards[0].astype(jnp.bfloat16), "seq").astype(jnp.float32),
        lax.psum(data_shards[1].astype(jnp.bfloat16), "seq").astype(jnp.float32),
        lax.psum(data_shards[2].astype(jnp.bfloat16), "seq").astype(jnp.float32),
        lax.psum(data_shards[3].astype(jnp.bfloat16), "seq").astype(jnp.float32),
        lax.psum(data_shards[4].astype(jnp.bfloat16), "seq").astype(jnp.float32),
        lax.psum(data_shards[5].astype(jnp.bfloat16), "seq").astype(jnp.float32),
        lax.psum(data_shards[6].astype(jnp.bfloat16), "seq").astype(jnp.float32),
        lax.psum(data_shards[7].astype(jnp.bfloat16), "seq").astype(jnp.float32),
        lax.psum(data_shards[8].astype(jnp.bfloat16), "seq").astype(jnp.float32),
        lax.psum(data_shards[9].astype(jnp.bfloat16), "seq").astype(jnp.float32),
        lax.psum(data_shards[10].astype(jnp.bfloat16), "seq").astype(jnp.float32),
        lax.psum(data_shards[11].astype(jnp.bfloat16), "seq").astype(jnp.float32),
    )
    limit = clip_threshold.astype(jnp.float32)
    root_factor = jnp.sqrt(limit / jnp.maximum(head_max, limit))
    head_cols = jnp.repeat(root_factor, HD)
    weight_scale = jnp.concatenate([head_cols, head_cols, jnp.ones((model_width,), jnp.float32)])
    clipped_weight = (qkv_weight.astype(jnp.float32) * weight_scale[None, :]).astype(jnp.bfloat16)
    bias_count = qv_bias.shape[0]
    bias_scale = jnp.concatenate([head_cols, jnp.ones((model_width,), jnp.float32)])
    shard_scale = lax.dynamic_slice_in_dim(
        bias_scale, lax.axis_index("dp") * bias_count, bias_count
    )
    clipped_bias = (qv_bias.astype(jnp.float32) * shard_scale).astype(jnp.bfloat16)
    return (
        block_out,
        tokens_grad,
        shards[0],
        shards[1],
        shards[2],
        shards[3],
        shards[4],
        shards[5],
        shards[6],
        shards[7],
        shards[8],
        shards[9],
        shards[10],
        shards[11],
        clipped_weight,
        clipped_bias,
        head_max,
    )


MESH = pl.DeviceIdType.MESH
BF = jnp.bfloat16
F32 = jnp.float32
SMALL = (128, 128, 256, 128, 128, 128, 512, 128)


def flip(d, m):
    y = lax.rem(lax.div(d, 4) + m // 4, 2)
    x = lax.rem(lax.rem(lax.div(d, 2), 2) + (m // 2) % 2, 2)
    k = lax.rem(lax.rem(d, 2) + m % 2, 2)
    return 4 * y + 2 * x + k


def flip_traced(d, m):
    y = lax.rem(lax.div(d, 4) + lax.div(m, 4), 2)
    x = lax.rem(lax.rem(lax.div(d, 2), 2) + lax.rem(lax.div(m, 2), 2), 2)
    k = lax.rem(lax.rem(d, 2) + lax.rem(m, 2), 2)
    return 4 * y + 2 * x + k


def dot_nn(a, b):
    return lax.dot_general(a, b, (((1,), (0,)), ((), ())), preferred_element_type=F32)


def dot_nt(a, b):
    return lax.dot_general(a, b, (((1,), (1,)), ((), ())), preferred_element_type=F32)


def dot_tn(a, b):
    return lax.dot_general(a, b, (((0,), (0,)), ((), ())), preferred_element_type=F32)


def rows_of(block, size, start=0, count=None):
    count = size if count is None else count
    step = math.gcd(size, start) if start else size
    return pl.ds(pl.multiple_of(block * size + start, step), count)


def normalized(v):
    center = jnp.mean(v, axis=-1, keepdims=True)
    centered = v - center
    spread = jnp.mean(centered * centered, axis=-1, keepdims=True)
    scale = lax.rsqrt(spread + epsilon)
    return centered * scale, scale


def half_masks():
    lane = lax.broadcasted_iota(jnp.int32, (1, 2 * HD), 1)
    low = jnp.where(lane < HD, 1.0, 0.0)
    return low.astype(BF), (1.0 - low).astype(BF), lane < HD


def front_kernel(
    tok_in, grad_in, fil_in, wq_in, wo_in, wu_in, wd_in, small_in,
    out_h, tok_h, h1_h, qkv_h, gx_h, go_h, dwo_h, dwu_h, dwd_h, wq_h,
    vec_o, dbup_o, top_o, mask_o,
    wq, wo, wu, wd, tok, grad, h1, qkv, att, x1, h2, h2t, y, dh, fil, small, col, dst, ust,
    own_s, own_r, rel_s, rel_r, fwd_s, fwd_r, tok_s, tok_r, fil_s, fil_r, sm_s, sm_r, loc, stg, hout,
):
    d, s = lax.axis_index("dp"), lax.axis_index("seq")
    images, part, width = tok_in.shape
    length = images * part
    pair_count = width // (2 * HD)
    weights = ((wq_in, wq), (wo_in, wo), (wu_in, wu), (wd_in, wd))
    sib, xn, yn, dn = flip(d, 1), flip(d, 2), flip(d, 4), flip(d, 6)

    barrier = pltpu.get_barrier_semaphore()
    for m in range(1, 8):
        pl.semaphore_signal(barrier, inc=1, device_id=(flip(d, m), s), device_id_type=MESH)
    for j in range(1, images):
        pl.semaphore_signal(
            barrier, inc=1, device_id=(d, lax.rem(s + j, images)), device_id_type=MESH
        )
    pl.semaphore_wait(barrier, 7 + images - 1)

    def send(src, dst, ss, rs, to_dp, to_seq):
        return pltpu.make_async_remote_copy(
            src_ref=src, dst_ref=dst, send_sem=ss, recv_sem=rs,
            device_id=(to_dp, to_seq), device_id_type=MESH,
        )

    def exchange(src, dst, ss, rs, rows):
        copies = []
        for j in range(1, images):
            to = lax.rem(s + j, images)
            copies.append(send(src.at[to], dst.at[rows], ss.at[j - 1], rs.at[j - 1], d, to))
        return copies

    my_rows = rows_of(s, part)
    sm_copies = [
        send(small_in, small.at[d], sm_s.at[m - 1], sm_r.at[m - 1], flip(d, m), s)
        for m in range(1, 8)
    ]
    fil_copies = exchange(fil_in, fil, fil_s, fil_r, s)
    tok_copies = exchange(tok_in, tok, tok_s.at[0], tok_r.at[0], my_rows)
    grad_copies = exchange(grad_in, grad, tok_s.at[1], tok_r.at[1], my_rows)

    def own(w):
        src, dst = weights[w]
        size = src.shape[0]
        half = size // 2
        def piece(way, to, h):
            return send(
                src.at[pl.ds(h * half, half)], dst.at[rows_of(d, size, h * half, half)],
                own_s.at[w, way, h], own_r.at[w, way, h], to, s,
            )
        return [
            piece(0, xn, 0), piece(1, yn, 1), piece(0, xn, 1), piece(1, yn, 0),
            send(src, dst.at[rows_of(d, size)], own_s.at[w, 2, 0], own_r.at[w, 2, 0], sib, s),
        ]

    def relays(w):
        dst = weights[w][1]
        size = weights[w][0].shape[0]
        half = size // 2
        lower, upper = rows_of(xn, size, 0, half), rows_of(yn, size, half, half)
        return [
            send(dst.at[lower], dst.at[lower], rel_s.at[w, 0], rel_r.at[w, 0], yn, s),
            send(dst.at[upper], dst.at[upper], rel_s.at[w, 1], rel_r.at[w, 1], xn, s),
        ]

    def forwards(w):
        dst = weights[w][1]
        size = weights[w][0].shape[0]
        return [
            send(dst.at[rows_of(b, size)], dst.at[rows_of(b, size)],
                 fwd_s.at[w, i], fwd_r.at[w, i], sib, s)
            for i, b in enumerate((xn, yn, dn))
        ]

    def start_own(w):
        for copy in own(w):
            copy.start()

    def on_first(w):
        mine, relay, forward = own(w), relays(w), forwards(w)
        mine[0].wait_recv()
        relay[0].start()
        mine[1].wait_recv()
        relay[1].start()
        mine[2].wait_recv()
        forward[0].start()
        mine[3].wait_recv()
        forward[1].start()

    def on_diag(w):
        relay = relays(w)
        relay[0].wait_recv()
        relay[1].wait_recv()
        forwards(w)[2].start()

    def on_sib(w):
        own(w)[4].wait_recv()
        for copy in forwards(w):
            copy.wait_recv()

    def drain(w):
        for copy in own(w) + relays(w) + forwards(w):
            copy.wait_send()

    def keep_own(w):
        src, dst = weights[w]
        return pltpu.make_async_copy(src, dst.at[rows_of(d, src.shape[0])], loc.at[w])

    for copy in sm_copies + fil_copies:
        copy.start()
    start_own(0)
    for copy in tok_copies:
        copy.start()
    start_own(1)
    locals_ = [keep_own(w) for w in range(4)]
    locals_ += [
        pltpu.make_async_copy(tok_in.at[s], tok.at[my_rows], loc.at[4]),
        pltpu.make_async_copy(grad_in.at[s], grad.at[my_rows], loc.at[5]),
        pltpu.make_async_copy(fil_in.at[s], fil.at[s], loc.at[6]),
        pltpu.make_async_copy(small_in, small.at[d], loc.at[7]),
    ]
    for copy in locals_:
        copy.start()

    on_first(0)
    start_own(2)

    for copy in sm_copies + fil_copies:
        copy.wait_recv()
    for copy in locals_:
        copy.wait()

    starts = [sum(SMALL[:i]) for i in range(len(SMALL))]

    def vector(i, first=0, last=8):
        return jnp.concatenate(
            [small[b, :, starts[i] : starts[i] + SMALL[i]] for b in range(first, last)], axis=1
        )

    mask = fil[0] + fil[1] + fil[2] + fil[3]
    mask_o[...] = mask
    col[...] = jnp.transpose(mask)

    for copy in tok_copies:
        copy.wait_recv()
    for copy in grad_copies:
        copy.start()

    block = 128
    gain1, shift1 = vector(0), vector(1)

    @pl.loop(0, length // block)
    def _(i):
        r = rows_of(i, block)
        xh, _ = normalized(tok[r, :].astype(F32))
        h1[r, :] = (xh * gain1 + shift1).astype(BF)

    on_diag(0)
    on_first(1)
    on_sib(0)

    tile = 512
    qkv_bias = jnp.concatenate(
        [vector(2, 0, 4), jnp.zeros((1, width), F32), vector(2, 4, 8)], axis=1
    )
    y[pl.ds(0, 1), :] = qkv_bias[:, :width]
    y[pl.ds(8, 1), :] = qkv_bias[:, width : 2 * width]
    y[pl.ds(16, 1), :] = qkv_bias[:, 2 * width :]

    for third in range(3):
        @pl.loop(0, width // tile)
        def _(n):
            c = pl.ds(pl.multiple_of(n * tile, tile), tile)
            cw = pl.ds(pl.multiple_of(third * width + n * tile, tile), tile)
            value = dot_nn(h1[...], wq[:, cw]) + y[pl.ds(8 * third, 1), c]
            qkv[:, cw] = value.astype(BF)

    saves = [
        pltpu.make_async_copy(tok, tok_h, hout.at[0]),
        pltpu.make_async_copy(h1, h1_h, hout.at[1]),
        pltpu.make_async_copy(qkv, qkv_h, hout.at[2]),
        pltpu.make_async_copy(wq, wq_h, hout.at[3]),
    ]
    for copy in saves:
        copy.start()

    low, high, low_lane = half_masks()
    pad = (mask[0:1, :] - 1.0) * 1e30
    pad2 = jnp.concatenate([pad, pad], axis=1)
    chunk = length // 2

    def attend(p, carry):
        c = pl.ds(pl.multiple_of(p * 2 * HD, 2 * HD), 2 * HD)
        ck = pl.ds(pl.multiple_of(width + p * 2 * HD, 2 * HD), 2 * HD)
        cv = pl.ds(pl.multiple_of(2 * width + p * 2 * HD, 2 * HD), 2 * HD)
        k, v = qkv[:, ck], qkv[:, cv]
        k2 = jnp.concatenate([k * low, k * high], axis=0)
        v2 = jnp.concatenate([v * low, v * high], axis=0)
        best = [jnp.full((1, 1), very_negative, F32)] * 2
        for j in range(2):
            r = pl.ds(j * chunk, chunk)
            q = qkv[r, c] * jnp.asarray(HD ** (-0.5), BF)
            scores = dot_nt(q, k2) + pad2
            probs = []
            for side in range(2):
                part_s = scores[:, side * length : (side + 1) * length]
                peak = jnp.max(part_s, axis=1, keepdims=True)
                e = jnp.exp(part_s - peak)
                total = jnp.sum(e, axis=1, keepdims=True)
                probs.append((e * (1.0 / total)).astype(BF))
                held = jnp.where(col[r, 0:1] > 0.5, peak, very_negative)
                best[side] = jnp.maximum(best[side], jnp.max(held, axis=0, keepdims=True))
            att[r, c] = dot_nn(jnp.concatenate(probs, axis=1), v2).astype(BF)
        top_o[pl.ds(p, 1), :] = jnp.where(
            low_lane, jnp.broadcast_to(best[0], (1, 2 * HD)), jnp.broadcast_to(best[1], (1, 2 * HD))
        )
        return carry

    early = (pair_count * 5) // 8
    lax.fori_loop(0, early, attend, 0)
    on_first(2)
    start_own(3)
    lax.fori_loop(early, pair_count, attend, 0)
    on_diag(1)
    on_sib(1)

    gain2, shift2, b_out, b_down = vector(4), vector(5), vector(3), vector(7)

    @pl.loop(0, length // block)
    def _(i):
        r = rows_of(i, block)
        mid = tok[r, :].astype(F32) + dot_nn(att[r, :], wo[...]) + b_out
        x1[r, :] = mid
        xh, _ = normalized(mid)
        h2[r, :] = (xh * gain2 + shift2).astype(BF)

    h2t[...] = jnp.transpose(h2[...])
    dbup_o[...] = vector(6)
    y[...] = x1[...] + b_down
    dh[...] = jnp.zeros_like(dh)
    for copy in grad_copies:
        copy.wait_recv()

    def add_grad(i, acc):
        return acc + jnp.sum(grad[rows_of(i, block), :].astype(F32), axis=0, keepdims=True)

    grad_sum = lax.fori_loop(0, length // block, add_grad, jnp.zeros((1, width), F32))

    on_diag(2)
    on_sib(2)

    ff_block = wd_in.shape[0]

    def stage_copies(slot, b):
        cols = pl.ds(pl.multiple_of(b * ff_block, ff_block), ff_block)
        return (
            pltpu.make_async_copy(dst.at[slot], dwd_h.at[rows_of(b, ff_block)], stg.at[0, slot]),
            pltpu.make_async_copy(ust.at[slot], dwu_h.at[:, cols], stg.at[1, slot]),
        )

    def mlp(i, carry):
        b = flip_traced(d, i)
        slot = lax.rem(i, 2)

        @pl.when(i == 1)
        def _():
            own(3)[4].wait_recv()

        @pl.when(i == 2)
        def _():
            on_first(3)

        for at, which in ((3, 0), (5, 1), (7, 2)):
            @pl.when(i == at)
            def _():
                forwards(3)[which].wait_recv()

        @pl.when(i == 6)
        def _():
            on_diag(3)

        cols = pl.ds(pl.multiple_of(b * ff_block, ff_block), ff_block)
        rows = rows_of(b, ff_block)
        u = dot_nn(h2[...], wu[:, cols]) + dbup_o[:, cols]
        phi = 0.5 * (1.0 + lax.erf(u * (0.5**0.5)))
        a = (u * phi).astype(BF)
        slope = phi + u * (jnp.exp(-0.5 * u * u) * (1.0 / math.sqrt(2.0 * math.pi)))
        gu_f = dot_nt(grad[...], wd[rows, :]) * slope
        gu = gu_f.astype(BF)
        y[...] += dot_nn(a, wd[rows, :])
        dh[...] += dot_nt(gu, wu[:, cols])

        @pl.when(i >= 2)
        def _():
            for copy in stage_copies(slot, b):
                copy.wait()

        dbup_o[:, cols] = jnp.sum(gu.astype(F32), axis=0, keepdims=True)
        dst[slot] = dot_tn(a, grad[...]).astype(BF)
        ust[slot] = dot_nn(h2t[...], gu).astype(BF)
        for copy in stage_copies(slot, b):
            copy.start()
        return carry

    lax.fori_loop(0, 8, mlp, 0)

    for slot in range(2):
        for copy in stage_copies(slot, d):
            copy.wait()
    for copy in saves:
        copy.wait()
    for w in range(4):
        drain(w)
    for copy in sm_copies + fil_copies + tok_copies + grad_copies:
        copy.wait_send()

    zero = jnp.zeros((1, width), F32)

    def norm_back(i, acc):
        r = rows_of(i, block)
        h1[r, :] = y[r, :].astype(BF)
        g = dh[r, :]
        xh, scale = normalized(x1[r, :])
        gg = g * gain2
        inner = gg - jnp.mean(gg, axis=1, keepdims=True)
        inner = inner - xh * jnp.mean(gg * xh, axis=1, keepdims=True)
        total = grad[r, :].astype(F32) + scale * inner
        dh[r, :] = total
        low_total = total.astype(BF)
        h2[r, :] = low_total
        tok[r, :] = dot_nt(low_total, wo[...]).astype(BF)
        return (
            acc[0] + jnp.sum(g * xh, axis=0, keepdims=True),
            acc[1] + jnp.sum(g, axis=0, keepdims=True),
            acc[2] + jnp.sum(low_total.astype(F32), axis=0, keepdims=True),
        )

    sums = lax.fori_loop(0, length // block, norm_back, (zero, zero, zero))
    finals = [
        pltpu.make_async_copy(h1, out_h, hout.at[4]),
        pltpu.make_async_copy(dh, gx_h, hout.at[5]),
        pltpu.make_async_copy(tok, go_h, hout.at[6]),
        pltpu.make_async_copy(wo, dwo_h, hout.at[7]),
    ]
    for copy in finals[:3]:
        copy.start()
    vec_o[pl.ds(0, 1), :] = sums[0]
    vec_o[pl.ds(1, 1), :] = sums[1]
    vec_o[pl.ds(2, 1), :] = sums[2]
    vec_o[pl.ds(3, 1), :] = grad_sum
    h2t[...] = jnp.transpose(att[...])

    @pl.loop(0, width // tile)
    def _(n):
        c = pl.ds(pl.multiple_of(n * tile, tile), tile)
        wo[:, c] = dot_nn(h2t[...], h2[:, c]).astype(BF)

    finals[3].start()
    for copy in finals:
        copy.wait()


def front(tokens, out_grad, filled_rows, qkv_weight, out_weight, up_weight, down_weight, small):
    images, part, width = tokens.shape
    length = images * part
    shards = lax.axis_size("dp")
    ff = up_weight.shape[1]
    wide = qkv_weight.shape[1]
    shape = jax.ShapeDtypeStruct
    any_spec = pl.BlockSpec(memory_space=pl.ANY)
    vmem_spec = pl.BlockSpec(memory_space=pltpu.VMEM)
    dma = pltpu.SemaphoreType.DMA
    vm = pltpu.VMEM
    return pl.pallas_call(
        front_kernel,
        name="front",
        out_shape=(
            shape((length, width), BF),
            shape((length, width), BF),
            shape((length, width), BF),
            shape((length, wide), BF),
            shape((length, width), F32),
            shape((length, width), BF),
            shape((width, width), BF),
            shape((width, ff), BF),
            shape((ff, width), BF),
            shape((width, wide), BF),
            shape((8, width), F32),
            shape((1, ff), F32),
            shape((8, 2 * HD), F32),
            shape((8, length), F32),
        ),
        in_specs=[any_spec] * 8,
        out_specs=[any_spec] * 10 + [vmem_spec] * 4,
        scratch_shapes=[
            vm((width, wide), BF), vm((width, width), BF), vm((width, ff), BF), vm((ff, width), BF),
            vm((length, width), BF), vm((length, width), BF), vm((length, width), BF),
            vm((length, wide), BF), vm((length, width), BF), vm((length, width), F32),
            vm((length, width), BF), vm((width, length), BF), vm((length, width), F32),
            vm((length, width), F32), vm((images, 8, length), F32), vm((shards, 1, sum(SMALL)), F32),
            vm((length, 8), F32), vm((2, down_weight.shape[0], width), BF),
            vm((2, width, down_weight.shape[0]), BF),
            dma((4, 3, 2)), dma((4, 3, 2)), dma((4, 2)), dma((4, 2)), dma((4, 3)), dma((4, 3)),
            dma((2, images - 1)), dma((2, images - 1)), dma((images - 1,)), dma((images - 1,)),
            dma((7,)), dma((7,)), dma((8,)), dma((2, 2)), dma((8,)),
        ],
        compiler_params=pltpu.CompilerParams(
            collective_id=0, has_side_effects=True, vmem_limit_bytes=60 << 20
        ),
    )(tokens, out_grad, filled_rows, qkv_weight, out_weight, up_weight, down_weight, small)


def by_image_local(
    tokens,
    filled,
    out_grad,
    norm1_gain,
    norm1_bias,
    qkv_weight,
    qv_bias,
    out_weight,
    out_bias,
    norm2_gain,
    norm2_bias,
    up_weight,
    up_bias,
    down_weight,
    down_bias,
    clip_threshold,
):
    images, local_rows, model_width = tokens.shape
    length = local_rows * images
    seq_index = lax.axis_index("seq")
    small = jnp.concatenate(
        [norm1_gain, norm1_bias, qv_bias, out_bias, norm2_gain, norm2_bias, up_bias, down_bias]
    ).astype(F32)[None]
    flags = lax.dynamic_update_slice(
        jnp.zeros((images, 8, length), F32),
        jnp.broadcast_to((filled > 0).astype(F32)[:, None, :], (images, 8, local_rows)),
        (0, 0, seq_index * local_rows),
    )
    (
        block_rows, tokens_low, hidden_one, projected, middle_grad, attn_grad,
        d_out, d_up, d_down, w_qkv, vec, d_bias_up, tops, mask,
    ) = front(tokens, out_grad, flags, qkv_weight, out_weight, up_weight, down_weight, small)
    gain_one = lax.all_gather(norm1_gain, "dp", axis=0, tiled=True).astype(F32)
    shift_one = jnp.zeros_like(gain_one)
    d_gain_two, d_shift_two, d_bias_out, d_bias_down = vec[0], vec[1], vec[2], vec[3]
    d_bias_up = d_bias_up[0]
    keep = mask[0] > 0.5
    head_max = lax.pmax(tops[:, ::HD].reshape(-1), ("dp", "seq"))
    tokens_flat = tokens_low.astype(F32)

    def from_image(rows):
        return lax.all_to_all(
            rows.reshape(1, length, -1), "seq", split_axis=1, concat_axis=0, tiled=True
        )

    block_out = from_image(block_rows).reshape(tokens.shape)
    heads_view = projected.reshape(length, 3, H, HD)
    queries, keys_all, values_all = heads_view[:, 0], heads_view[:, 1], heads_view[:, 2]
    masked = score_block(queries, keys_all, keep)[1]
    logsum = jax.nn.logsumexp(masked, axis=-1, keepdims=True)
    token_grads = attend_backward(
        (queries, keys_all, values_all, keep, logsum, attn_grad.reshape(length, H, HD))
    ).reshape(length, 3 * model_width)
    d_qkv = first_dot(hidden_one, token_grads)
    bias_sums = column_sum(token_grads)
    d_bias_qv = jnp.concatenate([bias_sums[:model_width], bias_sums[2 * model_width :]])
    first_grad = last_dot(token_grads, w_qkv)
    norm_out_one, pull_one = jax.vjp(norm_apply, tokens_flat, gain_one, shift_one)
    in_norm_grad, d_gain_one, d_shift_one = pull_one(first_grad)
    tokens_grad = from_image((middle_grad + in_norm_grad).astype(jnp.bfloat16)).reshape(
        tokens.shape
    )

    def reduce_matrix(term):
        part = lax.psum_scatter(
            term.astype(jnp.bfloat16), "dp", scatter_dimension=0, tiled=True
        )
        return lax.psum(part, "seq").astype(jnp.float32)

    small_terms = [
        d_gain_one,
        d_shift_one,
        d_bias_qv,
        d_bias_out,
        d_gain_two,
        d_shift_two,
        d_bias_up,
        d_bias_down,
    ]
    shards = lax.axis_size("dp")
    packed = jnp.concatenate([term.reshape(shards, -1) for term in small_terms], axis=1)
    mine = lax.psum(
        lax.psum_scatter(packed, "dp", scatter_dimension=0, tiled=True), "seq"
    ).reshape(-1)
    small_out, start = [], 0
    for term in small_terms:
        size = term.shape[0] // shards
        small_out.append(mine[start : start + size])
        start += size
    s_gain_one, s_shift_one, s_qv, s_out, s_gain_two, s_shift_two, s_up, s_down = small_out
    limit = clip_threshold.astype(jnp.float32)
    root_factor = jnp.sqrt(limit / jnp.maximum(head_max, limit))
    head_cols = jnp.repeat(root_factor, HD)
    weight_scale = jnp.concatenate([head_cols, head_cols, jnp.ones((model_width,), jnp.float32)])
    clipped_weight = (qkv_weight.astype(jnp.float32) * weight_scale[None, :]).astype(jnp.bfloat16)
    bias_count = qv_bias.shape[0]
    bias_scale = jnp.concatenate([head_cols, jnp.ones((model_width,), jnp.float32)])
    shard_scale = lax.dynamic_slice_in_dim(
        bias_scale, lax.axis_index("dp") * bias_count, bias_count
    )
    clipped_bias = (qv_bias.astype(jnp.float32) * shard_scale).astype(jnp.bfloat16)
    return (
        block_out,
        tokens_grad,
        s_gain_one,
        s_shift_one,
        reduce_matrix(d_qkv),
        s_qv,
        reduce_matrix(d_out),
        s_out,
        s_gain_two,
        s_shift_two,
        reduce_matrix(d_up),
        s_up,
        reduce_matrix(d_down),
        s_down,
        clipped_weight,
        clipped_bias,
        head_max,
    )


def local(*args):
    if args[0].shape[0] == lax.axis_size("seq") and lax.axis_size("dp") == 8:
        return by_image_local(*args)
    return by_head_local(*args)


def solution(mesh):
    return jax.shard_map(
        local,
        mesh=mesh,
        in_specs=(
            P("dp", "seq", None),
            P("dp", "seq"),
            P("dp", "seq", None),
            P("dp"),
            P("dp"),
            P("dp", None),
            P("dp"),
            P("dp", None),
            P("dp"),
            P("dp"),
            P("dp"),
            P("dp", None),
            P("dp"),
            P("dp", None),
            P("dp"),
            P(),
        ),
        out_specs=(
            P("dp", "seq", None),
            P("dp", "seq", None),
            P("dp"),
            P("dp"),
            P("dp", None),
            P("dp"),
            P("dp", None),
            P("dp"),
            P("dp"),
            P("dp"),
            P("dp", None),
            P("dp"),
            P("dp", None),
            P("dp"),
            P("dp", None),
            P("dp"),
            P(),
        ),
        check_vma=False,
    )
```

```python
import math

import jax
import jax.numpy as jnp
from jax import lax
from jax.experimental import pallas as pl
from jax.experimental.pallas import tpu as pltpu
from jax.sharding import PartitionSpec as P

H = 16
HD = 64


epsilon = 1e-06
very_negative = -1e30


def norm_apply(values, gain_vec, shift_vec):
    center = jnp.mean(values, axis=-1, keepdims=True)
    centered = values - center
    spread = jnp.mean(centered * centered, axis=-1, keepdims=True)
    return centered * lax.rsqrt(spread + epsilon) * gain_vec + shift_vec


def exact_gelu(values):
    return jax.nn.gelu(values, approximate=False)


def last_dot(left_op, right_op):
    return lax.dot_general(
        left_op, right_op, (((1,), (1,)), ((), ())), preferred_element_type=jnp.float32
    )


def first_dot(left_op, right_op):
    return lax.dot_general(
        left_op, right_op, (((0,), (0,)), ((), ())), preferred_element_type=jnp.float32
    )


def column_sum(values):
    return jnp.sum(values.astype(jnp.float32), axis=0)


def score_block(queries, keys_in, key_keep):
    raw_scores = jnp.einsum(
        "qhd,khd->hqk", queries, keys_in, preferred_element_type=jnp.float32
    ) * HD ** (-0.5)
    masked = jnp.where(key_keep[None, None, :], raw_scores, very_negative)
    return (raw_scores, masked)


def attend_forward(inputs):
    queries, keys_in, values_in, key_keep = inputs
    raw_scores, masked = score_block(queries, keys_in, key_keep)
    row_peak = jnp.max(masked, axis=-1, keepdims=True)
    exp_scores = jnp.exp(masked - row_peak)
    row_total = jnp.sum(exp_scores, axis=-1, keepdims=True)
    soft_probs = (exp_scores / row_total).astype(jnp.bfloat16)
    mixed_rows = jnp.einsum(
        "hqk,khd->qhd", soft_probs, values_in, preferred_element_type=jnp.float32
    )
    logsum = row_peak + jnp.log(row_total)
    pair_keep = key_keep[:, None] & key_keep[None, :]
    head_top = jnp.max(jnp.where(pair_keep[None], raw_scores, very_negative), axis=(1, 2))
    flat_rows = mixed_rows.astype(jnp.bfloat16).reshape(mixed_rows.shape[0], -1)
    return (flat_rows, logsum, head_top)


def attend_backward(inputs):
    queries, keys_in, values_in, key_keep, logsum, upstream = inputs
    raw_scores, masked = score_block(queries, keys_in, key_keep)
    soft_probs = jnp.exp(masked - logsum)
    probs_low = soft_probs.astype(jnp.bfloat16)
    value_grad = jnp.einsum("hqk,qhd->khd", probs_low, upstream, preferred_element_type=jnp.float32)
    prob_grad = jnp.einsum("qhd,khd->hqk", upstream, values_in, preferred_element_type=jnp.float32)
    inner_sum = jnp.sum(soft_probs * prob_grad, axis=-1, keepdims=True)
    score_grad = (soft_probs * (prob_grad - inner_sum)).astype(jnp.bfloat16)
    score_scale = HD ** (-0.5)
    query_grad = (
        jnp.einsum("hqk,khd->qhd", score_grad, keys_in, preferred_element_type=jnp.float32)
        * score_scale
    )
    key_grad = (
        jnp.einsum("hqk,qhd->khd", score_grad, queries, preferred_element_type=jnp.float32)
        * score_scale
    )
    stacked = jnp.stack([query_grad, key_grad, value_grad], axis=1)
    return stacked.astype(jnp.bfloat16).reshape(stacked.shape[0], 3, -1)


def by_head_local(
    tokens,
    filled,
    out_grad,
    norm1_gain,
    norm1_bias,
    qkv_weight,
    qv_bias,
    out_weight,
    out_bias,
    norm2_gain,
    norm2_bias,
    up_weight,
    up_bias,
    down_weight,
    down_bias,
    clip_threshold,
):
    gathered = (
        lax.all_gather(norm1_gain, "dp", axis=0, tiled=True),
        lax.all_gather(norm1_bias, "dp", axis=0, tiled=True),
        lax.all_gather(qkv_weight, "dp", axis=0, tiled=True),
        lax.all_gather(qv_bias, "dp", axis=0, tiled=True),
        lax.all_gather(out_weight, "dp", axis=0, tiled=True),
        lax.all_gather(out_bias, "dp", axis=0, tiled=True),
        lax.all_gather(norm2_gain, "dp", axis=0, tiled=True),
        lax.all_gather(norm2_bias, "dp", axis=0, tiled=True),
        lax.all_gather(up_weight, "dp", axis=0, tiled=True),
        lax.all_gather(up_bias, "dp", axis=0, tiled=True),
        lax.all_gather(down_weight, "dp", axis=0, tiled=True),
        lax.all_gather(down_bias, "dp", axis=0, tiled=True),
    )
    (
        gain_one,
        shift_one,
        w_qkv,
        b_qv,
        w_out,
        b_out,
        gain_two,
        shift_two,
        w_up,
        b_up,
        w_down,
        b_down,
    ) = gathered
    images, local_rows, model_width = tokens.shape
    groups = lax.axis_size("seq")
    group_width = model_width // groups
    local_heads = group_width // HD
    length = local_rows * groups
    row_count = images * local_rows
    tokens_flat = tokens.astype(jnp.float32).reshape(row_count, model_width)
    gain_one_f = gain_one.astype(jnp.float32)
    shift_one_f = shift_one.astype(jnp.float32)
    gain_two_f = gain_two.astype(jnp.float32)
    shift_two_f = shift_two.astype(jnp.float32)
    hidden_one = norm_apply(tokens_flat, gain_one_f, shift_one_f).astype(jnp.bfloat16)
    bias_float = b_qv.astype(jnp.float32)
    qkv_bias = jnp.concatenate(
        [bias_float[:model_width], jnp.zeros((model_width,), jnp.float32), bias_float[model_width:]]
    )
    projected = (jnp.dot(hidden_one, w_qkv, preferred_element_type=jnp.float32) + qkv_bias).astype(
        jnp.bfloat16
    )
    key_flags = lax.all_gather(filled, "seq", axis=1, tiled=True)
    keep_all = key_flags > 0
    by_heads = lax.all_to_all(
        projected.reshape(images, local_rows, 3, groups, group_width),
        "seq",
        split_axis=3,
        concat_axis=1,
        tiled=True,
    )
    by_heads = by_heads.reshape(images, length, 3, local_heads, HD)
    queries = by_heads[:, :, 0]
    keys_all = by_heads[:, :, 1]
    values_all = by_heads[:, :, 2]
    attended, logsums, tops = lax.map(attend_forward, (queries, keys_all, values_all, keep_all))
    local_peak = jnp.max(tops, axis=0)
    peak_vector = lax.dynamic_update_slice(
        jnp.full((H,), very_negative, jnp.float32),
        local_peak,
        (lax.axis_index("seq") * local_heads,),
    )
    head_max = lax.pmax(peak_vector, ("dp", "seq"))
    back_rows = lax.all_to_all(
        attended.reshape(images, groups, local_rows, group_width),
        "seq",
        split_axis=1,
        concat_axis=3,
        tiled=True,
    )
    attn_rows = back_rows.reshape(row_count, model_width)
    branch = jnp.dot(attn_rows, w_out, preferred_element_type=jnp.float32) + b_out.astype(
        jnp.float32
    )
    middle = tokens_flat + branch
    hidden_two = norm_apply(middle, gain_two_f, shift_two_f).astype(jnp.bfloat16)
    pre_act = jnp.dot(hidden_two, w_up, preferred_element_type=jnp.float32) + b_up.astype(
        jnp.float32
    )
    activated = exact_gelu(pre_act).astype(jnp.bfloat16)
    block_rows = middle + (
        jnp.dot(activated, w_down, preferred_element_type=jnp.float32) + b_down.astype(jnp.float32)
    )
    block_out = block_rows.astype(jnp.bfloat16).reshape(tokens.shape)
    gain_one_b, w_qkv_b, w_out_b, gain_two_b, w_up_b, w_down_b = (
        lax.all_gather(norm1_gain, "dp", axis=0, tiled=True),
        lax.all_gather(qkv_weight, "dp", axis=0, tiled=True),
        lax.all_gather(out_weight, "dp", axis=0, tiled=True),
        lax.all_gather(norm2_gain, "dp", axis=0, tiled=True),
        lax.all_gather(up_weight, "dp", axis=0, tiled=True),
        lax.all_gather(down_weight, "dp", axis=0, tiled=True),
    )
    upstream = out_grad.reshape(row_count, model_width)
    upstream_f = upstream.astype(jnp.float32)
    d_bias_down = jnp.sum(upstream_f, axis=0)
    d_down = first_dot(activated, upstream)
    act_grad = last_dot(upstream, w_down_b)
    gelu_out, gelu_pull = jax.vjp(exact_gelu, pre_act)
    pre_grad = gelu_pull(act_grad)[0].astype(jnp.bfloat16)
    d_bias_up = column_sum(pre_grad)
    d_up = first_dot(hidden_two, pre_grad)
    hidden_two_grad = last_dot(pre_grad, w_up_b)
    norm_out_two, pull_two = jax.vjp(
        norm_apply, middle, gain_two_b.astype(jnp.float32), shift_two_f
    )
    mid_norm_grad, d_gain_two, d_shift_two = pull_two(hidden_two_grad)
    middle_grad = upstream_f + mid_norm_grad
    branch_grad = middle_grad.astype(jnp.bfloat16)
    d_bias_out = column_sum(branch_grad)
    d_out = first_dot(attn_rows, branch_grad)
    attn_grad = last_dot(branch_grad, w_out_b).astype(jnp.bfloat16)
    grad_heads = lax.all_to_all(
        attn_grad.reshape(images, local_rows, groups, group_width),
        "seq",
        split_axis=2,
        concat_axis=1,
        tiled=True,
    )
    grad_heads = grad_heads.reshape(images, length, local_heads, HD)
    head_grads = lax.map(
        attend_backward, (queries, keys_all, values_all, keep_all, logsums, grad_heads)
    )
    token_grads = lax.all_to_all(
        head_grads.reshape(images, groups, local_rows, 3, group_width),
        "seq",
        split_axis=1,
        concat_axis=4,
        tiled=True,
    )
    token_grads = token_grads.reshape(row_count, 3 * model_width)
    d_qkv = first_dot(hidden_one, token_grads)
    bias_sums = column_sum(token_grads)
    d_bias_qv = jnp.concatenate([bias_sums[:model_width], bias_sums[2 * model_width :]])
    first_grad = last_dot(token_grads, w_qkv_b)
    norm_out_one, pull_one = jax.vjp(
        norm_apply, tokens_flat, gain_one_b.astype(jnp.float32), shift_one_f
    )
    in_norm_grad, d_gain_one, d_shift_one = pull_one(first_grad)
    tokens_grad = (middle_grad + in_norm_grad).astype(jnp.bfloat16).reshape(tokens.shape)
    terms = (
        d_gain_one,
        d_shift_one,
        d_qkv,
        d_bias_qv,
        d_out,
        d_bias_out,
        d_gain_two,
        d_shift_two,
        d_up,
        d_bias_up,
        d_down,
        d_bias_down,
    )
    data_shards = (
        lax.psum_scatter(
            terms[0].astype(jnp.bfloat16), "dp", scatter_dimension=0, tiled=True
        ).astype(jnp.float32),
        lax.psum_scatter(
            terms[1].astype(jnp.bfloat16), "dp", scatter_dimension=0, tiled=True
        ).astype(jnp.float32),
        lax.psum_scatter(
            terms[2].astype(jnp.bfloat16), "dp", scatter_dimension=0, tiled=True
        ).astype(jnp.float32),
        lax.psum_scatter(
            terms[3].astype(jnp.bfloat16), "dp", scatter_dimension=0, tiled=True
        ).astype(jnp.float32),
        lax.psum_scatter(
            terms[4].astype(jnp.bfloat16), "dp", scatter_dimension=0, tiled=True
        ).astype(jnp.float32),
        lax.psum_scatter(
            terms[5].astype(jnp.bfloat16), "dp", scatter_dimension=0, tiled=True
        ).astype(jnp.float32),
        lax.psum_scatter(
            terms[6].astype(jnp.bfloat16), "dp", scatter_dimension=0, tiled=True
        ).astype(jnp.float32),
        lax.psum_scatter(
            terms[7].astype(jnp.bfloat16), "dp", scatter_dimension=0, tiled=True
        ).astype(jnp.float32),
        lax.psum_scatter(
            terms[8].astype(jnp.bfloat16), "dp", scatter_dimension=0, tiled=True
        ).astype(jnp.float32),
        lax.psum_scatter(
            terms[9].astype(jnp.bfloat16), "dp", scatter_dimension=0, tiled=True
        ).astype(jnp.float32),
        lax.psum_scatter(
            terms[10].astype(jnp.bfloat16), "dp", scatter_dimension=0, tiled=True
        ).astype(jnp.float32),
        lax.psum_scatter(
            terms[11].astype(jnp.bfloat16), "dp", scatter_dimension=0, tiled=True
        ).astype(jnp.float32),
    )
    shards = (
        lax.psum(data_shards[0].astype(jnp.bfloat16), "seq").astype(jnp.float32),
        lax.psum(data_shards[1].astype(jnp.bfloat16), "seq").astype(jnp.float32),
        lax.psum(data_shards[2].astype(jnp.bfloat16), "seq").astype(jnp.float32),
        lax.psum(data_shards[3].astype(jnp.bfloat16), "seq").astype(jnp.float32),
        lax.psum(data_shards[4].astype(jnp.bfloat16), "seq").astype(jnp.float32),
        lax.psum(data_shards[5].astype(jnp.bfloat16), "seq").astype(jnp.float32),
        lax.psum(data_shards[6].astype(jnp.bfloat16), "seq").astype(jnp.float32),
        lax.psum(data_shards[7].astype(jnp.bfloat16), "seq").astype(jnp.float32),
        lax.psum(data_shards[8].astype(jnp.bfloat16), "seq").astype(jnp.float32),
        lax.psum(data_shards[9].astype(jnp.bfloat16), "seq").astype(jnp.float32),
        lax.psum(data_shards[10].astype(jnp.bfloat16), "seq").astype(jnp.float32),
        lax.psum(data_shards[11].astype(jnp.bfloat16), "seq").astype(jnp.float32),
    )
    limit = clip_threshold.astype(jnp.float32)
    root_factor = jnp.sqrt(limit / jnp.maximum(head_max, limit))
    head_cols = jnp.repeat(root_factor, HD)
    weight_scale = jnp.concatenate([head_cols, head_cols, jnp.ones((model_width,), jnp.float32)])
    clipped_weight = (qkv_weight.astype(jnp.float32) * weight_scale[None, :]).astype(jnp.bfloat16)
    bias_count = qv_bias.shape[0]
    bias_scale = jnp.concatenate([head_cols, jnp.ones((model_width,), jnp.float32)])
    shard_scale = lax.dynamic_slice_in_dim(
        bias_scale, lax.axis_index("dp") * bias_count, bias_count
    )
    clipped_bias = (qv_bias.astype(jnp.float32) * shard_scale).astype(jnp.bfloat16)
    return (
        block_out,
        tokens_grad,
        shards[0],
        shards[1],
        shards[2],
        shards[3],
        shards[4],
        shards[5],
        shards[6],
        shards[7],
        shards[8],
        shards[9],
        shards[10],
        shards[11],
        clipped_weight,
        clipped_bias,
        head_max,
    )


MESH = pl.DeviceIdType.MESH
BF = jnp.bfloat16
F32 = jnp.float32
SMALL = (128, 128, 256, 128, 128, 128, 512, 128)


def flip(d, m):
    y = lax.rem(lax.div(d, 4) + m // 4, 2)
    x = lax.rem(lax.rem(lax.div(d, 2), 2) + (m // 2) % 2, 2)
    k = lax.rem(lax.rem(d, 2) + m % 2, 2)
    return 4 * y + 2 * x + k


def flip_traced(d, m):
    y = lax.rem(lax.div(d, 4) + lax.div(m, 4), 2)
    x = lax.rem(lax.rem(lax.div(d, 2), 2) + lax.rem(lax.div(m, 2), 2), 2)
    k = lax.rem(lax.rem(d, 2) + lax.rem(m, 2), 2)
    return 4 * y + 2 * x + k


def dot_nn(a, b):
    return lax.dot_general(a, b, (((1,), (0,)), ((), ())), preferred_element_type=F32)


def dot_nt(a, b):
    return lax.dot_general(a, b, (((1,), (1,)), ((), ())), preferred_element_type=F32)


def dot_tn(a, b):
    return lax.dot_general(a, b, (((0,), (0,)), ((), ())), preferred_element_type=F32)


def rows_of(block, size, start=0, count=None):
    count = size if count is None else count
    step = math.gcd(size, start) if start else size
    return pl.ds(pl.multiple_of(block * size + start, step), count)


def normalized(v):
    center = jnp.mean(v, axis=-1, keepdims=True)
    centered = v - center
    spread = jnp.mean(centered * centered, axis=-1, keepdims=True)
    scale = lax.rsqrt(spread + epsilon)
    return centered * scale, scale


def half_masks():
    lane = lax.broadcasted_iota(jnp.int32, (1, 2 * HD), 1)
    low = jnp.where(lane < HD, 1.0, 0.0)
    return low.astype(BF), (1.0 - low).astype(BF), lane < HD


def front_kernel(
    tok_in, grad_in, fil_in, wq_in, wo_in, wu_in, wd_in, small_in,
    out_h, tok_h, h1_h, qkv_h, gx_h, go_h, dwo_h, dwu_h, dwd_h, wq_h,
    vec_o, dbup_o, top_o, mask_o,
    wq, wo, wu, wd, tok, grad, h1, qkv, att, x1, h2, h2t, y, dh, fil, small, col, dst, ust,
    own_s, own_r, rel_s, rel_r, fwd_s, fwd_r, tok_s, tok_r, fil_s, fil_r, sm_s, sm_r, loc, stg, hout,
):
    d, s = lax.axis_index("dp"), lax.axis_index("seq")
    images, part, width = tok_in.shape
    length = images * part
    pair_count = width // (2 * HD)
    weights = ((wq_in, wq), (wo_in, wo), (wu_in, wu), (wd_in, wd))
    sib, xn, yn, dn = flip(d, 1), flip(d, 2), flip(d, 4), flip(d, 6)

    barrier = pltpu.get_barrier_semaphore()
    for m in range(1, 8):
        pl.semaphore_signal(barrier, inc=1, device_id=(flip(d, m), s), device_id_type=MESH)
    for j in range(1, images):
        pl.semaphore_signal(
            barrier, inc=1, device_id=(d, lax.rem(s + j, images)), device_id_type=MESH
        )
    pl.semaphore_wait(barrier, 7 + images - 1)

    def send(src, dst, ss, rs, to_dp, to_seq):
        return pltpu.make_async_remote_copy(
            src_ref=src, dst_ref=dst, send_sem=ss, recv_sem=rs,
            device_id=(to_dp, to_seq), device_id_type=MESH,
        )

    def exchange(src, dst, ss, rs, rows):
        copies = []
        for j in range(1, images):
            to = lax.rem(s + j, images)
            copies.append(send(src.at[to], dst.at[rows], ss.at[j - 1], rs.at[j - 1], d, to))
        return copies

    my_rows = rows_of(s, part)
    sm_copies = [
        send(small_in, small.at[d], sm_s.at[m - 1], sm_r.at[m - 1], flip(d, m), s)
        for m in range(1, 8)
    ]
    fil_copies = exchange(fil_in, fil, fil_s, fil_r, s)
    tok_copies = exchange(tok_in, tok, tok_s.at[0], tok_r.at[0], my_rows)
    grad_copies = exchange(grad_in, grad, tok_s.at[1], tok_r.at[1], my_rows)

    def own(w, which=range(5)):
        src, dst = weights[w]
        size = src.shape[0]
        half = size // 2
        def piece(way, to, h):
            return send(
                src.at[pl.ds(h * half, half)], dst.at[rows_of(d, size, h * half, half)],
                own_s.at[w, way, h], own_r.at[w, way, h], to, s,
            )
        return [
            piece(0, xn, 0), piece(1, yn, 1), piece(0, xn, 1), piece(1, yn, 0),
            send(src, dst.at[rows_of(d, size)], own_s.at[w, 2, 0], own_r.at[w, 2, 0], sib, s),
        ]

    def relays(w):
        dst = weights[w][1]
        size = weights[w][0].shape[0]
        half = size // 2
        lower, upper = rows_of(xn, size, 0, half), rows_of(yn, size, half, half)
        return [
            send(dst.at[lower], dst.at[lower], rel_s.at[w, 0], rel_r.at[w, 0], yn, s),
            send(dst.at[upper], dst.at[upper], rel_s.at[w, 1], rel_r.at[w, 1], xn, s),
        ]

    def forwards(w):
        dst = weights[w][1]
        size = weights[w][0].shape[0]
        return [
            send(dst.at[rows_of(b, size)], dst.at[rows_of(b, size)],
                 fwd_s.at[w, i], fwd_r.at[w, i], sib, s)
            for i, b in enumerate((xn, yn, dn))
        ]

    def start_own(w):
        for copy in own(w):
            copy.start()

    def on_first(w):
        mine, relay, forward = own(w), relays(w), forwards(w)
        mine[0].wait_recv()
        relay[0].start()
        mine[1].wait_recv()
        relay[1].start()
        mine[2].wait_recv()
        forward[0].start()
        mine[3].wait_recv()
        forward[1].start()

    def on_diag(w):
        relay = relays(w)
        relay[0].wait_recv()
        relay[1].wait_recv()
        forwards(w)[2].start()

    def on_sib(w):
        own(w)[4].wait_recv()
        for copy in forwards(w):
            copy.wait_recv()

    def drain(w):
        for copy in own(w) + relays(w) + forwards(w):
            copy.wait_send()

    def keep_own(w):
        src, dst = weights[w]
        return pltpu.make_async_copy(src, dst.at[rows_of(d, src.shape[0])], loc.at[w])

    for copy in sm_copies + fil_copies:
        copy.start()
    start_own(0)
    for copy in tok_copies:
        copy.start()
    start_own(1)
    locals_ = [keep_own(w) for w in range(4)]
    locals_ += [
        pltpu.make_async_copy(tok_in.at[s], tok.at[my_rows], loc.at[4]),
        pltpu.make_async_copy(grad_in.at[s], grad.at[my_rows], loc.at[5]),
        pltpu.make_async_copy(fil_in.at[s], fil.at[s], loc.at[6]),
        pltpu.make_async_copy(small_in, small.at[d], loc.at[7]),
    ]
    for copy in locals_:
        copy.start()

    on_first(0)
    start_own(2)

    for copy in sm_copies + fil_copies:
        copy.wait_recv()
    for copy in locals_:
        copy.wait()

    starts = [sum(SMALL[:i]) for i in range(len(SMALL))]

    def vector(i, first=0, last=8):
        return jnp.concatenate(
            [small[b, :, starts[i] : starts[i] + SMALL[i]] for b in range(first, last)], axis=1
        )

    mask = fil[0] + fil[1] + fil[2] + fil[3]
    mask_o[...] = mask
    col[...] = jnp.transpose(mask)

    for copy in tok_copies:
        copy.wait_recv()
    for copy in grad_copies:
        copy.start()

    block = 128
    gain1, shift1 = vector(0), vector(1)

    @pl.loop(0, length // block)
    def _(i):
        r = rows_of(i, block)
        xh, _ = normalized(tok[r, :].astype(F32))
        h1[r, :] = (xh * gain1 + shift1).astype(BF)

    on_diag(0)
    on_first(1)
    on_sib(0)

    tile = 512
    qkv_bias = jnp.concatenate(
        [vector(2, 0, 4), jnp.zeros((1, width), F32), vector(2, 4, 8)], axis=1
    )
    y[pl.ds(0, 1), :] = qkv_bias[:, :width]
    y[pl.ds(8, 1), :] = qkv_bias[:, width : 2 * width]
    y[pl.ds(16, 1), :] = qkv_bias[:, 2 * width :]

    for third in range(3):
        @pl.loop(0, width // tile)
        def _(n):
            c = pl.ds(pl.multiple_of(n * tile, tile), tile)
            cw = pl.ds(pl.multiple_of(third * width + n * tile, tile), tile)
            value = dot_nn(h1[...], wq[:, cw]) + y[pl.ds(8 * third, 1), c]
            qkv[:, cw] = value.astype(BF)

    saves = [
        pltpu.make_async_copy(tok, tok_h, hout.at[0]),
        pltpu.make_async_copy(h1, h1_h, hout.at[1]),
        pltpu.make_async_copy(qkv, qkv_h, hout.at[2]),
        pltpu.make_async_copy(wq, wq_h, hout.at[3]),
    ]
    for copy in saves:
        copy.start()

    low, high, low_lane = half_masks()
    pad = (mask[0:1, :] - 1.0) * 1e30
    pad2 = jnp.concatenate([pad, pad], axis=1)
    chunk = length // 2

    def attend(p, carry):
        c = pl.ds(pl.multiple_of(p * 2 * HD, 2 * HD), 2 * HD)
        ck = pl.ds(pl.multiple_of(width + p * 2 * HD, 2 * HD), 2 * HD)
        cv = pl.ds(pl.multiple_of(2 * width + p * 2 * HD, 2 * HD), 2 * HD)
        k, v = qkv[:, ck], qkv[:, cv]
        k2 = jnp.concatenate([k * low, k * high], axis=0)
        v2 = jnp.concatenate([v * low, v * high], axis=0)
        best = [jnp.full((1, 1), very_negative, F32)] * 2
        for j in range(2):
            r = pl.ds(j * chunk, chunk)
            q = qkv[r, c] * jnp.asarray(HD ** (-0.5), BF)
            scores = dot_nt(q, k2) + pad2
            probs = []
            for side in range(2):
                part_s = scores[:, side * length : (side + 1) * length]
                peak = jnp.max(part_s, axis=1, keepdims=True)
                e = jnp.exp(part_s - peak)
                total = jnp.sum(e, axis=1, keepdims=True)
                probs.append((e * (1.0 / total)).astype(BF))
                held = jnp.where(col[r, 0:1] > 0.5, peak, very_negative)
                best[side] = jnp.maximum(best[side], jnp.max(held, axis=0, keepdims=True))
            att[r, c] = dot_nn(jnp.concatenate(probs, axis=1), v2).astype(BF)
        top_o[pl.ds(p, 1), :] = jnp.where(
            low_lane, jnp.broadcast_to(best[0], (1, 2 * HD)), jnp.broadcast_to(best[1], (1, 2 * HD))
        )
        return carry

    early = (pair_count * 5) // 8
    lax.fori_loop(0, early, attend, 0)
    on_first(2)
    start_own(3)
    lax.fori_loop(early, pair_count, attend, 0)
    on_diag(1)
    on_sib(1)

    gain2, shift2, b_out, b_down = vector(4), vector(5), vector(3), vector(7)

    @pl.loop(0, length // block)
    def _(i):
        r = rows_of(i, block)
        mid = tok[r, :].astype(F32) + dot_nn(att[r, :], wo[...]) + b_out
        x1[r, :] = mid
        xh, _ = normalized(mid)
        h2[r, :] = (xh * gain2 + shift2).astype(BF)

    h2t[...] = jnp.transpose(h2[...])
    dbup_o[...] = vector(6)
    y[...] = x1[...] + b_down
    dh[...] = jnp.zeros_like(dh)
    for copy in grad_copies:
        copy.wait_recv()

    def add_grad(i, acc):
        return acc + jnp.sum(grad[rows_of(i, block), :].astype(F32), axis=0, keepdims=True)

    grad_sum = lax.fori_loop(0, length // block, add_grad, jnp.zeros((1, width), F32))

    on_diag(2)
    on_sib(2)

    ff_block = wd_in.shape[0]

    def stage_copies(slot, b):
        cols = pl.ds(pl.multiple_of(b * ff_block, ff_block), ff_block)
        return (
            pltpu.make_async_copy(dst.at[slot], dwd_h.at[rows_of(b, ff_block)], stg.at[0, slot]),
            pltpu.make_async_copy(ust.at[slot], dwu_h.at[:, cols], stg.at[1, slot]),
        )

    def mlp(i, carry):
        b = flip_traced(d, i)
        slot = lax.rem(i, 2)

        @pl.when(i == 1)
        def _():
            own(3)[4].wait_recv()

        @pl.when(i == 2)
        def _():
            on_first(3)

        for at, which in ((3, 0), (5, 1), (7, 2)):
            @pl.when(i == at)
            def _():
                forwards(3)[which].wait_recv()

        @pl.when(i == 6)
        def _():
            on_diag(3)

        cols = pl.ds(pl.multiple_of(b * ff_block, ff_block), ff_block)
        rows = rows_of(b, ff_block)
        u = dot_nn(h2[...], wu[:, cols]) + dbup_o[:, cols]
        phi = 0.5 * (1.0 + lax.erf(u * (0.5**0.5)))
        a = (u * phi).astype(BF)
        slope = phi + u * (jnp.exp(-0.5 * u * u) * (1.0 / math.sqrt(2.0 * math.pi)))
        gu_f = dot_nt(grad[...], wd[rows, :]) * slope
        gu = gu_f.astype(BF)
        y[...] += dot_nn(a, wd[rows, :])
        dh[...] += dot_nt(gu, wu[:, cols])

        @pl.when(i >= 2)
        def _():
            for copy in stage_copies(slot, b):
                copy.wait()

        dbup_o[:, cols] = jnp.sum(gu.astype(F32), axis=0, keepdims=True)
        dst[slot] = dot_tn(a, grad[...]).astype(BF)
        ust[slot] = dot_nn(h2t[...], gu).astype(BF)
        for copy in stage_copies(slot, b):
            copy.start()
        return carry

    lax.fori_loop(0, 8, mlp, 0)

    for slot in range(2):
        for copy in stage_copies(slot, d):
            copy.wait()
    for copy in saves:
        copy.wait()
    for w in range(4):
        drain(w)
    for copy in sm_copies + fil_copies + tok_copies + grad_copies:
        copy.wait_send()

    zero = jnp.zeros((1, width), F32)

    def norm_back(i, acc):
        r = rows_of(i, block)
        h1[r, :] = y[r, :].astype(BF)
        g = dh[r, :]
        xh, scale = normalized(x1[r, :])
        gg = g * gain2
        inner = gg - jnp.mean(gg, axis=1, keepdims=True)
        inner = inner - xh * jnp.mean(gg * xh, axis=1, keepdims=True)
        total = grad[r, :].astype(F32) + scale * inner
        dh[r, :] = total
        low_total = total.astype(BF)
        h2[r, :] = low_total
        tok[r, :] = dot_nt(low_total, wo[...]).astype(BF)
        return (
            acc[0] + jnp.sum(g * xh, axis=0, keepdims=True),
            acc[1] + jnp.sum(g, axis=0, keepdims=True),
            acc[2] + jnp.sum(low_total.astype(F32), axis=0, keepdims=True),
        )

    sums = lax.fori_loop(0, length // block, norm_back, (zero, zero, zero))
    finals = [
        pltpu.make_async_copy(h1, out_h, hout.at[4]),
        pltpu.make_async_copy(dh, gx_h, hout.at[5]),
        pltpu.make_async_copy(tok, go_h, hout.at[6]),
        pltpu.make_async_copy(wo, dwo_h, hout.at[7]),
    ]
    for copy in finals[:3]:
        copy.start()
    vec_o[pl.ds(0, 1), :] = sums[0]
    vec_o[pl.ds(1, 1), :] = sums[1]
    vec_o[pl.ds(2, 1), :] = sums[2]
    vec_o[pl.ds(3, 1), :] = grad_sum
    vec_o[pl.ds(4, 1), :] = gain1
    h2t[...] = jnp.transpose(att[...])

    @pl.loop(0, width // tile)
    def _(n):
        c = pl.ds(pl.multiple_of(n * tile, tile), tile)
        wo[:, c] = dot_nn(h2t[...], h2[:, c]).astype(BF)

    finals[3].start()
    for copy in finals:
        copy.wait()


def front(tokens, out_grad, filled_rows, qkv_weight, out_weight, up_weight, down_weight, small):
    images, part, width = tokens.shape
    length = images * part
    shards = lax.axis_size("dp")
    ff = up_weight.shape[1]
    wide = qkv_weight.shape[1]
    shape = jax.ShapeDtypeStruct
    any_spec = pl.BlockSpec(memory_space=pl.ANY)
    vmem_spec = pl.BlockSpec(memory_space=pltpu.VMEM)
    dma = pltpu.SemaphoreType.DMA
    vm = pltpu.VMEM
    return pl.pallas_call(
        front_kernel,
        name="front",
        out_shape=(
            shape((length, width), BF),
            shape((length, width), BF),
            shape((length, width), BF),
            shape((length, wide), BF),
            shape((length, width), F32),
            shape((length, width), BF),
            shape((width, width), BF),
            shape((width, ff), BF),
            shape((ff, width), BF),
            shape((width, wide), BF),
            shape((8, width), F32),
            shape((1, ff), F32),
            shape((8, 2 * HD), F32),
            shape((8, length), F32),
        ),
        in_specs=[any_spec] * 8,
        out_specs=[any_spec] * 10 + [vmem_spec] * 4,
        scratch_shapes=[
            vm((width, wide), BF), vm((width, width), BF), vm((width, ff), BF), vm((ff, width), BF),
            vm((length, width), BF), vm((length, width), BF), vm((length, width), BF),
            vm((length, wide), BF), vm((length, width), BF), vm((length, width), F32),
            vm((length, width), BF), vm((width, length), BF), vm((length, width), F32),
            vm((length, width), F32), vm((images, 8, length), F32), vm((shards, 1, sum(SMALL)), F32),
            vm((length, 8), F32), vm((2, down_weight.shape[0], width), BF),
            vm((2, width, down_weight.shape[0]), BF),
            dma((4, 3, 2)), dma((4, 3, 2)), dma((4, 2)), dma((4, 2)), dma((4, 3)), dma((4, 3)),
            dma((2, images - 1)), dma((2, images - 1)), dma((images - 1,)), dma((images - 1,)),
            dma((7,)), dma((7,)), dma((8,)), dma((2, 2)), dma((8,)),
        ],
        compiler_params=pltpu.CompilerParams(
            collective_id=0, has_side_effects=True, vmem_limit_bytes=60 << 20
        ),
    )(tokens, out_grad, filled_rows, qkv_weight, out_weight, up_weight, down_weight, small)


def add_rows(target, other, rows, step=32):
    @pl.loop(0, rows // step)
    def _(i):
        r = rows_of(i, step)
        target[r, :] = target[r, :] + other[r, :]


def back_kernel(*refs):
    (
        blk_in, qkv_in, go_in, h1_in, gx_in, tok_in, wq_in, dwd_in, dwu_in, dwo_in,
        mask_in, vec_in, dbup_in, top_in,
        out_h, tg_h, dwq_h, dwo_h, dwu_h, dwd_h, small_o, top_o,
        qkv, go, h1t, buf, gx, dh, wqg, pq, gp, colm, stg_d, stg_u, stg_o, psm, rsm, zsm, rtop, ztop,
    ) = refs[:40]
    refs = refs[40:]
    count = 9
    recv0, recv1x, recv1y, recv2, za, zb = [refs[i * count : (i + 1) * count] for i in range(6)]
    (
        s0_s, s0_r, s1_s, s1_r, s2_s, s2_r, z_s, z_r, ex_s, ex_r, sm_s, sm_r, zs_s, zs_r,
        tp_s, tp_r, tz_s, tz_r, lsem, wsem, osem,
    ) = refs[6 * count :]
    d, s = lax.axis_index("dp"), lax.axis_index("seq")
    length, width = go.shape
    images = out_h.shape[0]
    part = length // images
    sib, xn, yn = flip(d, 1), flip(d, 2), flip(d, 4)
    group_cols = gp.shape[1] // 3
    groups = width // group_cols

    barrier = pltpu.get_barrier_semaphore()
    for m in range(1, 8):
        pl.semaphore_signal(barrier, inc=1, device_id=(flip(d, m), s), device_id_type=MESH)
    for j in range(1, images):
        pl.semaphore_signal(
            barrier, inc=1, device_id=(d, lax.rem(s + j, images)), device_id_type=MESH
        )
    pl.semaphore_wait(barrier, 7 + images - 1)

    def send(src, dst, ss, rs, to_dp, to_seq):
        return pltpu.make_async_remote_copy(
            src_ref=src, dst_ref=dst, send_sem=ss, recv_sem=rs,
            device_id=(to_dp, to_seq), device_id_type=MESH,
        )

    def exchange(src, dst, which):
        out = []
        for j in range(1, images):
            to = lax.rem(s + j, images)
            out.append(
                send(src.at[rows_of(to, part)], dst.at[s], ex_s.at[which, j - 1],
                     ex_r.at[which, j - 1], d, to)
            )
        return out

    down_rows, up_cols = dwd_in.shape[0] // 16, dwu_in.shape[1] // 2
    shard = width // 8

    def partial(i, b):
        if i < 2:
            return dwd_in.at[rows_of(b, 2 * down_rows, i * down_rows, down_rows)]
        if i < 4:
            return dwu_in.at[rows_of(b, shard), pl.ds((i - 2) * up_cols, up_cols)]
        if i == 4:
            return dwo_in.at[rows_of(b, shard)]
        return pq.at[(i - 5) % 2, rows_of(b, shard)]

    size = [down_rows] * 2 + [shard] * 7
    stages = [stg_d, stg_d, stg_u, stg_u, stg_o]
    flips = (6, 2, 4, 0)

    def s0(i):
        return [
            send(partial(i, flip(sib, m)), recv0[i].at[m // 2], s0_s.at[i, m // 2],
                 s0_r.at[i, m // 2], sib, s)
            for m in flips
        ]

    def load_own(i):
        return [
            pltpu.make_async_copy(partial(i, flip(d, m)), stages[i].at[m // 2],
                                  lsem.at[i, m // 2])
            for m in flips
        ]

    def add_own(i):
        copies = s0(i)
        loads = load_own(i) if i < 5 else None
        for n, m in enumerate(flips):
            copies[n].wait_recv()
            if loads is not None:
                loads[n].wait()
                add_rows(recv0[i].at[m // 2], stages[i].at[m // 2], size[i])
            else:
                add_rows(recv0[i].at[m // 2], partial(i, flip(d, m)), size[i])

    def s1(i):
        half = size[i] // 2
        lower, upper = pl.ds(0, half), pl.ds(half, half)
        plan = ((6, lower, recv1x[i].at[1], xn), (6, upper, recv1y[i].at[1], yn),
                (2, lower, recv1x[i].at[0], xn), (4, upper, recv1y[i].at[0], yn))
        return [
            send(recv0[i].at[m // 2, part_rows], dst, s1_s.at[i, n], s1_r.at[i, n], to, s)
            for n, (m, part_rows, dst, to) in enumerate(plan)
        ]

    def s2(i):
        half = size[i] // 2
        return [
            send(recv1x[i].at[1], recv2[i].at[pl.ds(0, half)], s2_s.at[i, 0], s2_r.at[i, 0], yn, s),
            send(recv1y[i].at[1], recv2[i].at[pl.ds(half, half)], s2_s.at[i, 1], s2_r.at[i, 1],
                 xn, s),
        ]

    mate = s + 1 - 2 * lax.rem(s, 2)
    across = 3 - s
    is_mid = jnp.logical_or(s == 1, s == 2)
    is_end = jnp.logical_or(s == 0, s == 3)

    def to_mid(i):
        return send(recv2[i], za[i], z_s.at[i, 0], z_r.at[i, 0], d, mate)

    def cross(i):
        return send(za[i], zb[i], z_s.at[i, 1], z_r.at[i, 1], d, across)

    def to_end(i):
        return send(zb[i], za[i], z_s.at[i, 2], z_r.at[i, 2], d, mate)

    def outputs(i, src):
        if i < 2:
            return [pltpu.make_async_copy(src, dwd_h.at[pl.ds(i * down_rows, down_rows)],
                                          osem.at[i, 0])]
        if i < 4:
            return [pltpu.make_async_copy(src, dwu_h.at[:, pl.ds((i - 2) * up_cols, up_cols)],
                                          osem.at[i, 0])]
        if i == 4:
            return [pltpu.make_async_copy(src, dwo_h, osem.at[i, 0])]
        return [
            pltpu.make_async_copy(
                src.at[:, pl.ds(third * group_cols, group_cols)],
                dwq_h.at[:, pl.ds(third * width + (i - 5) * group_cols, group_cols)],
                osem.at[i, third],
            )
            for third in range(3)
        ]

    def start_s1(i):
        for copy in s1(i):
            copy.start()

    def step1(i):
        add_own(i)
        start_s1(i)

    def step2(i):
        half = size[i] // 2
        arrivals = s1(i)
        sends = s2(i)
        arrivals[0].wait_recv()
        add_rows(recv1x[i].at[1], recv0[i].at[2, pl.ds(0, half)], half)
        sends[0].start()
        arrivals[1].wait_recv()
        add_rows(recv1y[i].at[1], recv0[i].at[1, pl.ds(half, half)], half)
        sends[1].start()
        arrivals[2].wait_recv()
        add_rows(recv1x[i].at[0], recv0[i].at[0, pl.ds(0, half)], half)
        arrivals[3].wait_recv()
        add_rows(recv1y[i].at[0], recv0[i].at[0, pl.ds(half, half)], half)

    def step3(i):
        half = size[i] // 2
        sends = s2(i)
        sends[0].wait_recv()
        add_rows(recv2[i].at[pl.ds(0, half)], recv1x[i].at[0], half)
        sends[1].wait_recv()
        add_rows(recv2[i].at[pl.ds(half, half)], recv1y[i].at[0], half)

        @pl.when(is_end)
        def _():
            to_mid(i).start()

    def step4(i):
        @pl.when(is_mid)
        def _():
            to_mid(i).wait_recv()
            add_rows(za[i], recv2[i], size[i])
            cross(i).start()

    def step5(i):
        @pl.when(is_mid)
        def _():
            cross(i).wait_recv()
            add_rows(zb[i], za[i], size[i])
            to_end(i).start()
            for copy in outputs(i, zb[i]):
                copy.start()

    def step6(i):
        @pl.when(is_end)
        def _():
            to_end(i).wait_recv()
            for copy in outputs(i, za[i]):
                copy.start()

    def drain(i):
        for copies in (s1(i), s2(i)):
            for copy in copies:
                copy.wait_send()

        @pl.when(is_end)
        def _():
            to_mid(i).wait_send()
            for copy in outputs(i, za[i]):
                copy.wait()

        @pl.when(is_mid)
        def _():
            cross(i).wait_send()
            to_end(i).wait_send()
            for copy in outputs(i, zb[i]):
                copy.wait()

    for i in range(2):
        for copy in s0(i):
            copy.start()
    for i in (0, 2, 4):
        for copy in load_own(i):
            copy.start()
    out_copies = exchange(blk_in, out_h, 0)
    for copy in out_copies:
        copy.start()
    top_copies = [
        send(top_in, rtop.at[d], tp_s.at[m - 1], tp_r.at[m - 1], flip(d, m), s)
        for m in range(1, 8)
    ]
    for copy in top_copies:
        copy.start()

    def weight_group(g):
        return [
            pltpu.make_async_copy(
                wq_in.at[:, pl.ds(third * width + g * group_cols, group_cols)],
                wqg.at[g % 2, :, pl.ds(third * group_cols, group_cols)],
                wsem.at[g % 2, third],
            )
            for third in range(3)
        ]

    loads = [
        pltpu.make_async_copy(h1_in, buf, osem.at[0, 1]),
        pltpu.make_async_copy(qkv_in, qkv, osem.at[0, 2]),
        pltpu.make_async_copy(go_in, go, osem.at[1, 1]),
        pltpu.make_async_copy(gx_in, gx, osem.at[1, 2]),
        pltpu.make_async_copy(tok_in, buf, osem.at[2, 1]),
        pltpu.make_async_copy(blk_in.at[rows_of(s, part)], out_h.at[s], osem.at[2, 2]),
    ]
    for n in (0, 1, 2, 3, 5):
        loads[n].start()
    for copy in weight_group(0):
        copy.start()
    for i in range(2, 5):
        for copy in s0(i):
            copy.start()

    step1(0)
    for copy in load_own(1):
        copy.start()
    loads[0].wait()
    h1t[...] = jnp.transpose(buf[...])
    loads[4].start()
    dh[...] = jnp.zeros_like(dh)
    step1(1)

    colm[...] = jnp.transpose((mask_in[...] - 1.0) * 1e30)
    low, high, low_lane = half_masks()
    scale = HD ** (-0.5)
    pair = 2 * HD
    per_group = group_cols // pair
    cuts = ((0, 256), (256, length - 256)) if length > 256 else ((0, length),)
    loads[1].wait()
    loads[2].wait()

    def attention(g):
        def body(n, carry):
            p = g * per_group + n
            c = pl.ds(pl.multiple_of(p * pair, pair), pair)
            ck = pl.ds(pl.multiple_of(width + p * pair, pair), pair)
            cv = pl.ds(pl.multiple_of(2 * width + p * pair, pair), pair)
            k, v = qkv[:, ck], qkv[:, cv]
            k2 = jnp.concatenate([k * low, k * high], axis=0)
            v2 = jnp.concatenate([v * low, v * high], axis=0)
            gk = jnp.zeros((2 * length, pair), F32)
            gv = jnp.zeros((2 * length, pair), F32)
            at_q = pl.ds(pl.multiple_of(n * pair, pair), pair)
            at_k = pl.ds(pl.multiple_of(group_cols + n * pair, pair), pair)
            at_v = pl.ds(pl.multiple_of(2 * group_cols + n * pair, pair), pair)
            for first, wide in cuts:
                r = pl.ds(first, wide)
                q = qkv[r, c] * jnp.asarray(scale, BF)
                g_rows = go[r, c]
                scores = dot_nt(k2, q)
                dprob = dot_nt(v2, g_rows)
                low_probs, low_grads = [], []
                for side in range(2):
                    rows = slice(side * length, (side + 1) * length)
                    part_s = scores[rows] + colm[:, 0:1]
                    e = jnp.exp(part_s - jnp.max(part_s, axis=0, keepdims=True))
                    probs = e * (1.0 / jnp.sum(e, axis=0, keepdims=True))
                    weighted = probs * dprob[rows]
                    inner = jnp.sum(weighted, axis=0, keepdims=True)
                    low_probs.append(probs.astype(BF))
                    low_grads.append((weighted - probs * inner).astype(BF))
                low_p = jnp.concatenate(low_probs, axis=0)
                low_g = jnp.concatenate(low_grads, axis=0)
                gv = gv + dot_nn(low_p, g_rows)
                gk = gk + dot_nn(low_g, q)
                gp[r, at_q] = (dot_tn(low_g, k2) * scale).astype(BF)
            gp[:, at_k] = jnp.where(low_lane, gk[:length], gk[length:]).astype(BF)
            gp[:, at_v] = jnp.where(low_lane, gv[:length], gv[length:]).astype(BF)
            return carry

        lax.fori_loop(0, per_group, body, 0)

    bias_rows = []

    def group(g):
        if g + 1 < groups:
            for copy in weight_group(g + 1):
                copy.start()
        attention(g)
        if g >= 2:
            for copy in s0(5 + g - 2):
                copy.wait_send()
        bias_rows.append(jnp.sum(gp[...].astype(F32), axis=0, keepdims=True))
        for third in range(3):
            cols = pl.ds(third * group_cols, group_cols)
            pq[g % 2, :, cols] = dot_nn(h1t[...], gp[:, cols]).astype(BF)
        for copy in s0(5 + g):
            copy.start()
        for copy in weight_group(g):
            copy.wait()
        for first in range(0, width, 512):
            dh[:, pl.ds(first, 512)] += dot_nt(gp[...], wqg[g % 2, pl.ds(first, 512), :])

    group(0)
    step2(0)
    add_own(2)
    for copy in load_own(3):
        copy.start()
    start_s1(2)
    group(1)
    add_own(5)
    step2(1)
    step1(3)
    step3(0)
    group(2)
    add_own(6)
    step2(2)
    step1(4)
    step3(1)
    step4(0)
    group(3)
    add_own(7)
    step2(3)
    start_s1(5)
    step3(2)
    step4(1)
    step5(0)

    loads[3].wait()
    loads[4].wait()
    block = 128
    gain1 = vec_in[pl.ds(4, 1), :]
    zero = jnp.zeros((1, width), F32)

    def norm_back(i, acc):
        r = rows_of(i, block)
        g = dh[r, :]
        xh, spread = normalized(buf[r, :].astype(F32))
        gg = g * gain1
        inner = gg - jnp.mean(gg, axis=1, keepdims=True)
        inner = inner - xh * jnp.mean(gg * xh, axis=1, keepdims=True)
        go[r, :] = (gx[r, :] + spread * inner).astype(BF)
        return (
            acc[0] + jnp.sum(g * xh, axis=0, keepdims=True),
            acc[1] + jnp.sum(g, axis=0, keepdims=True),
        )

    d_gain1, d_shift1 = lax.fori_loop(0, length // block, norm_back, (zero, zero))
    tg_copies = exchange(go, tg_h, 1)
    for copy in tg_copies:
        copy.start()
    own_tg = pltpu.make_async_copy(go.at[rows_of(s, part)], tg_h.at[s], osem.at[3, 1])
    own_tg.start()

    q_sum = jnp.concatenate([row[:, :group_cols] for row in bias_rows], axis=1)
    v_sum = jnp.concatenate([row[:, 2 * group_cols :] for row in bias_rows], axis=1)
    pieces = (
        d_gain1, d_shift1, jnp.concatenate([q_sum, v_sum], axis=1), vec_in[pl.ds(2, 1), :],
        vec_in[pl.ds(0, 1), :], vec_in[pl.ds(1, 1), :], dbup_in[...], vec_in[pl.ds(3, 1), :],
    )
    for b in range(8):
        psm[b] = jnp.concatenate(
            [piece[:, b * n : (b + 1) * n] for piece, n in zip(pieces, SMALL)], axis=1
        )
    sm_copies = [
        send(psm.at[flip(d, m)], rsm.at[m - 1], sm_s.at[m - 1], sm_r.at[m - 1], flip(d, m), s)
        for m in range(1, 8)
    ]
    for copy in sm_copies:
        copy.start()

    for copy in top_copies:
        copy.wait_recv()
    rtop[d] = top_in[...]
    best = rtop[0]
    for b in range(1, 8):
        best = jnp.maximum(best, rtop[b])
    ztop[s] = best
    top_z = []
    for j in range(1, images):
        to = lax.rem(s + j, images)
        top_z.append(send(ztop.at[s], ztop.at[s], tz_s.at[j - 1], tz_r.at[j - 1], d, to))
    for copy in top_z:
        copy.start()

    step2(4)
    add_own(8)
    start_s1(6)
    step3(3)
    step4(2)
    step5(1)
    step6(0)

    for copy in sm_copies:
        copy.wait_recv()
    mine = psm[d]
    for m in range(7):
        mine = mine + rsm[m]
    zsm[s] = mine
    sm_z = []
    for j in range(1, images):
        to = lax.rem(s + j, images)
        sm_z.append(send(zsm.at[s], zsm.at[s], zs_s.at[j - 1], zs_r.at[j - 1], d, to))
    for copy in sm_z:
        copy.start()

    step2(5)
    start_s1(7)
    step3(4)
    step4(3)
    step5(2)
    step6(1)
    step2(6)
    start_s1(8)
    step3(5)
    step4(4)
    step5(3)
    step6(2)
    step2(7)
    step3(6)
    step4(5)
    step5(4)
    step6(3)
    step2(8)
    step3(7)
    step4(6)
    step5(5)
    step6(4)
    step3(8)
    step4(7)
    step5(6)
    step6(5)
    step4(8)
    step5(7)
    step6(6)
    step5(8)
    step6(7)
    step6(8)

    for copy in top_z + sm_z:
        copy.wait_recv()
    top_o[...] = jnp.maximum(jnp.maximum(ztop[0], ztop[1]), jnp.maximum(ztop[2], ztop[3]))
    small_o[...] = (zsm[0] + zsm[1]) + (zsm[2] + zsm[3])
    reused = range(5, 5 + groups - 2)
    for i in range(count):
        if i not in reused:
            for copy in s0(i):
                copy.wait_send()
    for i in range(count):
        drain(i)
    for copy in top_copies + top_z + sm_copies + sm_z + out_copies + tg_copies:
        copy.wait_send()
    for copy in out_copies + tg_copies:
        copy.wait_recv()
    own_tg.wait()
    loads[5].wait()


def back(block_rows, qkv, go, h1, gx, tok, wq, dwd, dwu, dwo, mask, vec, dbup, tops, images):
    length, width = go.shape
    wide, ff = qkv.shape[1], dwu.shape[1]
    shard = width // 8
    shape = jax.ShapeDtypeStruct
    any_spec = pl.BlockSpec(memory_space=pl.ANY)
    vmem_spec = pl.BlockSpec(memory_space=pltpu.VMEM)
    dma = pltpu.SemaphoreType.DMA
    vm = pltpu.VMEM
    group_cols = 256
    groups = width // group_cols
    sizes = [(ff // 16, width)] * 2 + [(shard, ff // 2)] * 2 + [(shard, width)]
    sizes += [(shard, 3 * group_cols)] * groups
    count = len(sizes)
    halves = [vm((2, r // 2, c), BF) for r, c in sizes]
    whole = [vm((r, c), BF) for r, c in sizes]
    z_peers = images - 1
    return pl.pallas_call(
        back_kernel,
        name="back",
        out_shape=(
            shape((images, length // images, width), BF),
            shape((images, length // images, width), BF),
            shape((shard, wide), BF),
            shape((shard, width), BF),
            shape((shard, ff), BF),
            shape((ff // 8, width), BF),
            shape((1, sum(SMALL)), F32),
            shape((8, 2 * HD), F32),
        ),
        in_specs=[any_spec] * 10 + [vmem_spec] * 4,
        out_specs=[any_spec] * 6 + [vmem_spec] * 2,
        scratch_shapes=[
            vm((length, wide), BF), vm((length, width), BF), vm((width, length), BF),
            vm((length, width), BF), vm((length, width), F32), vm((length, width), F32),
            vm((2, width, 3 * group_cols), BF), vm((2, width, 3 * group_cols), BF),
            vm((length, 3 * group_cols), BF), vm((length, 8), F32),
            vm((4, ff // 16, width), BF), vm((4, shard, ff // 2), BF), vm((4, shard, width), BF),
            vm((8, 1, sum(SMALL)), F32), vm((7, 1, sum(SMALL)), F32),
            vm((images, 1, sum(SMALL)), F32), vm((8, 8, 2 * HD), F32), vm((images, 8, 2 * HD), F32),
            *[vm((4, r, c), BF) for r, c in sizes], *halves, *halves, *whole, *whole, *whole,
            dma((count, 4)), dma((count, 4)), dma((count, 4)), dma((count, 4)),
            dma((count, 2)), dma((count, 2)), dma((count, 3)), dma((count, 3)),
            dma((2, z_peers)), dma((2, z_peers)), dma((7,)), dma((7,)),
            dma((z_peers,)), dma((z_peers,)), dma((7,)), dma((7,)),
            dma((z_peers,)), dma((z_peers,)), dma((5, 4)), dma((2, 3)), dma((count, 3)),
        ],
        compiler_params=pltpu.CompilerParams(
            collective_id=1, has_side_effects=True, vmem_limit_bytes=62 << 20
        ),
    )(block_rows, qkv, go, h1, gx, tok, wq, dwd, dwu, dwo, mask, vec, dbup, tops)


def by_image_local(
    tokens,
    filled,
    out_grad,
    norm1_gain,
    norm1_bias,
    qkv_weight,
    qv_bias,
    out_weight,
    out_bias,
    norm2_gain,
    norm2_bias,
    up_weight,
    up_bias,
    down_weight,
    down_bias,
    clip_threshold,
):
    images, local_rows, model_width = tokens.shape
    length = local_rows * images
    seq_index = lax.axis_index("seq")
    small = jnp.concatenate(
        [norm1_gain, norm1_bias, qv_bias, out_bias, norm2_gain, norm2_bias, up_bias, down_bias]
    ).astype(F32)[None]
    flags = lax.dynamic_update_slice(
        jnp.zeros((images, 8, length), F32),
        jnp.broadcast_to((filled > 0).astype(F32)[:, None, :], (images, 8, local_rows)),
        (0, 0, seq_index * local_rows),
    )
    (
        block_rows, tokens_low, hidden_one, projected, middle_grad, attn_grad,
        d_out, d_up, d_down, w_qkv, vec, d_bias_up, tops, mask,
    ) = front(tokens, out_grad, flags, qkv_weight, out_weight, up_weight, down_weight, small)
    block_out, tokens_grad, g_qkv, g_out, g_up, g_down, mine, top = back(
        block_rows, projected, attn_grad, hidden_one, middle_grad, tokens_low, w_qkv,
        d_down, d_up, d_out, mask, vec, d_bias_up, tops, images,
    )
    head_max = top[:, ::HD].reshape(-1)
    small_out, start = [], 0
    for count in SMALL:
        small_out.append(mine[0, start : start + count])
        start += count
    s_gain_one, s_shift_one, s_qv, s_out, s_gain_two, s_shift_two, s_up, s_down = small_out
    limit = clip_threshold.astype(F32)
    root_factor = jnp.sqrt(limit / jnp.maximum(head_max, limit))
    head_cols = jnp.repeat(root_factor, HD)
    ones = jnp.ones((model_width,), F32)
    weight_scale = jnp.concatenate([head_cols, head_cols, ones])
    clipped_weight = (qkv_weight.astype(F32) * weight_scale[None, :]).astype(BF)
    bias_count = qv_bias.shape[0]
    bias_scale = jnp.concatenate([head_cols, ones])
    shard_scale = lax.dynamic_slice_in_dim(
        bias_scale, lax.axis_index("dp") * bias_count, bias_count
    )
    clipped_bias = (qv_bias.astype(F32) * shard_scale).astype(BF)
    return (
        block_out,
        tokens_grad,
        s_gain_one,
        s_shift_one,
        g_qkv.astype(F32),
        s_qv,
        g_out.astype(F32),
        s_out,
        s_gain_two,
        s_shift_two,
        g_up.astype(F32),
        s_up,
        g_down.astype(F32),
        s_down,
        clipped_weight,
        clipped_bias,
        head_max,
    )


def local(*args):
    if args[0].shape[0] == lax.axis_size("seq") == 4 and lax.axis_size("dp") == 8:
        return by_image_local(*args)
    return by_head_local(*args)


def solution(mesh):
    return jax.shard_map(
        local,
        mesh=mesh,
        in_specs=(
            P("dp", "seq", None),
            P("dp", "seq"),
            P("dp", "seq", None),
            P("dp"),
            P("dp"),
            P("dp", None),
            P("dp"),
            P("dp", None),
            P("dp"),
            P("dp"),
            P("dp"),
            P("dp", None),
            P("dp"),
            P("dp", None),
            P("dp"),
            P(),
        ),
        out_specs=(
            P("dp", "seq", None),
            P("dp", "seq", None),
            P("dp"),
            P("dp"),
            P("dp", None),
            P("dp"),
            P("dp", None),
            P("dp"),
            P("dp"),
            P("dp"),
            P("dp", None),
            P("dp"),
            P("dp", None),
            P("dp"),
            P("dp", None),
            P("dp"),
            P(),
        ),
        check_vma=False,
    )
```

```python
import math

import jax
import jax.numpy as jnp
from jax import lax
from jax.experimental import pallas as pl
from jax.experimental.pallas import tpu as pltpu
from jax.sharding import PartitionSpec as P

H = 16
HD = 64


epsilon = 1e-06
very_negative = -1e30


def norm_apply(values, gain_vec, shift_vec):
    center = jnp.mean(values, axis=-1, keepdims=True)
    centered = values - center
    spread = jnp.mean(centered * centered, axis=-1, keepdims=True)
    return centered * lax.rsqrt(spread + epsilon) * gain_vec + shift_vec


def exact_gelu(values):
    return jax.nn.gelu(values, approximate=False)


def last_dot(left_op, right_op):
    return lax.dot_general(
        left_op, right_op, (((1,), (1,)), ((), ())), preferred_element_type=jnp.float32
    )


def first_dot(left_op, right_op):
    return lax.dot_general(
        left_op, right_op, (((0,), (0,)), ((), ())), preferred_element_type=jnp.float32
    )


def column_sum(values):
    return jnp.sum(values.astype(jnp.float32), axis=0)


def score_block(queries, keys_in, key_keep):
    raw_scores = jnp.einsum(
        "qhd,khd->hqk", queries, keys_in, preferred_element_type=jnp.float32
    ) * HD ** (-0.5)
    masked = jnp.where(key_keep[None, None, :], raw_scores, very_negative)
    return (raw_scores, masked)


def attend_forward(inputs):
    queries, keys_in, values_in, key_keep = inputs
    raw_scores, masked = score_block(queries, keys_in, key_keep)
    row_peak = jnp.max(masked, axis=-1, keepdims=True)
    exp_scores = jnp.exp(masked - row_peak)
    row_total = jnp.sum(exp_scores, axis=-1, keepdims=True)
    soft_probs = (exp_scores / row_total).astype(jnp.bfloat16)
    mixed_rows = jnp.einsum(
        "hqk,khd->qhd", soft_probs, values_in, preferred_element_type=jnp.float32
    )
    logsum = row_peak + jnp.log(row_total)
    pair_keep = key_keep[:, None] & key_keep[None, :]
    head_top = jnp.max(jnp.where(pair_keep[None], raw_scores, very_negative), axis=(1, 2))
    flat_rows = mixed_rows.astype(jnp.bfloat16).reshape(mixed_rows.shape[0], -1)
    return (flat_rows, logsum, head_top)


def attend_backward(inputs):
    queries, keys_in, values_in, key_keep, logsum, upstream = inputs
    raw_scores, masked = score_block(queries, keys_in, key_keep)
    soft_probs = jnp.exp(masked - logsum)
    probs_low = soft_probs.astype(jnp.bfloat16)
    value_grad = jnp.einsum("hqk,qhd->khd", probs_low, upstream, preferred_element_type=jnp.float32)
    prob_grad = jnp.einsum("qhd,khd->hqk", upstream, values_in, preferred_element_type=jnp.float32)
    inner_sum = jnp.sum(soft_probs * prob_grad, axis=-1, keepdims=True)
    score_grad = (soft_probs * (prob_grad - inner_sum)).astype(jnp.bfloat16)
    score_scale = HD ** (-0.5)
    query_grad = (
        jnp.einsum("hqk,khd->qhd", score_grad, keys_in, preferred_element_type=jnp.float32)
        * score_scale
    )
    key_grad = (
        jnp.einsum("hqk,qhd->khd", score_grad, queries, preferred_element_type=jnp.float32)
        * score_scale
    )
    stacked = jnp.stack([query_grad, key_grad, value_grad], axis=1)
    return stacked.astype(jnp.bfloat16).reshape(stacked.shape[0], 3, -1)


def by_head_local(
    tokens,
    filled,
    out_grad,
    norm1_gain,
    norm1_bias,
    qkv_weight,
    qv_bias,
    out_weight,
    out_bias,
    norm2_gain,
    norm2_bias,
    up_weight,
    up_bias,
    down_weight,
    down_bias,
    clip_threshold,
):
    gathered = (
        lax.all_gather(norm1_gain, "dp", axis=0, tiled=True),
        lax.all_gather(norm1_bias, "dp", axis=0, tiled=True),
        lax.all_gather(qkv_weight, "dp", axis=0, tiled=True),
        lax.all_gather(qv_bias, "dp", axis=0, tiled=True),
        lax.all_gather(out_weight, "dp", axis=0, tiled=True),
        lax.all_gather(out_bias, "dp", axis=0, tiled=True),
        lax.all_gather(norm2_gain, "dp", axis=0, tiled=True),
        lax.all_gather(norm2_bias, "dp", axis=0, tiled=True),
        lax.all_gather(up_weight, "dp", axis=0, tiled=True),
        lax.all_gather(up_bias, "dp", axis=0, tiled=True),
        lax.all_gather(down_weight, "dp", axis=0, tiled=True),
        lax.all_gather(down_bias, "dp", axis=0, tiled=True),
    )
    (
        gain_one,
        shift_one,
        w_qkv,
        b_qv,
        w_out,
        b_out,
        gain_two,
        shift_two,
        w_up,
        b_up,
        w_down,
        b_down,
    ) = gathered
    images, local_rows, model_width = tokens.shape
    groups = lax.axis_size("seq")
    group_width = model_width // groups
    local_heads = group_width // HD
    length = local_rows * groups
    row_count = images * local_rows
    tokens_flat = tokens.astype(jnp.float32).reshape(row_count, model_width)
    gain_one_f = gain_one.astype(jnp.float32)
    shift_one_f = shift_one.astype(jnp.float32)
    gain_two_f = gain_two.astype(jnp.float32)
    shift_two_f = shift_two.astype(jnp.float32)
    hidden_one = norm_apply(tokens_flat, gain_one_f, shift_one_f).astype(jnp.bfloat16)
    bias_float = b_qv.astype(jnp.float32)
    qkv_bias = jnp.concatenate(
        [bias_float[:model_width], jnp.zeros((model_width,), jnp.float32), bias_float[model_width:]]
    )
    projected = (jnp.dot(hidden_one, w_qkv, preferred_element_type=jnp.float32) + qkv_bias).astype(
        jnp.bfloat16
    )
    key_flags = lax.all_gather(filled, "seq", axis=1, tiled=True)
    keep_all = key_flags > 0
    by_heads = lax.all_to_all(
        projected.reshape(images, local_rows, 3, groups, group_width),
        "seq",
        split_axis=3,
        concat_axis=1,
        tiled=True,
    )
    by_heads = by_heads.reshape(images, length, 3, local_heads, HD)
    queries = by_heads[:, :, 0]
    keys_all = by_heads[:, :, 1]
    values_all = by_heads[:, :, 2]
    attended, logsums, tops = lax.map(attend_forward, (queries, keys_all, values_all, keep_all))
    local_peak = jnp.max(tops, axis=0)
    peak_vector = lax.dynamic_update_slice(
        jnp.full((H,), very_negative, jnp.float32),
        local_peak,
        (lax.axis_index("seq") * local_heads,),
    )
    head_max = lax.pmax(peak_vector, ("dp", "seq"))
    back_rows = lax.all_to_all(
        attended.reshape(images, groups, local_rows, group_width),
        "seq",
        split_axis=1,
        concat_axis=3,
        tiled=True,
    )
    attn_rows = back_rows.reshape(row_count, model_width)
    branch = jnp.dot(attn_rows, w_out, preferred_element_type=jnp.float32) + b_out.astype(
        jnp.float32
    )
    middle = tokens_flat + branch
    hidden_two = norm_apply(middle, gain_two_f, shift_two_f).astype(jnp.bfloat16)
    pre_act = jnp.dot(hidden_two, w_up, preferred_element_type=jnp.float32) + b_up.astype(
        jnp.float32
    )
    activated = exact_gelu(pre_act).astype(jnp.bfloat16)
    block_rows = middle + (
        jnp.dot(activated, w_down, preferred_element_type=jnp.float32) + b_down.astype(jnp.float32)
    )
    block_out = block_rows.astype(jnp.bfloat16).reshape(tokens.shape)
    gain_one_b, w_qkv_b, w_out_b, gain_two_b, w_up_b, w_down_b = (
        lax.all_gather(norm1_gain, "dp", axis=0, tiled=True),
        lax.all_gather(qkv_weight, "dp", axis=0, tiled=True),
        lax.all_gather(out_weight, "dp", axis=0, tiled=True),
        lax.all_gather(norm2_gain, "dp", axis=0, tiled=True),
        lax.all_gather(up_weight, "dp", axis=0, tiled=True),
        lax.all_gather(down_weight, "dp", axis=0, tiled=True),
    )
    upstream = out_grad.reshape(row_count, model_width)
    upstream_f = upstream.astype(jnp.float32)
    d_bias_down = jnp.sum(upstream_f, axis=0)
    d_down = first_dot(activated, upstream)
    act_grad = last_dot(upstream, w_down_b)
    gelu_out, gelu_pull = jax.vjp(exact_gelu, pre_act)
    pre_grad = gelu_pull(act_grad)[0].astype(jnp.bfloat16)
    d_bias_up = column_sum(pre_grad)
    d_up = first_dot(hidden_two, pre_grad)
    hidden_two_grad = last_dot(pre_grad, w_up_b)
    norm_out_two, pull_two = jax.vjp(
        norm_apply, middle, gain_two_b.astype(jnp.float32), shift_two_f
    )
    mid_norm_grad, d_gain_two, d_shift_two = pull_two(hidden_two_grad)
    middle_grad = upstream_f + mid_norm_grad
    branch_grad = middle_grad.astype(jnp.bfloat16)
    d_bias_out = column_sum(branch_grad)
    d_out = first_dot(attn_rows, branch_grad)
    attn_grad = last_dot(branch_grad, w_out_b).astype(jnp.bfloat16)
    grad_heads = lax.all_to_all(
        attn_grad.reshape(images, local_rows, groups, group_width),
        "seq",
        split_axis=2,
        concat_axis=1,
        tiled=True,
    )
    grad_heads = grad_heads.reshape(images, length, local_heads, HD)
    head_grads = lax.map(
        attend_backward, (queries, keys_all, values_all, keep_all, logsums, grad_heads)
    )
    token_grads = lax.all_to_all(
        head_grads.reshape(images, groups, local_rows, 3, group_width),
        "seq",
        split_axis=1,
        concat_axis=4,
        tiled=True,
    )
    token_grads = token_grads.reshape(row_count, 3 * model_width)
    d_qkv = first_dot(hidden_one, token_grads)
    bias_sums = column_sum(token_grads)
    d_bias_qv = jnp.concatenate([bias_sums[:model_width], bias_sums[2 * model_width :]])
    first_grad = last_dot(token_grads, w_qkv_b)
    norm_out_one, pull_one = jax.vjp(
        norm_apply, tokens_flat, gain_one_b.astype(jnp.float32), shift_one_f
    )
    in_norm_grad, d_gain_one, d_shift_one = pull_one(first_grad)
    tokens_grad = (middle_grad + in_norm_grad).astype(jnp.bfloat16).reshape(tokens.shape)
    terms = (
        d_gain_one,
        d_shift_one,
        d_qkv,
        d_bias_qv,
        d_out,
        d_bias_out,
        d_gain_two,
        d_shift_two,
        d_up,
        d_bias_up,
        d_down,
        d_bias_down,
    )
    data_shards = (
        lax.psum_scatter(
            terms[0].astype(jnp.bfloat16), "dp", scatter_dimension=0, tiled=True
        ).astype(jnp.float32),
        lax.psum_scatter(
            terms[1].astype(jnp.bfloat16), "dp", scatter_dimension=0, tiled=True
        ).astype(jnp.float32),
        lax.psum_scatter(
            terms[2].astype(jnp.bfloat16), "dp", scatter_dimension=0, tiled=True
        ).astype(jnp.float32),
        lax.psum_scatter(
            terms[3].astype(jnp.bfloat16), "dp", scatter_dimension=0, tiled=True
        ).astype(jnp.float32),
        lax.psum_scatter(
            terms[4].astype(jnp.bfloat16), "dp", scatter_dimension=0, tiled=True
        ).astype(jnp.float32),
        lax.psum_scatter(
            terms[5].astype(jnp.bfloat16), "dp", scatter_dimension=0, tiled=True
        ).astype(jnp.float32),
        lax.psum_scatter(
            terms[6].astype(jnp.bfloat16), "dp", scatter_dimension=0, tiled=True
        ).astype(jnp.float32),
        lax.psum_scatter(
            terms[7].astype(jnp.bfloat16), "dp", scatter_dimension=0, tiled=True
        ).astype(jnp.float32),
        lax.psum_scatter(
            terms[8].astype(jnp.bfloat16), "dp", scatter_dimension=0, tiled=True
        ).astype(jnp.float32),
        lax.psum_scatter(
            terms[9].astype(jnp.bfloat16), "dp", scatter_dimension=0, tiled=True
        ).astype(jnp.float32),
        lax.psum_scatter(
            terms[10].astype(jnp.bfloat16), "dp", scatter_dimension=0, tiled=True
        ).astype(jnp.float32),
        lax.psum_scatter(
            terms[11].astype(jnp.bfloat16), "dp", scatter_dimension=0, tiled=True
        ).astype(jnp.float32),
    )
    shards = (
        lax.psum(data_shards[0].astype(jnp.bfloat16), "seq").astype(jnp.float32),
        lax.psum(data_shards[1].astype(jnp.bfloat16), "seq").astype(jnp.float32),
        lax.psum(data_shards[2].astype(jnp.bfloat16), "seq").astype(jnp.float32),
        lax.psum(data_shards[3].astype(jnp.bfloat16), "seq").astype(jnp.float32),
        lax.psum(data_shards[4].astype(jnp.bfloat16), "seq").astype(jnp.float32),
        lax.psum(data_shards[5].astype(jnp.bfloat16), "seq").astype(jnp.float32),
        lax.psum(data_shards[6].astype(jnp.bfloat16), "seq").astype(jnp.float32),
        lax.psum(data_shards[7].astype(jnp.bfloat16), "seq").astype(jnp.float32),
        lax.psum(data_shards[8].astype(jnp.bfloat16), "seq").astype(jnp.float32),
        lax.psum(data_shards[9].astype(jnp.bfloat16), "seq").astype(jnp.float32),
        lax.psum(data_shards[10].astype(jnp.bfloat16), "seq").astype(jnp.float32),
        lax.psum(data_shards[11].astype(jnp.bfloat16), "seq").astype(jnp.float32),
    )
    limit = clip_threshold.astype(jnp.float32)
    root_factor = jnp.sqrt(limit / jnp.maximum(head_max, limit))
    head_cols = jnp.repeat(root_factor, HD)
    weight_scale = jnp.concatenate([head_cols, head_cols, jnp.ones((model_width,), jnp.float32)])
    clipped_weight = (qkv_weight.astype(jnp.float32) * weight_scale[None, :]).astype(jnp.bfloat16)
    bias_count = qv_bias.shape[0]
    bias_scale = jnp.concatenate([head_cols, jnp.ones((model_width,), jnp.float32)])
    shard_scale = lax.dynamic_slice_in_dim(
        bias_scale, lax.axis_index("dp") * bias_count, bias_count
    )
    clipped_bias = (qv_bias.astype(jnp.float32) * shard_scale).astype(jnp.bfloat16)
    return (
        block_out,
        tokens_grad,
        shards[0],
        shards[1],
        shards[2],
        shards[3],
        shards[4],
        shards[5],
        shards[6],
        shards[7],
        shards[8],
        shards[9],
        shards[10],
        shards[11],
        clipped_weight,
        clipped_bias,
        head_max,
    )


MESH = pl.DeviceIdType.MESH
BF = jnp.bfloat16
F32 = jnp.float32
SMALL = (128, 128, 256, 128, 128, 128, 512, 128)


def flip(d, m):
    y = lax.rem(lax.div(d, 4) + m // 4, 2)
    x = lax.rem(lax.rem(lax.div(d, 2), 2) + (m // 2) % 2, 2)
    k = lax.rem(lax.rem(d, 2) + m % 2, 2)
    return 4 * y + 2 * x + k


def flip_traced(d, m):
    y = lax.rem(lax.div(d, 4) + lax.div(m, 4), 2)
    x = lax.rem(lax.rem(lax.div(d, 2), 2) + lax.rem(lax.div(m, 2), 2), 2)
    k = lax.rem(lax.rem(d, 2) + lax.rem(m, 2), 2)
    return 4 * y + 2 * x + k


def dot_nn(a, b):
    return lax.dot_general(a, b, (((1,), (0,)), ((), ())), preferred_element_type=F32)


def dot_nt(a, b):
    return lax.dot_general(a, b, (((1,), (1,)), ((), ())), preferred_element_type=F32)


def dot_tn(a, b):
    return lax.dot_general(a, b, (((0,), (0,)), ((), ())), preferred_element_type=F32)


def rows_of(block, size, start=0, count=None):
    count = size if count is None else count
    step = math.gcd(size, start) if start else size
    return pl.ds(pl.multiple_of(block * size + start, step), count)


def normalized(v):
    center = jnp.mean(v, axis=-1, keepdims=True)
    centered = v - center
    spread = jnp.mean(centered * centered, axis=-1, keepdims=True)
    scale = lax.rsqrt(spread + epsilon)
    return centered * scale, scale


def half_masks():
    lane = lax.broadcasted_iota(jnp.int32, (1, 2 * HD), 1)
    low = jnp.where(lane < HD, 1.0, 0.0)
    return low.astype(BF), (1.0 - low).astype(BF), lane < HD


def add_rows(target, other, rows, step=32):
    @pl.loop(0, rows // step)
    def _(i):
        r = rows_of(i, step)
        target[r, :] = target[r, :] + other[r, :]


def front_kernel(
    tok_in, grad_in, fil_in, wq_in, wo_in, wu_in, wd_in, small_in,
    tok_h, h1_h, qkv_h, gx_h, go_h, ga_h, h2_h, gu_h, att_h, atto_h, first_h, fx_h, fy_h,
    wq_h, wo_h, wu_h, wd_h, vec_o, dbup_o, bup_o, top_o, mask_o,
    wq, wo, wu, wd, tok, grad, h1, qkv, att, x1, h2, dh, fil, small, col, slp, ust, bias,
    dst, first, mine,
    own_s, own_r, rel_s, rel_r, fwd_s, fwd_r, tok_s, tok_r, att_s, att_r, fil_s, fil_r,
    sm_s, sm_r, dn_s, dn_r, fs_s, fs_r, loc, stg, hout,
):
    d, s = lax.axis_index("dp"), lax.axis_index("seq")
    images, part, width = tok_in.shape
    length = images * part
    pair_count = width // (2 * HD)
    weights = ((wq_in, wq), (wo_in, wo), (wu_in, wu), (wd_in, wd))
    sib, xn, yn, dn = flip(d, 1), flip(d, 2), flip(d, 4), flip(d, 6)

    barrier = pltpu.get_barrier_semaphore()
    for m in range(1, 8):
        pl.semaphore_signal(barrier, inc=1, device_id=(flip(d, m), s), device_id_type=MESH)
    for j in range(1, images):
        pl.semaphore_signal(
            barrier, inc=1, device_id=(d, lax.rem(s + j, images)), device_id_type=MESH
        )
    pl.semaphore_wait(barrier, 7 + images - 1)

    def send(src, dst, ss, rs, to_dp, to_seq):
        return pltpu.make_async_remote_copy(
            src_ref=src, dst_ref=dst, send_sem=ss, recv_sem=rs,
            device_id=(to_dp, to_seq), device_id_type=MESH,
        )

    def exchange(src, dst, ss, rs, rows):
        copies = []
        for j in range(1, images):
            to = lax.rem(s + j, images)
            copies.append(send(src.at[to], dst.at[rows], ss.at[j - 1], rs.at[j - 1], d, to))
        return copies

    my_rows = rows_of(s, part)
    sm_copies = [
        send(mine, small.at[d], sm_s.at[m - 1], sm_r.at[m - 1], flip(d, m), s)
        for m in range(1, 8)
    ]
    fil_copies = exchange(fil_in, fil, fil_s, fil_r, s)
    tok_copies = exchange(tok_in, tok, tok_s.at[0], tok_r.at[0], my_rows)
    grad_copies = exchange(grad_in, grad, tok_s.at[1], tok_r.at[1], my_rows)

    def own(w, which=range(5)):
        src, dst = weights[w]
        size = src.shape[0]
        half = size // 2
        def piece(way, to, h):
            return send(
                src.at[pl.ds(h * half, half)], dst.at[rows_of(d, size, h * half, half)],
                own_s.at[w, way, h], own_r.at[w, way, h], to, s,
            )
        return [
            piece(0, xn, 0), piece(1, yn, 1), piece(0, xn, 1), piece(1, yn, 0),
            send(src, dst.at[rows_of(d, size)], own_s.at[w, 2, 0], own_r.at[w, 2, 0], sib, s),
        ]

    def relays(w):
        dst = weights[w][1]
        size = weights[w][0].shape[0]
        half = size // 2
        lower, upper = rows_of(xn, size, 0, half), rows_of(yn, size, half, half)
        return [
            send(dst.at[lower], dst.at[lower], rel_s.at[w, 0], rel_r.at[w, 0], yn, s),
            send(dst.at[upper], dst.at[upper], rel_s.at[w, 1], rel_r.at[w, 1], xn, s),
        ]

    def forwards(w):
        dst = weights[w][1]
        size = weights[w][0].shape[0]
        return [
            send(dst.at[rows_of(b, size)], dst.at[rows_of(b, size)],
                 fwd_s.at[w, i], fwd_r.at[w, i], sib, s)
            for i, b in enumerate((xn, yn, dn))
        ]

    def start_own(w):
        for copy in own(w):
            copy.start()

    def on_first(w):
        mine, relay, forward = own(w), relays(w), forwards(w)
        mine[0].wait_recv()
        relay[0].start()
        mine[1].wait_recv()
        relay[1].start()
        mine[2].wait_recv()
        forward[0].start()
        mine[3].wait_recv()
        forward[1].start()

    def on_diag(w):
        relay = relays(w)
        relay[0].wait_recv()
        relay[1].wait_recv()
        forwards(w)[2].start()

    def on_sib(w):
        own(w)[4].wait_recv()
        for copy in forwards(w):
            copy.wait_recv()

    def drain(w):
        for copy in own(w) + relays(w) + forwards(w):
            copy.wait_send()

    def keep_own(w):
        src, dst = weights[w]
        return pltpu.make_async_copy(src, dst.at[rows_of(d, src.shape[0])], loc.at[w])

    start_own(0)
    mine[...] = small_in[...]
    for copy in sm_copies + fil_copies:
        copy.start()
    for copy in tok_copies:
        copy.start()
    start_own(1)
    locals_ = [keep_own(w) for w in range(4)]
    locals_ += [
        pltpu.make_async_copy(tok_in.at[s], tok.at[my_rows], loc.at[4]),
        pltpu.make_async_copy(grad_in.at[s], grad.at[my_rows], loc.at[5]),
        pltpu.make_async_copy(fil_in.at[s], fil.at[s], loc.at[6]),
        pltpu.make_async_copy(mine, small.at[d], loc.at[7]),
    ]
    for copy in locals_:
        copy.start()

    on_first(0)
    start_own(2)

    for copy in sm_copies + fil_copies:
        copy.wait_recv()
    for copy in locals_:
        copy.wait()

    starts = [sum(SMALL[:i]) for i in range(len(SMALL))]

    def vector(i, first=0, last=8):
        return jnp.concatenate(
            [small[b, :, starts[i] : starts[i] + SMALL[i]] for b in range(first, last)], axis=1
        )

    mask = fil[0] + fil[1] + fil[2] + fil[3]
    mask_o[...] = mask
    col[...] = jnp.transpose(mask)

    for copy in tok_copies:
        copy.wait_recv()
    for copy in grad_copies:
        copy.start()

    block = 128
    gain1, shift1 = vector(0), vector(1)

    @pl.loop(0, length // block)
    def _(i):
        r = rows_of(i, block)
        xh, _ = normalized(tok[r, :].astype(F32))
        h1[r, :] = (xh * gain1 + shift1).astype(BF)

    on_diag(0)
    on_first(1)
    on_sib(0)

    tile = 512
    qkv_bias = jnp.concatenate(
        [vector(2, 0, 4), jnp.zeros((1, width), F32), vector(2, 4, 8)], axis=1
    )
    bias[pl.ds(0, 1), :] = qkv_bias[:, :width]
    bias[pl.ds(1, 1), :] = qkv_bias[:, width : 2 * width]
    bias[pl.ds(2, 1), :] = qkv_bias[:, 2 * width :]

    for third in range(3):
        @pl.loop(0, width // tile)
        def _(n):
            c = pl.ds(pl.multiple_of(n * tile, tile), tile)
            cw = pl.ds(pl.multiple_of(third * width + n * tile, tile), tile)
            value = dot_nn(h1[...], wq[:, cw]) + bias[pl.ds(third, 1), c]
            qkv[:, cw] = value.astype(BF)

    saves = [
        pltpu.make_async_copy(tok, tok_h, hout.at[0]),
        pltpu.make_async_copy(h1, h1_h, hout.at[1]),
        pltpu.make_async_copy(qkv, qkv_h, hout.at[2]),
        pltpu.make_async_copy(wq, wq_h, hout.at[3]),
        pltpu.make_async_copy(wo, wo_h, hout.at[4]),
        pltpu.make_async_copy(wu, wu_h, hout.at[5]),
        pltpu.make_async_copy(wd, wd_h, hout.at[6]),
        pltpu.make_async_copy(att, att_h, hout.at[7]),
        pltpu.make_async_copy(first, first_h, hout.at[8]),
        pltpu.make_async_copy(h2, h2_h, hout.at[9]),
    ]
    for copy in saves[:4]:
        copy.start()

    low, high, low_lane = half_masks()
    pad = (mask[0:1, :] - 1.0) * 1e30
    pad2 = jnp.concatenate([pad, pad], axis=1)
    chunk = length // 2

    def attend(p, carry):
        c = pl.ds(pl.multiple_of(p * 2 * HD, 2 * HD), 2 * HD)
        ck = pl.ds(pl.multiple_of(width + p * 2 * HD, 2 * HD), 2 * HD)
        cv = pl.ds(pl.multiple_of(2 * width + p * 2 * HD, 2 * HD), 2 * HD)
        k, v = qkv[:, ck], qkv[:, cv]
        k2 = jnp.concatenate([k * low, k * high], axis=0)
        v2 = jnp.concatenate([v * low, v * high], axis=0)
        best = [jnp.full((1, 1), very_negative, F32)] * 2
        for j in range(2):
            r = pl.ds(j * chunk, chunk)
            q = qkv[r, c] * jnp.asarray(HD ** (-0.5), BF)
            scores = dot_nt(q, k2) + pad2
            probs = []
            for side in range(2):
                part_s = scores[:, side * length : (side + 1) * length]
                peak = jnp.max(part_s, axis=1, keepdims=True)
                e = jnp.exp(part_s - peak)
                total = jnp.sum(e, axis=1, keepdims=True)
                probs.append((e * (1.0 / total)).astype(BF))
                held = jnp.where(col[r, 0:1] > 0.5, peak, very_negative)
                best[side] = jnp.maximum(best[side], jnp.max(held, axis=0, keepdims=True))
            att[r, c] = dot_nn(jnp.concatenate(probs, axis=1), v2).astype(BF)
        top_o[pl.ds(p, 1), :] = jnp.where(
            low_lane, jnp.broadcast_to(best[0], (1, 2 * HD)), jnp.broadcast_to(best[1], (1, 2 * HD))
        )
        return carry

    def give_back(part_of):
        wide = width // 2
        cols = pl.ds(part_of * wide, wide)
        copies = []
        for j in range(1, images):
            to = lax.rem(s + j, images)
            copies.append(
                send(att.at[rows_of(to, part), cols], atto_h.at[s, :, cols],
                     att_s.at[part_of, j - 1], att_r.at[part_of, j - 1], d, to)
            )
        return copies

    lax.fori_loop(0, pair_count // 2, attend, 0)
    back_copies = give_back(0)
    for copy in back_copies:
        copy.start()
    on_first(2)
    start_own(3)
    lax.fori_loop(pair_count // 2, pair_count, attend, 0)
    back_copies += give_back(1)
    for copy in back_copies[images - 1 :]:
        copy.start()
    keep_att = pltpu.make_async_copy(att.at[my_rows], atto_h.at[s], hout.at[10])
    keep_att.start()
    saves[7].start()
    on_diag(1)
    on_sib(1)
    saves[4].start()

    gain2, shift2, b_out, b_down = vector(4), vector(5), vector(3), vector(7)

    @pl.loop(0, length // block)
    def _(i):
        r = rows_of(i, block)
        mid = tok[r, :].astype(F32) + dot_nn(att[r, :], wo[...]) + b_out
        x1[r, :] = mid
        xh, _ = normalized(mid)
        h2[r, :] = (xh * gain2 + shift2).astype(BF)

    saves[9].start()
    bup_o[...] = vector(6)
    dh[...] = jnp.zeros_like(dh)
    for copy in grad_copies:
        copy.wait_recv()

    def add_grad(i, acc):
        return acc + jnp.sum(grad[rows_of(i, block), :].astype(F32), axis=0, keepdims=True)

    grad_sum = lax.fori_loop(0, length // block, add_grad, jnp.zeros((1, width), F32))

    on_diag(2)
    on_sib(2)
    saves[5].start()

    ff_block = wd_in.shape[0]

    half_rows = ff_block // 2

    def activation(b):
        cols = pl.ds(pl.multiple_of(b * ff_block, ff_block), ff_block)
        u = dot_nn(h2[...], wu[:, cols]) + bup_o[:, cols]
        phi = 0.5 * (1.0 + lax.erf(u * (0.5**0.5)))
        slope = phi + u * (jnp.exp(-0.5 * u * u) * (1.0 / math.sqrt(2.0 * math.pi)))
        slp[:, cols] = slope.astype(BF)
        return (u * phi).astype(BF)

    def down_send(mi):
        return send(dst.at[1], first.at[mi], dn_s.at[mi], dn_r.at[mi], sib, s)

    def down(j, carry):
        m = lax.rem(6 * (j + 1), 8)
        mi = lax.div(m, 2)

        @pl.when(j > 0)
        def _():
            down_send(lax.div(lax.rem(6 * j, 8), 2)).wait_send()

        for slot in (1, 0):
            a = activation(flip_traced(d, m + slot))
            dst[slot] = dot_tn(a, grad[...]).astype(BF)
            if slot:
                down_send(mi).start()
        down_send(mi).wait_recv()
        add_rows(first.at[mi], dst.at[0], ff_block)
        return carry

    lax.fori_loop(0, 4, down, 0)
    down_send(0).wait_send()
    saves[8].start()

    def first_stage(n):
        quarter = half_rows // 2
        lower, upper = pl.ds(0, quarter), pl.ds(quarter, quarter)
        m, rows, to_ref, to = (
            (6, lower, fx_h.at[1], xn), (6, upper, fy_h.at[1], yn),
            (2, lower, fx_h.at[0], xn), (4, upper, fy_h.at[0], yn),
        )[n]
        return send(first.at[m // 2, rows], to_ref, fs_s.at[n], fs_r.at[n], to, s)

    def stage_copy(slot, b):
        cols = pl.ds(pl.multiple_of(b * ff_block, ff_block), ff_block)
        return pltpu.make_async_copy(ust.at[slot], gu_h.at[:, cols], stg.at[slot])

    def mlp(i, carry):
        b = flip_traced(d, i)
        slot = lax.rem(i, 2)

        @pl.when(i == 1)
        def _():
            own(3)[4].wait_recv()

        @pl.when(i == 2)
        def _():
            on_first(3)
            for n in range(4):
                first_stage(n).start()

        for at, which in ((3, 0), (5, 1), (7, 2)):
            @pl.when(i == at)
            def _():
                forwards(3)[which].wait_recv()

        @pl.when(i == 6)
        def _():
            on_diag(3)

        cols = pl.ds(pl.multiple_of(b * ff_block, ff_block), ff_block)
        rows = rows_of(b, ff_block)
        gu = (dot_nt(grad[...], wd[rows, :]) * slp[:, cols].astype(F32)).astype(BF)
        dh[...] += dot_nt(gu, wu[:, cols])

        @pl.when(i >= 2)
        def _():
            stage_copy(slot, b).wait()

        dbup_o[:, cols] = jnp.sum(gu.astype(F32), axis=0, keepdims=True)
        ust[slot] = gu
        stage_copy(slot, b).start()
        return carry

    lax.fori_loop(0, 8, mlp, 0)
    saves[6].start()
    for n in (0, 9):
        saves[n].wait()

    zero = jnp.zeros((1, width), F32)

    def norm_back(i, acc):
        r = rows_of(i, block)
        g = dh[r, :]
        xh, scale = normalized(x1[r, :])
        gg = g * gain2
        inner = gg - jnp.mean(gg, axis=1, keepdims=True)
        inner = inner - xh * jnp.mean(gg * xh, axis=1, keepdims=True)
        total = grad[r, :].astype(F32) + scale * inner
        dh[r, :] = total
        low_total = total.astype(BF)
        h2[r, :] = low_total
        tok[r, :] = dot_nt(low_total, wo[...]).astype(BF)
        return (
            acc[0] + jnp.sum(g * xh, axis=0, keepdims=True),
            acc[1] + jnp.sum(g, axis=0, keepdims=True),
            acc[2] + jnp.sum(low_total.astype(F32), axis=0, keepdims=True),
        )

    sums = lax.fori_loop(0, length // block, norm_back, (zero, zero, zero))
    finals = [
        pltpu.make_async_copy(dh, gx_h, hout.at[11]),
        pltpu.make_async_copy(tok, go_h, hout.at[12]),
        pltpu.make_async_copy(h2, ga_h, hout.at[13]),
    ]
    for copy in finals:
        copy.start()
    for n, row in enumerate((sums[0], sums[1], sums[2], grad_sum)):
        vec_o[pl.ds(n, 1), :] = row
    for n, row in enumerate((gain1, gain2, shift2, b_out, b_down)):
        vec_o[pl.ds(8 + n, 1), :] = row
    for slot in range(2):
        stage_copy(slot, d).wait()
    for n in range(4):
        first_stage(n).wait()
    for n in (1, 2, 3, 4, 5, 6, 7, 8):
        saves[n].wait()
    keep_att.wait()
    for w in range(4):
        drain(w)
    for copy in sm_copies + fil_copies + tok_copies + grad_copies + back_copies:
        copy.wait_send()
    for copy in back_copies:
        copy.wait_recv()
    for copy in finals:
        copy.wait()


def front(tokens, out_grad, filled_rows, qkv_weight, out_weight, up_weight, down_weight, small):
    images, part, width = tokens.shape
    length = images * part
    shards = lax.axis_size("dp")
    ff = up_weight.shape[1]
    wide = qkv_weight.shape[1]
    shape = jax.ShapeDtypeStruct
    any_spec = pl.BlockSpec(memory_space=pl.ANY)
    vmem_spec = pl.BlockSpec(memory_space=pltpu.VMEM)
    dma = pltpu.SemaphoreType.DMA
    vm = pltpu.VMEM
    return pl.pallas_call(
        front_kernel,
        name="front",
        out_shape=(
            shape((length, width), BF),
            shape((length, width), BF),
            shape((length, wide), BF),
            shape((length, width), F32),
            shape((length, width), BF),
            shape((length, width), BF),
            shape((length, width), BF),
            shape((length, ff), BF),
            shape((length, width), BF),
            shape((images, part, width), BF),
            shape((4, ff // 8, width), BF),
            shape((2, ff // 32, width), BF),
            shape((2, ff // 32, width), BF),
            shape((width, wide), BF),
            shape((width, width), BF),
            shape((width, ff), BF),
            shape((ff, width), BF),
            shape((16, width), F32),
            shape((1, ff), F32),
            shape((1, ff), F32),
            shape((8, 2 * HD), F32),
            shape((8, length), F32),
        ),
        in_specs=[any_spec] * 7 + [vmem_spec],
        out_specs=[any_spec] * 17 + [vmem_spec] * 5,
        scratch_shapes=[
            vm((width, wide), BF), vm((width, width), BF), vm((width, ff), BF), vm((ff, width), BF),
            vm((length, width), BF), vm((length, width), BF), vm((length, width), BF),
            vm((length, wide), BF), vm((length, width), BF), vm((length, width), F32),
            vm((length, width), BF), vm((length, width), F32),
            vm((images, 8, length), F32), vm((shards, 1, sum(SMALL)), F32),
            vm((length, 8), F32), vm((length, ff), BF),
            vm((2, length, down_weight.shape[0]), BF), vm((8, width), F32),
            vm((2, ff // 8, width), BF), vm((4, ff // 8, width), BF), vm((1, sum(SMALL)), F32),
            dma((4, 3, 2)), dma((4, 3, 2)), dma((4, 2)), dma((4, 2)), dma((4, 3)), dma((4, 3)),
            dma((2, images - 1)), dma((2, images - 1)), dma((2, images - 1)), dma((2, images - 1)),
            dma((images - 1,)), dma((images - 1,)), dma((7,)), dma((7,)),
            dma((4,)), dma((4,)), dma((4,)), dma((4,)), dma((8,)), dma((2,)), dma((14,)),
        ],
        compiler_params=pltpu.CompilerParams(
            collective_id=0, has_side_effects=True, vmem_limit_bytes=63 << 20
        ),
    )(tokens, out_grad, filled_rows, qkv_weight, out_weight, up_weight, down_weight, small)


def back_kernel(*refs):
    (
        qkv_in, go_in, h1_in, gx_in, tok_in, ga_in, h2_in, gu_in, att_in, atto_in, first_in,
        fx_in, fy_in, mine_in, wq_in, wo_in, wu_in, wd_in,
        mask_in, vec_in, dbup_in, bup_in, top_in,
        out_h, tg_h, dwq_h, dwo_h, dwu_h, dwd_h, small_o, top_o,
        qkv, go, ht, gbuf, buf, dh, wqg, pq, gp, colm, dst, own_u, ust, stg_o, ast, gxs,
        psm, rsm, zsm, rtop, ztop,
    ) = refs[:52]
    refs = refs[52:]
    count = 11
    recv0, recv1x, recv1y, recv2, za, zb = [refs[i * count : (i + 1) * count] for i in range(6)]
    (
        s0_s, s0_r, u0_s, u0_r, s1_s, s1_r, s2_s, s2_r, z_s, z_r, ex_s, ex_r, sm_s, sm_r,
        zs_s, zs_r, tp_s, tp_r, tz_s, tz_r, asem, wsem, osem, lsem, gsem,
    ) = refs[6 * count :]
    d, s = lax.axis_index("dp"), lax.axis_index("seq")
    length, width = go.shape
    images, part = mine_in.shape[0], mine_in.shape[1]
    sib, xn, yn = flip(d, 1), flip(d, 2), flip(d, 4)
    group_cols = gp.shape[1] // 3
    groups = width // group_cols
    ff_block = dst.shape[1]
    shard = width // 8
    block = 128
    tile = 512

    barrier = pltpu.get_barrier_semaphore()
    for m in range(1, 8):
        pl.semaphore_signal(barrier, inc=1, device_id=(flip(d, m), s), device_id_type=MESH)
    for j in range(1, images):
        pl.semaphore_signal(
            barrier, inc=1, device_id=(d, lax.rem(s + j, images)), device_id_type=MESH
        )

    def load(src, dst_ref, n):
        return pltpu.make_async_copy(src, dst_ref, lsem.at[n])

    def send(src, dst_ref, ss, rs, to_dp, to_seq):
        return pltpu.make_async_remote_copy(
            src_ref=src, dst_ref=dst_ref, send_sem=ss, recv_sem=rs,
            device_id=(to_dp, to_seq), device_id_type=MESH,
        )

    down_rows, up_cols = recv0[0].shape[1], recv0[2].shape[2]
    size = [down_rows] * 2 + [shard] * 9

    def s1(i, n):
        half = size[i] // 2
        lower, upper = pl.ds(0, half), pl.ds(half, half)
        m, part_rows, to_ref, to = (
            (6, lower, recv1x[i].at[1], xn), (6, upper, recv1y[i].at[1], yn),
            (2, lower, recv1x[i].at[0], xn), (4, upper, recv1y[i].at[0], yn),
        )[n]
        return send(recv0[i].at[m // 2, part_rows], to_ref, s1_s.at[i, n], s1_r.at[i, n], to, s)

    def s2(i, n):
        half = size[i] // 2
        if n == 0:
            return send(recv1x[i].at[1], recv2[i].at[pl.ds(0, half)],
                        s2_s.at[i, 0], s2_r.at[i, 0], yn, s)
        return send(recv1y[i].at[1], recv2[i].at[pl.ds(half, half)],
                    s2_s.at[i, 1], s2_r.at[i, 1], xn, s)

    mate = s + 1 - 2 * lax.rem(s, 2)
    across = 3 - s
    is_mid = jnp.logical_or(s == 1, s == 2)
    is_end = jnp.logical_or(s == 0, s == 3)

    def to_mid(i):
        return send(recv2[i], za[i], z_s.at[i, 0], z_r.at[i, 0], d, mate)

    def cross(i):
        return send(za[i], zb[i], z_s.at[i, 1], z_r.at[i, 1], d, across)

    def to_end(i):
        return send(zb[i], za[i], z_s.at[i, 2], z_r.at[i, 2], d, mate)

    def outputs(i, src):
        if i < 2:
            return [pltpu.make_async_copy(src, dwd_h.at[pl.ds(i * down_rows, down_rows)],
                                          osem.at[i, 0])]
        if i < 6:
            return [pltpu.make_async_copy(src, dwu_h.at[:, pl.ds((i - 2) * up_cols, up_cols)],
                                          osem.at[i, 0])]
        if i == 6:
            return [pltpu.make_async_copy(src, dwo_h, osem.at[i, 0])]
        return [
            pltpu.make_async_copy(
                src.at[:, pl.ds(third * group_cols, group_cols)],
                dwq_h.at[:, pl.ds(third * width + (i - 7) * group_cols, group_cols)],
                osem.at[i, third],
            )
            for third in range(3)
        ]

    def step1(i):
        for n in range(4):
            s1(i, n).start()

    def arrived(i, n):
        if i:
            s1(i, n).wait_recv()
        elif n == 0:
            for copy in ready_first:
                copy.wait()

    def step2(i):
        half = size[i] // 2
        arrived(i, 0)
        add_rows(recv1x[i].at[1], recv0[i].at[2, pl.ds(0, half)], half)
        s2(i, 0).start()
        arrived(i, 1)
        add_rows(recv1y[i].at[1], recv0[i].at[1, pl.ds(half, half)], half)
        s2(i, 1).start()
        arrived(i, 2)
        add_rows(recv1x[i].at[0], recv0[i].at[0, pl.ds(0, half)], half)
        arrived(i, 3)
        add_rows(recv1y[i].at[0], recv0[i].at[0, pl.ds(half, half)], half)

    def step3(i):
        half = size[i] // 2
        s2(i, 0).wait_recv()
        add_rows(recv2[i].at[pl.ds(0, half)], recv1x[i].at[0], half)
        s2(i, 1).wait_recv()
        add_rows(recv2[i].at[pl.ds(half, half)], recv1y[i].at[0], half)

        @pl.when(is_end)
        def _():
            to_mid(i).start()

    def step4(i):
        @pl.when(is_mid)
        def _():
            to_mid(i).wait_recv()
            add_rows(za[i], recv2[i], size[i])
            cross(i).start()

    def step5(i):
        @pl.when(is_mid)
        def _():
            cross(i).wait_recv()
            add_rows(zb[i], za[i], size[i])
            to_end(i).start()
            for copy in outputs(i, zb[i]):
                copy.start()

    def step6(i):
        @pl.when(is_end)
        def _():
            to_end(i).wait_recv()
            for copy in outputs(i, za[i]):
                copy.start()

    def drain(i):
        for n in range(4 if i else 0):
            s1(i, n).wait_send()
        for n in range(2):
            s2(i, n).wait_send()

        @pl.when(is_end)
        def _():
            to_mid(i).wait_send()
            for copy in outputs(i, za[i]):
                copy.wait()

        @pl.when(is_mid)
        def _():
            cross(i).wait_send()
            to_end(i).wait_send()
            for copy in outputs(i, zb[i]):
                copy.wait()

    def cols_of(b, n=ff_block):
        return pl.ds(pl.multiple_of(b * n, n), n)

    def gu_load(slot, b):
        return pltpu.make_async_copy(gu_in.at[:, cols_of(b)], ast.at[slot], asem.at[slot])

    lower_rows, upper_rows = pl.ds(0, down_rows), pl.ds(down_rows, down_rows)
    ready_first = [
        load(fx_in, recv1x[0], 11 + 2 * images), load(fy_in, recv1y[0], 12 + 2 * images),
        load(first_in.at[:, lower_rows], recv0[0], 13 + 2 * images),
    ]
    ready_second = load(first_in.at[:, upper_rows], recv0[1], 0)
    ready_second.start()
    for copy in ready_first:
        copy.start()
    load_h2 = load(h2_in, buf, 1)
    load_h2.start()
    load_qkv = load(qkv_in, qkv, 2)
    load_qkv.start()
    load_go = load(go_in, go, 3)
    load_go.start()

    def weight_group(g):
        return [
            pltpu.make_async_copy(
                wq_in.at[:, pl.ds(third * width + g * group_cols, group_cols)],
                wqg.at[g % 2, :, pl.ds(third * group_cols, group_cols)],
                wsem.at[g % 2, third],
            )
            for third in range(3)
        ]

    for copy in weight_group(0):
        copy.start()
    pl.semaphore_wait(barrier, 7 + images - 1)
    top_copies = [
        send(top_in, rtop.at[d], tp_s.at[m - 1], tp_r.at[m - 1], flip(d, m), s)
        for m in range(1, 8)
    ]
    for copy in top_copies:
        copy.start()
    gu_load(0, 0).start()
    load_ga = load(ga_in, gbuf, 4)
    load_ga.start()
    dh[...] = jnp.zeros_like(dh)
    colm[...] = jnp.transpose((mask_in[...] - 1.0) * 1e30)
    ready_second.wait()

    def turned(src):
        @pl.loop(0, 8)
        def _(m):
            at = pl.ds(pl.multiple_of(flip_traced(d, m) * shard, shard), shard)
            ht[rows_of(m, shard), :] = jnp.transpose(src[:, at])

    load_att = load(att_in, buf, 5)
    load_h1 = load(h1_in, buf, 6)
    load_tok = load(tok_in, gbuf, 7)

    def turn1():
        load_h2.wait()
        turned(buf)
        load_att.start()

    def split_store(value, keep, give, cols_keep, cols_give):
        for m in range(8):
            piece = value[m * shard : (m + 1) * shard].astype(BF)
            if m % 2 == 0:
                keep[m // 2, :, cols_keep] = piece
            else:
                give[m // 2, :, cols_give] = piece

    blocks = up_cols // tile

    def up_send(i, n):
        return send(ust.at[n], recv0[2 + i].at[:, :, cols_of(n, tile)],
                    u0_s.at[i, n], u0_r.at[i, n], sib, s)

    def up(i):
        if i:
            for n in range(blocks):
                up_send(i - 1, n).wait_send()

        def body(n, carry):
            b = i * blocks + n
            slot = lax.rem(b, 2)
            gu_load(slot, b).wait()

            @pl.when(b + 1 < 4 * blocks)
            def _():
                gu_load(1 - slot, b + 1).start()

            value = dot_nn(ht[...], ast[slot])
            split_store(value, own_u.at[i % 2], ust.at[n], cols_of(n, tile), slice(None))
            up_send(i, n).start()
            return carry

        lax.fori_loop(0, blocks, body, 0)

    def add_up(i):
        for n in range(blocks):
            up_send(i, n).wait_recv()
        for m in (6, 2, 4, 0):
            add_rows(recv0[2 + i].at[m // 2], own_u.at[i % 2, m // 2], shard)

    def out_send(n):
        return send(ust.at[n], recv0[6].at[:, :, pl.ds(n * tile, tile)],
                    s0_s.at[0, n], s0_r.at[0, n], sib, s)

    def out():
        load_ga.wait()
        load_att.wait()
        turned(buf)
        load_h1.start()
        for n in range(blocks):
            up_send(3, n).wait_send()
        for n in range(width // tile):
            value = dot_nn(ht[...], gbuf[:, pl.ds(n * tile, tile)])
            split_store(value, stg_o, ust.at[n], pl.ds(n * tile, tile), slice(None))
            out_send(n).start()
        load_tok.start()

    def turn3():
        load_h1.wait()
        turned(buf)

    def add_out():
        for n in range(width // tile):
            out_send(n).wait_recv()
            out_send(n).wait_send()
        for m in (6, 2, 4, 0):
            add_rows(recv0[6].at[m // 2], stg_o.at[m // 2], shard)

    low, high, low_lane = half_masks()
    scale = HD ** (-0.5)
    pair = 2 * HD
    per_group = group_cols // pair
    cuts = ((0, 256), (256, length - 256)) if length > 256 else ((0, length),)
    def attention(g):
        if g == 0:
            load_qkv.wait()
            load_go.wait()
        if g + 1 < groups:
            for copy in weight_group(g + 1):
                copy.start()

        def body(n, carry):
            p = g * per_group + n
            c = pl.ds(pl.multiple_of(p * pair, pair), pair)
            ck = pl.ds(pl.multiple_of(width + p * pair, pair), pair)
            cv = pl.ds(pl.multiple_of(2 * width + p * pair, pair), pair)
            k, v = qkv[:, ck], qkv[:, cv]
            k2 = jnp.concatenate([k * low, k * high], axis=0)
            v2 = jnp.concatenate([v * low, v * high], axis=0)
            gk = jnp.zeros((2 * length, pair), F32)
            gv = jnp.zeros((2 * length, pair), F32)
            at_q = pl.ds(pl.multiple_of(n * pair, pair), pair)
            at_k = pl.ds(pl.multiple_of(group_cols + n * pair, pair), pair)
            at_v = pl.ds(pl.multiple_of(2 * group_cols + n * pair, pair), pair)
            for first, wide in cuts:
                r = pl.ds(first, wide)
                q = qkv[r, c] * jnp.asarray(scale, BF)
                g_rows = go[r, c]
                scores = dot_nt(k2, q)
                dprob = dot_nt(v2, g_rows)
                low_probs, low_grads = [], []
                for side in range(2):
                    rows = slice(side * length, (side + 1) * length)
                    part_s = scores[rows] + colm[:, 0:1]
                    e = jnp.exp(part_s - jnp.max(part_s, axis=0, keepdims=True))
                    probs = e * (1.0 / jnp.sum(e, axis=0, keepdims=True))
                    weighted = probs * dprob[rows]
                    inner = jnp.sum(weighted, axis=0, keepdims=True)
                    low_probs.append(probs.astype(BF))
                    low_grads.append((weighted - probs * inner).astype(BF))
                low_p = jnp.concatenate(low_probs, axis=0)
                low_g = jnp.concatenate(low_grads, axis=0)
                gv = gv + dot_nn(low_p, g_rows)
                gk = gk + dot_nn(low_g, q)
                gp[r, at_q] = (dot_tn(low_g, k2) * scale).astype(BF)
            gp[:, at_k] = jnp.where(low_lane, gk[:length], gk[length:]).astype(BF)
            gp[:, at_v] = jnp.where(low_lane, gv[:length], gv[length:]).astype(BF)
            return carry

        lax.fori_loop(0, per_group, body, 0)

    bias_rows = []

    def q_send(g):
        return send(pq.at[g % 2, 1], recv0[7 + g], s0_s.at[1 + g, 0], s0_r.at[1 + g, 0], sib, s)

    def group(g):
        if g >= 2:
            q_send(g - 2).wait_send()
        bias_rows.append(jnp.sum(gp[...].astype(F32), axis=0, keepdims=True))
        for third in range(3):
            cols = pl.ds(third * group_cols, group_cols)
            value = dot_nn(ht[...], gp[:, cols])
            split_store(value, pq.at[g % 2, 0], pq.at[g % 2, 1], cols, cols)
        q_send(g).start()
        for copy in weight_group(g):
            copy.wait()
        for first in range(0, width, tile):
            dh[:, pl.ds(first, tile)] += dot_nt(gp[...], wqg[g % 2, pl.ds(first, tile), :])

    def add_q(g):
        q_send(g).wait_recv()
        for m in (6, 2, 4, 0):
            add_rows(recv0[7 + g].at[m // 2], pq.at[g % 2, 0, m // 2], shard)

    gain1 = vec_in[pl.ds(8, 1), :]
    zero = jnp.zeros((1, width), F32)

    def gx_load(slot, i):
        return pltpu.make_async_copy(gx_in.at[rows_of(i, block)], gxs.at[slot], gsem.at[slot])

    def norm_back(i, acc):
        slot = lax.rem(i, 2)
        gx_load(slot, i).wait()

        @pl.when(i + 1 < length // block)
        def _():
            gx_load(1 - slot, i + 1).start()

        r = rows_of(i, block)
        g = dh[r, :]
        xh, spread = normalized(gbuf[r, :].astype(F32))
        gg = g * gain1
        inner = gg - jnp.mean(gg, axis=1, keepdims=True)
        inner = inner - xh * jnp.mean(gg * xh, axis=1, keepdims=True)
        go[r, :] = (gxs[slot] + spread * inner).astype(BF)
        return (
            acc[0] + jnp.sum(g * xh, axis=0, keepdims=True),
            acc[1] + jnp.sum(g, axis=0, keepdims=True),
        )

    late = {}
    tg_copies = []
    for j in range(1, images):
        to = lax.rem(s + j, images)
        tg_copies.append(
            send(go.at[rows_of(to, part)], tg_h.at[s], ex_s.at[j - 1], ex_r.at[j - 1], d, to)
        )
    own_tg = load(go.at[rows_of(s, part)], tg_h.at[s], 8)

    own_loads = []
    for j in range(images):
        rows = pl.ds(j * part, part)
        own_loads.append(load(mine_in.at[j], qkv.at[rows, pl.ds(0, width)], 9 + j))
        own_loads.append(load(atto_in.at[j], qkv.at[rows, pl.ds(width, width)], 9 + images + j))
    own_loads.append(load(wo_in.at[pl.ds(0, tile)], dst.at[0], 9 + 2 * images))
    own_loads.append(load(wo_in.at[pl.ds(tile, tile)], dst.at[1], 10 + 2 * images))

    def norm1():
        for copy in own_loads:
            copy.start()
        load_tok.wait()
        gx_load(0, 0).start()
        late["norm"] = lax.fori_loop(0, length // block, norm_back, (zero, zero))

    def tg():
        for copy in tg_copies:
            copy.start()
        own_tg.start()

    sm_copies = [
        send(psm.at[flip(d, m)], rsm.at[m - 1], sm_s.at[m - 1], sm_r.at[m - 1], flip(d, m), s)
        for m in range(1, 8)
    ]
    top_z, sm_z = [], []
    for j in range(1, images):
        to = lax.rem(s + j, images)
        top_z.append(send(ztop.at[s], ztop.at[s], tz_s.at[j - 1], tz_r.at[j - 1], d, to))
        sm_z.append(send(zsm.at[s], zsm.at[s], zs_s.at[j - 1], zs_r.at[j - 1], d, to))

    def smalls():
        d_gain1, d_shift1 = late["norm"]
        q_sum = jnp.concatenate([row[:, :group_cols] for row in bias_rows], axis=1)
        v_sum = jnp.concatenate([row[:, 2 * group_cols :] for row in bias_rows], axis=1)
        pieces = (
            d_gain1, d_shift1, jnp.concatenate([q_sum, v_sum], axis=1), vec_in[pl.ds(2, 1), :],
            vec_in[pl.ds(0, 1), :], vec_in[pl.ds(1, 1), :], dbup_in[...], vec_in[pl.ds(3, 1), :],
        )
        for b in range(8):
            psm[b] = jnp.concatenate(
                [piece[:, b * n : (b + 1) * n] for piece, n in zip(pieces, SMALL)], axis=1
            )
        for copy in sm_copies:
            copy.start()
        for copy in top_copies:
            copy.wait_recv()
        rtop[d] = top_in[...]
        best = rtop[0]
        for b in range(1, 8):
            best = jnp.maximum(best, rtop[b])
        ztop[s] = best
        for copy in top_z:
            copy.start()

    def smalls_z():
        for copy in sm_copies:
            copy.wait_recv()
        mine = psm[d]
        for m in range(7):
            mine = mine + rsm[m]
        zsm[s] = mine
        for copy in sm_z:
            copy.start()

    gain2, shift2 = vec_in[pl.ds(9, 1), :], vec_in[pl.ds(10, 1), :]
    b_out, b_down = vec_in[pl.ds(11, 1), :], vec_in[pl.ds(12, 1), :]

    def owners():
        for copy in own_loads:
            copy.wait()

        @pl.loop(0, length // block)
        def _(i):
            r = rows_of(i, block)
            mid = qkv[r, 0:width].astype(F32) + b_out
            mid = mid + dot_nn(qkv[r, width : width + tile], dst[0])
            mid = mid + dot_nn(qkv[r, width + tile : 2 * width], dst[1])
            xh, _ = normalized(mid)
            dh[r, :] = mid + b_down
            qkv[r, 2 * width :] = (xh * gain2 + shift2).astype(BF)

        for copy in ff_loads(0, 0):
            copy.start()

    def ff_loads(slot, b):
        return (
            pltpu.make_async_copy(wu_in.at[:, cols_of(b)], wqg.at[slot, :, pl.ds(0, ff_block)],
                                  wsem.at[slot, 0]),
            pltpu.make_async_copy(wd_in.at[rows_of(b, ff_block)], dst.at[slot],
                                  wsem.at[slot, 1]),
        )

    def feed_block(b, carry):
        slot = lax.rem(b, 2)
        for copy in ff_loads(slot, b):
            copy.wait()

        @pl.when(b < 7)
        def _():
            for copy in ff_loads(1 - slot, b + 1):
                copy.start()

        u = dot_nn(qkv[:, 2 * width :], wqg[slot, :, 0:ff_block]) + bup_in[:, cols_of(b)]
        a = (u * (0.5 * (1.0 + lax.erf(u * (0.5**0.5))))).astype(BF)
        dh[...] += dot_nn(a, dst[slot])
        return carry

    keep_out = load(buf, out_h, 1)

    def feed(n):
        lax.fori_loop(2 * n, 2 * n + 2, feed_block, 0)
        if n == 1:
            smalls_z()
        if n == 3:
            buf[...] = dh[...].astype(BF)
            keep_out.start()

    step2(0)
    turn1()
    up(0)
    step1(1)
    up(1)
    add_up(0)
    step3(0)
    up(2)
    add_up(1)
    up(3)
    step1(3)
    out()
    step2(1)
    turn3()
    add_out()
    step1(6)
    attention(0)
    step3(1)
    step4(0)
    step2(3)
    group(0)
    step1(2)
    attention(1)
    step2(6)
    step3(3)
    add_up(2)
    step4(1)
    step5(0)
    add_up(3)
    step2(2)
    step1(5)
    group(1)
    step3(6)
    step1(4)
    step4(3)
    attention(2)
    step5(1)
    add_q(1)
    add_q(0)
    step4(6)
    step3(2)
    step2(5)
    group(2)
    step5(3)
    step2(4)
    step4(2)
    step1(7)
    step3(5)
    attention(3)
    step4(5)
    step3(4)
    step2(7)
    add_q(2)
    step5(6)
    step1(8)
    group(3)
    step5(2)
    step3(7)
    step4(4)
    norm1()
    step4(7)
    tg()
    step5(4)
    step6(0)
    add_q(3)
    owners()
    step5(5)
    smalls()
    step6(1)
    step1(9)
    feed(0)
    step1(10)
    step6(6)
    step2(9)
    feed(1)
    step6(2)
    step6(3)
    step2(8)
    step3(9)
    step3(8)
    step2(10)
    step3(10)
    step4(8)
    step5(7)
    step4(10)
    step6(5)
    step4(9)
    feed(2)
    step5(8)
    step5(10)
    step6(8)
    step6(4)
    feed(3)
    step5(9)
    step6(10)
    step6(7)
    step6(9)

    for copy in top_z + sm_z:
        copy.wait_recv()
    top_o[...] = jnp.maximum(jnp.maximum(ztop[0], ztop[1]), jnp.maximum(ztop[2], ztop[3]))
    small_o[...] = (zsm[0] + zsm[1]) + (zsm[2] + zsm[3])
    for g in range(groups - 2, groups):
        q_send(g).wait_send()
    for i in range(count):
        drain(i)
    for copy in top_copies + top_z + sm_copies + sm_z + tg_copies:
        copy.wait_send()
    for copy in tg_copies:
        copy.wait_recv()
    own_tg.wait()
    keep_out.wait()


def back(tokens, saved, vecs):
    images, part, width = tokens.shape
    (
        tok, h1, qkv, gx, go, ga, h2, gu, att, atto, first, fx, fy, wq, wo, wu, wd,
    ) = saved
    vec, dbup, bup, tops, mask = vecs
    length = images * part
    wide, ff = wq.shape[1], wu.shape[1]
    shard = width // 8
    shape = jax.ShapeDtypeStruct
    any_spec = pl.BlockSpec(memory_space=pl.ANY)
    vmem_spec = pl.BlockSpec(memory_space=pltpu.VMEM)
    dma = pltpu.SemaphoreType.DMA
    vm = pltpu.VMEM
    group_cols = 256
    groups = width // group_cols
    sizes = [(ff // 16, width)] * 2 + [(shard, ff // 4)] * 4 + [(shard, width)]
    sizes += [(shard, 3 * group_cols)] * groups
    count = len(sizes)
    halves = [vm((2, r // 2, c), BF) for r, c in sizes]
    whole = [vm((r, c), BF) for r, c in sizes]
    z_peers = images - 1
    small = sum(SMALL)
    return pl.pallas_call(
        back_kernel,
        name="back",
        out_shape=(
            shape((length, width), BF),
            shape((images, part, width), BF),
            shape((shard, wide), BF),
            shape((shard, width), BF),
            shape((shard, ff), BF),
            shape((ff // 8, width), BF),
            shape((1, small), F32),
            shape((8, 2 * HD), F32),
        ),
        in_specs=[any_spec] * 18 + [vmem_spec] * 5,
        out_specs=[any_spec] * 6 + [vmem_spec] * 2,
        scratch_shapes=[
            vm((length, wide), BF), vm((length, width), BF), vm((width, length), BF),
            vm((length, width), BF), vm((length, width), BF), vm((length, width), F32),
            vm((2, width, 3 * group_cols), BF), vm((2, 2, 4, shard, 3 * group_cols), BF),
            vm((length, 3 * group_cols), BF), vm((length, 8), F32),
            vm((2, ff // 8, width), BF), vm((2, 4, shard, ff // 4), BF), vm((2, 4, shard, 512), BF),
            vm((4, shard, width), BF), vm((2, length, ff // 8), BF), vm((2, 128, width), F32),
            vm((8, 1, small), F32), vm((7, 1, small), F32),
            vm((images, 1, small), F32), vm((8, 8, 2 * HD), F32), vm((images, 8, 2 * HD), F32),
            *[vm((4, r, c), BF) for r, c in sizes], *halves, *halves, *whole, *whole, *whole,
            dma((5, 2)), dma((5, 2)), dma((4, 2)), dma((4, 2)), dma((count, 4)),
            dma((count, 4)), dma((count, 2)), dma((count, 2)), dma((count, 3)), dma((count, 3)),
            dma((z_peers,)), dma((z_peers,)), dma((7,)), dma((7,)),
            dma((z_peers,)), dma((z_peers,)), dma((7,)), dma((7,)),
            dma((z_peers,)), dma((z_peers,)), dma((2,)), dma((2, 3)), dma((count, 3)),
            dma((14 + 2 * images,)), dma((2,)),
        ],
        compiler_params=pltpu.CompilerParams(
            collective_id=1, has_side_effects=True, vmem_limit_bytes=63 << 20
        ),
    )(
        qkv, go, h1, gx, tok, ga, h2, gu, att, atto, first, fx, fy, tokens, wq, wo, wu, wd,
        mask, vec, dbup, bup, tops,
    )


def by_image_local(
    tokens,
    filled,
    out_grad,
    norm1_gain,
    norm1_bias,
    qkv_weight,
    qv_bias,
    out_weight,
    out_bias,
    norm2_gain,
    norm2_bias,
    up_weight,
    up_bias,
    down_weight,
    down_bias,
    clip_threshold,
):
    images, local_rows, model_width = tokens.shape
    length = local_rows * images
    seq_index = lax.axis_index("seq")
    small, start = 0.0, 0
    for piece in (
        norm1_gain, norm1_bias, qv_bias, out_bias, norm2_gain, norm2_bias, up_bias, down_bias
    ):
        count = piece.shape[0]
        small = small + jnp.pad(piece.astype(F32), (start, sum(SMALL) - start - count))
        start += count
    small = small[None]
    flags = lax.dynamic_update_slice(
        jnp.zeros((images, 8, length), F32),
        jnp.broadcast_to((filled > 0).astype(F32)[:, None, :], (images, 8, local_rows)),
        (0, 0, seq_index * local_rows),
    )
    made = front(tokens, out_grad, flags, qkv_weight, out_weight, up_weight, down_weight, small)
    block_out, tokens_grad, g_qkv, g_out, g_up, g_down, mine, top = back(
        tokens, made[:17], made[17:]
    )
    block_out = block_out.reshape(tokens.shape)
    head_max = top[:, ::HD].reshape(-1)
    small_out, start = [], 0
    for count in SMALL:
        small_out.append(mine[0, start : start + count])
        start += count
    s_gain_one, s_shift_one, s_qv, s_out, s_gain_two, s_shift_two, s_up, s_down = small_out
    limit = clip_threshold.astype(F32)
    root_factor = jnp.sqrt(limit / jnp.maximum(head_max, limit))
    head_cols = jnp.repeat(root_factor, HD)
    ones = jnp.ones((model_width,), F32)
    weight_scale = jnp.concatenate([head_cols, head_cols, ones])
    clipped_weight = (qkv_weight.astype(F32) * weight_scale[None, :]).astype(BF)
    bias_count = qv_bias.shape[0]
    bias_scale = jnp.concatenate([head_cols, ones])
    shard_scale = lax.dynamic_slice_in_dim(
        bias_scale, lax.axis_index("dp") * bias_count, bias_count
    )
    clipped_bias = (qv_bias.astype(F32) * shard_scale).astype(BF)
    return (
        block_out,
        tokens_grad,
        s_gain_one,
        s_shift_one,
        g_qkv.astype(F32),
        s_qv,
        g_out.astype(F32),
        s_out,
        s_gain_two,
        s_shift_two,
        g_up.astype(F32),
        s_up,
        g_down.astype(F32),
        s_down,
        clipped_weight,
        clipped_bias,
        head_max,
    )


def local(*args):
    if args[0].shape[0] == lax.axis_size("seq") == 4 and lax.axis_size("dp") == 8:
        return by_image_local(*args)
    return by_head_local(*args)


def solution(mesh):
    return jax.shard_map(
        local,
        mesh=mesh,
        in_specs=(
            P("dp", "seq", None),
            P("dp", "seq"),
            P("dp", "seq", None),
            P("dp"),
            P("dp"),
            P("dp", None),
            P("dp"),
            P("dp", None),
            P("dp"),
            P("dp"),
            P("dp"),
            P("dp", None),
            P("dp"),
            P("dp", None),
            P("dp"),
            P(),
        ),
        out_specs=(
            P("dp", "seq", None),
            P("dp", "seq", None),
            P("dp"),
            P("dp"),
            P("dp", None),
            P("dp"),
            P("dp", None),
            P("dp"),
            P("dp"),
            P("dp"),
            P("dp", None),
            P("dp"),
            P("dp", None),
            P("dp"),
            P("dp", None),
            P("dp"),
            P(),
        ),
        check_vma=False,
    )
```

```python
import math

import jax
import jax.numpy as jnp
from jax import lax
from jax.experimental import pallas as pl
from jax.experimental.pallas import tpu as pltpu
from jax.sharding import PartitionSpec as P

H = 16
HD = 64


epsilon = 1e-06
very_negative = -1e30


def norm_apply(values, gain_vec, shift_vec):
    center = jnp.mean(values, axis=-1, keepdims=True)
    centered = values - center
    spread = jnp.mean(centered * centered, axis=-1, keepdims=True)
    return centered * lax.rsqrt(spread + epsilon) * gain_vec + shift_vec


def exact_gelu(values):
    return jax.nn.gelu(values, approximate=False)


def last_dot(left_op, right_op):
    return lax.dot_general(
        left_op, right_op, (((1,), (1,)), ((), ())), preferred_element_type=jnp.float32
    )


def first_dot(left_op, right_op):
    return lax.dot_general(
        left_op, right_op, (((0,), (0,)), ((), ())), preferred_element_type=jnp.float32
    )


def column_sum(values):
    return jnp.sum(values.astype(jnp.float32), axis=0)


def score_block(queries, keys_in, key_keep):
    raw_scores = jnp.einsum(
        "qhd,khd->hqk", queries, keys_in, preferred_element_type=jnp.float32
    ) * HD ** (-0.5)
    masked = jnp.where(key_keep[None, None, :], raw_scores, very_negative)
    return (raw_scores, masked)


def attend_forward(inputs):
    queries, keys_in, values_in, key_keep = inputs
    raw_scores, masked = score_block(queries, keys_in, key_keep)
    row_peak = jnp.max(masked, axis=-1, keepdims=True)
    exp_scores = jnp.exp(masked - row_peak)
    row_total = jnp.sum(exp_scores, axis=-1, keepdims=True)
    soft_probs = (exp_scores / row_total).astype(jnp.bfloat16)
    mixed_rows = jnp.einsum(
        "hqk,khd->qhd", soft_probs, values_in, preferred_element_type=jnp.float32
    )
    logsum = row_peak + jnp.log(row_total)
    pair_keep = key_keep[:, None] & key_keep[None, :]
    head_top = jnp.max(jnp.where(pair_keep[None], raw_scores, very_negative), axis=(1, 2))
    flat_rows = mixed_rows.astype(jnp.bfloat16).reshape(mixed_rows.shape[0], -1)
    return (flat_rows, logsum, head_top)


def attend_backward(inputs):
    queries, keys_in, values_in, key_keep, logsum, upstream = inputs
    raw_scores, masked = score_block(queries, keys_in, key_keep)
    soft_probs = jnp.exp(masked - logsum)
    probs_low = soft_probs.astype(jnp.bfloat16)
    value_grad = jnp.einsum("hqk,qhd->khd", probs_low, upstream, preferred_element_type=jnp.float32)
    prob_grad = jnp.einsum("qhd,khd->hqk", upstream, values_in, preferred_element_type=jnp.float32)
    inner_sum = jnp.sum(soft_probs * prob_grad, axis=-1, keepdims=True)
    score_grad = (soft_probs * (prob_grad - inner_sum)).astype(jnp.bfloat16)
    score_scale = HD ** (-0.5)
    query_grad = (
        jnp.einsum("hqk,khd->qhd", score_grad, keys_in, preferred_element_type=jnp.float32)
        * score_scale
    )
    key_grad = (
        jnp.einsum("hqk,qhd->khd", score_grad, queries, preferred_element_type=jnp.float32)
        * score_scale
    )
    stacked = jnp.stack([query_grad, key_grad, value_grad], axis=1)
    return stacked.astype(jnp.bfloat16).reshape(stacked.shape[0], 3, -1)


def by_head_local(
    tokens,
    filled,
    out_grad,
    norm1_gain,
    norm1_bias,
    qkv_weight,
    qv_bias,
    out_weight,
    out_bias,
    norm2_gain,
    norm2_bias,
    up_weight,
    up_bias,
    down_weight,
    down_bias,
    clip_threshold,
):
    gathered = (
        lax.all_gather(norm1_gain, "dp", axis=0, tiled=True),
        lax.all_gather(norm1_bias, "dp", axis=0, tiled=True),
        lax.all_gather(qkv_weight, "dp", axis=0, tiled=True),
        lax.all_gather(qv_bias, "dp", axis=0, tiled=True),
        lax.all_gather(out_weight, "dp", axis=0, tiled=True),
        lax.all_gather(out_bias, "dp", axis=0, tiled=True),
        lax.all_gather(norm2_gain, "dp", axis=0, tiled=True),
        lax.all_gather(norm2_bias, "dp", axis=0, tiled=True),
        lax.all_gather(up_weight, "dp", axis=0, tiled=True),
        lax.all_gather(up_bias, "dp", axis=0, tiled=True),
        lax.all_gather(down_weight, "dp", axis=0, tiled=True),
        lax.all_gather(down_bias, "dp", axis=0, tiled=True),
    )
    (
        gain_one,
        shift_one,
        w_qkv,
        b_qv,
        w_out,
        b_out,
        gain_two,
        shift_two,
        w_up,
        b_up,
        w_down,
        b_down,
    ) = gathered
    images, local_rows, model_width = tokens.shape
    groups = lax.axis_size("seq")
    group_width = model_width // groups
    local_heads = group_width // HD
    length = local_rows * groups
    row_count = images * local_rows
    tokens_flat = tokens.astype(jnp.float32).reshape(row_count, model_width)
    gain_one_f = gain_one.astype(jnp.float32)
    shift_one_f = shift_one.astype(jnp.float32)
    gain_two_f = gain_two.astype(jnp.float32)
    shift_two_f = shift_two.astype(jnp.float32)
    hidden_one = norm_apply(tokens_flat, gain_one_f, shift_one_f).astype(jnp.bfloat16)
    bias_float = b_qv.astype(jnp.float32)
    qkv_bias = jnp.concatenate(
        [bias_float[:model_width], jnp.zeros((model_width,), jnp.float32), bias_float[model_width:]]
    )
    projected = (jnp.dot(hidden_one, w_qkv, preferred_element_type=jnp.float32) + qkv_bias).astype(
        jnp.bfloat16
    )
    key_flags = lax.all_gather(filled, "seq", axis=1, tiled=True)
    keep_all = key_flags > 0
    by_heads = lax.all_to_all(
        projected.reshape(images, local_rows, 3, groups, group_width),
        "seq",
        split_axis=3,
        concat_axis=1,
        tiled=True,
    )
    by_heads = by_heads.reshape(images, length, 3, local_heads, HD)
    queries = by_heads[:, :, 0]
    keys_all = by_heads[:, :, 1]
    values_all = by_heads[:, :, 2]
    attended, logsums, tops = lax.map(attend_forward, (queries, keys_all, values_all, keep_all))
    local_peak = jnp.max(tops, axis=0)
    peak_vector = lax.dynamic_update_slice(
        jnp.full((H,), very_negative, jnp.float32),
        local_peak,
        (lax.axis_index("seq") * local_heads,),
    )
    head_max = lax.pmax(peak_vector, ("dp", "seq"))
    back_rows = lax.all_to_all(
        attended.reshape(images, groups, local_rows, group_width),
        "seq",
        split_axis=1,
        concat_axis=3,
        tiled=True,
    )
    attn_rows = back_rows.reshape(row_count, model_width)
    branch = jnp.dot(attn_rows, w_out, preferred_element_type=jnp.float32) + b_out.astype(
        jnp.float32
    )
    middle = tokens_flat + branch
    hidden_two = norm_apply(middle, gain_two_f, shift_two_f).astype(jnp.bfloat16)
    pre_act = jnp.dot(hidden_two, w_up, preferred_element_type=jnp.float32) + b_up.astype(
        jnp.float32
    )
    activated = exact_gelu(pre_act).astype(jnp.bfloat16)
    block_rows = middle + (
        jnp.dot(activated, w_down, preferred_element_type=jnp.float32) + b_down.astype(jnp.float32)
    )
    block_out = block_rows.astype(jnp.bfloat16).reshape(tokens.shape)
    gain_one_b, w_qkv_b, w_out_b, gain_two_b, w_up_b, w_down_b = (
        lax.all_gather(norm1_gain, "dp", axis=0, tiled=True),
        lax.all_gather(qkv_weight, "dp", axis=0, tiled=True),
        lax.all_gather(out_weight, "dp", axis=0, tiled=True),
        lax.all_gather(norm2_gain, "dp", axis=0, tiled=True),
        lax.all_gather(up_weight, "dp", axis=0, tiled=True),
        lax.all_gather(down_weight, "dp", axis=0, tiled=True),
    )
    upstream = out_grad.reshape(row_count, model_width)
    upstream_f = upstream.astype(jnp.float32)
    d_bias_down = jnp.sum(upstream_f, axis=0)
    d_down = first_dot(activated, upstream)
    act_grad = last_dot(upstream, w_down_b)
    gelu_out, gelu_pull = jax.vjp(exact_gelu, pre_act)
    pre_grad = gelu_pull(act_grad)[0].astype(jnp.bfloat16)
    d_bias_up = column_sum(pre_grad)
    d_up = first_dot(hidden_two, pre_grad)
    hidden_two_grad = last_dot(pre_grad, w_up_b)
    norm_out_two, pull_two = jax.vjp(
        norm_apply, middle, gain_two_b.astype(jnp.float32), shift_two_f
    )
    mid_norm_grad, d_gain_two, d_shift_two = pull_two(hidden_two_grad)
    middle_grad = upstream_f + mid_norm_grad
    branch_grad = middle_grad.astype(jnp.bfloat16)
    d_bias_out = column_sum(branch_grad)
    d_out = first_dot(attn_rows, branch_grad)
    attn_grad = last_dot(branch_grad, w_out_b).astype(jnp.bfloat16)
    grad_heads = lax.all_to_all(
        attn_grad.reshape(images, local_rows, groups, group_width),
        "seq",
        split_axis=2,
        concat_axis=1,
        tiled=True,
    )
    grad_heads = grad_heads.reshape(images, length, local_heads, HD)
    head_grads = lax.map(
        attend_backward, (queries, keys_all, values_all, keep_all, logsums, grad_heads)
    )
    token_grads = lax.all_to_all(
        head_grads.reshape(images, groups, local_rows, 3, group_width),
        "seq",
        split_axis=1,
        concat_axis=4,
        tiled=True,
    )
    token_grads = token_grads.reshape(row_count, 3 * model_width)
    d_qkv = first_dot(hidden_one, token_grads)
    bias_sums = column_sum(token_grads)
    d_bias_qv = jnp.concatenate([bias_sums[:model_width], bias_sums[2 * model_width :]])
    first_grad = last_dot(token_grads, w_qkv_b)
    norm_out_one, pull_one = jax.vjp(
        norm_apply, tokens_flat, gain_one_b.astype(jnp.float32), shift_one_f
    )
    in_norm_grad, d_gain_one, d_shift_one = pull_one(first_grad)
    tokens_grad = (middle_grad + in_norm_grad).astype(jnp.bfloat16).reshape(tokens.shape)
    terms = (
        d_gain_one,
        d_shift_one,
        d_qkv,
        d_bias_qv,
        d_out,
        d_bias_out,
        d_gain_two,
        d_shift_two,
        d_up,
        d_bias_up,
        d_down,
        d_bias_down,
    )
    data_shards = (
        lax.psum_scatter(
            terms[0].astype(jnp.bfloat16), "dp", scatter_dimension=0, tiled=True
        ).astype(jnp.float32),
        lax.psum_scatter(
            terms[1].astype(jnp.bfloat16), "dp", scatter_dimension=0, tiled=True
        ).astype(jnp.float32),
        lax.psum_scatter(
            terms[2].astype(jnp.bfloat16), "dp", scatter_dimension=0, tiled=True
        ).astype(jnp.float32),
        lax.psum_scatter(
            terms[3].astype(jnp.bfloat16), "dp", scatter_dimension=0, tiled=True
        ).astype(jnp.float32),
        lax.psum_scatter(
            terms[4].astype(jnp.bfloat16), "dp", scatter_dimension=0, tiled=True
        ).astype(jnp.float32),
        lax.psum_scatter(
            terms[5].astype(jnp.bfloat16), "dp", scatter_dimension=0, tiled=True
        ).astype(jnp.float32),
        lax.psum_scatter(
            terms[6].astype(jnp.bfloat16), "dp", scatter_dimension=0, tiled=True
        ).astype(jnp.float32),
        lax.psum_scatter(
            terms[7].astype(jnp.bfloat16), "dp", scatter_dimension=0, tiled=True
        ).astype(jnp.float32),
        lax.psum_scatter(
            terms[8].astype(jnp.bfloat16), "dp", scatter_dimension=0, tiled=True
        ).astype(jnp.float32),
        lax.psum_scatter(
            terms[9].astype(jnp.bfloat16), "dp", scatter_dimension=0, tiled=True
        ).astype(jnp.float32),
        lax.psum_scatter(
            terms[10].astype(jnp.bfloat16), "dp", scatter_dimension=0, tiled=True
        ).astype(jnp.float32),
        lax.psum_scatter(
            terms[11].astype(jnp.bfloat16), "dp", scatter_dimension=0, tiled=True
        ).astype(jnp.float32),
    )
    shards = (
        lax.psum(data_shards[0].astype(jnp.bfloat16), "seq").astype(jnp.float32),
        lax.psum(data_shards[1].astype(jnp.bfloat16), "seq").astype(jnp.float32),
        lax.psum(data_shards[2].astype(jnp.bfloat16), "seq").astype(jnp.float32),
        lax.psum(data_shards[3].astype(jnp.bfloat16), "seq").astype(jnp.float32),
        lax.psum(data_shards[4].astype(jnp.bfloat16), "seq").astype(jnp.float32),
        lax.psum(data_shards[5].astype(jnp.bfloat16), "seq").astype(jnp.float32),
        lax.psum(data_shards[6].astype(jnp.bfloat16), "seq").astype(jnp.float32),
        lax.psum(data_shards[7].astype(jnp.bfloat16), "seq").astype(jnp.float32),
        lax.psum(data_shards[8].astype(jnp.bfloat16), "seq").astype(jnp.float32),
        lax.psum(data_shards[9].astype(jnp.bfloat16), "seq").astype(jnp.float32),
        lax.psum(data_shards[10].astype(jnp.bfloat16), "seq").astype(jnp.float32),
        lax.psum(data_shards[11].astype(jnp.bfloat16), "seq").astype(jnp.float32),
    )
    limit = clip_threshold.astype(jnp.float32)
    root_factor = jnp.sqrt(limit / jnp.maximum(head_max, limit))
    head_cols = jnp.repeat(root_factor, HD)
    weight_scale = jnp.concatenate([head_cols, head_cols, jnp.ones((model_width,), jnp.float32)])
    clipped_weight = (qkv_weight.astype(jnp.float32) * weight_scale[None, :]).astype(jnp.bfloat16)
    bias_count = qv_bias.shape[0]
    bias_scale = jnp.concatenate([head_cols, jnp.ones((model_width,), jnp.float32)])
    shard_scale = lax.dynamic_slice_in_dim(
        bias_scale, lax.axis_index("dp") * bias_count, bias_count
    )
    clipped_bias = (qv_bias.astype(jnp.float32) * shard_scale).astype(jnp.bfloat16)
    return (
        block_out,
        tokens_grad,
        shards[0],
        shards[1],
        shards[2],
        shards[3],
        shards[4],
        shards[5],
        shards[6],
        shards[7],
        shards[8],
        shards[9],
        shards[10],
        shards[11],
        clipped_weight,
        clipped_bias,
        head_max,
    )


MESH = pl.DeviceIdType.MESH
BF = jnp.bfloat16
F32 = jnp.float32
SMALL = (128, 128, 256, 128, 128, 128, 512, 128)


def flip(d, m):
    y = lax.rem(lax.div(d, 4) + m // 4, 2)
    x = lax.rem(lax.rem(lax.div(d, 2), 2) + (m // 2) % 2, 2)
    k = lax.rem(lax.rem(d, 2) + m % 2, 2)
    return 4 * y + 2 * x + k


def flip_traced(d, m):
    y = lax.rem(lax.div(d, 4) + lax.div(m, 4), 2)
    x = lax.rem(lax.rem(lax.div(d, 2), 2) + lax.rem(lax.div(m, 2), 2), 2)
    k = lax.rem(lax.rem(d, 2) + lax.rem(m, 2), 2)
    return 4 * y + 2 * x + k


def dot_nn(a, b):
    return lax.dot_general(a, b, (((1,), (0,)), ((), ())), preferred_element_type=F32)


def dot_nt(a, b):
    return lax.dot_general(a, b, (((1,), (1,)), ((), ())), preferred_element_type=F32)


def dot_tn(a, b):
    return lax.dot_general(a, b, (((0,), (0,)), ((), ())), preferred_element_type=F32)


def rows_of(block, size, start=0, count=None):
    count = size if count is None else count
    step = math.gcd(size, start) if start else size
    return pl.ds(pl.multiple_of(block * size + start, step), count)


def normalized(v):
    center = jnp.mean(v, axis=-1, keepdims=True)
    centered = v - center
    spread = jnp.mean(centered * centered, axis=-1, keepdims=True)
    scale = lax.rsqrt(spread + epsilon)
    return centered * scale, scale


def half_masks():
    lane = lax.broadcasted_iota(jnp.int32, (1, 2 * HD), 1)
    low = jnp.where(lane < HD, 1.0, 0.0)
    return low.astype(BF), (1.0 - low).astype(BF), lane < HD


def add_rows(target, other, rows, step=32):
    @pl.loop(0, rows // step)
    def _(i):
        r = rows_of(i, step)
        target[r, :] = target[r, :] + other[r, :]


def front_kernel(
    tok_in, grad_in, fil_in, wq_in, wo_in, wu_in, wd_in, small_in,
    tok_h, h1_h, qkv_h, gx_h, go_h, ga_h, h2_h, gu_h, att_h, atto_h, first_h, fx_h, fy_h,
    wq_h, wo_h, wu_h, wd_h, vec_o, dbup_o, bup_o, top_o, mask_o,
    wq, wo, wu, wd, tok, grad, h1, qkv, att, x1, h2, dh, fil, small, col, slp, ust, bias,
    dst, first, mine,
    own_s, own_r, rel_s, rel_r, fwd_s, fwd_r, tok_s, tok_r, att_s, att_r, fil_s, fil_r,
    sm_s, sm_r, dn_s, dn_r, fs_s, fs_r, loc, stg, hout,
):
    d, s = lax.axis_index("dp"), lax.axis_index("seq")
    images, part, width = tok_in.shape
    length = images * part
    pair_count = width // (2 * HD)
    weights = ((wq_in, wq), (wo_in, wo), (wu_in, wu), (wd_in, wd))
    sib, xn, yn, dn = flip(d, 1), flip(d, 2), flip(d, 4), flip(d, 6)

    barrier = pltpu.get_barrier_semaphore()
    for m in range(1, 8):
        pl.semaphore_signal(barrier, inc=1, device_id=(flip(d, m), s), device_id_type=MESH)
    for j in range(1, images):
        pl.semaphore_signal(
            barrier, inc=1, device_id=(d, lax.rem(s + j, images)), device_id_type=MESH
        )
    pl.semaphore_wait(barrier, 7 + images - 1)

    def send(src, dst, ss, rs, to_dp, to_seq):
        return pltpu.make_async_remote_copy(
            src_ref=src, dst_ref=dst, send_sem=ss, recv_sem=rs,
            device_id=(to_dp, to_seq), device_id_type=MESH,
        )

    def exchange(src, dst, ss, rs, rows):
        copies = []
        for j in range(1, images):
            to = lax.rem(s + j, images)
            copies.append(send(src.at[to], dst.at[rows], ss.at[j - 1], rs.at[j - 1], d, to))
        return copies

    my_rows = rows_of(s, part)
    sm_copies = [
        send(mine, small.at[d], sm_s.at[m - 1], sm_r.at[m - 1], flip(d, m), s)
        for m in range(1, 8)
    ]
    fil_copies = exchange(fil_in, fil, fil_s, fil_r, s)
    tok_copies = exchange(tok_in, tok, tok_s.at[0], tok_r.at[0], my_rows)
    grad_copies = exchange(grad_in, grad, tok_s.at[1], tok_r.at[1], my_rows)

    def own(w, which=range(5)):
        src, dst = weights[w]
        size = src.shape[0]
        half = size // 2
        def piece(way, to, h):
            return send(
                src.at[pl.ds(h * half, half)], dst.at[rows_of(d, size, h * half, half)],
                own_s.at[w, way, h], own_r.at[w, way, h], to, s,
            )
        return [
            piece(0, xn, 0), piece(1, yn, 1), piece(0, xn, 1), piece(1, yn, 0),
            send(src, dst.at[rows_of(d, size)], own_s.at[w, 2, 0], own_r.at[w, 2, 0], sib, s),
        ]

    def relays(w):
        dst = weights[w][1]
        size = weights[w][0].shape[0]
        half = size // 2
        lower, upper = rows_of(xn, size, 0, half), rows_of(yn, size, half, half)
        return [
            send(dst.at[lower], dst.at[lower], rel_s.at[w, 0], rel_r.at[w, 0], yn, s),
            send(dst.at[upper], dst.at[upper], rel_s.at[w, 1], rel_r.at[w, 1], xn, s),
        ]

    def forwards(w):
        dst = weights[w][1]
        size = weights[w][0].shape[0]
        return [
            send(dst.at[rows_of(b, size)], dst.at[rows_of(b, size)],
                 fwd_s.at[w, i], fwd_r.at[w, i], sib, s)
            for i, b in enumerate((xn, yn, dn))
        ]

    def start_own(w):
        for copy in own(w):
            copy.start()

    def on_halves(w):
        held, relay = own(w), relays(w)
        held[0].wait_recv()
        relay[0].start()
        held[1].wait_recv()
        relay[1].start()

    def on_rest(w):
        held, forward = own(w), forwards(w)
        held[2].wait_recv()
        forward[0].start()
        held[3].wait_recv()
        forward[1].start()

    def on_first(w):
        on_halves(w)
        on_rest(w)

    def on_diag(w):
        relay = relays(w)
        relay[0].wait_recv()
        relay[1].wait_recv()
        forwards(w)[2].start()

    def on_sib(w):
        own(w)[4].wait_recv()
        for copy in forwards(w):
            copy.wait_recv()

    def drain(w):
        for copy in own(w) + relays(w) + forwards(w):
            copy.wait_send()

    def keep_own(w):
        src, dst = weights[w]
        return pltpu.make_async_copy(src, dst.at[rows_of(d, src.shape[0])], loc.at[w])

    start_own(0)
    mine[...] = small_in[...]
    for copy in sm_copies + fil_copies:
        copy.start()
    for copy in tok_copies:
        copy.start()
    start_own(1)
    locals_ = [keep_own(w) for w in range(4)]
    locals_ += [
        pltpu.make_async_copy(tok_in.at[s], tok.at[my_rows], loc.at[4]),
        pltpu.make_async_copy(grad_in.at[s], grad.at[my_rows], loc.at[5]),
        pltpu.make_async_copy(fil_in.at[s], fil.at[s], loc.at[6]),
        pltpu.make_async_copy(mine, small.at[d], loc.at[7]),
    ]
    for copy in locals_:
        copy.start()

    on_first(0)
    start_own(2)

    for copy in sm_copies + fil_copies:
        copy.wait_recv()
    for copy in locals_:
        copy.wait()

    starts = [sum(SMALL[:i]) for i in range(len(SMALL))]

    def vector(i, first=0, last=8):
        return jnp.concatenate(
            [small[b, :, starts[i] : starts[i] + SMALL[i]] for b in range(first, last)], axis=1
        )

    mask = fil[0] + fil[1] + fil[2] + fil[3]
    mask_o[...] = mask
    col[...] = jnp.transpose(mask)

    for copy in tok_copies:
        copy.wait_recv()
    for copy in grad_copies:
        copy.start()

    block = 128
    gain1, shift1 = vector(0), vector(1)

    @pl.loop(0, length // block)
    def _(i):
        r = rows_of(i, block)
        xh, _ = normalized(tok[r, :].astype(F32))
        h1[r, :] = (xh * gain1 + shift1).astype(BF)

    on_diag(0)
    on_first(1)
    on_sib(0)

    tile = 512
    qkv_bias = jnp.concatenate(
        [vector(2, 0, 4), jnp.zeros((1, width), F32), vector(2, 4, 8)], axis=1
    )
    bias[pl.ds(0, 1), :] = qkv_bias[:, :width]
    bias[pl.ds(1, 1), :] = qkv_bias[:, width : 2 * width]
    bias[pl.ds(2, 1), :] = qkv_bias[:, 2 * width :]

    for third in range(3):
        @pl.loop(0, width // tile)
        def _(n):
            c = pl.ds(pl.multiple_of(n * tile, tile), tile)
            cw = pl.ds(pl.multiple_of(third * width + n * tile, tile), tile)
            value = dot_nn(h1[...], wq[:, cw]) + bias[pl.ds(third, 1), c]
            qkv[:, cw] = value.astype(BF)

    saves = [
        pltpu.make_async_copy(tok, tok_h, hout.at[0]),
        pltpu.make_async_copy(h1, h1_h, hout.at[1]),
        pltpu.make_async_copy(qkv, qkv_h, hout.at[2]),
        pltpu.make_async_copy(wq, wq_h, hout.at[3]),
        pltpu.make_async_copy(wo, wo_h, hout.at[4]),
        pltpu.make_async_copy(wu, wu_h, hout.at[5]),
        pltpu.make_async_copy(wd, wd_h, hout.at[6]),
        pltpu.make_async_copy(att, att_h, hout.at[7]),
        pltpu.make_async_copy(first, first_h, hout.at[8]),
        pltpu.make_async_copy(h2, h2_h, hout.at[9]),
    ]
    for copy in saves[:4]:
        copy.start()

    low, high, low_lane = half_masks()
    pad = (mask[0:1, :] - 1.0) * 1e30
    pad2 = jnp.concatenate([pad, pad], axis=1)
    chunk = length // 2

    def attend(p, carry):
        c = pl.ds(pl.multiple_of(p * 2 * HD, 2 * HD), 2 * HD)
        ck = pl.ds(pl.multiple_of(width + p * 2 * HD, 2 * HD), 2 * HD)
        cv = pl.ds(pl.multiple_of(2 * width + p * 2 * HD, 2 * HD), 2 * HD)
        k, v = qkv[:, ck], qkv[:, cv]
        k2 = jnp.concatenate([k * low, k * high], axis=0)
        v2 = jnp.concatenate([v * low, v * high], axis=0)
        best = [jnp.full((1, 1), very_negative, F32)] * 2
        for j in range(2):
            r = pl.ds(j * chunk, chunk)
            q = qkv[r, c] * jnp.asarray(HD ** (-0.5), BF)
            scores = dot_nt(q, k2) + pad2
            probs = []
            for side in range(2):
                part_s = scores[:, side * length : (side + 1) * length]
                peak = jnp.max(part_s, axis=1, keepdims=True)
                e = jnp.exp(part_s - peak)
                total = jnp.sum(e, axis=1, keepdims=True)
                probs.append((e * (1.0 / total)).astype(BF))
                held = jnp.where(col[r, 0:1] > 0.5, peak, very_negative)
                best[side] = jnp.maximum(best[side], jnp.max(held, axis=0, keepdims=True))
            att[r, c] = dot_nn(jnp.concatenate(probs, axis=1), v2).astype(BF)
        top_o[pl.ds(p, 1), :] = jnp.where(
            low_lane, jnp.broadcast_to(best[0], (1, 2 * HD)), jnp.broadcast_to(best[1], (1, 2 * HD))
        )
        return carry

    def give_back(part_of):
        wide = width // 2
        cols = pl.ds(part_of * wide, wide)
        copies = []
        for j in range(1, images):
            to = lax.rem(s + j, images)
            copies.append(
                send(att.at[rows_of(to, part), cols], atto_h.at[s, :, cols],
                     att_s.at[part_of, j - 1], att_r.at[part_of, j - 1], d, to)
            )
        return copies

    lax.fori_loop(0, pair_count // 2, attend, 0)
    back_copies = give_back(0)
    for copy in back_copies:
        copy.start()
    on_first(2)
    start_own(3)
    lax.fori_loop(pair_count // 2, pair_count, attend, 0)
    back_copies += give_back(1)
    for copy in back_copies[images - 1 :]:
        copy.start()
    keep_att = pltpu.make_async_copy(att.at[my_rows], atto_h.at[s], hout.at[10])
    keep_att.start()
    saves[7].start()
    on_diag(1)
    on_sib(1)
    saves[4].start()

    gain2, shift2, b_out, b_down = vector(4), vector(5), vector(3), vector(7)

    @pl.loop(0, length // block)
    def _(i):
        r = rows_of(i, block)
        mid = tok[r, :].astype(F32) + dot_nn(att[r, :], wo[...]) + b_out
        x1[r, :] = mid
        xh, _ = normalized(mid)
        h2[r, :] = (xh * gain2 + shift2).astype(BF)

    saves[9].start()
    bup_o[...] = vector(6)
    dh[...] = jnp.zeros_like(dh)
    for copy in grad_copies:
        copy.wait_recv()

    def add_grad(i, acc):
        return acc + jnp.sum(grad[rows_of(i, block), :].astype(F32), axis=0, keepdims=True)

    grad_sum = lax.fori_loop(0, length // block, add_grad, jnp.zeros((1, width), F32))

    on_diag(2)
    on_sib(2)
    saves[5].start()

    ff_block = wd_in.shape[0]

    half_rows = ff_block // 2

    def activation(b):
        cols = pl.ds(pl.multiple_of(b * ff_block, ff_block), ff_block)
        u = dot_nn(h2[...], wu[:, cols]) + bup_o[:, cols]
        phi = 0.5 * (1.0 + lax.erf(u * (0.5**0.5)))
        slope = phi + u * (jnp.exp(-0.5 * u * u) * (1.0 / math.sqrt(2.0 * math.pi)))
        slp[:, cols] = slope.astype(BF)
        return (u * phi).astype(BF)

    def down_send(mi):
        return send(dst.at[1], first.at[mi], dn_s.at[mi], dn_r.at[mi], sib, s)

    def down(j, carry):
        m = lax.rem(6 * (j + 1), 8)
        mi = lax.div(m, 2)

        @pl.when(j > 0)
        def _():
            down_send(lax.div(lax.rem(6 * j, 8), 2)).wait_send()

        @pl.when(j == 2)
        def _():
            on_halves(3)

        for slot in (1, 0):
            a = activation(flip_traced(d, m + slot))
            dst[slot] = dot_tn(a, grad[...]).astype(BF)
            if slot:
                down_send(mi).start()
        down_send(mi).wait_recv()
        add_rows(first.at[mi], dst.at[0], ff_block)
        return carry

    lax.fori_loop(0, 4, down, 0)
    down_send(0).wait_send()
    saves[8].start()

    def first_stage(n):
        quarter = half_rows // 2
        lower, upper = pl.ds(0, quarter), pl.ds(quarter, quarter)
        m, rows, to_ref, to = (
            (6, lower, fx_h.at[1], xn), (6, upper, fy_h.at[1], yn),
            (2, lower, fx_h.at[0], xn), (4, upper, fy_h.at[0], yn),
        )[n]
        return send(first.at[m // 2, rows], to_ref, fs_s.at[n], fs_r.at[n], to, s)

    def stage_copy(slot, b):
        cols = pl.ds(pl.multiple_of(b * ff_block, ff_block), ff_block)
        return pltpu.make_async_copy(ust.at[slot], gu_h.at[:, cols], stg.at[slot])

    def mlp(i, carry):
        b = flip_traced(d, i)
        slot = lax.rem(i, 2)

        @pl.when(i == 1)
        def _():
            own(3)[4].wait_recv()

        @pl.when(i == 2)
        def _():
            on_rest(3)
            for n in range(4):
                first_stage(n).start()

        for at, which in ((3, 0), (5, 1), (7, 2)):
            @pl.when(i == at)
            def _():
                forwards(3)[which].wait_recv()

        @pl.when(i == 6)
        def _():
            on_diag(3)

        cols = pl.ds(pl.multiple_of(b * ff_block, ff_block), ff_block)
        rows = rows_of(b, ff_block)
        gu = (dot_nt(grad[...], wd[rows, :]) * slp[:, cols].astype(F32)).astype(BF)
        dh[...] += dot_nt(gu, wu[:, cols])

        @pl.when(i >= 2)
        def _():
            stage_copy(slot, b).wait()

        dbup_o[:, cols] = jnp.sum(gu.astype(F32), axis=0, keepdims=True)
        ust[slot] = gu
        stage_copy(slot, b).start()
        return carry

    lax.fori_loop(0, 8, mlp, 0)
    saves[6].start()
    for n in (0, 9):
        saves[n].wait()

    zero = jnp.zeros((1, width), F32)

    def norm_back(i, acc):
        r = rows_of(i, block)
        g = dh[r, :]
        xh, scale = normalized(x1[r, :])
        gg = g * gain2
        inner = gg - jnp.mean(gg, axis=1, keepdims=True)
        inner = inner - xh * jnp.mean(gg * xh, axis=1, keepdims=True)
        total = grad[r, :].astype(F32) + scale * inner
        dh[r, :] = total
        low_total = total.astype(BF)
        h2[r, :] = low_total
        tok[r, :] = dot_nt(low_total, wo[...]).astype(BF)
        return (
            acc[0] + jnp.sum(g * xh, axis=0, keepdims=True),
            acc[1] + jnp.sum(g, axis=0, keepdims=True),
            acc[2] + jnp.sum(low_total.astype(F32), axis=0, keepdims=True),
        )

    sums = lax.fori_loop(0, length // block, norm_back, (zero, zero, zero))
    finals = [
        pltpu.make_async_copy(dh, gx_h, hout.at[11]),
        pltpu.make_async_copy(tok, go_h, hout.at[12]),
        pltpu.make_async_copy(h2, ga_h, hout.at[13]),
    ]
    for copy in finals:
        copy.start()
    for n, row in enumerate((sums[0], sums[1], sums[2], grad_sum)):
        vec_o[pl.ds(n, 1), :] = row
    for n, row in enumerate((gain1, gain2, shift2, b_out, b_down)):
        vec_o[pl.ds(8 + n, 1), :] = row
    for slot in range(2):
        stage_copy(slot, d).wait()
    for n in range(4):
        first_stage(n).wait()
    for n in (1, 2, 3, 4, 5, 6, 7, 8):
        saves[n].wait()
    keep_att.wait()
    for w in range(4):
        drain(w)
    for copy in sm_copies + fil_copies + tok_copies + grad_copies + back_copies:
        copy.wait_send()
    for copy in back_copies:
        copy.wait_recv()
    for copy in finals:
        copy.wait()


def front(tokens, out_grad, filled_rows, qkv_weight, out_weight, up_weight, down_weight, small):
    images, part, width = tokens.shape
    length = images * part
    shards = lax.axis_size("dp")
    ff = up_weight.shape[1]
    wide = qkv_weight.shape[1]
    shape = jax.ShapeDtypeStruct
    any_spec = pl.BlockSpec(memory_space=pl.ANY)
    vmem_spec = pl.BlockSpec(memory_space=pltpu.VMEM)
    dma = pltpu.SemaphoreType.DMA
    vm = pltpu.VMEM
    return pl.pallas_call(
        front_kernel,
        name="front",
        out_shape=(
            shape((length, width), BF),
            shape((length, width), BF),
            shape((length, wide), BF),
            shape((length, width), F32),
            shape((length, width), BF),
            shape((length, width), BF),
            shape((length, width), BF),
            shape((length, ff), BF),
            shape((length, width), BF),
            shape((images, part, width), BF),
            shape((4, ff // 8, width), BF),
            shape((2, ff // 32, width), BF),
            shape((2, ff // 32, width), BF),
            shape((width, wide), BF),
            shape((width, width), BF),
            shape((width, ff), BF),
            shape((ff, width), BF),
            shape((16, width), F32),
            shape((1, ff), F32),
            shape((1, ff), F32),
            shape((8, 2 * HD), F32),
            shape((8, length), F32),
        ),
        in_specs=[any_spec] * 7 + [vmem_spec],
        out_specs=[any_spec] * 17 + [vmem_spec] * 5,
        scratch_shapes=[
            vm((width, wide), BF), vm((width, width), BF), vm((width, ff), BF), vm((ff, width), BF),
            vm((length, width), BF), vm((length, width), BF), vm((length, width), BF),
            vm((length, wide), BF), vm((length, width), BF), vm((length, width), F32),
            vm((length, width), BF), vm((length, width), F32),
            vm((images, 8, length), F32), vm((shards, 1, sum(SMALL)), F32),
            vm((length, 8), F32), vm((length, ff), BF),
            vm((2, length, down_weight.shape[0]), BF), vm((8, width), F32),
            vm((2, ff // 8, width), BF), vm((4, ff // 8, width), BF), vm((1, sum(SMALL)), F32),
            dma((4, 3, 2)), dma((4, 3, 2)), dma((4, 2)), dma((4, 2)), dma((4, 3)), dma((4, 3)),
            dma((2, images - 1)), dma((2, images - 1)), dma((2, images - 1)), dma((2, images - 1)),
            dma((images - 1,)), dma((images - 1,)), dma((7,)), dma((7,)),
            dma((4,)), dma((4,)), dma((4,)), dma((4,)), dma((8,)), dma((2,)), dma((14,)),
        ],
        compiler_params=pltpu.CompilerParams(
            collective_id=0, has_side_effects=True, vmem_limit_bytes=63 << 20
        ),
    )(tokens, out_grad, filled_rows, qkv_weight, out_weight, up_weight, down_weight, small)


def back_kernel(*refs):
    (
        qkv_in, go_in, h1_in, gx_in, tok_in, ga_in, h2_in, gu_in, att_in, atto_in, first_in,
        fx_in, fy_in, mine_in, wq_in, wo_in, wu_in, wd_in,
        mask_in, vec_in, dbup_in, bup_in, top_in,
        out_h, tg_h, dwq_h, dwo_h, dwu_h, dwd_h, small_o, top_o,
        qkv, go, ht, gbuf, buf, dh, wqg, pq, gp, colm, dst, own_u, ust, stg_o, ast, gxs,
        psm, rsm, zsm, rtop, ztop,
    ) = refs[:52]
    refs = refs[52:]
    count = 11
    recv0, recv1x, recv1y, recv2, za, zb = [refs[i * count : (i + 1) * count] for i in range(6)]
    (
        s0_s, s0_r, u0_s, u0_r, s1_s, s1_r, s2_s, s2_r, z_s, z_r, ex_s, ex_r, sm_s, sm_r,
        zs_s, zs_r, tp_s, tp_r, tz_s, tz_r, asem, wsem, osem, lsem, gsem,
    ) = refs[6 * count :]
    d, s = lax.axis_index("dp"), lax.axis_index("seq")
    length, width = go.shape
    images, part = mine_in.shape[0], mine_in.shape[1]
    sib, xn, yn = flip(d, 1), flip(d, 2), flip(d, 4)
    group_cols = gp.shape[1] // 3
    groups = width // group_cols
    ff_block = dst.shape[1]
    shard = width // 8
    block = 128
    tile = 512

    barrier = pltpu.get_barrier_semaphore()
    for m in range(1, 8):
        pl.semaphore_signal(barrier, inc=1, device_id=(flip(d, m), s), device_id_type=MESH)
    for j in range(1, images):
        pl.semaphore_signal(
            barrier, inc=1, device_id=(d, lax.rem(s + j, images)), device_id_type=MESH
        )

    def load(src, dst_ref, n):
        return pltpu.make_async_copy(src, dst_ref, lsem.at[n])

    def send(src, dst_ref, ss, rs, to_dp, to_seq):
        return pltpu.make_async_remote_copy(
            src_ref=src, dst_ref=dst_ref, send_sem=ss, recv_sem=rs,
            device_id=(to_dp, to_seq), device_id_type=MESH,
        )

    down_rows, up_cols = recv0[0].shape[1], recv0[2].shape[2]
    size = [down_rows] * 2 + [shard] * 9

    def s1(i, n):
        half = size[i] // 2
        lower, upper = pl.ds(0, half), pl.ds(half, half)
        m, part_rows, to_ref, to = (
            (6, lower, recv1x[i].at[1], xn), (6, upper, recv1y[i].at[1], yn),
            (2, lower, recv1x[i].at[0], xn), (4, upper, recv1y[i].at[0], yn),
        )[n]
        return send(recv0[i].at[m // 2, part_rows], to_ref, s1_s.at[i, n], s1_r.at[i, n], to, s)

    def s2(i, n):
        half = size[i] // 2
        if n == 0:
            return send(recv1x[i].at[1], recv2[i].at[pl.ds(0, half)],
                        s2_s.at[i, 0], s2_r.at[i, 0], yn, s)
        return send(recv1y[i].at[1], recv2[i].at[pl.ds(half, half)],
                    s2_s.at[i, 1], s2_r.at[i, 1], xn, s)

    mate = s + 1 - 2 * lax.rem(s, 2)
    across = 3 - s
    is_mid = jnp.logical_or(s == 1, s == 2)
    is_end = jnp.logical_or(s == 0, s == 3)

    def to_mid(i):
        return send(recv2[i], za[i], z_s.at[i, 0], z_r.at[i, 0], d, mate)

    def cross(i):
        return send(za[i], zb[i], z_s.at[i, 1], z_r.at[i, 1], d, across)

    def to_end(i):
        return send(zb[i], za[i], z_s.at[i, 2], z_r.at[i, 2], d, mate)

    def outputs(i, src):
        if i < 2:
            return [pltpu.make_async_copy(src, dwd_h.at[pl.ds(i * down_rows, down_rows)],
                                          osem.at[i, 0])]
        if i < 6:
            return [pltpu.make_async_copy(src, dwu_h.at[:, pl.ds((i - 2) * up_cols, up_cols)],
                                          osem.at[i, 0])]
        if i == 6:
            return [pltpu.make_async_copy(src, dwo_h, osem.at[i, 0])]
        return [
            pltpu.make_async_copy(
                src.at[:, pl.ds(third * group_cols, group_cols)],
                dwq_h.at[:, pl.ds(third * width + (i - 7) * group_cols, group_cols)],
                osem.at[i, third],
            )
            for third in range(3)
        ]

    def step1(i):
        for n in range(4):
            s1(i, n).start()

    def arrived(i, n):
        if i:
            s1(i, n).wait_recv()
        elif n == 0:
            for copy in ready_first:
                copy.wait()

    def step2(i):
        half = size[i] // 2
        arrived(i, 0)
        add_rows(recv1x[i].at[1], recv0[i].at[2, pl.ds(0, half)], half)
        s2(i, 0).start()
        arrived(i, 1)
        add_rows(recv1y[i].at[1], recv0[i].at[1, pl.ds(half, half)], half)
        s2(i, 1).start()
        arrived(i, 2)
        add_rows(recv1x[i].at[0], recv0[i].at[0, pl.ds(0, half)], half)
        arrived(i, 3)
        add_rows(recv1y[i].at[0], recv0[i].at[0, pl.ds(half, half)], half)

    def step3(i):
        half = size[i] // 2
        s2(i, 0).wait_recv()
        add_rows(recv2[i].at[pl.ds(0, half)], recv1x[i].at[0], half)
        s2(i, 1).wait_recv()
        add_rows(recv2[i].at[pl.ds(half, half)], recv1y[i].at[0], half)

        @pl.when(is_end)
        def _():
            to_mid(i).start()

    def step4(i):
        @pl.when(is_mid)
        def _():
            to_mid(i).wait_recv()
            add_rows(za[i], recv2[i], size[i])
            cross(i).start()

    def step5(i):
        @pl.when(is_mid)
        def _():
            cross(i).wait_recv()
            add_rows(zb[i], za[i], size[i])
            to_end(i).start()
            for copy in outputs(i, zb[i]):
                copy.start()

    def step6(i):
        @pl.when(is_end)
        def _():
            to_end(i).wait_recv()
            for copy in outputs(i, za[i]):
                copy.start()

    def drain(i):
        for n in range(4 if i else 0):
            s1(i, n).wait_send()
        for n in range(2):
            s2(i, n).wait_send()

        @pl.when(is_end)
        def _():
            to_mid(i).wait_send()
            for copy in outputs(i, za[i]):
                copy.wait()

        @pl.when(is_mid)
        def _():
            cross(i).wait_send()
            to_end(i).wait_send()
            for copy in outputs(i, zb[i]):
                copy.wait()

    def cols_of(b, n=ff_block):
        return pl.ds(pl.multiple_of(b * n, n), n)

    def gu_load(slot, b):
        return pltpu.make_async_copy(gu_in.at[:, cols_of(b)], ast.at[slot], asem.at[slot])

    lower_rows, upper_rows = pl.ds(0, down_rows), pl.ds(down_rows, down_rows)
    ready_first = [
        load(fx_in, recv1x[0], 11 + 2 * images), load(fy_in, recv1y[0], 12 + 2 * images),
        load(first_in.at[:, lower_rows], recv0[0], 13 + 2 * images),
    ]
    ready_second = load(first_in.at[:, upper_rows], recv0[1], 0)
    ready_second.start()
    for copy in ready_first:
        copy.start()
    load_h2 = load(h2_in, buf, 1)
    load_h2.start()
    load_qkv = load(qkv_in, qkv, 2)
    load_qkv.start()
    load_go = load(go_in, go, 3)
    load_go.start()

    def weight_group(g):
        return [
            pltpu.make_async_copy(
                wq_in.at[:, pl.ds(third * width + g * group_cols, group_cols)],
                wqg.at[g % 2, :, pl.ds(third * group_cols, group_cols)],
                wsem.at[g % 2, third],
            )
            for third in range(3)
        ]

    for copy in weight_group(0):
        copy.start()
    pl.semaphore_wait(barrier, 7 + images - 1)
    top_copies = [
        send(top_in, rtop.at[d], tp_s.at[m - 1], tp_r.at[m - 1], flip(d, m), s)
        for m in range(1, 8)
    ]
    for copy in top_copies:
        copy.start()
    gu_load(0, 0).start()
    load_ga = load(ga_in, gbuf, 4)
    load_ga.start()
    dh[...] = jnp.zeros_like(dh)
    colm[...] = jnp.transpose((mask_in[...] - 1.0) * 1e30)
    ready_second.wait()

    def turned(src):
        @pl.loop(0, 8)
        def _(m):
            at = pl.ds(pl.multiple_of(flip_traced(d, m) * shard, shard), shard)
            ht[rows_of(m, shard), :] = jnp.transpose(src[:, at])

    load_att = load(att_in, buf, 5)
    load_h1 = load(h1_in, buf, 6)
    load_tok = load(tok_in, gbuf, 7)

    def turn1():
        load_h2.wait()
        turned(buf)
        load_att.start()

    def split_store(value, keep, give, cols_keep, cols_give):
        for m in range(8):
            piece = value[m * shard : (m + 1) * shard].astype(BF)
            if m % 2 == 0:
                keep[m // 2, :, cols_keep] = piece
            else:
                give[m // 2, :, cols_give] = piece

    blocks = up_cols // tile

    def up_send(i, n):
        return send(ust.at[n], recv0[2 + i].at[:, :, cols_of(n, tile)],
                    u0_s.at[i, n], u0_r.at[i, n], sib, s)

    def up(i):
        if i:
            for n in range(blocks):
                up_send(i - 1, n).wait_send()

        def body(n, carry):
            b = i * blocks + n
            slot = lax.rem(b, 2)
            gu_load(slot, b).wait()

            @pl.when(b + 1 < 4 * blocks)
            def _():
                gu_load(1 - slot, b + 1).start()

            value = dot_nn(ht[...], ast[slot])
            split_store(value, own_u.at[i % 2], ust.at[n], cols_of(n, tile), slice(None))
            up_send(i, n).start()
            return carry

        lax.fori_loop(0, blocks, body, 0)

    def add_up(i):
        for n in range(blocks):
            up_send(i, n).wait_recv()
        for m in (6, 2, 4, 0):
            add_rows(recv0[2 + i].at[m // 2], own_u.at[i % 2, m // 2], shard)

    def out_send(n):
        return send(ust.at[n], recv0[6].at[:, :, pl.ds(n * tile, tile)],
                    s0_s.at[0, n], s0_r.at[0, n], sib, s)

    def out():
        load_ga.wait()
        load_att.wait()
        turned(buf)
        load_h1.start()
        for n in range(blocks):
            up_send(3, n).wait_send()
        for n in range(width // tile):
            value = dot_nn(ht[...], gbuf[:, pl.ds(n * tile, tile)])
            split_store(value, stg_o, ust.at[n], pl.ds(n * tile, tile), slice(None))
            out_send(n).start()
        load_tok.start()

    def turn3():
        load_h1.wait()
        turned(buf)

    def add_out():
        for n in range(width // tile):
            out_send(n).wait_recv()
            out_send(n).wait_send()
        for m in (6, 2, 4, 0):
            add_rows(recv0[6].at[m // 2], stg_o.at[m // 2], shard)

    low, high, low_lane = half_masks()
    scale = HD ** (-0.5)
    pair = 2 * HD
    per_group = group_cols // pair
    cuts = ((0, 256), (256, length - 256)) if length > 256 else ((0, length),)
    def attention(g):
        if g == 0:
            load_qkv.wait()
            load_go.wait()
        if g + 1 < groups:
            for copy in weight_group(g + 1):
                copy.start()

        def body(n, carry):
            p = g * per_group + n
            c = pl.ds(pl.multiple_of(p * pair, pair), pair)
            ck = pl.ds(pl.multiple_of(width + p * pair, pair), pair)
            cv = pl.ds(pl.multiple_of(2 * width + p * pair, pair), pair)
            k, v = qkv[:, ck], qkv[:, cv]
            k2 = jnp.concatenate([k * low, k * high], axis=0)
            v2 = jnp.concatenate([v * low, v * high], axis=0)
            gk = jnp.zeros((2 * length, pair), F32)
            gv = jnp.zeros((2 * length, pair), F32)
            at_q = pl.ds(pl.multiple_of(n * pair, pair), pair)
            at_k = pl.ds(pl.multiple_of(group_cols + n * pair, pair), pair)
            at_v = pl.ds(pl.multiple_of(2 * group_cols + n * pair, pair), pair)
            for first, wide in cuts:
                r = pl.ds(first, wide)
                q = qkv[r, c] * jnp.asarray(scale, BF)
                g_rows = go[r, c]
                scores = dot_nt(k2, q)
                dprob = dot_nt(v2, g_rows)
                low_probs, low_grads = [], []
                for side in range(2):
                    rows = slice(side * length, (side + 1) * length)
                    part_s = scores[rows] + colm[:, 0:1]
                    e = jnp.exp(part_s - jnp.max(part_s, axis=0, keepdims=True))
                    probs = e * (1.0 / jnp.sum(e, axis=0, keepdims=True))
                    weighted = probs * dprob[rows]
                    inner = jnp.sum(weighted, axis=0, keepdims=True)
                    low_probs.append(probs.astype(BF))
                    low_grads.append((weighted - probs * inner).astype(BF))
                low_p = jnp.concatenate(low_probs, axis=0)
                low_g = jnp.concatenate(low_grads, axis=0)
                gv = gv + dot_nn(low_p, g_rows)
                gk = gk + dot_nn(low_g, q)
                gp[r, at_q] = (dot_tn(low_g, k2) * scale).astype(BF)
            gp[:, at_k] = jnp.where(low_lane, gk[:length], gk[length:]).astype(BF)
            gp[:, at_v] = jnp.where(low_lane, gv[:length], gv[length:]).astype(BF)
            return carry

        lax.fori_loop(0, per_group, body, 0)

    bias_rows = []

    def q_send(g):
        return send(pq.at[g % 2, 1], recv0[7 + g], s0_s.at[1 + g, 0], s0_r.at[1 + g, 0], sib, s)

    def group(g):
        if g >= 2:
            q_send(g - 2).wait_send()
        bias_rows.append(jnp.sum(gp[...].astype(F32), axis=0, keepdims=True))
        for third in range(3):
            cols = pl.ds(third * group_cols, group_cols)
            value = dot_nn(ht[...], gp[:, cols])
            split_store(value, pq.at[g % 2, 0], pq.at[g % 2, 1], cols, cols)
        q_send(g).start()
        for copy in weight_group(g):
            copy.wait()
        for first in range(0, width, tile):
            dh[:, pl.ds(first, tile)] += dot_nt(gp[...], wqg[g % 2, pl.ds(first, tile), :])

    def add_q(g):
        q_send(g).wait_recv()
        for m in (6, 2, 4, 0):
            add_rows(recv0[7 + g].at[m // 2], pq.at[g % 2, 0, m // 2], shard)

    gain1 = vec_in[pl.ds(8, 1), :]
    zero = jnp.zeros((1, width), F32)

    def gx_load(slot, i):
        return pltpu.make_async_copy(gx_in.at[rows_of(i, block)], gxs.at[slot], gsem.at[slot])

    def norm_back(i, acc):
        slot = lax.rem(i, 2)
        gx_load(slot, i).wait()

        @pl.when(i + 1 < length // block)
        def _():
            gx_load(1 - slot, i + 1).start()

        r = rows_of(i, block)
        g = dh[r, :]
        xh, spread = normalized(gbuf[r, :].astype(F32))
        gg = g * gain1
        inner = gg - jnp.mean(gg, axis=1, keepdims=True)
        inner = inner - xh * jnp.mean(gg * xh, axis=1, keepdims=True)
        go[r, :] = (gxs[slot] + spread * inner).astype(BF)
        return (
            acc[0] + jnp.sum(g * xh, axis=0, keepdims=True),
            acc[1] + jnp.sum(g, axis=0, keepdims=True),
        )

    late = {}
    tg_copies = []
    for j in range(1, images):
        to = lax.rem(s + j, images)
        tg_copies.append(
            send(go.at[rows_of(to, part)], tg_h.at[s], ex_s.at[j - 1], ex_r.at[j - 1], d, to)
        )
    own_tg = load(go.at[rows_of(s, part)], tg_h.at[s], 8)

    own_loads = []
    for j in range(images):
        rows = pl.ds(j * part, part)
        own_loads.append(load(mine_in.at[j], qkv.at[rows, pl.ds(0, width)], 9 + j))
        own_loads.append(load(atto_in.at[j], qkv.at[rows, pl.ds(width, width)], 9 + images + j))
    own_loads.append(load(wo_in.at[pl.ds(0, tile)], dst.at[0], 9 + 2 * images))
    own_loads.append(load(wo_in.at[pl.ds(tile, tile)], dst.at[1], 10 + 2 * images))

    def norm1():
        for copy in own_loads:
            copy.start()
        load_tok.wait()
        gx_load(0, 0).start()
        late["norm"] = lax.fori_loop(0, length // block, norm_back, (zero, zero))

    def tg():
        for copy in tg_copies:
            copy.start()
        own_tg.start()

    sm_copies = [
        send(psm.at[flip(d, m)], rsm.at[m - 1], sm_s.at[m - 1], sm_r.at[m - 1], flip(d, m), s)
        for m in range(1, 8)
    ]
    top_z, sm_z = [], []
    for j in range(1, images):
        to = lax.rem(s + j, images)
        top_z.append(send(ztop.at[s], ztop.at[s], tz_s.at[j - 1], tz_r.at[j - 1], d, to))
        sm_z.append(send(zsm.at[s], zsm.at[s], zs_s.at[j - 1], zs_r.at[j - 1], d, to))

    def smalls():
        d_gain1, d_shift1 = late["norm"]
        q_sum = jnp.concatenate([row[:, :group_cols] for row in bias_rows], axis=1)
        v_sum = jnp.concatenate([row[:, 2 * group_cols :] for row in bias_rows], axis=1)
        pieces = (
            d_gain1, d_shift1, jnp.concatenate([q_sum, v_sum], axis=1), vec_in[pl.ds(2, 1), :],
            vec_in[pl.ds(0, 1), :], vec_in[pl.ds(1, 1), :], dbup_in[...], vec_in[pl.ds(3, 1), :],
        )
        for b in range(8):
            psm[b] = jnp.concatenate(
                [piece[:, b * n : (b + 1) * n] for piece, n in zip(pieces, SMALL)], axis=1
            )
        for copy in sm_copies:
            copy.start()
        for copy in top_copies:
            copy.wait_recv()
        rtop[d] = top_in[...]
        best = rtop[0]
        for b in range(1, 8):
            best = jnp.maximum(best, rtop[b])
        ztop[s] = best
        for copy in top_z:
            copy.start()

    def smalls_z():
        for copy in sm_copies:
            copy.wait_recv()
        mine = psm[d]
        for m in range(7):
            mine = mine + rsm[m]
        zsm[s] = mine
        for copy in sm_z:
            copy.start()

    gain2, shift2 = vec_in[pl.ds(9, 1), :], vec_in[pl.ds(10, 1), :]
    b_out, b_down = vec_in[pl.ds(11, 1), :], vec_in[pl.ds(12, 1), :]

    def owners():
        for copy in own_loads:
            copy.wait()

        @pl.loop(0, length // block)
        def _(i):
            r = rows_of(i, block)
            mid = qkv[r, 0:width].astype(F32) + b_out
            mid = mid + dot_nn(qkv[r, width : width + tile], dst[0])
            mid = mid + dot_nn(qkv[r, width + tile : 2 * width], dst[1])
            xh, _ = normalized(mid)
            dh[r, :] = mid + b_down
            qkv[r, 2 * width :] = (xh * gain2 + shift2).astype(BF)

        for copy in ff_loads(0, 0):
            copy.start()

    def ff_loads(slot, b):
        return (
            pltpu.make_async_copy(wu_in.at[:, cols_of(b)], wqg.at[slot, :, pl.ds(0, ff_block)],
                                  wsem.at[slot, 0]),
            pltpu.make_async_copy(wd_in.at[rows_of(b, ff_block)], dst.at[slot],
                                  wsem.at[slot, 1]),
        )

    def feed_block(b, carry):
        slot = lax.rem(b, 2)
        for copy in ff_loads(slot, b):
            copy.wait()

        @pl.when(b < 7)
        def _():
            for copy in ff_loads(1 - slot, b + 1):
                copy.start()

        u = dot_nn(qkv[:, 2 * width :], wqg[slot, :, 0:ff_block]) + bup_in[:, cols_of(b)]
        a = (u * (0.5 * (1.0 + lax.erf(u * (0.5**0.5))))).astype(BF)
        dh[...] += dot_nn(a, dst[slot])
        return carry

    keep_out = load(buf, out_h, 1)

    def feed(n):
        lax.fori_loop(2 * n, 2 * n + 2, feed_block, 0)
        if n == 1:
            smalls_z()
        if n == 3:
            buf[...] = dh[...].astype(BF)
            keep_out.start()

    step2(0)
    turn1()
    up(0)
    step1(1)
    up(1)
    add_up(0)
    step3(0)
    up(2)
    add_up(1)
    up(3)
    step1(3)
    out()
    step2(1)
    turn3()
    add_out()
    step1(6)
    attention(0)
    step3(1)
    step4(0)
    step2(3)
    group(0)
    step1(2)
    attention(1)
    step2(6)
    step3(3)
    add_up(2)
    step4(1)
    step5(0)
    add_up(3)
    step2(2)
    step1(5)
    group(1)
    step3(6)
    step1(4)
    step4(3)
    attention(2)
    step5(1)
    add_q(1)
    add_q(0)
    step4(6)
    step3(2)
    step2(5)
    group(2)
    step5(3)
    step2(4)
    step4(2)
    step1(7)
    step3(5)
    attention(3)
    step4(5)
    step3(4)
    step2(7)
    add_q(2)
    step5(6)
    step1(8)
    group(3)
    step5(2)
    step3(7)
    step4(4)
    norm1()
    step4(7)
    tg()
    step5(4)
    step6(0)
    add_q(3)
    owners()
    step5(5)
    smalls()
    step6(1)
    step1(9)
    feed(0)
    step1(10)
    step6(6)
    step2(9)
    feed(1)
    step6(2)
    step6(3)
    step2(8)
    step3(9)
    step3(8)
    step2(10)
    step3(10)
    step4(8)
    step5(7)
    step4(10)
    step6(5)
    step4(9)
    feed(2)
    step5(8)
    step5(10)
    step6(8)
    step6(4)
    feed(3)
    step5(9)
    step6(10)
    step6(7)
    step6(9)

    for copy in top_z + sm_z:
        copy.wait_recv()
    top_o[...] = jnp.maximum(jnp.maximum(ztop[0], ztop[1]), jnp.maximum(ztop[2], ztop[3]))
    small_o[...] = (zsm[0] + zsm[1]) + (zsm[2] + zsm[3])
    for g in range(groups - 2, groups):
        q_send(g).wait_send()
    for i in range(count):
        drain(i)
    for copy in top_copies + top_z + sm_copies + sm_z + tg_copies:
        copy.wait_send()
    for copy in tg_copies:
        copy.wait_recv()
    own_tg.wait()
    keep_out.wait()


def back(tokens, saved, vecs):
    images, part, width = tokens.shape
    (
        tok, h1, qkv, gx, go, ga, h2, gu, att, atto, first, fx, fy, wq, wo, wu, wd,
    ) = saved
    vec, dbup, bup, tops, mask = vecs
    length = images * part
    wide, ff = wq.shape[1], wu.shape[1]
    shard = width // 8
    shape = jax.ShapeDtypeStruct
    any_spec = pl.BlockSpec(memory_space=pl.ANY)
    vmem_spec = pl.BlockSpec(memory_space=pltpu.VMEM)
    dma = pltpu.SemaphoreType.DMA
    vm = pltpu.VMEM
    group_cols = 256
    groups = width // group_cols
    sizes = [(ff // 16, width)] * 2 + [(shard, ff // 4)] * 4 + [(shard, width)]
    sizes += [(shard, 3 * group_cols)] * groups
    count = len(sizes)
    halves = [vm((2, r // 2, c), BF) for r, c in sizes]
    whole = [vm((r, c), BF) for r, c in sizes]
    z_peers = images - 1
    small = sum(SMALL)
    return pl.pallas_call(
        back_kernel,
        name="back",
        out_shape=(
            shape((length, width), BF),
            shape((images, part, width), BF),
            shape((shard, wide), BF),
            shape((shard, width), BF),
            shape((shard, ff), BF),
            shape((ff // 8, width), BF),
            shape((1, small), F32),
            shape((8, 2 * HD), F32),
        ),
        in_specs=[any_spec] * 18 + [vmem_spec] * 5,
        out_specs=[any_spec] * 6 + [vmem_spec] * 2,
        scratch_shapes=[
            vm((length, wide), BF), vm((length, width), BF), vm((width, length), BF),
            vm((length, width), BF), vm((length, width), BF), vm((length, width), F32),
            vm((2, width, 3 * group_cols), BF), vm((2, 2, 4, shard, 3 * group_cols), BF),
            vm((length, 3 * group_cols), BF), vm((length, 8), F32),
            vm((2, ff // 8, width), BF), vm((2, 4, shard, ff // 4), BF), vm((2, 4, shard, 512), BF),
            vm((4, shard, width), BF), vm((2, length, ff // 8), BF), vm((2, 128, width), F32),
            vm((8, 1, small), F32), vm((7, 1, small), F32),
            vm((images, 1, small), F32), vm((8, 8, 2 * HD), F32), vm((images, 8, 2 * HD), F32),
            *[vm((4, r, c), BF) for r, c in sizes], *halves, *halves, *whole, *whole, *whole,
            dma((5, 2)), dma((5, 2)), dma((4, 2)), dma((4, 2)), dma((count, 4)),
            dma((count, 4)), dma((count, 2)), dma((count, 2)), dma((count, 3)), dma((count, 3)),
            dma((z_peers,)), dma((z_peers,)), dma((7,)), dma((7,)),
            dma((z_peers,)), dma((z_peers,)), dma((7,)), dma((7,)),
            dma((z_peers,)), dma((z_peers,)), dma((2,)), dma((2, 3)), dma((count, 3)),
            dma((14 + 2 * images,)), dma((2,)),
        ],
        compiler_params=pltpu.CompilerParams(
            collective_id=1, has_side_effects=True, vmem_limit_bytes=63 << 20
        ),
    )(
        qkv, go, h1, gx, tok, ga, h2, gu, att, atto, first, fx, fy, tokens, wq, wo, wu, wd,
        mask, vec, dbup, bup, tops,
    )


def finish_kernel(
    limit_in, top_in, out_in, tg_in, dwq_in, dwo_in, dwu_in, dwd_in, w_in, small_in,
    out_o, tg_o, dwq_o, dwo_o, dwu_o, dwd_o, w_o, *small_o
):
    out_o[...] = out_in[...]
    tg_o[...] = tg_in[...]
    for src, to in ((dwq_in, dwq_o), (dwo_in, dwo_o), (dwu_in, dwu_o), (dwd_in, dwd_o)):
        to[...] = src[...].astype(F32)
    limit = jnp.full((1, 1), limit_in[0], jnp.int32).astype(F32)
    root = jnp.sqrt(limit / jnp.maximum(top_in[...], limit))
    row = jnp.concatenate([root[p : p + 1, :] for p in range(root.shape[0])], axis=1)
    width = row.shape[1]
    for third in range(3):
        c = slice(third * width, (third + 1) * width)
        if third < 2:
            w_o[:, c] = (w_in[:, c].astype(F32) * row).astype(BF)
        else:
            w_o[:, c] = w_in[:, c]
    start = 0
    for to in small_o:
        n = to.shape[1]
        to[...] = small_in[:, start : start + n]
        start += n


def finish(limit, top, out, tg, dwq, dwo, dwu, dwd, weight, small):
    steps = 4
    parts = (out, tg, dwq, dwo, dwu, dwd, weight)
    specs = [pl.BlockSpec((p.shape[0] // steps, p.shape[1]), lambda i: (i, 0)) for p in parts]

    def fixed(shape):
        return pl.BlockSpec(shape, lambda i: (0, 0))

    shape = jax.ShapeDtypeStruct
    kinds = (BF, BF, F32, F32, F32, F32, BF)
    return pl.pallas_call(
        finish_kernel,
        name="finish",
        grid=(steps,),
        out_shape=[shape(p.shape, kind) for p, kind in zip(parts, kinds)]
        + [shape((1, n), F32) for n in SMALL],
        in_specs=[pl.BlockSpec(memory_space=pltpu.SMEM), fixed(top.shape)]
        + specs + [fixed(small.shape)],
        out_specs=specs + [fixed((1, n)) for n in SMALL],
        compiler_params=pltpu.CompilerParams(vmem_limit_bytes=63 << 20),
    )(limit, top, out, tg, dwq, dwo, dwu, dwd, weight, small)


def by_image_local(
    tokens,
    filled,
    out_grad,
    norm1_gain,
    norm1_bias,
    qkv_weight,
    qv_bias,
    out_weight,
    out_bias,
    norm2_gain,
    norm2_bias,
    up_weight,
    up_bias,
    down_weight,
    down_bias,
    clip_threshold,
):
    images, local_rows, model_width = tokens.shape
    length = local_rows * images
    seq_index = lax.axis_index("seq")
    small, start = 0.0, 0
    for piece in (
        norm1_gain, norm1_bias, qv_bias, out_bias, norm2_gain, norm2_bias, up_bias, down_bias
    ):
        count = piece.shape[0]
        small = small + jnp.pad(piece.astype(F32), (start, sum(SMALL) - start - count))
        start += count
    small = small[None]
    flags = lax.dynamic_update_slice(
        jnp.zeros((images, 8, length), F32),
        jnp.broadcast_to((filled > 0).astype(F32)[:, None, :], (images, 8, local_rows)),
        (0, 0, seq_index * local_rows),
    )
    made = front(tokens, out_grad, flags, qkv_weight, out_weight, up_weight, down_weight, small)
    block_out, tokens_grad, g_qkv, g_out, g_up, g_down, mine, top = back(
        tokens, made[:17], made[17:]
    )
    (
        block_out, tokens_grad, g_qkv, g_out, g_up, g_down, clipped_weight, *small_out
    ) = finish(
        clip_threshold[None], top, block_out, tokens_grad.reshape(length, model_width),
        g_qkv, g_out, g_up, g_down, qkv_weight, mine,
    )
    s_gain_one, s_shift_one, s_qv, s_out, s_gain_two, s_shift_two, s_up, s_down = [
        piece.reshape(-1) for piece in small_out
    ]
    block_out = block_out.reshape(tokens.shape)
    tokens_grad = tokens_grad.reshape(tokens.shape)
    head_max = top[:, ::HD].reshape(-1)
    limit = clip_threshold.astype(F32)
    root_factor = jnp.sqrt(limit / jnp.maximum(head_max, limit))
    head_cols = jnp.repeat(root_factor, HD)
    ones = jnp.ones((model_width,), F32)
    bias_count = qv_bias.shape[0]
    bias_scale = jnp.concatenate([head_cols, ones])
    shard_scale = lax.dynamic_slice_in_dim(
        bias_scale, lax.axis_index("dp") * bias_count, bias_count
    )
    clipped_bias = (qv_bias.astype(F32) * shard_scale).astype(BF)
    return (
        block_out,
        tokens_grad,
        s_gain_one,
        s_shift_one,
        g_qkv,
        s_qv,
        g_out,
        s_out,
        s_gain_two,
        s_shift_two,
        g_up,
        s_up,
        g_down,
        s_down,
        clipped_weight,
        clipped_bias,
        head_max,
    )


def local(*args):
    if args[0].shape[0] == lax.axis_size("seq") == 4 and lax.axis_size("dp") == 8:
        return by_image_local(*args)
    return by_head_local(*args)


def solution(mesh):
    return jax.shard_map(
        local,
        mesh=mesh,
        in_specs=(
            P("dp", "seq", None),
            P("dp", "seq"),
            P("dp", "seq", None),
            P("dp"),
            P("dp"),
            P("dp", None),
            P("dp"),
            P("dp", None),
            P("dp"),
            P("dp"),
            P("dp"),
            P("dp", None),
            P("dp"),
            P("dp", None),
            P("dp"),
            P(),
        ),
        out_specs=(
            P("dp", "seq", None),
            P("dp", "seq", None),
            P("dp"),
            P("dp"),
            P("dp", None),
            P("dp"),
            P("dp", None),
            P("dp"),
            P("dp"),
            P("dp"),
            P("dp", None),
            P("dp"),
            P("dp", None),
            P("dp"),
            P("dp", None),
            P("dp"),
            P(),
        ),
        check_vma=False,
    )
```

```python
import math

import jax
import jax.numpy as jnp
from jax import lax
from jax.experimental import pallas as pl
from jax.experimental.pallas import tpu as pltpu
from jax.sharding import PartitionSpec as P

H = 16
HD = 64


epsilon = 1e-06
very_negative = -1e30


def norm_apply(values, gain_vec, shift_vec):
    center = jnp.mean(values, axis=-1, keepdims=True)
    centered = values - center
    spread = jnp.mean(centered * centered, axis=-1, keepdims=True)
    return centered * lax.rsqrt(spread + epsilon) * gain_vec + shift_vec


def exact_gelu(values):
    return jax.nn.gelu(values, approximate=False)


def last_dot(left_op, right_op):
    return lax.dot_general(
        left_op, right_op, (((1,), (1,)), ((), ())), preferred_element_type=jnp.float32
    )


def first_dot(left_op, right_op):
    return lax.dot_general(
        left_op, right_op, (((0,), (0,)), ((), ())), preferred_element_type=jnp.float32
    )


def column_sum(values):
    return jnp.sum(values.astype(jnp.float32), axis=0)


def score_block(queries, keys_in, key_keep):
    raw_scores = jnp.einsum(
        "qhd,khd->hqk", queries, keys_in, preferred_element_type=jnp.float32
    ) * HD ** (-0.5)
    masked = jnp.where(key_keep[None, None, :], raw_scores, very_negative)
    return (raw_scores, masked)


def attend_forward(inputs):
    queries, keys_in, values_in, key_keep = inputs
    raw_scores, masked = score_block(queries, keys_in, key_keep)
    row_peak = jnp.max(masked, axis=-1, keepdims=True)
    exp_scores = jnp.exp(masked - row_peak)
    row_total = jnp.sum(exp_scores, axis=-1, keepdims=True)
    soft_probs = (exp_scores / row_total).astype(jnp.bfloat16)
    mixed_rows = jnp.einsum(
        "hqk,khd->qhd", soft_probs, values_in, preferred_element_type=jnp.float32
    )
    logsum = row_peak + jnp.log(row_total)
    pair_keep = key_keep[:, None] & key_keep[None, :]
    head_top = jnp.max(jnp.where(pair_keep[None], raw_scores, very_negative), axis=(1, 2))
    flat_rows = mixed_rows.astype(jnp.bfloat16).reshape(mixed_rows.shape[0], -1)
    return (flat_rows, logsum, head_top)


def attend_backward(inputs):
    queries, keys_in, values_in, key_keep, logsum, upstream = inputs
    raw_scores, masked = score_block(queries, keys_in, key_keep)
    soft_probs = jnp.exp(masked - logsum)
    probs_low = soft_probs.astype(jnp.bfloat16)
    value_grad = jnp.einsum("hqk,qhd->khd", probs_low, upstream, preferred_element_type=jnp.float32)
    prob_grad = jnp.einsum("qhd,khd->hqk", upstream, values_in, preferred_element_type=jnp.float32)
    inner_sum = jnp.sum(soft_probs * prob_grad, axis=-1, keepdims=True)
    score_grad = (soft_probs * (prob_grad - inner_sum)).astype(jnp.bfloat16)
    score_scale = HD ** (-0.5)
    query_grad = (
        jnp.einsum("hqk,khd->qhd", score_grad, keys_in, preferred_element_type=jnp.float32)
        * score_scale
    )
    key_grad = (
        jnp.einsum("hqk,qhd->khd", score_grad, queries, preferred_element_type=jnp.float32)
        * score_scale
    )
    stacked = jnp.stack([query_grad, key_grad, value_grad], axis=1)
    return stacked.astype(jnp.bfloat16).reshape(stacked.shape[0], 3, -1)


def by_head_local(
    tokens,
    filled,
    out_grad,
    norm1_gain,
    norm1_bias,
    qkv_weight,
    qv_bias,
    out_weight,
    out_bias,
    norm2_gain,
    norm2_bias,
    up_weight,
    up_bias,
    down_weight,
    down_bias,
    clip_threshold,
):
    gathered = (
        lax.all_gather(norm1_gain, "dp", axis=0, tiled=True),
        lax.all_gather(norm1_bias, "dp", axis=0, tiled=True),
        lax.all_gather(qkv_weight, "dp", axis=0, tiled=True),
        lax.all_gather(qv_bias, "dp", axis=0, tiled=True),
        lax.all_gather(out_weight, "dp", axis=0, tiled=True),
        lax.all_gather(out_bias, "dp", axis=0, tiled=True),
        lax.all_gather(norm2_gain, "dp", axis=0, tiled=True),
        lax.all_gather(norm2_bias, "dp", axis=0, tiled=True),
        lax.all_gather(up_weight, "dp", axis=0, tiled=True),
        lax.all_gather(up_bias, "dp", axis=0, tiled=True),
        lax.all_gather(down_weight, "dp", axis=0, tiled=True),
        lax.all_gather(down_bias, "dp", axis=0, tiled=True),
    )
    (
        gain_one,
        shift_one,
        w_qkv,
        b_qv,
        w_out,
        b_out,
        gain_two,
        shift_two,
        w_up,
        b_up,
        w_down,
        b_down,
    ) = gathered
    images, local_rows, model_width = tokens.shape
    groups = lax.axis_size("seq")
    group_width = model_width // groups
    local_heads = group_width // HD
    length = local_rows * groups
    row_count = images * local_rows
    tokens_flat = tokens.astype(jnp.float32).reshape(row_count, model_width)
    gain_one_f = gain_one.astype(jnp.float32)
    shift_one_f = shift_one.astype(jnp.float32)
    gain_two_f = gain_two.astype(jnp.float32)
    shift_two_f = shift_two.astype(jnp.float32)
    hidden_one = norm_apply(tokens_flat, gain_one_f, shift_one_f).astype(jnp.bfloat16)
    bias_float = b_qv.astype(jnp.float32)
    qkv_bias = jnp.concatenate(
        [bias_float[:model_width], jnp.zeros((model_width,), jnp.float32), bias_float[model_width:]]
    )
    projected = (jnp.dot(hidden_one, w_qkv, preferred_element_type=jnp.float32) + qkv_bias).astype(
        jnp.bfloat16
    )
    key_flags = lax.all_gather(filled, "seq", axis=1, tiled=True)
    keep_all = key_flags > 0
    by_heads = lax.all_to_all(
        projected.reshape(images, local_rows, 3, groups, group_width),
        "seq",
        split_axis=3,
        concat_axis=1,
        tiled=True,
    )
    by_heads = by_heads.reshape(images, length, 3, local_heads, HD)
    queries = by_heads[:, :, 0]
    keys_all = by_heads[:, :, 1]
    values_all = by_heads[:, :, 2]
    attended, logsums, tops = lax.map(attend_forward, (queries, keys_all, values_all, keep_all))
    local_peak = jnp.max(tops, axis=0)
    peak_vector = lax.dynamic_update_slice(
        jnp.full((H,), very_negative, jnp.float32),
        local_peak,
        (lax.axis_index("seq") * local_heads,),
    )
    head_max = lax.pmax(peak_vector, ("dp", "seq"))
    back_rows = lax.all_to_all(
        attended.reshape(images, groups, local_rows, group_width),
        "seq",
        split_axis=1,
        concat_axis=3,
        tiled=True,
    )
    attn_rows = back_rows.reshape(row_count, model_width)
    branch = jnp.dot(attn_rows, w_out, preferred_element_type=jnp.float32) + b_out.astype(
        jnp.float32
    )
    middle = tokens_flat + branch
    hidden_two = norm_apply(middle, gain_two_f, shift_two_f).astype(jnp.bfloat16)
    pre_act = jnp.dot(hidden_two, w_up, preferred_element_type=jnp.float32) + b_up.astype(
        jnp.float32
    )
    activated = exact_gelu(pre_act).astype(jnp.bfloat16)
    block_rows = middle + (
        jnp.dot(activated, w_down, preferred_element_type=jnp.float32) + b_down.astype(jnp.float32)
    )
    block_out = block_rows.astype(jnp.bfloat16).reshape(tokens.shape)
    gain_one_b, w_qkv_b, w_out_b, gain_two_b, w_up_b, w_down_b = (
        lax.all_gather(norm1_gain, "dp", axis=0, tiled=True),
        lax.all_gather(qkv_weight, "dp", axis=0, tiled=True),
        lax.all_gather(out_weight, "dp", axis=0, tiled=True),
        lax.all_gather(norm2_gain, "dp", axis=0, tiled=True),
        lax.all_gather(up_weight, "dp", axis=0, tiled=True),
        lax.all_gather(down_weight, "dp", axis=0, tiled=True),
    )
    upstream = out_grad.reshape(row_count, model_width)
    upstream_f = upstream.astype(jnp.float32)
    d_bias_down = jnp.sum(upstream_f, axis=0)
    d_down = first_dot(activated, upstream)
    act_grad = last_dot(upstream, w_down_b)
    gelu_out, gelu_pull = jax.vjp(exact_gelu, pre_act)
    pre_grad = gelu_pull(act_grad)[0].astype(jnp.bfloat16)
    d_bias_up = column_sum(pre_grad)
    d_up = first_dot(hidden_two, pre_grad)
    hidden_two_grad = last_dot(pre_grad, w_up_b)
    norm_out_two, pull_two = jax.vjp(
        norm_apply, middle, gain_two_b.astype(jnp.float32), shift_two_f
    )
    mid_norm_grad, d_gain_two, d_shift_two = pull_two(hidden_two_grad)
    middle_grad = upstream_f + mid_norm_grad
    branch_grad = middle_grad.astype(jnp.bfloat16)
    d_bias_out = column_sum(branch_grad)
    d_out = first_dot(attn_rows, branch_grad)
    attn_grad = last_dot(branch_grad, w_out_b).astype(jnp.bfloat16)
    grad_heads = lax.all_to_all(
        attn_grad.reshape(images, local_rows, groups, group_width),
        "seq",
        split_axis=2,
        concat_axis=1,
        tiled=True,
    )
    grad_heads = grad_heads.reshape(images, length, local_heads, HD)
    head_grads = lax.map(
        attend_backward, (queries, keys_all, values_all, keep_all, logsums, grad_heads)
    )
    token_grads = lax.all_to_all(
        head_grads.reshape(images, groups, local_rows, 3, group_width),
        "seq",
        split_axis=1,
        concat_axis=4,
        tiled=True,
    )
    token_grads = token_grads.reshape(row_count, 3 * model_width)
    d_qkv = first_dot(hidden_one, token_grads)
    bias_sums = column_sum(token_grads)
    d_bias_qv = jnp.concatenate([bias_sums[:model_width], bias_sums[2 * model_width :]])
    first_grad = last_dot(token_grads, w_qkv_b)
    norm_out_one, pull_one = jax.vjp(
        norm_apply, tokens_flat, gain_one_b.astype(jnp.float32), shift_one_f
    )
    in_norm_grad, d_gain_one, d_shift_one = pull_one(first_grad)
    tokens_grad = (middle_grad + in_norm_grad).astype(jnp.bfloat16).reshape(tokens.shape)
    terms = (
        d_gain_one,
        d_shift_one,
        d_qkv,
        d_bias_qv,
        d_out,
        d_bias_out,
        d_gain_two,
        d_shift_two,
        d_up,
        d_bias_up,
        d_down,
        d_bias_down,
    )
    data_shards = (
        lax.psum_scatter(
            terms[0].astype(jnp.bfloat16), "dp", scatter_dimension=0, tiled=True
        ).astype(jnp.float32),
        lax.psum_scatter(
            terms[1].astype(jnp.bfloat16), "dp", scatter_dimension=0, tiled=True
        ).astype(jnp.float32),
        lax.psum_scatter(
            terms[2].astype(jnp.bfloat16), "dp", scatter_dimension=0, tiled=True
        ).astype(jnp.float32),
        lax.psum_scatter(
            terms[3].astype(jnp.bfloat16), "dp", scatter_dimension=0, tiled=True
        ).astype(jnp.float32),
        lax.psum_scatter(
            terms[4].astype(jnp.bfloat16), "dp", scatter_dimension=0, tiled=True
        ).astype(jnp.float32),
        lax.psum_scatter(
            terms[5].astype(jnp.bfloat16), "dp", scatter_dimension=0, tiled=True
        ).astype(jnp.float32),
        lax.psum_scatter(
            terms[6].astype(jnp.bfloat16), "dp", scatter_dimension=0, tiled=True
        ).astype(jnp.float32),
        lax.psum_scatter(
            terms[7].astype(jnp.bfloat16), "dp", scatter_dimension=0, tiled=True
        ).astype(jnp.float32),
        lax.psum_scatter(
            terms[8].astype(jnp.bfloat16), "dp", scatter_dimension=0, tiled=True
        ).astype(jnp.float32),
        lax.psum_scatter(
            terms[9].astype(jnp.bfloat16), "dp", scatter_dimension=0, tiled=True
        ).astype(jnp.float32),
        lax.psum_scatter(
            terms[10].astype(jnp.bfloat16), "dp", scatter_dimension=0, tiled=True
        ).astype(jnp.float32),
        lax.psum_scatter(
            terms[11].astype(jnp.bfloat16), "dp", scatter_dimension=0, tiled=True
        ).astype(jnp.float32),
    )
    shards = (
        lax.psum(data_shards[0].astype(jnp.bfloat16), "seq").astype(jnp.float32),
        lax.psum(data_shards[1].astype(jnp.bfloat16), "seq").astype(jnp.float32),
        lax.psum(data_shards[2].astype(jnp.bfloat16), "seq").astype(jnp.float32),
        lax.psum(data_shards[3].astype(jnp.bfloat16), "seq").astype(jnp.float32),
        lax.psum(data_shards[4].astype(jnp.bfloat16), "seq").astype(jnp.float32),
        lax.psum(data_shards[5].astype(jnp.bfloat16), "seq").astype(jnp.float32),
        lax.psum(data_shards[6].astype(jnp.bfloat16), "seq").astype(jnp.float32),
        lax.psum(data_shards[7].astype(jnp.bfloat16), "seq").astype(jnp.float32),
        lax.psum(data_shards[8].astype(jnp.bfloat16), "seq").astype(jnp.float32),
        lax.psum(data_shards[9].astype(jnp.bfloat16), "seq").astype(jnp.float32),
        lax.psum(data_shards[10].astype(jnp.bfloat16), "seq").astype(jnp.float32),
        lax.psum(data_shards[11].astype(jnp.bfloat16), "seq").astype(jnp.float32),
    )
    limit = clip_threshold.astype(jnp.float32)
    root_factor = jnp.sqrt(limit / jnp.maximum(head_max, limit))
    head_cols = jnp.repeat(root_factor, HD)
    weight_scale = jnp.concatenate([head_cols, head_cols, jnp.ones((model_width,), jnp.float32)])
    clipped_weight = (qkv_weight.astype(jnp.float32) * weight_scale[None, :]).astype(jnp.bfloat16)
    bias_count = qv_bias.shape[0]
    bias_scale = jnp.concatenate([head_cols, jnp.ones((model_width,), jnp.float32)])
    shard_scale = lax.dynamic_slice_in_dim(
        bias_scale, lax.axis_index("dp") * bias_count, bias_count
    )
    clipped_bias = (qv_bias.astype(jnp.float32) * shard_scale).astype(jnp.bfloat16)
    return (
        block_out,
        tokens_grad,
        shards[0],
        shards[1],
        shards[2],
        shards[3],
        shards[4],
        shards[5],
        shards[6],
        shards[7],
        shards[8],
        shards[9],
        shards[10],
        shards[11],
        clipped_weight,
        clipped_bias,
        head_max,
    )


MESH = pl.DeviceIdType.MESH
BF = jnp.bfloat16
F32 = jnp.float32
SMALL = (128, 128, 256, 128, 128, 128, 512, 128)


def flip(d, m):
    y = lax.rem(lax.div(d, 4) + m // 4, 2)
    x = lax.rem(lax.rem(lax.div(d, 2), 2) + (m // 2) % 2, 2)
    k = lax.rem(lax.rem(d, 2) + m % 2, 2)
    return 4 * y + 2 * x + k


def flip_traced(d, m):
    y = lax.rem(lax.div(d, 4) + lax.div(m, 4), 2)
    x = lax.rem(lax.rem(lax.div(d, 2), 2) + lax.rem(lax.div(m, 2), 2), 2)
    k = lax.rem(lax.rem(d, 2) + lax.rem(m, 2), 2)
    return 4 * y + 2 * x + k


def dot_nn(a, b):
    return lax.dot_general(a, b, (((1,), (0,)), ((), ())), preferred_element_type=F32)


def dot_nt(a, b):
    return lax.dot_general(a, b, (((1,), (1,)), ((), ())), preferred_element_type=F32)


def dot_tn(a, b):
    return lax.dot_general(a, b, (((0,), (0,)), ((), ())), preferred_element_type=F32)


def rows_of(block, size, start=0, count=None):
    count = size if count is None else count
    step = math.gcd(size, start) if start else size
    return pl.ds(pl.multiple_of(block * size + start, step), count)


def normalized(v):
    center = jnp.mean(v, axis=-1, keepdims=True)
    centered = v - center
    spread = jnp.mean(centered * centered, axis=-1, keepdims=True)
    scale = lax.rsqrt(spread + epsilon)
    return centered * scale, scale


def half_masks():
    lane = lax.broadcasted_iota(jnp.int32, (1, 2 * HD), 1)
    low = jnp.where(lane < HD, 1.0, 0.0)
    return low.astype(BF), (1.0 - low).astype(BF), lane < HD


def add_rows(target, other, rows, step=32):
    @pl.loop(0, rows // step)
    def _(i):
        r = rows_of(i, step)
        target[r, :] = target[r, :] + other[r, :]


def front_kernel(
    tok_in, grad_in, wq_in, wo_in, wu_in, wd_in, small_in, flag_in,
    tok_h, h1_h, qkv_h, gx_h, go_h, ga_h, h2_h, gu_h, att_h, atto_h, first_h, fx_h, fy_h,
    wq_h, wo_h, wu_h, wd_h, vec_o, dbup_o, bup_o, top_o, mask_o,
    wq, wo, wu, wd, tok, grad, h1, qkv, att, x1, h2, dh, fil, small, col, slp, ust, bias,
    dst, first, mine, flags,
    own_s, own_r, rel_s, rel_r, fwd_s, fwd_r, tok_s, tok_r, att_s, att_r, fil_s, fil_r,
    sm_s, sm_r, dn_s, dn_r, fs_s, fs_r, loc, stg, hout, wsv, fin,
):
    d, s = lax.axis_index("dp"), lax.axis_index("seq")
    images, part, width = tok_in.shape
    length = images * part
    pair_count = width // (2 * HD)
    weights = ((wq_in, wq), (wo_in, wo), (wu_in, wu), (wd_in, wd))
    sib, xn, yn, dn = flip(d, 1), flip(d, 2), flip(d, 4), flip(d, 6)

    barrier = pltpu.get_barrier_semaphore()
    for m in range(1, 8):
        pl.semaphore_signal(barrier, inc=1, device_id=(flip(d, m), s), device_id_type=MESH)
    for j in range(1, images):
        pl.semaphore_signal(
            barrier, inc=1, device_id=(d, lax.rem(s + j, images)), device_id_type=MESH
        )
    pl.semaphore_wait(barrier, 7 + images - 1)

    def send(src, dst, ss, rs, to_dp, to_seq):
        return pltpu.make_async_remote_copy(
            src_ref=src, dst_ref=dst, send_sem=ss, recv_sem=rs,
            device_id=(to_dp, to_seq), device_id_type=MESH,
        )

    def exchange(src, dst, ss, rs, rows):
        copies = []
        for j in range(1, images):
            to = lax.rem(s + j, images)
            copies.append(send(src.at[to], dst.at[rows], ss.at[j - 1], rs.at[j - 1], d, to))
        return copies

    my_rows = rows_of(s, part)
    sm_copies = [
        send(mine, small.at[d], sm_s.at[m - 1], sm_r.at[m - 1], flip(d, m), s)
        for m in range(1, 8)
    ]
    fil_copies = exchange(flags, fil, fil_s, fil_r, s)
    tok_copies = exchange(tok_in, tok, tok_s.at[0], tok_r.at[0], my_rows)
    grad_copies = exchange(grad_in, grad, tok_s.at[1], tok_r.at[1], my_rows)

    def own(w, which=range(5)):
        src, dst = weights[w]
        size = src.shape[0]
        half = size // 2
        def piece(way, to, h):
            return send(
                src.at[pl.ds(h * half, half)], dst.at[rows_of(d, size, h * half, half)],
                own_s.at[w, way, h], own_r.at[w, way, h], to, s,
            )
        return [
            piece(0, xn, 0), piece(1, yn, 1), piece(0, xn, 1), piece(1, yn, 0),
            send(src, dst.at[rows_of(d, size)], own_s.at[w, 2, 0], own_r.at[w, 2, 0], sib, s),
        ]

    def relays(w):
        dst = weights[w][1]
        size = weights[w][0].shape[0]
        half = size // 2
        lower, upper = rows_of(xn, size, 0, half), rows_of(yn, size, half, half)
        return [
            send(dst.at[lower], dst.at[lower], rel_s.at[w, 0], rel_r.at[w, 0], yn, s),
            send(dst.at[upper], dst.at[upper], rel_s.at[w, 1], rel_r.at[w, 1], xn, s),
        ]

    def forwards(w):
        dst = weights[w][1]
        size = weights[w][0].shape[0]
        return [
            send(dst.at[rows_of(b, size)], dst.at[rows_of(b, size)],
                 fwd_s.at[w, i], fwd_r.at[w, i], sib, s)
            for i, b in enumerate((xn, yn, dn))
        ]

    def start_own(w):
        for copy in own(w):
            copy.start()

    def on_halves(w):
        held, relay = own(w), relays(w)
        held[0].wait_recv()
        relay[0].start()
        held[1].wait_recv()
        relay[1].start()

    def on_rest(w):
        held, forward = own(w), forwards(w)
        held[2].wait_recv()
        forward[0].start()
        held[3].wait_recv()
        forward[1].start()

    def on_first(w):
        on_halves(w)
        on_rest(w)

    def on_diag(w):
        relay = relays(w)
        relay[0].wait_recv()
        relay[1].wait_recv()
        forwards(w)[2].start()

    def on_sib(w):
        own(w)[4].wait_recv()
        for copy in forwards(w):
            copy.wait_recv()

    def drain(w):
        for copy in own(w) + relays(w) + forwards(w):
            copy.wait_send()

    def keep_own(w):
        src, dst = weights[w]
        return pltpu.make_async_copy(src, dst.at[rows_of(d, src.shape[0])], loc.at[w])

    for copy in tok_copies:
        copy.start()
    start_own(0)
    mine[...] = small_in[...]
    flags[...] = jnp.zeros_like(flags)
    held = jnp.where(flag_in[...] > 0, 1.0, 0.0)
    for place in range(images):
        @pl.when(s == place)
        def _():
            for image in range(images):
                flags[image, :, place * part : (place + 1) * part] = jnp.broadcast_to(
                    held[image : image + 1, :], (8, part)
                )
    for copy in sm_copies + fil_copies:
        copy.start()
    start_own(1)
    locals_ = [keep_own(w) for w in range(4)]
    locals_ += [
        pltpu.make_async_copy(tok_in.at[s], tok.at[my_rows], loc.at[4]),
        pltpu.make_async_copy(grad_in.at[s], grad.at[my_rows], loc.at[5]),
        pltpu.make_async_copy(flags.at[s], fil.at[s], loc.at[6]),
        pltpu.make_async_copy(mine, small.at[d], loc.at[7]),
    ]
    for copy in locals_:
        copy.start()

    on_first(0)
    start_own(2)

    for copy in sm_copies + fil_copies:
        copy.wait_recv()
    for copy in locals_:
        copy.wait()

    starts = [sum(SMALL[:i]) for i in range(len(SMALL))]

    def vector(i, first=0, last=8):
        return jnp.concatenate(
            [small[b, :, starts[i] : starts[i] + SMALL[i]] for b in range(first, last)], axis=1
        )

    mask = fil[0] + fil[1] + fil[2] + fil[3]
    mask_o[...] = mask
    col[...] = jnp.transpose(mask)

    for copy in tok_copies:
        copy.wait_recv()
    for copy in grad_copies:
        copy.start()

    block = 128
    gain1, shift1 = vector(0), vector(1)

    @pl.loop(0, length // block)
    def _(i):
        r = rows_of(i, block)
        xh, _ = normalized(tok[r, :].astype(F32))
        h1[r, :] = (xh * gain1 + shift1).astype(BF)

    on_diag(0)
    on_first(1)
    on_sib(0)

    tile = 512
    qkv_bias = jnp.concatenate(
        [vector(2, 0, 4), jnp.zeros((1, width), F32), vector(2, 4, 8)], axis=1
    )
    bias[pl.ds(0, 1), :] = qkv_bias[:, :width]
    bias[pl.ds(1, 1), :] = qkv_bias[:, width : 2 * width]
    bias[pl.ds(2, 1), :] = qkv_bias[:, 2 * width :]

    for third in range(3):
        @pl.loop(0, width // tile)
        def _(n):
            c = pl.ds(pl.multiple_of(n * tile, tile), tile)
            cw = pl.ds(pl.multiple_of(third * width + n * tile, tile), tile)
            value = dot_nn(h1[...], wq[:, cw]) + bias[pl.ds(third, 1), c]
            qkv[:, cw] = value.astype(BF)

    saves = [
        pltpu.make_async_copy(tok, tok_h, hout.at[0]),
        pltpu.make_async_copy(h1, h1_h, hout.at[1]),
        pltpu.make_async_copy(qkv, qkv_h, hout.at[2]),
        pltpu.make_async_copy(wq, wq_h, hout.at[3]),
        pltpu.make_async_copy(wo, wo_h, hout.at[4]),
        pltpu.make_async_copy(wu, wu_h, hout.at[5]),
        None,
        pltpu.make_async_copy(att, att_h, hout.at[7]),
        pltpu.make_async_copy(first, first_h, hout.at[8]),
        pltpu.make_async_copy(h2, h2_h, hout.at[9]),
    ]
    for copy in saves[:4]:
        copy.start()

    low, high, low_lane = half_masks()
    pad = (mask[0:1, :] - 1.0) * 1e30
    pad2 = jnp.concatenate([pad, pad], axis=1)
    chunk = length // 2

    def attend(p, carry):
        c = pl.ds(pl.multiple_of(p * 2 * HD, 2 * HD), 2 * HD)
        ck = pl.ds(pl.multiple_of(width + p * 2 * HD, 2 * HD), 2 * HD)
        cv = pl.ds(pl.multiple_of(2 * width + p * 2 * HD, 2 * HD), 2 * HD)
        k, v = qkv[:, ck], qkv[:, cv]
        k2 = jnp.concatenate([k * low, k * high], axis=0)
        v2 = jnp.concatenate([v * low, v * high], axis=0)
        best = [jnp.full((1, 1), very_negative, F32)] * 2
        for j in range(2):
            r = pl.ds(j * chunk, chunk)
            q = qkv[r, c] * jnp.asarray(HD ** (-0.5), BF)
            scores = dot_nt(q, k2) + pad2
            probs = []
            for side in range(2):
                part_s = scores[:, side * length : (side + 1) * length]
                peak = jnp.max(part_s, axis=1, keepdims=True)
                e = jnp.exp(part_s - peak)
                total = jnp.sum(e, axis=1, keepdims=True)
                probs.append((e * (1.0 / total)).astype(BF))
                held = jnp.where(col[r, 0:1] > 0.5, peak, very_negative)
                best[side] = jnp.maximum(best[side], jnp.max(held, axis=0, keepdims=True))
            att[r, c] = dot_nn(jnp.concatenate(probs, axis=1), v2).astype(BF)
        top_o[pl.ds(p, 1), :] = jnp.where(
            low_lane, jnp.broadcast_to(best[0], (1, 2 * HD)), jnp.broadcast_to(best[1], (1, 2 * HD))
        )
        return carry

    def give_back(part_of):
        wide = width // 2
        cols = pl.ds(part_of * wide, wide)
        copies = []
        for j in range(1, images):
            to = lax.rem(s + j, images)
            copies.append(
                send(att.at[rows_of(to, part), cols], atto_h.at[s, :, cols],
                     att_s.at[part_of, j - 1], att_r.at[part_of, j - 1], d, to)
            )
        return copies

    lax.fori_loop(0, pair_count // 2, attend, 0)
    back_copies = give_back(0)
    for copy in back_copies:
        copy.start()
    on_first(2)
    start_own(3)
    lax.fori_loop(pair_count // 2, pair_count, attend, 0)
    back_copies += give_back(1)
    for copy in back_copies[images - 1 :]:
        copy.start()
    keep_att = pltpu.make_async_copy(att.at[my_rows], atto_h.at[s], hout.at[10])
    keep_att.start()
    saves[7].start()
    on_diag(1)
    on_sib(1)
    saves[4].start()

    gain2, shift2, b_out, b_down = vector(4), vector(5), vector(3), vector(7)

    @pl.loop(0, length // block)
    def _(i):
        r = rows_of(i, block)
        mid = tok[r, :].astype(F32) + dot_nn(att[r, :], wo[...]) + b_out
        x1[r, :] = mid
        xh, _ = normalized(mid)
        h2[r, :] = (xh * gain2 + shift2).astype(BF)

    saves[9].start()
    bup_o[...] = vector(6)
    dh[...] = jnp.zeros_like(dh)
    for copy in grad_copies:
        copy.wait_recv()

    def add_grad(i, acc):
        return acc + jnp.sum(grad[rows_of(i, block), :].astype(F32), axis=0, keepdims=True)

    grad_sum = lax.fori_loop(0, length // block, add_grad, jnp.zeros((1, width), F32))

    on_diag(2)
    on_sib(2)
    saves[5].start()

    ff_block = wd_in.shape[0]

    half_rows = ff_block // 2

    def activation(b):
        cols = pl.ds(pl.multiple_of(b * ff_block, ff_block), ff_block)
        u = dot_nn(h2[...], wu[:, cols]) + bup_o[:, cols]
        phi = 0.5 * (1.0 + lax.erf(u * (0.5**0.5)))
        slope = phi + u * (jnp.exp(-0.5 * u * u) * (1.0 / math.sqrt(2.0 * math.pi)))
        slp[:, cols] = slope.astype(BF)
        return (u * phi).astype(BF)

    def down_send(mi):
        return send(dst.at[1], first.at[mi], dn_s.at[mi], dn_r.at[mi], sib, s)

    def down(j, carry):
        m = lax.rem(6 * (j + 1), 8)
        mi = lax.div(m, 2)

        @pl.when(j > 0)
        def _():
            down_send(lax.div(lax.rem(6 * j, 8), 2)).wait_send()

        @pl.when(j == 2)
        def _():
            on_halves(3)

        for slot in (1, 0):
            a = activation(flip_traced(d, m + slot))
            dst[slot] = dot_tn(a, grad[...]).astype(BF)
            if slot:
                down_send(mi).start()
        down_send(mi).wait_recv()
        add_rows(first.at[mi], dst.at[0], ff_block)
        return carry

    lax.fori_loop(0, 4, down, 0)
    down_send(0).wait_send()
    saves[8].start()

    def first_stage(n):
        quarter = half_rows // 2
        lower, upper = pl.ds(0, quarter), pl.ds(quarter, quarter)
        m, rows, to_ref, to = (
            (6, lower, fx_h.at[1], xn), (6, upper, fy_h.at[1], yn),
            (2, lower, fx_h.at[0], xn), (4, upper, fy_h.at[0], yn),
        )[n]
        return send(first.at[m // 2, rows], to_ref, fs_s.at[n], fs_r.at[n], to, s)

    def stage_copy(slot, b):
        cols = pl.ds(pl.multiple_of(b * ff_block, ff_block), ff_block)
        return pltpu.make_async_copy(ust.at[slot], gu_h.at[:, cols], stg.at[slot])

    def save_down(i):
        rows = rows_of(flip_traced(d, i), ff_block)
        return pltpu.make_async_copy(wd.at[rows], wd_h.at[rows], wsv.at[i])

    def mlp(i, carry):
        b = flip_traced(d, i)
        slot = lax.rem(i, 2)

        @pl.when(i == 1)
        def _():
            own(3)[4].wait_recv()

        @pl.when(i == 2)
        def _():
            on_rest(3)
            for n in range(4):
                first_stage(n).start()

        for at, which in ((3, 0), (5, 1), (7, 2)):
            @pl.when(i == at)
            def _():
                forwards(3)[which].wait_recv()

        @pl.when(i == 6)
        def _():
            on_diag(3)

        cols = pl.ds(pl.multiple_of(b * ff_block, ff_block), ff_block)
        rows = rows_of(b, ff_block)
        save_down(i).start()
        gu = (dot_nt(grad[...], wd[rows, :]) * slp[:, cols].astype(F32)).astype(BF)
        dh[...] += dot_nt(gu, wu[:, cols])

        @pl.when(i >= 2)
        def _():
            stage_copy(slot, b).wait()

        dbup_o[:, cols] = jnp.sum(gu.astype(F32), axis=0, keepdims=True)
        ust[slot] = gu
        stage_copy(slot, b).start()
        return carry

    lax.fori_loop(0, 8, mlp, 0)
    for n in (0, 9):
        saves[n].wait()

    zero = jnp.zeros((1, width), F32)

    def finals(i):
        r = rows_of(i, block)
        return [
            pltpu.make_async_copy(dh.at[r], gx_h.at[r], fin.at[0, i]),
            pltpu.make_async_copy(tok.at[r], go_h.at[r], fin.at[1, i]),
            pltpu.make_async_copy(h2.at[r], ga_h.at[r], fin.at[2, i]),
        ]

    def norm_back(i, acc):
        r = rows_of(i, block)
        g = dh[r, :]
        xh, scale = normalized(x1[r, :])
        gg = g * gain2
        inner = gg - jnp.mean(gg, axis=1, keepdims=True)
        inner = inner - xh * jnp.mean(gg * xh, axis=1, keepdims=True)
        total = grad[r, :].astype(F32) + scale * inner
        dh[r, :] = total
        low_total = total.astype(BF)
        h2[r, :] = low_total
        tok[r, :] = dot_nt(low_total, wo[...]).astype(BF)
        for copy in finals(i):
            copy.start()
        return (
            acc[0] + jnp.sum(g * xh, axis=0, keepdims=True),
            acc[1] + jnp.sum(g, axis=0, keepdims=True),
            acc[2] + jnp.sum(low_total.astype(F32), axis=0, keepdims=True),
        )

    sums = lax.fori_loop(0, length // block, norm_back, (zero, zero, zero))
    for n, row in enumerate((sums[0], sums[1], sums[2], grad_sum)):
        vec_o[pl.ds(n, 1), :] = row
    for n, row in enumerate((gain1, gain2, shift2, b_out, b_down)):
        vec_o[pl.ds(8 + n, 1), :] = row
    for slot in range(2):
        stage_copy(slot, d).wait()
    for n in range(4):
        first_stage(n).wait()
    for n in (1, 2, 3, 4, 5, 7, 8):
        saves[n].wait()
    for n in range(8):
        save_down(n).wait()
    keep_att.wait()
    for w in range(4):
        drain(w)
    for copy in sm_copies + fil_copies + tok_copies + grad_copies + back_copies:
        copy.wait_send()
    for copy in back_copies:
        copy.wait_recv()
    for i in range(length // block):
        for copy in finals(i):
            copy.wait()


def front(tokens, out_grad, filled_rows, qkv_weight, out_weight, up_weight, down_weight, small):
    images, part, width = tokens.shape
    length = images * part
    shards = lax.axis_size("dp")
    ff = up_weight.shape[1]
    wide = qkv_weight.shape[1]
    shape = jax.ShapeDtypeStruct
    any_spec = pl.BlockSpec(memory_space=pl.ANY)
    vmem_spec = pl.BlockSpec(memory_space=pltpu.VMEM)
    dma = pltpu.SemaphoreType.DMA
    vm = pltpu.VMEM
    return pl.pallas_call(
        front_kernel,
        name="front",
        out_shape=(
            shape((length, width), BF),
            shape((length, width), BF),
            shape((length, wide), BF),
            shape((length, width), F32),
            shape((length, width), BF),
            shape((length, width), BF),
            shape((length, width), BF),
            shape((length, ff), BF),
            shape((length, width), BF),
            shape((images, part, width), BF),
            shape((4, ff // 8, width), BF),
            shape((2, ff // 32, width), BF),
            shape((2, ff // 32, width), BF),
            shape((width, wide), BF),
            shape((width, width), BF),
            shape((width, ff), BF),
            shape((ff, width), BF),
            shape((16, width), F32),
            shape((1, ff), F32),
            shape((1, ff), F32),
            shape((8, 2 * HD), F32),
            shape((8, length), F32),
        ),
        in_specs=[any_spec] * 6 + [vmem_spec] * 2,
        out_specs=[any_spec] * 17 + [vmem_spec] * 5,
        scratch_shapes=[
            vm((width, wide), BF), vm((width, width), BF), vm((width, ff), BF), vm((ff, width), BF),
            vm((length, width), BF), vm((length, width), BF), vm((length, width), BF),
            vm((length, wide), BF), vm((length, width), BF), vm((length, width), F32),
            vm((length, width), BF), vm((length, width), F32),
            vm((images, 8, length), F32), vm((shards, 1, sum(SMALL)), F32),
            vm((length, 8), F32), vm((length, ff), BF),
            vm((2, length, down_weight.shape[0]), BF), vm((8, width), F32),
            vm((2, ff // 8, width), BF), vm((4, ff // 8, width), BF), vm((1, sum(SMALL)), F32),
            vm((images, 8, length), F32),
            dma((4, 3, 2)), dma((4, 3, 2)), dma((4, 2)), dma((4, 2)), dma((4, 3)), dma((4, 3)),
            dma((2, images - 1)), dma((2, images - 1)), dma((2, images - 1)), dma((2, images - 1)),
            dma((images - 1,)), dma((images - 1,)), dma((7,)), dma((7,)),
            dma((4,)), dma((4,)), dma((4,)), dma((4,)), dma((8,)), dma((2,)), dma((14,)), dma((8,)),
            dma((3, length // 128)),
        ],
        compiler_params=pltpu.CompilerParams(
            collective_id=0, has_side_effects=True, vmem_limit_bytes=63 << 20
        ),
    )(tokens, out_grad, qkv_weight, out_weight, up_weight, down_weight, small, filled_rows)


def back_kernel(*refs):
    (
        qkv_in, go_in, h1_in, gx_in, tok_in, ga_in, h2_in, gu_in, att_in, atto_in, first_in,
        fx_in, fy_in, mine_in, wq_in, wo_in, wu_in, wd_in,
        mask_in, vec_in, dbup_in, bup_in, top_in,
        out_h, tg_h, dwq_h, dwo_h, dwu_h, dwd_h, small_o, top_o,
        qkv, go, ht, gbuf, buf, dh, wqg, pq, gp, colm, dst, own_u, ust, stg_o, ast, gxs,
        psm, rsm, zsm, rtop, ztop,
    ) = refs[:52]
    refs = refs[52:]
    count = 11
    recv0, recv1x, recv1y, recv2, za, zb = [refs[i * count : (i + 1) * count] for i in range(6)]
    (
        s0_s, s0_r, u0_s, u0_r, s1_s, s1_r, s2_s, s2_r, z_s, z_r, ex_s, ex_r, sm_s, sm_r,
        zs_s, zs_r, tp_s, tp_r, tz_s, tz_r, asem, wsem, osem, lsem, gsem,
    ) = refs[6 * count :]
    d, s = lax.axis_index("dp"), lax.axis_index("seq")
    length, width = go.shape
    images, part = mine_in.shape[0], mine_in.shape[1]
    sib, xn, yn = flip(d, 1), flip(d, 2), flip(d, 4)
    group_cols = gp.shape[1] // 3
    groups = width // group_cols
    ff_block = dst.shape[1]
    shard = width // 8
    block = 128
    tile = 512

    barrier = pltpu.get_barrier_semaphore()
    for m in range(1, 8):
        pl.semaphore_signal(barrier, inc=1, device_id=(flip(d, m), s), device_id_type=MESH)
    for j in range(1, images):
        pl.semaphore_signal(
            barrier, inc=1, device_id=(d, lax.rem(s + j, images)), device_id_type=MESH
        )

    def load(src, dst_ref, n):
        return pltpu.make_async_copy(src, dst_ref, lsem.at[n])

    def send(src, dst_ref, ss, rs, to_dp, to_seq):
        return pltpu.make_async_remote_copy(
            src_ref=src, dst_ref=dst_ref, send_sem=ss, recv_sem=rs,
            device_id=(to_dp, to_seq), device_id_type=MESH,
        )

    down_rows, up_cols = recv0[0].shape[1], recv0[2].shape[2]
    size = [down_rows] * 2 + [shard] * 9

    def s1(i, n):
        half = size[i] // 2
        lower, upper = pl.ds(0, half), pl.ds(half, half)
        m, part_rows, to_ref, to = (
            (6, lower, recv1x[i].at[1], xn), (6, upper, recv1y[i].at[1], yn),
            (2, lower, recv1x[i].at[0], xn), (4, upper, recv1y[i].at[0], yn),
        )[n]
        return send(recv0[i].at[m // 2, part_rows], to_ref, s1_s.at[i, n], s1_r.at[i, n], to, s)

    def s2(i, n):
        half = size[i] // 2
        if n == 0:
            return send(recv1x[i].at[1], recv2[i].at[pl.ds(0, half)],
                        s2_s.at[i, 0], s2_r.at[i, 0], yn, s)
        return send(recv1y[i].at[1], recv2[i].at[pl.ds(half, half)],
                    s2_s.at[i, 1], s2_r.at[i, 1], xn, s)

    mate = s + 1 - 2 * lax.rem(s, 2)
    across = 3 - s
    is_mid = jnp.logical_or(s == 1, s == 2)
    is_end = jnp.logical_or(s == 0, s == 3)

    def to_mid(i):
        return send(recv2[i], za[i], z_s.at[i, 0], z_r.at[i, 0], d, mate)

    def cross(i):
        return send(za[i], zb[i], z_s.at[i, 1], z_r.at[i, 1], d, across)

    def to_end(i):
        return send(zb[i], za[i], z_s.at[i, 2], z_r.at[i, 2], d, mate)

    def outputs(i, src):
        if i < 2:
            return [pltpu.make_async_copy(src, dwd_h.at[pl.ds(i * down_rows, down_rows)],
                                          osem.at[i, 0])]
        if i < 6:
            return [pltpu.make_async_copy(src, dwu_h.at[:, pl.ds((i - 2) * up_cols, up_cols)],
                                          osem.at[i, 0])]
        if i == 6:
            return [pltpu.make_async_copy(src, dwo_h, osem.at[i, 0])]
        return [
            pltpu.make_async_copy(
                src.at[:, pl.ds(third * group_cols, group_cols)],
                dwq_h.at[:, pl.ds(third * width + (i - 7) * group_cols, group_cols)],
                osem.at[i, third],
            )
            for third in range(3)
        ]

    def step1(i):
        for n in range(4):
            s1(i, n).start()

    def arrived(i, n):
        if i:
            s1(i, n).wait_recv()
        elif n == 0:
            for copy in ready_first:
                copy.wait()

    def step2(i):
        half = size[i] // 2
        arrived(i, 0)
        add_rows(recv1x[i].at[1], recv0[i].at[2, pl.ds(0, half)], half)
        s2(i, 0).start()
        arrived(i, 1)
        add_rows(recv1y[i].at[1], recv0[i].at[1, pl.ds(half, half)], half)
        s2(i, 1).start()
        arrived(i, 2)
        add_rows(recv1x[i].at[0], recv0[i].at[0, pl.ds(0, half)], half)
        arrived(i, 3)
        add_rows(recv1y[i].at[0], recv0[i].at[0, pl.ds(half, half)], half)

    def step3(i):
        half = size[i] // 2
        s2(i, 0).wait_recv()
        add_rows(recv2[i].at[pl.ds(0, half)], recv1x[i].at[0], half)
        s2(i, 1).wait_recv()
        add_rows(recv2[i].at[pl.ds(half, half)], recv1y[i].at[0], half)

        @pl.when(is_end)
        def _():
            to_mid(i).start()

    def step4(i):
        @pl.when(is_mid)
        def _():
            to_mid(i).wait_recv()
            add_rows(za[i], recv2[i], size[i])
            cross(i).start()

    def step5(i):
        @pl.when(is_mid)
        def _():
            cross(i).wait_recv()
            add_rows(zb[i], za[i], size[i])
            to_end(i).start()
            for copy in outputs(i, zb[i]):
                copy.start()

    def step6(i):
        @pl.when(is_end)
        def _():
            to_end(i).wait_recv()
            for copy in outputs(i, za[i]):
                copy.start()

    def drain(i):
        for n in range(4 if i else 0):
            s1(i, n).wait_send()
        for n in range(2):
            s2(i, n).wait_send()

        @pl.when(is_end)
        def _():
            to_mid(i).wait_send()
            for copy in outputs(i, za[i]):
                copy.wait()

        @pl.when(is_mid)
        def _():
            cross(i).wait_send()
            to_end(i).wait_send()
            for copy in outputs(i, zb[i]):
                copy.wait()

    def cols_of(b, n=ff_block):
        return pl.ds(pl.multiple_of(b * n, n), n)

    def gu_load(slot, b):
        return pltpu.make_async_copy(gu_in.at[:, cols_of(b)], ast.at[slot], asem.at[slot])

    lower_rows, upper_rows = pl.ds(0, down_rows), pl.ds(down_rows, down_rows)
    ready_first = [
        load(fx_in, recv1x[0], 11 + 2 * images), load(fy_in, recv1y[0], 12 + 2 * images),
        load(first_in.at[:, lower_rows], recv0[0], 13 + 2 * images),
    ]
    ready_second = load(first_in.at[:, upper_rows], recv0[1], 0)
    ready_second.start()
    for copy in ready_first:
        copy.start()
    load_h2 = load(h2_in, buf, 1)
    load_h2.start()
    load_qkv = load(qkv_in, qkv, 2)
    load_qkv.start()
    load_go = load(go_in, go, 3)
    load_go.start()

    def weight_group(g):
        return [
            pltpu.make_async_copy(
                wq_in.at[:, pl.ds(third * width + g * group_cols, group_cols)],
                wqg.at[g % 2, :, pl.ds(third * group_cols, group_cols)],
                wsem.at[g % 2, third],
            )
            for third in range(3)
        ]

    for copy in weight_group(0):
        copy.start()
    pl.semaphore_wait(barrier, 7 + images - 1)
    top_copies = [
        send(top_in, rtop.at[d], tp_s.at[m - 1], tp_r.at[m - 1], flip(d, m), s)
        for m in range(1, 8)
    ]
    for copy in top_copies:
        copy.start()
    gu_load(0, 0).start()
    load_ga = load(ga_in, gbuf, 4)
    load_ga.start()
    dh[...] = jnp.zeros_like(dh)
    colm[...] = jnp.transpose((mask_in[...] - 1.0) * 1e30)
    ready_second.wait()

    def turned(src):
        @pl.loop(0, 8)
        def _(m):
            at = pl.ds(pl.multiple_of(flip_traced(d, m) * shard, shard), shard)
            ht[rows_of(m, shard), :] = jnp.transpose(src[:, at])

    load_att = load(att_in, buf, 5)
    load_h1 = load(h1_in, buf, 6)
    load_tok = load(tok_in, gbuf, 7)

    def turn1():
        load_h2.wait()
        turned(buf)
        load_att.start()

    def split_store(value, keep, give, cols_keep, cols_give):
        for m in range(8):
            piece = value[m * shard : (m + 1) * shard].astype(BF)
            if m % 2 == 0:
                keep[m // 2, :, cols_keep] = piece
            else:
                give[m // 2, :, cols_give] = piece

    blocks = up_cols // tile

    def up_send(i, n):
        return send(ust.at[n], recv0[2 + i].at[:, :, cols_of(n, tile)],
                    u0_s.at[i, n], u0_r.at[i, n], sib, s)

    def up(i):
        if i:
            for n in range(blocks):
                up_send(i - 1, n).wait_send()

        def body(n, carry):
            b = i * blocks + n
            slot = lax.rem(b, 2)
            gu_load(slot, b).wait()

            @pl.when(b + 1 < 4 * blocks)
            def _():
                gu_load(1 - slot, b + 1).start()

            value = dot_nn(ht[...], ast[slot])
            split_store(value, own_u.at[i % 2], ust.at[n], cols_of(n, tile), slice(None))
            up_send(i, n).start()
            return carry

        lax.fori_loop(0, blocks, body, 0)

    def add_up(i):
        for n in range(blocks):
            up_send(i, n).wait_recv()
        for m in (6, 2, 4, 0):
            add_rows(recv0[2 + i].at[m // 2], own_u.at[i % 2, m // 2], shard)

    def out_send(n):
        return send(ust.at[n], recv0[6].at[:, :, pl.ds(n * tile, tile)],
                    s0_s.at[0, n], s0_r.at[0, n], sib, s)

    def out():
        load_ga.wait()
        load_att.wait()
        turned(buf)
        load_h1.start()
        for n in range(blocks):
            up_send(3, n).wait_send()
        for n in range(width // tile):
            value = dot_nn(ht[...], gbuf[:, pl.ds(n * tile, tile)])
            split_store(value, stg_o, ust.at[n], pl.ds(n * tile, tile), slice(None))
            out_send(n).start()
        load_tok.start()

    def turn3():
        load_h1.wait()
        turned(buf)

    def add_out():
        for n in range(width // tile):
            out_send(n).wait_recv()
            out_send(n).wait_send()
        for m in (6, 2, 4, 0):
            add_rows(recv0[6].at[m // 2], stg_o.at[m // 2], shard)

    low, high, low_lane = half_masks()
    scale = HD ** (-0.5)
    pair = 2 * HD
    per_group = group_cols // pair
    cuts = ((0, 256), (256, length - 256)) if length > 256 else ((0, length),)
    def attention(g):
        if g == 0:
            load_qkv.wait()
            load_go.wait()
        if g + 1 < groups:
            for copy in weight_group(g + 1):
                copy.start()

        def body(n, carry):
            p = g * per_group + n
            c = pl.ds(pl.multiple_of(p * pair, pair), pair)
            ck = pl.ds(pl.multiple_of(width + p * pair, pair), pair)
            cv = pl.ds(pl.multiple_of(2 * width + p * pair, pair), pair)
            k, v = qkv[:, ck], qkv[:, cv]
            k2 = jnp.concatenate([k * low, k * high], axis=0)
            v2 = jnp.concatenate([v * low, v * high], axis=0)
            gk = jnp.zeros((2 * length, pair), F32)
            gv = jnp.zeros((2 * length, pair), F32)
            at_q = pl.ds(pl.multiple_of(n * pair, pair), pair)
            at_k = pl.ds(pl.multiple_of(group_cols + n * pair, pair), pair)
            at_v = pl.ds(pl.multiple_of(2 * group_cols + n * pair, pair), pair)
            for first, wide in cuts:
                r = pl.ds(first, wide)
                q = qkv[r, c] * jnp.asarray(scale, BF)
                g_rows = go[r, c]
                scores = dot_nt(k2, q)
                dprob = dot_nt(v2, g_rows)
                low_probs, low_grads = [], []
                for side in range(2):
                    rows = slice(side * length, (side + 1) * length)
                    part_s = scores[rows] + colm[:, 0:1]
                    e = jnp.exp(part_s - jnp.max(part_s, axis=0, keepdims=True))
                    probs = e * (1.0 / jnp.sum(e, axis=0, keepdims=True))
                    weighted = probs * dprob[rows]
                    inner = jnp.sum(weighted, axis=0, keepdims=True)
                    low_probs.append(probs.astype(BF))
                    low_grads.append((weighted - probs * inner).astype(BF))
                low_p = jnp.concatenate(low_probs, axis=0)
                low_g = jnp.concatenate(low_grads, axis=0)
                gv = gv + dot_nn(low_p, g_rows)
                gk = gk + dot_nn(low_g, q)
                gp[r, at_q] = (dot_tn(low_g, k2) * scale).astype(BF)
            gp[:, at_k] = jnp.where(low_lane, gk[:length], gk[length:]).astype(BF)
            gp[:, at_v] = jnp.where(low_lane, gv[:length], gv[length:]).astype(BF)
            return carry

        lax.fori_loop(0, per_group, body, 0)

    bias_rows = []

    def q_send(g):
        return send(pq.at[g % 2, 1], recv0[7 + g], s0_s.at[1 + g, 0], s0_r.at[1 + g, 0], sib, s)

    def group(g):
        if g >= 2:
            q_send(g - 2).wait_send()
        bias_rows.append(jnp.sum(gp[...].astype(F32), axis=0, keepdims=True))
        for third in range(3):
            cols = pl.ds(third * group_cols, group_cols)
            value = dot_nn(ht[...], gp[:, cols])
            split_store(value, pq.at[g % 2, 0], pq.at[g % 2, 1], cols, cols)
        q_send(g).start()
        for copy in weight_group(g):
            copy.wait()
        for first in range(0, width, tile):
            dh[:, pl.ds(first, tile)] += dot_nt(gp[...], wqg[g % 2, pl.ds(first, tile), :])

    def add_q(g):
        q_send(g).wait_recv()
        for m in (6, 2, 4, 0):
            add_rows(recv0[7 + g].at[m // 2], pq.at[g % 2, 0, m // 2], shard)

    gain1 = vec_in[pl.ds(8, 1), :]
    zero = jnp.zeros((1, width), F32)

    def gx_load(slot, i):
        return pltpu.make_async_copy(gx_in.at[rows_of(i, block)], gxs.at[slot], gsem.at[slot])

    def norm_back(i, acc):
        slot = lax.rem(i, 2)
        gx_load(slot, i).wait()

        @pl.when(i + 1 < length // block)
        def _():
            gx_load(1 - slot, i + 1).start()

        r = rows_of(i, block)
        g = dh[r, :]
        xh, spread = normalized(gbuf[r, :].astype(F32))
        gg = g * gain1
        inner = gg - jnp.mean(gg, axis=1, keepdims=True)
        inner = inner - xh * jnp.mean(gg * xh, axis=1, keepdims=True)
        go[r, :] = (gxs[slot] + spread * inner).astype(BF)
        return (
            acc[0] + jnp.sum(g * xh, axis=0, keepdims=True),
            acc[1] + jnp.sum(g, axis=0, keepdims=True),
        )

    late = {}
    tg_copies = []
    for j in range(1, images):
        to = lax.rem(s + j, images)
        tg_copies.append(
            send(go.at[rows_of(to, part)], tg_h.at[s], ex_s.at[j - 1], ex_r.at[j - 1], d, to)
        )
    own_tg = load(go.at[rows_of(s, part)], tg_h.at[s], 8)

    own_loads = []
    for j in range(images):
        rows = pl.ds(j * part, part)
        own_loads.append(load(mine_in.at[j], qkv.at[rows, pl.ds(0, width)], 9 + j))
        own_loads.append(load(atto_in.at[j], qkv.at[rows, pl.ds(width, width)], 9 + images + j))
    own_loads.append(load(wo_in.at[pl.ds(0, tile)], dst.at[0], 9 + 2 * images))
    own_loads.append(load(wo_in.at[pl.ds(tile, tile)], dst.at[1], 10 + 2 * images))

    def norm1():
        for copy in own_loads:
            copy.start()
        load_tok.wait()
        gx_load(0, 0).start()
        late["norm"] = lax.fori_loop(0, length // block, norm_back, (zero, zero))

    def tg():
        for copy in tg_copies:
            copy.start()
        own_tg.start()

    sm_copies = [
        send(psm.at[flip(d, m)], rsm.at[m - 1], sm_s.at[m - 1], sm_r.at[m - 1], flip(d, m), s)
        for m in range(1, 8)
    ]
    top_z, sm_z = [], []
    for j in range(1, images):
        to = lax.rem(s + j, images)
        top_z.append(send(ztop.at[s], ztop.at[s], tz_s.at[j - 1], tz_r.at[j - 1], d, to))
        sm_z.append(send(zsm.at[s], zsm.at[s], zs_s.at[j - 1], zs_r.at[j - 1], d, to))

    def smalls():
        d_gain1, d_shift1 = late["norm"]
        q_sum = jnp.concatenate([row[:, :group_cols] for row in bias_rows], axis=1)
        v_sum = jnp.concatenate([row[:, 2 * group_cols :] for row in bias_rows], axis=1)
        pieces = (
            d_gain1, d_shift1, jnp.concatenate([q_sum, v_sum], axis=1), vec_in[pl.ds(2, 1), :],
            vec_in[pl.ds(0, 1), :], vec_in[pl.ds(1, 1), :], dbup_in[...], vec_in[pl.ds(3, 1), :],
        )
        for b in range(8):
            psm[b] = jnp.concatenate(
                [piece[:, b * n : (b + 1) * n] for piece, n in zip(pieces, SMALL)], axis=1
            )
        for copy in sm_copies:
            copy.start()
        for copy in top_copies:
            copy.wait_recv()
        rtop[d] = top_in[...]
        best = rtop[0]
        for b in range(1, 8):
            best = jnp.maximum(best, rtop[b])
        ztop[s] = best
        for copy in top_z:
            copy.start()

    def smalls_z():
        for copy in sm_copies:
            copy.wait_recv()
        mine = psm[d]
        for m in range(7):
            mine = mine + rsm[m]
        zsm[s] = mine
        for copy in sm_z:
            copy.start()

    gain2, shift2 = vec_in[pl.ds(9, 1), :], vec_in[pl.ds(10, 1), :]
    b_out, b_down = vec_in[pl.ds(11, 1), :], vec_in[pl.ds(12, 1), :]

    def owners():
        for copy in own_loads:
            copy.wait()

        @pl.loop(0, length // block)
        def _(i):
            r = rows_of(i, block)
            mid = qkv[r, 0:width].astype(F32) + b_out
            mid = mid + dot_nn(qkv[r, width : width + tile], dst[0])
            mid = mid + dot_nn(qkv[r, width + tile : 2 * width], dst[1])
            xh, _ = normalized(mid)
            dh[r, :] = mid + b_down
            qkv[r, 2 * width :] = (xh * gain2 + shift2).astype(BF)

        for copy in ff_loads(0, 0):
            copy.start()

    def ff_loads(slot, b):
        return (
            pltpu.make_async_copy(wu_in.at[:, cols_of(b)], wqg.at[slot, :, pl.ds(0, ff_block)],
                                  wsem.at[slot, 0]),
            pltpu.make_async_copy(wd_in.at[rows_of(b, ff_block)], dst.at[slot],
                                  wsem.at[slot, 1]),
        )

    def feed_block(b, carry):
        slot = lax.rem(b, 2)
        for copy in ff_loads(slot, b):
            copy.wait()

        @pl.when(b < 7)
        def _():
            for copy in ff_loads(1 - slot, b + 1):
                copy.start()

        u = dot_nn(qkv[:, 2 * width :], wqg[slot, :, 0:ff_block]) + bup_in[:, cols_of(b)]
        a = (u * (0.5 * (1.0 + lax.erf(u * (0.5**0.5))))).astype(BF)
        dh[...] += dot_nn(a, dst[slot])
        return carry

    keep_out = load(buf, out_h, 1)

    def feed(n):
        lax.fori_loop(2 * n, 2 * n + 2, feed_block, 0)
        if n == 1:
            smalls_z()
        if n == 3:
            buf[...] = dh[...].astype(BF)
            keep_out.start()

    step2(0)
    turn1()
    up(0)
    step1(1)
    up(1)
    add_up(0)
    step3(0)
    up(2)
    add_up(1)
    up(3)
    step1(3)
    out()
    step2(1)
    turn3()
    add_out()
    step1(6)
    attention(0)
    step3(1)
    step4(0)
    step2(3)
    group(0)
    step1(2)
    attention(1)
    step2(6)
    step3(3)
    add_up(2)
    step4(1)
    step5(0)
    add_up(3)
    step2(2)
    step1(5)
    group(1)
    step3(6)
    step1(4)
    step4(3)
    attention(2)
    step5(1)
    add_q(1)
    add_q(0)
    step4(6)
    step3(2)
    step2(5)
    group(2)
    step5(3)
    step2(4)
    step4(2)
    step1(7)
    step3(5)
    attention(3)
    step4(5)
    step3(4)
    step2(7)
    add_q(2)
    step5(6)
    step1(8)
    group(3)
    step5(2)
    step3(7)
    step4(4)
    norm1()
    step4(7)
    tg()
    step5(4)
    step6(0)
    add_q(3)
    owners()
    step5(5)
    smalls()
    step6(1)
    step1(9)
    feed(0)
    step1(10)
    step6(6)
    step2(9)
    feed(1)
    step6(2)
    step6(3)
    step2(8)
    step3(9)
    step3(8)
    step2(10)
    step3(10)
    step4(8)
    step5(7)
    step4(10)
    step6(5)
    step4(9)
    feed(2)
    step5(8)
    step5(10)
    step6(8)
    step6(4)
    feed(3)
    step5(9)
    step6(10)
    step6(7)
    step6(9)

    for copy in top_z + sm_z:
        copy.wait_recv()
    top_o[...] = jnp.maximum(jnp.maximum(ztop[0], ztop[1]), jnp.maximum(ztop[2], ztop[3]))
    small_o[...] = (zsm[0] + zsm[1]) + (zsm[2] + zsm[3])
    for g in range(groups - 2, groups):
        q_send(g).wait_send()
    for i in range(count):
        drain(i)
    for copy in top_copies + top_z + sm_copies + sm_z + tg_copies:
        copy.wait_send()
    for copy in tg_copies:
        copy.wait_recv()
    own_tg.wait()
    keep_out.wait()


def back(tokens, saved, vecs):
    images, part, width = tokens.shape
    (
        tok, h1, qkv, gx, go, ga, h2, gu, att, atto, first, fx, fy, wq, wo, wu, wd,
    ) = saved
    vec, dbup, bup, tops, mask = vecs
    length = images * part
    wide, ff = wq.shape[1], wu.shape[1]
    shard = width // 8
    shape = jax.ShapeDtypeStruct
    any_spec = pl.BlockSpec(memory_space=pl.ANY)
    vmem_spec = pl.BlockSpec(memory_space=pltpu.VMEM)
    dma = pltpu.SemaphoreType.DMA
    vm = pltpu.VMEM
    group_cols = 256
    groups = width // group_cols
    sizes = [(ff // 16, width)] * 2 + [(shard, ff // 4)] * 4 + [(shard, width)]
    sizes += [(shard, 3 * group_cols)] * groups
    count = len(sizes)
    halves = [vm((2, r // 2, c), BF) for r, c in sizes]
    whole = [vm((r, c), BF) for r, c in sizes]
    z_peers = images - 1
    small = sum(SMALL)
    return pl.pallas_call(
        back_kernel,
        name="back",
        out_shape=(
            shape((length, width), BF),
            shape((images, part, width), BF),
            shape((shard, wide), BF),
            shape((shard, width), BF),
            shape((shard, ff), BF),
            shape((ff // 8, width), BF),
            shape((1, small), F32),
            shape((8, 2 * HD), F32),
        ),
        in_specs=[any_spec] * 18 + [vmem_spec] * 5,
        out_specs=[any_spec] * 6 + [vmem_spec] * 2,
        scratch_shapes=[
            vm((length, wide), BF), vm((length, width), BF), vm((width, length), BF),
            vm((length, width), BF), vm((length, width), BF), vm((length, width), F32),
            vm((2, width, 3 * group_cols), BF), vm((2, 2, 4, shard, 3 * group_cols), BF),
            vm((length, 3 * group_cols), BF), vm((length, 8), F32),
            vm((2, ff // 8, width), BF), vm((2, 4, shard, ff // 4), BF), vm((2, 4, shard, 512), BF),
            vm((4, shard, width), BF), vm((2, length, ff // 8), BF), vm((2, 128, width), F32),
            vm((8, 1, small), F32), vm((7, 1, small), F32),
            vm((images, 1, small), F32), vm((8, 8, 2 * HD), F32), vm((images, 8, 2 * HD), F32),
            *[vm((4, r, c), BF) for r, c in sizes], *halves, *halves, *whole, *whole, *whole,
            dma((5, 2)), dma((5, 2)), dma((4, 2)), dma((4, 2)), dma((count, 4)),
            dma((count, 4)), dma((count, 2)), dma((count, 2)), dma((count, 3)), dma((count, 3)),
            dma((z_peers,)), dma((z_peers,)), dma((7,)), dma((7,)),
            dma((z_peers,)), dma((z_peers,)), dma((7,)), dma((7,)),
            dma((z_peers,)), dma((z_peers,)), dma((2,)), dma((2, 3)), dma((count, 3)),
            dma((14 + 2 * images,)), dma((2,)),
        ],
        compiler_params=pltpu.CompilerParams(
            collective_id=1, has_side_effects=True, vmem_limit_bytes=63 << 20
        ),
    )(
        qkv, go, h1, gx, tok, ga, h2, gu, att, atto, first, fx, fy, tokens, wq, wo, wu, wd,
        mask, vec, dbup, bup, tops,
    )


def finish_kernel(
    limit_in, top_in, out_in, tg_in, dwq_in, dwo_in, dwu_in, dwd_in, w_in, small_in,
    out_o, tg_o, dwq_o, dwo_o, dwu_o, dwd_o, w_o, *small_o
):
    out_o[...] = out_in[...]
    tg_o[...] = tg_in[...]
    for src, to in ((dwq_in, dwq_o), (dwo_in, dwo_o), (dwu_in, dwu_o), (dwd_in, dwd_o)):
        to[...] = src[...].astype(F32)
    limit = jnp.full((1, 1), limit_in[0], jnp.int32).astype(F32)
    root = jnp.sqrt(limit / jnp.maximum(top_in[...], limit))
    row = jnp.concatenate([root[p : p + 1, :] for p in range(root.shape[0])], axis=1)
    width = row.shape[1]
    for third in range(3):
        c = slice(third * width, (third + 1) * width)
        if third < 2:
            w_o[:, c] = (w_in[:, c].astype(F32) * row).astype(BF)
        else:
            w_o[:, c] = w_in[:, c]
    start = 0
    for to in small_o:
        n = to.shape[1]
        to[...] = small_in[:, start : start + n]
        start += n


def finish(limit, top, out, tg, dwq, dwo, dwu, dwd, weight, small):
    steps = 2
    parts = (out, tg, dwq, dwo, dwu, dwd, weight)
    specs = [pl.BlockSpec((p.shape[0] // steps, p.shape[1]), lambda i: (i, 0)) for p in parts]

    def fixed(shape):
        return pl.BlockSpec(shape, lambda i: (0, 0))

    shape = jax.ShapeDtypeStruct
    kinds = (BF, BF, F32, F32, F32, F32, BF)
    return pl.pallas_call(
        finish_kernel,
        name="finish",
        grid=(steps,),
        out_shape=[shape(p.shape, kind) for p, kind in zip(parts, kinds)]
        + [shape((1, n), F32) for n in SMALL],
        in_specs=[pl.BlockSpec(memory_space=pltpu.SMEM), fixed(top.shape)]
        + specs + [fixed(small.shape)],
        out_specs=specs + [fixed((1, n)) for n in SMALL],
        compiler_params=pltpu.CompilerParams(vmem_limit_bytes=63 << 20),
    )(limit, top, out, tg, dwq, dwo, dwu, dwd, weight, small)


def by_image_local(
    tokens,
    filled,
    out_grad,
    norm1_gain,
    norm1_bias,
    qkv_weight,
    qv_bias,
    out_weight,
    out_bias,
    norm2_gain,
    norm2_bias,
    up_weight,
    up_bias,
    down_weight,
    down_bias,
    clip_threshold,
):
    images, local_rows, model_width = tokens.shape
    length = local_rows * images
    small, start = 0.0, 0
    for piece in (
        norm1_gain, norm1_bias, qv_bias, out_bias, norm2_gain, norm2_bias, up_bias, down_bias
    ):
        count = piece.shape[0]
        after = sum(SMALL) - start - count
        small = small + jnp.pad(piece[None], ((0, 0), (start, after))).astype(F32)
        start += count
    made = front(tokens, out_grad, filled, qkv_weight, out_weight, up_weight, down_weight, small)
    block_out, tokens_grad, g_qkv, g_out, g_up, g_down, mine, top = back(
        tokens, made[:17], made[17:]
    )
    (
        block_out, tokens_grad, g_qkv, g_out, g_up, g_down, clipped_weight, *small_out
    ) = finish(
        clip_threshold[None], top, block_out, tokens_grad.reshape(length, model_width),
        g_qkv, g_out, g_up, g_down, qkv_weight, mine,
    )
    s_gain_one, s_shift_one, s_qv, s_out, s_gain_two, s_shift_two, s_up, s_down = [
        piece.reshape(-1) for piece in small_out
    ]
    block_out = block_out.reshape(tokens.shape)
    tokens_grad = tokens_grad.reshape(tokens.shape)
    head_max = top[:, ::HD].reshape(-1)
    limit = clip_threshold.astype(F32)
    root_factor = jnp.sqrt(limit / jnp.maximum(head_max, limit))
    head_cols = jnp.repeat(root_factor, HD)
    ones = jnp.ones((model_width,), F32)
    bias_count = qv_bias.shape[0]
    bias_scale = jnp.concatenate([head_cols, ones])
    shard_scale = lax.dynamic_slice_in_dim(
        bias_scale, lax.axis_index("dp") * bias_count, bias_count
    )
    clipped_bias = (qv_bias.astype(F32) * shard_scale).astype(BF)
    return (
        block_out,
        tokens_grad,
        s_gain_one,
        s_shift_one,
        g_qkv,
        s_qv,
        g_out,
        s_out,
        s_gain_two,
        s_shift_two,
        g_up,
        s_up,
        g_down,
        s_down,
        clipped_weight,
        clipped_bias,
        head_max,
    )


def local(*args):
    if args[0].shape[0] == lax.axis_size("seq") == 4 and lax.axis_size("dp") == 8:
        return by_image_local(*args)
    return by_head_local(*args)


def solution(mesh):
    return jax.shard_map(
        local,
        mesh=mesh,
        in_specs=(
            P("dp", "seq", None),
            P("dp", "seq"),
            P("dp", "seq", None),
            P("dp"),
            P("dp"),
            P("dp", None),
            P("dp"),
            P("dp", None),
            P("dp"),
            P("dp"),
            P("dp"),
            P("dp", None),
            P("dp"),
            P("dp", None),
            P("dp"),
            P(),
        ),
        out_specs=(
            P("dp", "seq", None),
            P("dp", "seq", None),
            P("dp"),
            P("dp"),
            P("dp", None),
            P("dp"),
            P("dp", None),
            P("dp"),
            P("dp"),
            P("dp"),
            P("dp", None),
            P("dp"),
            P("dp", None),
            P("dp"),
            P("dp", None),
            P("dp"),
            P(),
        ),
        check_vma=False,
    )
```

```python
import math

import jax
import jax.numpy as jnp
from jax import lax
from jax.experimental import pallas as pl
from jax.experimental.pallas import tpu as pltpu
from jax.sharding import PartitionSpec as P

H = 16
HD = 64


epsilon = 1e-06
very_negative = -1e30


def norm_apply(values, gain_vec, shift_vec):
    center = jnp.mean(values, axis=-1, keepdims=True)
    centered = values - center
    spread = jnp.mean(centered * centered, axis=-1, keepdims=True)
    return centered * lax.rsqrt(spread + epsilon) * gain_vec + shift_vec


def exact_gelu(values):
    return jax.nn.gelu(values, approximate=False)


def last_dot(left_op, right_op):
    return lax.dot_general(
        left_op, right_op, (((1,), (1,)), ((), ())), preferred_element_type=jnp.float32
    )


def first_dot(left_op, right_op):
    return lax.dot_general(
        left_op, right_op, (((0,), (0,)), ((), ())), preferred_element_type=jnp.float32
    )


def column_sum(values):
    return jnp.sum(values.astype(jnp.float32), axis=0)


def score_block(queries, keys_in, key_keep):
    raw_scores = jnp.einsum(
        "qhd,khd->hqk", queries, keys_in, preferred_element_type=jnp.float32
    ) * HD ** (-0.5)
    masked = jnp.where(key_keep[None, None, :], raw_scores, very_negative)
    return (raw_scores, masked)


def attend_forward(inputs):
    queries, keys_in, values_in, key_keep = inputs
    raw_scores, masked = score_block(queries, keys_in, key_keep)
    row_peak = jnp.max(masked, axis=-1, keepdims=True)
    exp_scores = jnp.exp(masked - row_peak)
    row_total = jnp.sum(exp_scores, axis=-1, keepdims=True)
    soft_probs = (exp_scores / row_total).astype(jnp.bfloat16)
    mixed_rows = jnp.einsum(
        "hqk,khd->qhd", soft_probs, values_in, preferred_element_type=jnp.float32
    )
    logsum = row_peak + jnp.log(row_total)
    pair_keep = key_keep[:, None] & key_keep[None, :]
    head_top = jnp.max(jnp.where(pair_keep[None], raw_scores, very_negative), axis=(1, 2))
    flat_rows = mixed_rows.astype(jnp.bfloat16).reshape(mixed_rows.shape[0], -1)
    return (flat_rows, logsum, head_top)


def attend_backward(inputs):
    queries, keys_in, values_in, key_keep, logsum, upstream = inputs
    raw_scores, masked = score_block(queries, keys_in, key_keep)
    soft_probs = jnp.exp(masked - logsum)
    probs_low = soft_probs.astype(jnp.bfloat16)
    value_grad = jnp.einsum("hqk,qhd->khd", probs_low, upstream, preferred_element_type=jnp.float32)
    prob_grad = jnp.einsum("qhd,khd->hqk", upstream, values_in, preferred_element_type=jnp.float32)
    inner_sum = jnp.sum(soft_probs * prob_grad, axis=-1, keepdims=True)
    score_grad = (soft_probs * (prob_grad - inner_sum)).astype(jnp.bfloat16)
    score_scale = HD ** (-0.5)
    query_grad = (
        jnp.einsum("hqk,khd->qhd", score_grad, keys_in, preferred_element_type=jnp.float32)
        * score_scale
    )
    key_grad = (
        jnp.einsum("hqk,qhd->khd", score_grad, queries, preferred_element_type=jnp.float32)
        * score_scale
    )
    stacked = jnp.stack([query_grad, key_grad, value_grad], axis=1)
    return stacked.astype(jnp.bfloat16).reshape(stacked.shape[0], 3, -1)


def by_head_local(
    tokens,
    filled,
    out_grad,
    norm1_gain,
    norm1_bias,
    qkv_weight,
    qv_bias,
    out_weight,
    out_bias,
    norm2_gain,
    norm2_bias,
    up_weight,
    up_bias,
    down_weight,
    down_bias,
    clip_threshold,
):
    gathered = (
        lax.all_gather(norm1_gain, "dp", axis=0, tiled=True),
        lax.all_gather(norm1_bias, "dp", axis=0, tiled=True),
        lax.all_gather(qkv_weight, "dp", axis=0, tiled=True),
        lax.all_gather(qv_bias, "dp", axis=0, tiled=True),
        lax.all_gather(out_weight, "dp", axis=0, tiled=True),
        lax.all_gather(out_bias, "dp", axis=0, tiled=True),
        lax.all_gather(norm2_gain, "dp", axis=0, tiled=True),
        lax.all_gather(norm2_bias, "dp", axis=0, tiled=True),
        lax.all_gather(up_weight, "dp", axis=0, tiled=True),
        lax.all_gather(up_bias, "dp", axis=0, tiled=True),
        lax.all_gather(down_weight, "dp", axis=0, tiled=True),
        lax.all_gather(down_bias, "dp", axis=0, tiled=True),
    )
    (
        gain_one,
        shift_one,
        w_qkv,
        b_qv,
        w_out,
        b_out,
        gain_two,
        shift_two,
        w_up,
        b_up,
        w_down,
        b_down,
    ) = gathered
    images, local_rows, model_width = tokens.shape
    groups = lax.axis_size("seq")
    group_width = model_width // groups
    local_heads = group_width // HD
    length = local_rows * groups
    row_count = images * local_rows
    tokens_flat = tokens.astype(jnp.float32).reshape(row_count, model_width)
    gain_one_f = gain_one.astype(jnp.float32)
    shift_one_f = shift_one.astype(jnp.float32)
    gain_two_f = gain_two.astype(jnp.float32)
    shift_two_f = shift_two.astype(jnp.float32)
    hidden_one = norm_apply(tokens_flat, gain_one_f, shift_one_f).astype(jnp.bfloat16)
    bias_float = b_qv.astype(jnp.float32)
    qkv_bias = jnp.concatenate(
        [bias_float[:model_width], jnp.zeros((model_width,), jnp.float32), bias_float[model_width:]]
    )
    projected = (jnp.dot(hidden_one, w_qkv, preferred_element_type=jnp.float32) + qkv_bias).astype(
        jnp.bfloat16
    )
    key_flags = lax.all_gather(filled, "seq", axis=1, tiled=True)
    keep_all = key_flags > 0
    by_heads = lax.all_to_all(
        projected.reshape(images, local_rows, 3, groups, group_width),
        "seq",
        split_axis=3,
        concat_axis=1,
        tiled=True,
    )
    by_heads = by_heads.reshape(images, length, 3, local_heads, HD)
    queries = by_heads[:, :, 0]
    keys_all = by_heads[:, :, 1]
    values_all = by_heads[:, :, 2]
    attended, logsums, tops = lax.map(attend_forward, (queries, keys_all, values_all, keep_all))
    local_peak = jnp.max(tops, axis=0)
    peak_vector = lax.dynamic_update_slice(
        jnp.full((H,), very_negative, jnp.float32),
        local_peak,
        (lax.axis_index("seq") * local_heads,),
    )
    head_max = lax.pmax(peak_vector, ("dp", "seq"))
    back_rows = lax.all_to_all(
        attended.reshape(images, groups, local_rows, group_width),
        "seq",
        split_axis=1,
        concat_axis=3,
        tiled=True,
    )
    attn_rows = back_rows.reshape(row_count, model_width)
    branch = jnp.dot(attn_rows, w_out, preferred_element_type=jnp.float32) + b_out.astype(
        jnp.float32
    )
    middle = tokens_flat + branch
    hidden_two = norm_apply(middle, gain_two_f, shift_two_f).astype(jnp.bfloat16)
    pre_act = jnp.dot(hidden_two, w_up, preferred_element_type=jnp.float32) + b_up.astype(
        jnp.float32
    )
    activated = exact_gelu(pre_act).astype(jnp.bfloat16)
    block_rows = middle + (
        jnp.dot(activated, w_down, preferred_element_type=jnp.float32) + b_down.astype(jnp.float32)
    )
    block_out = block_rows.astype(jnp.bfloat16).reshape(tokens.shape)
    gain_one_b, w_qkv_b, w_out_b, gain_two_b, w_up_b, w_down_b = (
        lax.all_gather(norm1_gain, "dp", axis=0, tiled=True),
        lax.all_gather(qkv_weight, "dp", axis=0, tiled=True),
        lax.all_gather(out_weight, "dp", axis=0, tiled=True),
        lax.all_gather(norm2_gain, "dp", axis=0, tiled=True),
        lax.all_gather(up_weight, "dp", axis=0, tiled=True),
        lax.all_gather(down_weight, "dp", axis=0, tiled=True),
    )
    upstream = out_grad.reshape(row_count, model_width)
    upstream_f = upstream.astype(jnp.float32)
    d_bias_down = jnp.sum(upstream_f, axis=0)
    d_down = first_dot(activated, upstream)
    act_grad = last_dot(upstream, w_down_b)
    gelu_out, gelu_pull = jax.vjp(exact_gelu, pre_act)
    pre_grad = gelu_pull(act_grad)[0].astype(jnp.bfloat16)
    d_bias_up = column_sum(pre_grad)
    d_up = first_dot(hidden_two, pre_grad)
    hidden_two_grad = last_dot(pre_grad, w_up_b)
    norm_out_two, pull_two = jax.vjp(
        norm_apply, middle, gain_two_b.astype(jnp.float32), shift_two_f
    )
    mid_norm_grad, d_gain_two, d_shift_two = pull_two(hidden_two_grad)
    middle_grad = upstream_f + mid_norm_grad
    branch_grad = middle_grad.astype(jnp.bfloat16)
    d_bias_out = column_sum(branch_grad)
    d_out = first_dot(attn_rows, branch_grad)
    attn_grad = last_dot(branch_grad, w_out_b).astype(jnp.bfloat16)
    grad_heads = lax.all_to_all(
        attn_grad.reshape(images, local_rows, groups, group_width),
        "seq",
        split_axis=2,
        concat_axis=1,
        tiled=True,
    )
    grad_heads = grad_heads.reshape(images, length, local_heads, HD)
    head_grads = lax.map(
        attend_backward, (queries, keys_all, values_all, keep_all, logsums, grad_heads)
    )
    token_grads = lax.all_to_all(
        head_grads.reshape(images, groups, local_rows, 3, group_width),
        "seq",
        split_axis=1,
        concat_axis=4,
        tiled=True,
    )
    token_grads = token_grads.reshape(row_count, 3 * model_width)
    d_qkv = first_dot(hidden_one, token_grads)
    bias_sums = column_sum(token_grads)
    d_bias_qv = jnp.concatenate([bias_sums[:model_width], bias_sums[2 * model_width :]])
    first_grad = last_dot(token_grads, w_qkv_b)
    norm_out_one, pull_one = jax.vjp(
        norm_apply, tokens_flat, gain_one_b.astype(jnp.float32), shift_one_f
    )
    in_norm_grad, d_gain_one, d_shift_one = pull_one(first_grad)
    tokens_grad = (middle_grad + in_norm_grad).astype(jnp.bfloat16).reshape(tokens.shape)
    terms = (
        d_gain_one,
        d_shift_one,
        d_qkv,
        d_bias_qv,
        d_out,
        d_bias_out,
        d_gain_two,
        d_shift_two,
        d_up,
        d_bias_up,
        d_down,
        d_bias_down,
    )
    data_shards = (
        lax.psum_scatter(
            terms[0].astype(jnp.bfloat16), "dp", scatter_dimension=0, tiled=True
        ).astype(jnp.float32),
        lax.psum_scatter(
            terms[1].astype(jnp.bfloat16), "dp", scatter_dimension=0, tiled=True
        ).astype(jnp.float32),
        lax.psum_scatter(
            terms[2].astype(jnp.bfloat16), "dp", scatter_dimension=0, tiled=True
        ).astype(jnp.float32),
        lax.psum_scatter(
            terms[3].astype(jnp.bfloat16), "dp", scatter_dimension=0, tiled=True
        ).astype(jnp.float32),
        lax.psum_scatter(
            terms[4].astype(jnp.bfloat16), "dp", scatter_dimension=0, tiled=True
        ).astype(jnp.float32),
        lax.psum_scatter(
            terms[5].astype(jnp.bfloat16), "dp", scatter_dimension=0, tiled=True
        ).astype(jnp.float32),
        lax.psum_scatter(
            terms[6].astype(jnp.bfloat16), "dp", scatter_dimension=0, tiled=True
        ).astype(jnp.float32),
        lax.psum_scatter(
            terms[7].astype(jnp.bfloat16), "dp", scatter_dimension=0, tiled=True
        ).astype(jnp.float32),
        lax.psum_scatter(
            terms[8].astype(jnp.bfloat16), "dp", scatter_dimension=0, tiled=True
        ).astype(jnp.float32),
        lax.psum_scatter(
            terms[9].astype(jnp.bfloat16), "dp", scatter_dimension=0, tiled=True
        ).astype(jnp.float32),
        lax.psum_scatter(
            terms[10].astype(jnp.bfloat16), "dp", scatter_dimension=0, tiled=True
        ).astype(jnp.float32),
        lax.psum_scatter(
            terms[11].astype(jnp.bfloat16), "dp", scatter_dimension=0, tiled=True
        ).astype(jnp.float32),
    )
    shards = (
        lax.psum(data_shards[0].astype(jnp.bfloat16), "seq").astype(jnp.float32),
        lax.psum(data_shards[1].astype(jnp.bfloat16), "seq").astype(jnp.float32),
        lax.psum(data_shards[2].astype(jnp.bfloat16), "seq").astype(jnp.float32),
        lax.psum(data_shards[3].astype(jnp.bfloat16), "seq").astype(jnp.float32),
        lax.psum(data_shards[4].astype(jnp.bfloat16), "seq").astype(jnp.float32),
        lax.psum(data_shards[5].astype(jnp.bfloat16), "seq").astype(jnp.float32),
        lax.psum(data_shards[6].astype(jnp.bfloat16), "seq").astype(jnp.float32),
        lax.psum(data_shards[7].astype(jnp.bfloat16), "seq").astype(jnp.float32),
        lax.psum(data_shards[8].astype(jnp.bfloat16), "seq").astype(jnp.float32),
        lax.psum(data_shards[9].astype(jnp.bfloat16), "seq").astype(jnp.float32),
        lax.psum(data_shards[10].astype(jnp.bfloat16), "seq").astype(jnp.float32),
        lax.psum(data_shards[11].astype(jnp.bfloat16), "seq").astype(jnp.float32),
    )
    limit = clip_threshold.astype(jnp.float32)
    root_factor = jnp.sqrt(limit / jnp.maximum(head_max, limit))
    head_cols = jnp.repeat(root_factor, HD)
    weight_scale = jnp.concatenate([head_cols, head_cols, jnp.ones((model_width,), jnp.float32)])
    clipped_weight = (qkv_weight.astype(jnp.float32) * weight_scale[None, :]).astype(jnp.bfloat16)
    bias_count = qv_bias.shape[0]
    bias_scale = jnp.concatenate([head_cols, jnp.ones((model_width,), jnp.float32)])
    shard_scale = lax.dynamic_slice_in_dim(
        bias_scale, lax.axis_index("dp") * bias_count, bias_count
    )
    clipped_bias = (qv_bias.astype(jnp.float32) * shard_scale).astype(jnp.bfloat16)
    return (
        block_out,
        tokens_grad,
        shards[0],
        shards[1],
        shards[2],
        shards[3],
        shards[4],
        shards[5],
        shards[6],
        shards[7],
        shards[8],
        shards[9],
        shards[10],
        shards[11],
        clipped_weight,
        clipped_bias,
        head_max,
    )


MESH = pl.DeviceIdType.MESH
BF = jnp.bfloat16
F32 = jnp.float32
SMALL = (128, 128, 256, 128, 128, 128, 512, 128)


def flip(d, m):
    y = lax.rem(lax.div(d, 4) + m // 4, 2)
    x = lax.rem(lax.rem(lax.div(d, 2), 2) + (m // 2) % 2, 2)
    k = lax.rem(lax.rem(d, 2) + m % 2, 2)
    return 4 * y + 2 * x + k


def flip_traced(d, m):
    y = lax.rem(lax.div(d, 4) + lax.div(m, 4), 2)
    x = lax.rem(lax.rem(lax.div(d, 2), 2) + lax.rem(lax.div(m, 2), 2), 2)
    k = lax.rem(lax.rem(d, 2) + lax.rem(m, 2), 2)
    return 4 * y + 2 * x + k


def dot_nn(a, b):
    return lax.dot_general(a, b, (((1,), (0,)), ((), ())), preferred_element_type=F32)


def dot_nt(a, b):
    return lax.dot_general(a, b, (((1,), (1,)), ((), ())), preferred_element_type=F32)


def dot_tn(a, b):
    return lax.dot_general(a, b, (((0,), (0,)), ((), ())), preferred_element_type=F32)


def rows_of(block, size, start=0, count=None):
    count = size if count is None else count
    step = math.gcd(size, start) if start else size
    return pl.ds(pl.multiple_of(block * size + start, step), count)


def normalized(v):
    center = jnp.mean(v, axis=-1, keepdims=True)
    centered = v - center
    spread = jnp.mean(centered * centered, axis=-1, keepdims=True)
    scale = lax.rsqrt(spread + epsilon)
    return centered * scale, scale


def half_masks():
    lane = lax.broadcasted_iota(jnp.int32, (1, 2 * HD), 1)
    low = jnp.where(lane < HD, 1.0, 0.0)
    return low.astype(BF), (1.0 - low).astype(BF), lane < HD


def add_rows(target, other, rows, step=32):
    @pl.loop(0, rows // step)
    def _(i):
        r = rows_of(i, step)
        target[r, :] = target[r, :] + other[r, :]


def front_kernel(
    tok_in, grad_in, wq_in, wo_in, wu_in, wd_in, small_in, flag_in,
    tok_h, h1_h, qkv_h, gx_h, go_h, ga_h, h2_h, gu_h, att_h, atto_h, first_h, fx_h, fy_h,
    wq_h, wo_h, wu_h, wd_h, vec_o, dbup_o, bup_o, top_o, mask_o,
    wq, wo, wu, wd, tok, grad, h1, qkv, att, x1, h2, dh, fil, small, col, slp, ust, bias,
    dst, first, mine, flags,
    own_s, own_r, rel_s, rel_r, fwd_s, fwd_r, tok_s, tok_r, att_s, att_r, fil_s, fil_r,
    sm_s, sm_r, dn_s, dn_r, fs_s, fs_r, loc, stg, hout, wsv, fin,
):
    d, s = lax.axis_index("dp"), lax.axis_index("seq")
    images, part, width = tok_in.shape
    length = images * part
    pair_count = width // (2 * HD)
    weights = ((wq_in, wq), (wo_in, wo), (wu_in, wu), (wd_in, wd))
    sib, xn, yn, dn = flip(d, 1), flip(d, 2), flip(d, 4), flip(d, 6)

    barrier = pltpu.get_barrier_semaphore()
    for m in range(1, 8):
        pl.semaphore_signal(barrier, inc=1, device_id=(flip(d, m), s), device_id_type=MESH)
    for j in range(1, images):
        pl.semaphore_signal(
            barrier, inc=1, device_id=(d, lax.rem(s + j, images)), device_id_type=MESH
        )
    pl.semaphore_wait(barrier, 7 + images - 1)

    def send(src, dst, ss, rs, to_dp, to_seq):
        return pltpu.make_async_remote_copy(
            src_ref=src, dst_ref=dst, send_sem=ss, recv_sem=rs,
            device_id=(to_dp, to_seq), device_id_type=MESH,
        )

    def exchange(src, dst, ss, rs, rows):
        copies = []
        for j in range(1, images):
            to = lax.rem(s + j, images)
            copies.append(send(src.at[to], dst.at[rows], ss.at[j - 1], rs.at[j - 1], d, to))
        return copies

    my_rows = rows_of(s, part)
    sm_copies = [
        send(mine, small.at[d], sm_s.at[m - 1], sm_r.at[m - 1], flip(d, m), s)
        for m in range(1, 8)
    ]
    fil_copies = exchange(flags, fil, fil_s, fil_r, s)
    tok_copies = exchange(tok_in, tok, tok_s.at[0], tok_r.at[0], my_rows)
    grad_copies = exchange(grad_in, grad, tok_s.at[1], tok_r.at[1], my_rows)

    def own(w, which=range(5)):
        src, dst = weights[w]
        size = src.shape[0]
        half = size // 2
        def piece(way, to, h):
            return send(
                src.at[pl.ds(h * half, half)], dst.at[rows_of(d, size, h * half, half)],
                own_s.at[w, way, h], own_r.at[w, way, h], to, s,
            )
        return [
            piece(0, xn, 0), piece(1, yn, 1), piece(0, xn, 1), piece(1, yn, 0),
            send(src, dst.at[rows_of(d, size)], own_s.at[w, 2, 0], own_r.at[w, 2, 0], sib, s),
        ]

    def relays(w):
        dst = weights[w][1]
        size = weights[w][0].shape[0]
        half = size // 2
        lower, upper = rows_of(xn, size, 0, half), rows_of(yn, size, half, half)
        return [
            send(dst.at[lower], dst.at[lower], rel_s.at[w, 0], rel_r.at[w, 0], yn, s),
            send(dst.at[upper], dst.at[upper], rel_s.at[w, 1], rel_r.at[w, 1], xn, s),
        ]

    def forwards(w):
        dst = weights[w][1]
        size = weights[w][0].shape[0]
        return [
            send(dst.at[rows_of(b, size)], dst.at[rows_of(b, size)],
                 fwd_s.at[w, i], fwd_r.at[w, i], sib, s)
            for i, b in enumerate((xn, yn, dn))
        ]

    def start_own(w):
        for copy in own(w):
            copy.start()

    def on_halves(w):
        held, relay = own(w), relays(w)
        held[0].wait_recv()
        relay[0].start()
        held[1].wait_recv()
        relay[1].start()

    def on_rest(w):
        held, forward = own(w), forwards(w)
        held[2].wait_recv()
        forward[0].start()
        held[3].wait_recv()
        forward[1].start()

    def on_first(w):
        on_halves(w)
        on_rest(w)

    def on_diag(w):
        relay = relays(w)
        relay[0].wait_recv()
        relay[1].wait_recv()
        forwards(w)[2].start()

    def on_sib(w):
        own(w)[4].wait_recv()
        for copy in forwards(w):
            copy.wait_recv()

    def drain(w):
        for copy in own(w) + relays(w) + forwards(w):
            copy.wait_send()

    def keep_own(w):
        src, dst = weights[w]
        return pltpu.make_async_copy(src, dst.at[rows_of(d, src.shape[0])], loc.at[w])

    for copy in tok_copies:
        copy.start()
    start_own(0)
    mine[...] = small_in[...].astype(F32)
    flags[...] = jnp.zeros_like(flags)
    held = jnp.where(flag_in[...] > 0, 1.0, 0.0)
    for place in range(images):
        @pl.when(s == place)
        def _():
            for image in range(images):
                flags[image, :, place * part : (place + 1) * part] = jnp.broadcast_to(
                    held[image : image + 1, :], (8, part)
                )
    for copy in sm_copies + fil_copies:
        copy.start()
    start_own(1)
    locals_ = [keep_own(w) for w in range(4)]
    locals_ += [
        pltpu.make_async_copy(tok_in.at[s], tok.at[my_rows], loc.at[4]),
        pltpu.make_async_copy(grad_in.at[s], grad.at[my_rows], loc.at[5]),
        pltpu.make_async_copy(flags.at[s], fil.at[s], loc.at[6]),
        pltpu.make_async_copy(mine, small.at[d], loc.at[7]),
    ]
    for copy in locals_:
        copy.start()

    on_first(0)
    start_own(2)

    for copy in sm_copies + fil_copies:
        copy.wait_recv()
    for copy in locals_:
        copy.wait()

    starts = [sum(SMALL[:i]) for i in range(len(SMALL))]

    def vector(i, first=0, last=8):
        return jnp.concatenate(
            [small[b, :, starts[i] : starts[i] + SMALL[i]] for b in range(first, last)], axis=1
        )

    mask = fil[0] + fil[1] + fil[2] + fil[3]
    mask_o[...] = mask
    col[...] = jnp.transpose(mask)

    for copy in tok_copies:
        copy.wait_recv()
    for copy in grad_copies:
        copy.start()

    block = 128
    gain1, shift1 = vector(0), vector(1)

    @pl.loop(0, length // block)
    def _(i):
        r = rows_of(i, block)
        xh, _ = normalized(tok[r, :].astype(F32))
        h1[r, :] = (xh * gain1 + shift1).astype(BF)

    on_diag(0)
    on_first(1)
    on_sib(0)

    tile = 512
    qkv_bias = jnp.concatenate(
        [vector(2, 0, 4), jnp.zeros((1, width), F32), vector(2, 4, 8)], axis=1
    )
    bias[pl.ds(0, 1), :] = qkv_bias[:, :width]
    bias[pl.ds(1, 1), :] = qkv_bias[:, width : 2 * width]
    bias[pl.ds(2, 1), :] = qkv_bias[:, 2 * width :]

    for third in range(3):
        @pl.loop(0, width // tile)
        def _(n):
            c = pl.ds(pl.multiple_of(n * tile, tile), tile)
            cw = pl.ds(pl.multiple_of(third * width + n * tile, tile), tile)
            value = dot_nn(h1[...], wq[:, cw]) + bias[pl.ds(third, 1), c]
            qkv[:, cw] = value.astype(BF)

    saves = [
        pltpu.make_async_copy(tok, tok_h, hout.at[0]),
        pltpu.make_async_copy(h1, h1_h, hout.at[1]),
        pltpu.make_async_copy(qkv, qkv_h, hout.at[2]),
        pltpu.make_async_copy(wq, wq_h, hout.at[3]),
        pltpu.make_async_copy(wo, wo_h, hout.at[4]),
        pltpu.make_async_copy(wu, wu_h, hout.at[5]),
        None,
        pltpu.make_async_copy(att, att_h, hout.at[7]),
        pltpu.make_async_copy(first, first_h, hout.at[8]),
        pltpu.make_async_copy(h2, h2_h, hout.at[9]),
    ]
    for copy in saves[:4]:
        copy.start()

    low, high, low_lane = half_masks()
    pad = (mask[0:1, :] - 1.0) * 1e30
    pad2 = jnp.concatenate([pad, pad], axis=1)
    chunk = length // 2

    def attend(p, carry):
        c = pl.ds(pl.multiple_of(p * 2 * HD, 2 * HD), 2 * HD)
        ck = pl.ds(pl.multiple_of(width + p * 2 * HD, 2 * HD), 2 * HD)
        cv = pl.ds(pl.multiple_of(2 * width + p * 2 * HD, 2 * HD), 2 * HD)
        k, v = qkv[:, ck], qkv[:, cv]
        k2 = jnp.concatenate([k * low, k * high], axis=0)
        v2 = jnp.concatenate([v * low, v * high], axis=0)
        best = [jnp.full((1, 1), very_negative, F32)] * 2
        for j in range(2):
            r = pl.ds(j * chunk, chunk)
            q = qkv[r, c] * jnp.asarray(HD ** (-0.5), BF)
            scores = dot_nt(q, k2) + pad2
            probs = []
            for side in range(2):
                part_s = scores[:, side * length : (side + 1) * length]
                peak = jnp.max(part_s, axis=1, keepdims=True)
                e = jnp.exp(part_s - peak)
                total = jnp.sum(e, axis=1, keepdims=True)
                probs.append((e * (1.0 / total)).astype(BF))
                held = jnp.where(col[r, 0:1] > 0.5, peak, very_negative)
                best[side] = jnp.maximum(best[side], jnp.max(held, axis=0, keepdims=True))
            att[r, c] = dot_nn(jnp.concatenate(probs, axis=1), v2).astype(BF)
        top_o[pl.ds(p, 1), :] = jnp.where(
            low_lane, jnp.broadcast_to(best[0], (1, 2 * HD)), jnp.broadcast_to(best[1], (1, 2 * HD))
        )
        return carry

    def give_back(part_of):
        wide = width // 2
        cols = pl.ds(part_of * wide, wide)
        copies = []
        for j in range(1, images):
            to = lax.rem(s + j, images)
            copies.append(
                send(att.at[rows_of(to, part), cols], atto_h.at[s, :, cols],
                     att_s.at[part_of, j - 1], att_r.at[part_of, j - 1], d, to)
            )
        return copies

    lax.fori_loop(0, pair_count // 2, attend, 0)
    back_copies = give_back(0)
    for copy in back_copies:
        copy.start()
    on_first(2)
    start_own(3)
    lax.fori_loop(pair_count // 2, pair_count, attend, 0)
    back_copies += give_back(1)
    for copy in back_copies[images - 1 :]:
        copy.start()
    keep_att = pltpu.make_async_copy(att.at[my_rows], atto_h.at[s], hout.at[10])
    keep_att.start()
    saves[7].start()
    on_diag(1)
    on_sib(1)
    saves[4].start()

    gain2, shift2, b_out, b_down = vector(4), vector(5), vector(3), vector(7)

    @pl.loop(0, length // block)
    def _(i):
        r = rows_of(i, block)
        mid = tok[r, :].astype(F32) + dot_nn(att[r, :], wo[...]) + b_out
        x1[r, :] = mid
        xh, _ = normalized(mid)
        h2[r, :] = (xh * gain2 + shift2).astype(BF)

    saves[9].start()
    bup_o[...] = vector(6)
    dh[...] = jnp.zeros_like(dh)
    for copy in grad_copies:
        copy.wait_recv()

    def add_grad(i, acc):
        return acc + jnp.sum(grad[rows_of(i, block), :].astype(F32), axis=0, keepdims=True)

    grad_sum = lax.fori_loop(0, length // block, add_grad, jnp.zeros((1, width), F32))

    on_diag(2)
    on_sib(2)
    saves[5].start()

    ff_block = wd_in.shape[0]

    half_rows = ff_block // 2

    def activation(b):
        cols = pl.ds(pl.multiple_of(b * ff_block, ff_block), ff_block)
        u = dot_nn(h2[...], wu[:, cols]) + bup_o[:, cols]
        phi = 0.5 * (1.0 + lax.erf(u * (0.5**0.5)))
        slope = phi + u * (jnp.exp(-0.5 * u * u) * (1.0 / math.sqrt(2.0 * math.pi)))
        slp[:, cols] = slope.astype(BF)
        return (u * phi).astype(BF)

    def down_send(mi):
        return send(dst.at[1], first.at[mi], dn_s.at[mi], dn_r.at[mi], sib, s)

    def down(j, carry):
        m = lax.rem(6 * (j + 1), 8)
        mi = lax.div(m, 2)

        @pl.when(j > 0)
        def _():
            down_send(lax.div(lax.rem(6 * j, 8), 2)).wait_send()

        @pl.when(j == 2)
        def _():
            on_halves(3)

        for slot in (1, 0):
            a = activation(flip_traced(d, m + slot))
            dst[slot] = dot_tn(a, grad[...]).astype(BF)
            if slot:
                down_send(mi).start()
        down_send(mi).wait_recv()
        add_rows(first.at[mi], dst.at[0], ff_block)
        return carry

    lax.fori_loop(0, 4, down, 0)
    down_send(0).wait_send()
    saves[8].start()

    def first_stage(n):
        quarter = half_rows // 2
        lower, upper = pl.ds(0, quarter), pl.ds(quarter, quarter)
        m, rows, to_ref, to = (
            (6, lower, fx_h.at[1], xn), (6, upper, fy_h.at[1], yn),
            (2, lower, fx_h.at[0], xn), (4, upper, fy_h.at[0], yn),
        )[n]
        return send(first.at[m // 2, rows], to_ref, fs_s.at[n], fs_r.at[n], to, s)

    def stage_copy(slot, b):
        cols = pl.ds(pl.multiple_of(b * ff_block, ff_block), ff_block)
        return pltpu.make_async_copy(ust.at[slot], gu_h.at[:, cols], stg.at[slot])

    def save_down(i):
        rows = rows_of(flip_traced(d, i), ff_block)
        return pltpu.make_async_copy(wd.at[rows], wd_h.at[rows], wsv.at[i])

    def mlp(i, carry):
        b = flip_traced(d, i)
        slot = lax.rem(i, 2)

        @pl.when(i == 1)
        def _():
            own(3)[4].wait_recv()

        @pl.when(i == 2)
        def _():
            on_rest(3)
            for n in range(4):
                first_stage(n).start()

        for at, which in ((3, 0), (5, 1), (7, 2)):
            @pl.when(i == at)
            def _():
                forwards(3)[which].wait_recv()

        @pl.when(i == 6)
        def _():
            on_diag(3)

        cols = pl.ds(pl.multiple_of(b * ff_block, ff_block), ff_block)
        rows = rows_of(b, ff_block)
        save_down(i).start()
        gu = (dot_nt(grad[...], wd[rows, :]) * slp[:, cols].astype(F32)).astype(BF)
        dh[...] += dot_nt(gu, wu[:, cols])

        @pl.when(i >= 2)
        def _():
            stage_copy(slot, b).wait()

        dbup_o[:, cols] = jnp.sum(gu.astype(F32), axis=0, keepdims=True)
        ust[slot] = gu
        stage_copy(slot, b).start()
        return carry

    lax.fori_loop(0, 8, mlp, 0)
    for n in (0, 9):
        saves[n].wait()

    zero = jnp.zeros((1, width), F32)

    def finals(i):
        r = rows_of(i, block)
        return [
            pltpu.make_async_copy(dh.at[r], gx_h.at[r], fin.at[0, i]),
            pltpu.make_async_copy(tok.at[r], go_h.at[r], fin.at[1, i]),
            pltpu.make_async_copy(h2.at[r], ga_h.at[r], fin.at[2, i]),
        ]

    def norm_back(i, acc):
        r = rows_of(i, block)
        g = dh[r, :]
        xh, scale = normalized(x1[r, :])
        gg = g * gain2
        inner = gg - jnp.mean(gg, axis=1, keepdims=True)
        inner = inner - xh * jnp.mean(gg * xh, axis=1, keepdims=True)
        total = grad[r, :].astype(F32) + scale * inner
        dh[r, :] = total
        low_total = total.astype(BF)
        h2[r, :] = low_total
        tok[r, :] = dot_nt(low_total, wo[...]).astype(BF)
        for copy in finals(i):
            copy.start()
        return (
            acc[0] + jnp.sum(g * xh, axis=0, keepdims=True),
            acc[1] + jnp.sum(g, axis=0, keepdims=True),
            acc[2] + jnp.sum(low_total.astype(F32), axis=0, keepdims=True),
        )

    sums = lax.fori_loop(0, length // block, norm_back, (zero, zero, zero))
    for n, row in enumerate((sums[0], sums[1], sums[2], grad_sum)):
        vec_o[pl.ds(n, 1), :] = row
    for n, row in enumerate((gain1, gain2, shift2, b_out, b_down)):
        vec_o[pl.ds(8 + n, 1), :] = row
    for slot in range(2):
        stage_copy(slot, d).wait()
    for n in range(4):
        first_stage(n).wait()
    for n in (1, 2, 3, 4, 5, 7, 8):
        saves[n].wait()
    for n in range(8):
        save_down(n).wait()
    keep_att.wait()
    for w in range(4):
        drain(w)
    for copy in sm_copies + fil_copies + tok_copies + grad_copies + back_copies:
        copy.wait_send()
    for copy in back_copies:
        copy.wait_recv()
    for i in range(length // block):
        for copy in finals(i):
            copy.wait()


def front(tokens, out_grad, filled_rows, qkv_weight, out_weight, up_weight, down_weight, small):
    images, part, width = tokens.shape
    length = images * part
    shards = lax.axis_size("dp")
    ff = up_weight.shape[1]
    wide = qkv_weight.shape[1]
    shape = jax.ShapeDtypeStruct
    any_spec = pl.BlockSpec(memory_space=pl.ANY)
    vmem_spec = pl.BlockSpec(memory_space=pltpu.VMEM)
    dma = pltpu.SemaphoreType.DMA
    vm = pltpu.VMEM
    return pl.pallas_call(
        front_kernel,
        name="front",
        out_shape=(
            shape((length, width), BF),
            shape((length, width), BF),
            shape((length, wide), BF),
            shape((length, width), F32),
            shape((length, width), BF),
            shape((length, width), BF),
            shape((length, width), BF),
            shape((length, ff), BF),
            shape((length, width), BF),
            shape((images, part, width), BF),
            shape((4, ff // 8, width), BF),
            shape((2, ff // 32, width), BF),
            shape((2, ff // 32, width), BF),
            shape((width, wide), BF),
            shape((width, width), BF),
            shape((width, ff), BF),
            shape((ff, width), BF),
            shape((16, width), F32),
            shape((1, ff), F32),
            shape((1, ff), F32),
            shape((8, 2 * HD), F32),
            shape((8, length), F32),
        ),
        in_specs=[any_spec] * 6 + [vmem_spec] * 2,
        out_specs=[any_spec] * 17 + [vmem_spec] * 5,
        scratch_shapes=[
            vm((width, wide), BF), vm((width, width), BF), vm((width, ff), BF), vm((ff, width), BF),
            vm((length, width), BF), vm((length, width), BF), vm((length, width), BF),
            vm((length, wide), BF), vm((length, width), BF), vm((length, width), F32),
            vm((length, width), BF), vm((length, width), F32),
            vm((images, 8, length), F32), vm((shards, 1, sum(SMALL)), F32),
            vm((length, 8), F32), vm((length, ff), BF),
            vm((2, length, down_weight.shape[0]), BF), vm((8, width), F32),
            vm((2, ff // 8, width), BF), vm((4, ff // 8, width), BF), vm((1, sum(SMALL)), F32),
            vm((images, 8, length), F32),
            dma((4, 3, 2)), dma((4, 3, 2)), dma((4, 2)), dma((4, 2)), dma((4, 3)), dma((4, 3)),
            dma((2, images - 1)), dma((2, images - 1)), dma((2, images - 1)), dma((2, images - 1)),
            dma((images - 1,)), dma((images - 1,)), dma((7,)), dma((7,)),
            dma((4,)), dma((4,)), dma((4,)), dma((4,)), dma((8,)), dma((2,)), dma((14,)), dma((8,)),
            dma((3, length // 128)),
        ],
        compiler_params=pltpu.CompilerParams(
            collective_id=0, has_side_effects=True, vmem_limit_bytes=63 << 20
        ),
    )(tokens, out_grad, qkv_weight, out_weight, up_weight, down_weight, small, filled_rows)


def back_kernel(*refs):
    (
        qkv_in, go_in, h1_in, gx_in, tok_in, ga_in, h2_in, gu_in, att_in, atto_in, first_in,
        fx_in, fy_in, mine_in, wq_in, wo_in, wu_in, wd_in,
        mask_in, vec_in, dbup_in, bup_in, top_in,
        out_h, tg_h, dwq_h, dwo_h, dwu_h, dwd_h, small_o, top_o,
        qkv, go, ht, gbuf, buf, dh, wqg, pq, gp, colm, dst, own_u, ust, stg_o, ast, gxs,
        psm, rsm, zsm, rtop, ztop,
    ) = refs[:52]
    refs = refs[52:]
    count = 11
    recv0, recv1x, recv1y, recv2, za, zb = [refs[i * count : (i + 1) * count] for i in range(6)]
    (
        s0_s, s0_r, u0_s, u0_r, s1_s, s1_r, s2_s, s2_r, z_s, z_r, ex_s, ex_r, sm_s, sm_r,
        zs_s, zs_r, tp_s, tp_r, tz_s, tz_r, asem, wsem, osem, lsem, gsem,
    ) = refs[6 * count :]
    d, s = lax.axis_index("dp"), lax.axis_index("seq")
    length, width = go.shape
    images, part = mine_in.shape[0], mine_in.shape[1]
    sib, xn, yn = flip(d, 1), flip(d, 2), flip(d, 4)
    group_cols = gp.shape[1] // 3
    groups = width // group_cols
    ff_block = dst.shape[1]
    shard = width // 8
    block = 128
    tile = 512

    barrier = pltpu.get_barrier_semaphore()
    for m in range(1, 8):
        pl.semaphore_signal(barrier, inc=1, device_id=(flip(d, m), s), device_id_type=MESH)
    for j in range(1, images):
        pl.semaphore_signal(
            barrier, inc=1, device_id=(d, lax.rem(s + j, images)), device_id_type=MESH
        )

    def load(src, dst_ref, n):
        return pltpu.make_async_copy(src, dst_ref, lsem.at[n])

    def send(src, dst_ref, ss, rs, to_dp, to_seq):
        return pltpu.make_async_remote_copy(
            src_ref=src, dst_ref=dst_ref, send_sem=ss, recv_sem=rs,
            device_id=(to_dp, to_seq), device_id_type=MESH,
        )

    down_rows, up_cols = recv0[0].shape[1], recv0[2].shape[2]
    size = [down_rows] * 2 + [shard] * 9

    def s1(i, n):
        half = size[i] // 2
        lower, upper = pl.ds(0, half), pl.ds(half, half)
        m, part_rows, to_ref, to = (
            (6, lower, recv1x[i].at[1], xn), (6, upper, recv1y[i].at[1], yn),
            (2, lower, recv1x[i].at[0], xn), (4, upper, recv1y[i].at[0], yn),
        )[n]
        return send(recv0[i].at[m // 2, part_rows], to_ref, s1_s.at[i, n], s1_r.at[i, n], to, s)

    def s2(i, n):
        half = size[i] // 2
        if n == 0:
            return send(recv1x[i].at[1], recv2[i].at[pl.ds(0, half)],
                        s2_s.at[i, 0], s2_r.at[i, 0], yn, s)
        return send(recv1y[i].at[1], recv2[i].at[pl.ds(half, half)],
                    s2_s.at[i, 1], s2_r.at[i, 1], xn, s)

    mate = s + 1 - 2 * lax.rem(s, 2)
    across = 3 - s
    is_mid = jnp.logical_or(s == 1, s == 2)
    is_end = jnp.logical_or(s == 0, s == 3)

    def to_mid(i):
        return send(recv2[i], za[i], z_s.at[i, 0], z_r.at[i, 0], d, mate)

    def cross(i):
        return send(za[i], zb[i], z_s.at[i, 1], z_r.at[i, 1], d, across)

    def to_end(i):
        return send(zb[i], za[i], z_s.at[i, 2], z_r.at[i, 2], d, mate)

    def outputs(i, src):
        if i < 2:
            return [pltpu.make_async_copy(src, dwd_h.at[pl.ds(i * down_rows, down_rows)],
                                          osem.at[i, 0])]
        if i < 6:
            return [pltpu.make_async_copy(src, dwu_h.at[:, pl.ds((i - 2) * up_cols, up_cols)],
                                          osem.at[i, 0])]
        if i == 6:
            return [pltpu.make_async_copy(src, dwo_h, osem.at[i, 0])]
        return [
            pltpu.make_async_copy(
                src.at[:, pl.ds(third * group_cols, group_cols)],
                dwq_h.at[:, pl.ds(third * width + (i - 7) * group_cols, group_cols)],
                osem.at[i, third],
            )
            for third in range(3)
        ]

    def step1(i):
        for n in range(4):
            s1(i, n).start()

    def arrived(i, n):
        if i:
            s1(i, n).wait_recv()
        elif n == 0:
            for copy in ready_first:
                copy.wait()

    def step2(i):
        half = size[i] // 2
        arrived(i, 0)
        add_rows(recv1x[i].at[1], recv0[i].at[2, pl.ds(0, half)], half)
        s2(i, 0).start()
        arrived(i, 1)
        add_rows(recv1y[i].at[1], recv0[i].at[1, pl.ds(half, half)], half)
        s2(i, 1).start()
        arrived(i, 2)
        add_rows(recv1x[i].at[0], recv0[i].at[0, pl.ds(0, half)], half)
        arrived(i, 3)
        add_rows(recv1y[i].at[0], recv0[i].at[0, pl.ds(half, half)], half)

    def step3(i):
        half = size[i] // 2
        s2(i, 0).wait_recv()
        add_rows(recv2[i].at[pl.ds(0, half)], recv1x[i].at[0], half)
        s2(i, 1).wait_recv()
        add_rows(recv2[i].at[pl.ds(half, half)], recv1y[i].at[0], half)

        @pl.when(is_end)
        def _():
            to_mid(i).start()

    def step4(i):
        @pl.when(is_mid)
        def _():
            to_mid(i).wait_recv()
            add_rows(za[i], recv2[i], size[i])
            cross(i).start()

    def step5(i):
        @pl.when(is_mid)
        def _():
            cross(i).wait_recv()
            add_rows(zb[i], za[i], size[i])
            to_end(i).start()
            for copy in outputs(i, zb[i]):
                copy.start()

    def step6(i):
        @pl.when(is_end)
        def _():
            to_end(i).wait_recv()
            for copy in outputs(i, za[i]):
                copy.start()

    def drain(i):
        for n in range(4 if i else 0):
            s1(i, n).wait_send()
        for n in range(2):
            s2(i, n).wait_send()

        @pl.when(is_end)
        def _():
            to_mid(i).wait_send()
            for copy in outputs(i, za[i]):
                copy.wait()

        @pl.when(is_mid)
        def _():
            cross(i).wait_send()
            to_end(i).wait_send()
            for copy in outputs(i, zb[i]):
                copy.wait()

    def cols_of(b, n=ff_block):
        return pl.ds(pl.multiple_of(b * n, n), n)

    def gu_load(slot, b):
        return pltpu.make_async_copy(gu_in.at[:, cols_of(b)], ast.at[slot], asem.at[slot])

    lower_rows, upper_rows = pl.ds(0, down_rows), pl.ds(down_rows, down_rows)
    ready_first = [
        load(fx_in, recv1x[0], 11 + 2 * images), load(fy_in, recv1y[0], 12 + 2 * images),
        load(first_in.at[:, lower_rows], recv0[0], 13 + 2 * images),
    ]
    ready_second = load(first_in.at[:, upper_rows], recv0[1], 0)
    ready_second.start()
    for copy in ready_first:
        copy.start()
    load_h2 = load(h2_in, buf, 1)
    load_h2.start()
    load_qkv = load(qkv_in, qkv, 2)
    load_qkv.start()
    load_go = load(go_in, go, 3)
    load_go.start()

    def weight_group(g):
        return [
            pltpu.make_async_copy(
                wq_in.at[:, pl.ds(third * width + g * group_cols, group_cols)],
                wqg.at[g % 2, :, pl.ds(third * group_cols, group_cols)],
                wsem.at[g % 2, third],
            )
            for third in range(3)
        ]

    for copy in weight_group(0):
        copy.start()
    pl.semaphore_wait(barrier, 7 + images - 1)
    top_copies = [
        send(top_in, rtop.at[d], tp_s.at[m - 1], tp_r.at[m - 1], flip(d, m), s)
        for m in range(1, 8)
    ]
    for copy in top_copies:
        copy.start()
    gu_load(0, 0).start()
    load_ga = load(ga_in, gbuf, 4)
    load_ga.start()
    dh[...] = jnp.zeros_like(dh)
    colm[...] = jnp.transpose((mask_in[...] - 1.0) * 1e30)
    ready_second.wait()

    def turned(src):
        @pl.loop(0, 8)
        def _(m):
            at = pl.ds(pl.multiple_of(flip_traced(d, m) * shard, shard), shard)
            ht[rows_of(m, shard), :] = jnp.transpose(src[:, at])

    load_att = load(att_in, buf, 5)
    load_h1 = load(h1_in, buf, 6)
    load_tok = load(tok_in, gbuf, 7)

    def turn1():
        load_h2.wait()
        turned(buf)
        load_att.start()

    def split_store(value, keep, give, cols_keep, cols_give):
        for m in range(8):
            piece = value[m * shard : (m + 1) * shard].astype(BF)
            if m % 2 == 0:
                keep[m // 2, :, cols_keep] = piece
            else:
                give[m // 2, :, cols_give] = piece

    blocks = up_cols // tile

    def up_send(i, n):
        return send(ust.at[n], recv0[2 + i].at[:, :, cols_of(n, tile)],
                    u0_s.at[i, n], u0_r.at[i, n], sib, s)

    def up(i):
        if i:
            for n in range(blocks):
                up_send(i - 1, n).wait_send()

        def body(n, carry):
            b = i * blocks + n
            slot = lax.rem(b, 2)
            gu_load(slot, b).wait()

            @pl.when(b + 1 < 4 * blocks)
            def _():
                gu_load(1 - slot, b + 1).start()

            value = dot_nn(ht[...], ast[slot])
            split_store(value, own_u.at[i % 2], ust.at[n], cols_of(n, tile), slice(None))
            up_send(i, n).start()
            return carry

        lax.fori_loop(0, blocks, body, 0)

    def add_up(i):
        for n in range(blocks):
            up_send(i, n).wait_recv()
        for m in (6, 2, 4, 0):
            add_rows(recv0[2 + i].at[m // 2], own_u.at[i % 2, m // 2], shard)

    def out_send(n):
        return send(ust.at[n], recv0[6].at[:, :, pl.ds(n * tile, tile)],
                    s0_s.at[0, n], s0_r.at[0, n], sib, s)

    def out():
        load_ga.wait()
        load_att.wait()
        turned(buf)
        load_h1.start()
        for n in range(blocks):
            up_send(3, n).wait_send()
        for n in range(width // tile):
            value = dot_nn(ht[...], gbuf[:, pl.ds(n * tile, tile)])
            split_store(value, stg_o, ust.at[n], pl.ds(n * tile, tile), slice(None))
            out_send(n).start()
        load_tok.start()

    def turn3():
        load_h1.wait()
        turned(buf)

    def add_out():
        for n in range(width // tile):
            out_send(n).wait_recv()
            out_send(n).wait_send()
        for m in (6, 2, 4, 0):
            add_rows(recv0[6].at[m // 2], stg_o.at[m // 2], shard)

    low, high, low_lane = half_masks()
    scale = HD ** (-0.5)
    pair = 2 * HD
    per_group = group_cols // pair
    cuts = ((0, 256), (256, length - 256)) if length > 256 else ((0, length),)
    def attention(g):
        if g == 0:
            load_qkv.wait()
            load_go.wait()
        if g + 1 < groups:
            for copy in weight_group(g + 1):
                copy.start()

        def body(n, carry):
            p = g * per_group + n
            c = pl.ds(pl.multiple_of(p * pair, pair), pair)
            ck = pl.ds(pl.multiple_of(width + p * pair, pair), pair)
            cv = pl.ds(pl.multiple_of(2 * width + p * pair, pair), pair)
            k, v = qkv[:, ck], qkv[:, cv]
            k2 = jnp.concatenate([k * low, k * high], axis=0)
            v2 = jnp.concatenate([v * low, v * high], axis=0)
            gk = jnp.zeros((2 * length, pair), F32)
            gv = jnp.zeros((2 * length, pair), F32)
            at_q = pl.ds(pl.multiple_of(n * pair, pair), pair)
            at_k = pl.ds(pl.multiple_of(group_cols + n * pair, pair), pair)
            at_v = pl.ds(pl.multiple_of(2 * group_cols + n * pair, pair), pair)
            for first, wide in cuts:
                r = pl.ds(first, wide)
                q = qkv[r, c] * jnp.asarray(scale, BF)
                g_rows = go[r, c]
                scores = dot_nt(k2, q)
                dprob = dot_nt(v2, g_rows)
                low_probs, low_grads = [], []
                for side in range(2):
                    rows = slice(side * length, (side + 1) * length)
                    part_s = scores[rows] + colm[:, 0:1]
                    e = jnp.exp(part_s - jnp.max(part_s, axis=0, keepdims=True))
                    probs = e * (1.0 / jnp.sum(e, axis=0, keepdims=True))
                    weighted = probs * dprob[rows]
                    inner = jnp.sum(weighted, axis=0, keepdims=True)
                    low_probs.append(probs.astype(BF))
                    low_grads.append((weighted - probs * inner).astype(BF))
                low_p = jnp.concatenate(low_probs, axis=0)
                low_g = jnp.concatenate(low_grads, axis=0)
                gv = gv + dot_nn(low_p, g_rows)
                gk = gk + dot_nn(low_g, q)
                gp[r, at_q] = (dot_tn(low_g, k2) * scale).astype(BF)
            gp[:, at_k] = jnp.where(low_lane, gk[:length], gk[length:]).astype(BF)
            gp[:, at_v] = jnp.where(low_lane, gv[:length], gv[length:]).astype(BF)
            return carry

        lax.fori_loop(0, per_group, body, 0)

    bias_rows = []

    def q_send(g):
        return send(pq.at[g % 2, 1], recv0[7 + g], s0_s.at[1 + g, 0], s0_r.at[1 + g, 0], sib, s)

    def group(g):
        if g >= 2:
            q_send(g - 2).wait_send()
        bias_rows.append(jnp.sum(gp[...].astype(F32), axis=0, keepdims=True))
        for third in range(3):
            cols = pl.ds(third * group_cols, group_cols)
            value = dot_nn(ht[...], gp[:, cols])
            split_store(value, pq.at[g % 2, 0], pq.at[g % 2, 1], cols, cols)
        q_send(g).start()
        for copy in weight_group(g):
            copy.wait()
        for first in range(0, width, tile):
            dh[:, pl.ds(first, tile)] += dot_nt(gp[...], wqg[g % 2, pl.ds(first, tile), :])

    def add_q(g):
        q_send(g).wait_recv()
        for m in (6, 2, 4, 0):
            add_rows(recv0[7 + g].at[m // 2], pq.at[g % 2, 0, m // 2], shard)

    gain1 = vec_in[pl.ds(8, 1), :]
    zero = jnp.zeros((1, width), F32)

    def gx_load(slot, i):
        return pltpu.make_async_copy(gx_in.at[rows_of(i, block)], gxs.at[slot], gsem.at[slot])

    def norm_back(i, acc):
        slot = lax.rem(i, 2)
        gx_load(slot, i).wait()

        @pl.when(i + 1 < length // block)
        def _():
            gx_load(1 - slot, i + 1).start()

        r = rows_of(i, block)
        g = dh[r, :]
        xh, spread = normalized(gbuf[r, :].astype(F32))
        gg = g * gain1
        inner = gg - jnp.mean(gg, axis=1, keepdims=True)
        inner = inner - xh * jnp.mean(gg * xh, axis=1, keepdims=True)
        go[r, :] = (gxs[slot] + spread * inner).astype(BF)
        return (
            acc[0] + jnp.sum(g * xh, axis=0, keepdims=True),
            acc[1] + jnp.sum(g, axis=0, keepdims=True),
        )

    late = {}
    tg_copies = []
    for j in range(1, images):
        to = lax.rem(s + j, images)
        tg_copies.append(
            send(go.at[rows_of(to, part)], tg_h.at[s], ex_s.at[j - 1], ex_r.at[j - 1], d, to)
        )
    own_tg = load(go.at[rows_of(s, part)], tg_h.at[s], 8)

    own_loads = []
    for j in range(images):
        rows = pl.ds(j * part, part)
        own_loads.append(load(mine_in.at[j], qkv.at[rows, pl.ds(0, width)], 9 + j))
        own_loads.append(load(atto_in.at[j], qkv.at[rows, pl.ds(width, width)], 9 + images + j))
    own_loads.append(load(wo_in.at[pl.ds(0, tile)], dst.at[0], 9 + 2 * images))
    own_loads.append(load(wo_in.at[pl.ds(tile, tile)], dst.at[1], 10 + 2 * images))

    def norm1():
        for copy in own_loads:
            copy.start()
        load_tok.wait()
        gx_load(0, 0).start()
        late["norm"] = lax.fori_loop(0, length // block, norm_back, (zero, zero))

    def tg():
        for copy in tg_copies:
            copy.start()
        own_tg.start()

    sm_copies = [
        send(psm.at[flip(d, m)], rsm.at[m - 1], sm_s.at[m - 1], sm_r.at[m - 1], flip(d, m), s)
        for m in range(1, 8)
    ]
    top_z, sm_z = [], []
    for j in range(1, images):
        to = lax.rem(s + j, images)
        top_z.append(send(ztop.at[s], ztop.at[s], tz_s.at[j - 1], tz_r.at[j - 1], d, to))
        sm_z.append(send(zsm.at[s], zsm.at[s], zs_s.at[j - 1], zs_r.at[j - 1], d, to))

    def smalls():
        d_gain1, d_shift1 = late["norm"]
        q_sum = jnp.concatenate([row[:, :group_cols] for row in bias_rows], axis=1)
        v_sum = jnp.concatenate([row[:, 2 * group_cols :] for row in bias_rows], axis=1)
        pieces = (
            d_gain1, d_shift1, jnp.concatenate([q_sum, v_sum], axis=1), vec_in[pl.ds(2, 1), :],
            vec_in[pl.ds(0, 1), :], vec_in[pl.ds(1, 1), :], dbup_in[...], vec_in[pl.ds(3, 1), :],
        )
        for b in range(8):
            psm[b] = jnp.concatenate(
                [piece[:, b * n : (b + 1) * n] for piece, n in zip(pieces, SMALL)], axis=1
            )
        for copy in sm_copies:
            copy.start()
        for copy in top_copies:
            copy.wait_recv()
        rtop[d] = top_in[...]
        best = rtop[0]
        for b in range(1, 8):
            best = jnp.maximum(best, rtop[b])
        ztop[s] = best
        for copy in top_z:
            copy.start()

    def smalls_z():
        for copy in sm_copies:
            copy.wait_recv()
        mine = psm[d]
        for m in range(7):
            mine = mine + rsm[m]
        zsm[s] = mine
        for copy in sm_z:
            copy.start()

    gain2, shift2 = vec_in[pl.ds(9, 1), :], vec_in[pl.ds(10, 1), :]
    b_out, b_down = vec_in[pl.ds(11, 1), :], vec_in[pl.ds(12, 1), :]

    def owners():
        for copy in own_loads:
            copy.wait()

        @pl.loop(0, length // block)
        def _(i):
            r = rows_of(i, block)
            mid = qkv[r, 0:width].astype(F32) + b_out
            mid = mid + dot_nn(qkv[r, width : width + tile], dst[0])
            mid = mid + dot_nn(qkv[r, width + tile : 2 * width], dst[1])
            xh, _ = normalized(mid)
            dh[r, :] = mid + b_down
            qkv[r, 2 * width :] = (xh * gain2 + shift2).astype(BF)

        for copy in ff_loads(0, 0):
            copy.start()

    def ff_loads(slot, b):
        return (
            pltpu.make_async_copy(wu_in.at[:, cols_of(b)], wqg.at[slot, :, pl.ds(0, ff_block)],
                                  wsem.at[slot, 0]),
            pltpu.make_async_copy(wd_in.at[rows_of(b, ff_block)], dst.at[slot],
                                  wsem.at[slot, 1]),
        )

    def feed_block(b, carry):
        slot = lax.rem(b, 2)
        for copy in ff_loads(slot, b):
            copy.wait()

        @pl.when(b < 7)
        def _():
            for copy in ff_loads(1 - slot, b + 1):
                copy.start()

        u = dot_nn(qkv[:, 2 * width :], wqg[slot, :, 0:ff_block]) + bup_in[:, cols_of(b)]
        a = (u * (0.5 * (1.0 + lax.erf(u * (0.5**0.5))))).astype(BF)
        dh[...] += dot_nn(a, dst[slot])
        return carry

    keep_out = load(buf, out_h, 1)

    def feed(n):
        lax.fori_loop(2 * n, 2 * n + 2, feed_block, 0)
        if n == 1:
            smalls_z()
        if n == 3:
            buf[...] = dh[...].astype(BF)
            keep_out.start()

    step2(0)
    turn1()
    step1(1)
    up(0)
    up(1)
    step3(0)
    add_up(0)
    add_up(1)
    step1(2)
    up(2)
    up(3)
    out()
    step2(1)
    step4(0)
    turn3()
    step1(3)
    attention(0)
    step2(2)
    step3(1)
    group(0)
    add_q(0)
    add_up(2)
    step2(3)
    step1(7)
    step1(4)
    attention(1)
    step4(1)
    step3(3)
    step5(0)
    add_out()
    group(1)
    step3(2)
    step2(7)
    step1(6)
    attention(2)
    step4(3)
    step5(1)
    step2(4)
    step3(7)
    group(2)
    step4(2)
    step2(6)
    add_up(3)
    add_q(2)
    add_q(1)
    step5(3)
    step4(7)
    step1(5)
    step6(0)
    step3(6)
    step1(9)
    attention(3)
    step4(6)
    step5(2)
    step3(4)
    step2(5)
    group(3)
    step1(8)
    step5(7)
    step4(4)
    step5(6)
    add_q(3)
    step3(5)
    step2(8)
    step2(9)
    step4(5)
    step1(10)
    step5(4)
    step3(8)
    step4(8)
    step3(9)
    step5(5)
    step6(7)
    step4(9)
    step2(10)
    step5(8)
    step3(10)
    step4(10)
    norm1()
    step6(1)
    tg()
    owners()
    step5(9)
    step6(6)
    feed(0)
    step6(4)
    smalls()
    feed(1)
    feed(2)
    step5(10)
    step6(3)
    step6(8)
    feed(3)
    step6(9)
    step6(10)
    step6(5)
    step6(2)

    for copy in top_z + sm_z:
        copy.wait_recv()
    top_o[...] = jnp.maximum(jnp.maximum(ztop[0], ztop[1]), jnp.maximum(ztop[2], ztop[3]))
    small_o[...] = (zsm[0] + zsm[1]) + (zsm[2] + zsm[3])
    for g in range(groups - 2, groups):
        q_send(g).wait_send()
    for i in range(count):
        drain(i)
    for copy in top_copies + top_z + sm_copies + sm_z + tg_copies:
        copy.wait_send()
    for copy in tg_copies:
        copy.wait_recv()
    own_tg.wait()
    keep_out.wait()


def back(tokens, saved, vecs):
    images, part, width = tokens.shape
    (
        tok, h1, qkv, gx, go, ga, h2, gu, att, atto, first, fx, fy, wq, wo, wu, wd,
    ) = saved
    vec, dbup, bup, tops, mask = vecs
    length = images * part
    wide, ff = wq.shape[1], wu.shape[1]
    shard = width // 8
    shape = jax.ShapeDtypeStruct
    any_spec = pl.BlockSpec(memory_space=pl.ANY)
    vmem_spec = pl.BlockSpec(memory_space=pltpu.VMEM)
    dma = pltpu.SemaphoreType.DMA
    vm = pltpu.VMEM
    group_cols = 256
    groups = width // group_cols
    sizes = [(ff // 16, width)] * 2 + [(shard, ff // 4)] * 4 + [(shard, width)]
    sizes += [(shard, 3 * group_cols)] * groups
    count = len(sizes)
    halves = [vm((2, r // 2, c), BF) for r, c in sizes]
    whole = [vm((r, c), BF) for r, c in sizes]
    z_peers = images - 1
    small = sum(SMALL)
    return pl.pallas_call(
        back_kernel,
        name="back",
        out_shape=(
            shape((length, width), BF),
            shape((images, part, width), BF),
            shape((shard, wide), BF),
            shape((shard, width), BF),
            shape((shard, ff), BF),
            shape((ff // 8, width), BF),
            shape((1, small), F32),
            shape((8, 2 * HD), F32),
        ),
        in_specs=[any_spec] * 18 + [vmem_spec] * 5,
        out_specs=[any_spec] * 6 + [vmem_spec] * 2,
        scratch_shapes=[
            vm((length, wide), BF), vm((length, width), BF), vm((width, length), BF),
            vm((length, width), BF), vm((length, width), BF), vm((length, width), F32),
            vm((2, width, 3 * group_cols), BF), vm((2, 2, 4, shard, 3 * group_cols), BF),
            vm((length, 3 * group_cols), BF), vm((length, 8), F32),
            vm((2, ff // 8, width), BF), vm((2, 4, shard, ff // 4), BF), vm((2, 4, shard, 512), BF),
            vm((4, shard, width), BF), vm((2, length, ff // 8), BF), vm((2, 128, width), F32),
            vm((8, 1, small), F32), vm((7, 1, small), F32),
            vm((images, 1, small), F32), vm((8, 8, 2 * HD), F32), vm((images, 8, 2 * HD), F32),
            *[vm((4, r, c), BF) for r, c in sizes], *halves, *halves, *whole, *whole, *whole,
            dma((5, 2)), dma((5, 2)), dma((4, 2)), dma((4, 2)), dma((count, 4)),
            dma((count, 4)), dma((count, 2)), dma((count, 2)), dma((count, 3)), dma((count, 3)),
            dma((z_peers,)), dma((z_peers,)), dma((7,)), dma((7,)),
            dma((z_peers,)), dma((z_peers,)), dma((7,)), dma((7,)),
            dma((z_peers,)), dma((z_peers,)), dma((2,)), dma((2, 3)), dma((count, 3)),
            dma((14 + 2 * images,)), dma((2,)),
        ],
        compiler_params=pltpu.CompilerParams(
            collective_id=1, has_side_effects=True, vmem_limit_bytes=63 << 20
        ),
    )(
        qkv, go, h1, gx, tok, ga, h2, gu, att, atto, first, fx, fy, tokens, wq, wo, wu, wd,
        mask, vec, dbup, bup, tops,
    )


def finish_kernel(
    limit_in, top_in, out_in, tg_in, dwq_in, dwo_in, dwu_in, dwd_in, w_in, small_in,
    out_o, tg_o, dwq_o, dwo_o, dwu_o, dwd_o, w_o, *small_o
):
    out_o[...] = out_in[...]
    tg_o[...] = tg_in[...]
    for src, to in ((dwq_in, dwq_o), (dwo_in, dwo_o), (dwu_in, dwu_o), (dwd_in, dwd_o)):
        to[...] = src[...].astype(F32)
    limit = jnp.full((1, 1), limit_in[0], jnp.int32).astype(F32)
    root = jnp.sqrt(limit / jnp.maximum(top_in[...], limit))
    row = jnp.concatenate([root[p : p + 1, :] for p in range(root.shape[0])], axis=1)
    width = row.shape[1]
    for third in range(3):
        c = slice(third * width, (third + 1) * width)
        if third < 2:
            w_o[:, c] = (w_in[:, c].astype(F32) * row).astype(BF)
        else:
            w_o[:, c] = w_in[:, c]
    start = 0
    for to in small_o:
        n = to.shape[1]
        to[...] = small_in[:, start : start + n]
        start += n


def finish(limit, top, out, tg, dwq, dwo, dwu, dwd, weight, small):
    steps = 2
    parts = (out, tg, dwq, dwo, dwu, dwd, weight)
    specs = [pl.BlockSpec((p.shape[0] // steps, p.shape[1]), lambda i: (i, 0)) for p in parts]

    def fixed(shape):
        return pl.BlockSpec(shape, lambda i: (0, 0))

    shape = jax.ShapeDtypeStruct
    kinds = (BF, BF, F32, F32, F32, F32, BF)
    return pl.pallas_call(
        finish_kernel,
        name="finish",
        grid=(steps,),
        out_shape=[shape(p.shape, kind) for p, kind in zip(parts, kinds)]
        + [shape((1, n), F32) for n in SMALL],
        in_specs=[pl.BlockSpec(memory_space=pltpu.SMEM), fixed(top.shape)]
        + specs + [fixed(small.shape)],
        out_specs=specs + [fixed((1, n)) for n in SMALL],
        compiler_params=pltpu.CompilerParams(vmem_limit_bytes=63 << 20),
    )(limit, top, out, tg, dwq, dwo, dwu, dwd, weight, small)


def by_image_local(
    tokens,
    filled,
    out_grad,
    norm1_gain,
    norm1_bias,
    qkv_weight,
    qv_bias,
    out_weight,
    out_bias,
    norm2_gain,
    norm2_bias,
    up_weight,
    up_bias,
    down_weight,
    down_bias,
    clip_threshold,
):
    images, local_rows, model_width = tokens.shape
    length = local_rows * images
    small, start = jnp.zeros((sum(SMALL),), BF), 0
    for piece in (
        norm1_gain, norm1_bias, qv_bias, out_bias, norm2_gain, norm2_bias, up_bias, down_bias
    ):
        count = piece.shape[0]
        small = small + jnp.pad(piece, (start, sum(SMALL) - start - count))
        start += count
    small = small[None]
    made = front(tokens, out_grad, filled, qkv_weight, out_weight, up_weight, down_weight, small)
    block_out, tokens_grad, g_qkv, g_out, g_up, g_down, mine, top = back(
        tokens, made[:17], made[17:]
    )
    (
        block_out, tokens_grad, g_qkv, g_out, g_up, g_down, clipped_weight, *small_out
    ) = finish(
        clip_threshold[None], top, block_out, tokens_grad.reshape(length, model_width),
        g_qkv, g_out, g_up, g_down, qkv_weight, mine,
    )
    s_gain_one, s_shift_one, s_qv, s_out, s_gain_two, s_shift_two, s_up, s_down = [
        piece.reshape(-1) for piece in small_out
    ]
    block_out = block_out.reshape(tokens.shape)
    tokens_grad = tokens_grad.reshape(tokens.shape)
    head_max = top[:, ::HD].reshape(-1)
    limit = clip_threshold.astype(F32)
    root_factor = jnp.sqrt(limit / jnp.maximum(head_max, limit))
    head_cols = jnp.repeat(root_factor, HD)
    ones = jnp.ones((model_width,), F32)
    bias_count = qv_bias.shape[0]
    bias_scale = jnp.concatenate([head_cols, ones])
    shard_scale = lax.dynamic_slice_in_dim(
        bias_scale, lax.axis_index("dp") * bias_count, bias_count
    )
    clipped_bias = (qv_bias.astype(F32) * shard_scale).astype(BF)
    return (
        block_out,
        tokens_grad,
        s_gain_one,
        s_shift_one,
        g_qkv,
        s_qv,
        g_out,
        s_out,
        s_gain_two,
        s_shift_two,
        g_up,
        s_up,
        g_down,
        s_down,
        clipped_weight,
        clipped_bias,
        head_max,
    )


def local(*args):
    if args[0].shape[0] == lax.axis_size("seq") == 4 and lax.axis_size("dp") == 8:
        return by_image_local(*args)
    return by_head_local(*args)


def solution(mesh):
    return jax.shard_map(
        local,
        mesh=mesh,
        in_specs=(
            P("dp", "seq", None),
            P("dp", "seq"),
            P("dp", "seq", None),
            P("dp"),
            P("dp"),
            P("dp", None),
            P("dp"),
            P("dp", None),
            P("dp"),
            P("dp"),
            P("dp"),
            P("dp", None),
            P("dp"),
            P("dp", None),
            P("dp"),
            P(),
        ),
        out_specs=(
            P("dp", "seq", None),
            P("dp", "seq", None),
            P("dp"),
            P("dp"),
            P("dp", None),
            P("dp"),
            P("dp", None),
            P("dp"),
            P("dp"),
            P("dp"),
            P("dp", None),
            P("dp"),
            P("dp", None),
            P("dp"),
            P("dp", None),
            P("dp"),
            P(),
        ),
        check_vma=False,
    )
```

```python
import math

import jax
import jax.numpy as jnp
from jax import lax
from jax.experimental import pallas as pl
from jax.experimental.pallas import tpu as pltpu
from jax.sharding import PartitionSpec as P

H = 16
HD = 64


epsilon = 1e-06
very_negative = -1e30


def norm_apply(values, gain_vec, shift_vec):
    center = jnp.mean(values, axis=-1, keepdims=True)
    centered = values - center
    spread = jnp.mean(centered * centered, axis=-1, keepdims=True)
    return centered * lax.rsqrt(spread + epsilon) * gain_vec + shift_vec


def exact_gelu(values):
    return jax.nn.gelu(values, approximate=False)


def last_dot(left_op, right_op):
    return lax.dot_general(
        left_op, right_op, (((1,), (1,)), ((), ())), preferred_element_type=jnp.float32
    )


def first_dot(left_op, right_op):
    return lax.dot_general(
        left_op, right_op, (((0,), (0,)), ((), ())), preferred_element_type=jnp.float32
    )


def column_sum(values):
    return jnp.sum(values.astype(jnp.float32), axis=0)


def score_block(queries, keys_in, key_keep):
    raw_scores = jnp.einsum(
        "qhd,khd->hqk", queries, keys_in, preferred_element_type=jnp.float32
    ) * HD ** (-0.5)
    masked = jnp.where(key_keep[None, None, :], raw_scores, very_negative)
    return (raw_scores, masked)


def attend_forward(inputs):
    queries, keys_in, values_in, key_keep = inputs
    raw_scores, masked = score_block(queries, keys_in, key_keep)
    row_peak = jnp.max(masked, axis=-1, keepdims=True)
    exp_scores = jnp.exp(masked - row_peak)
    row_total = jnp.sum(exp_scores, axis=-1, keepdims=True)
    soft_probs = (exp_scores / row_total).astype(jnp.bfloat16)
    mixed_rows = jnp.einsum(
        "hqk,khd->qhd", soft_probs, values_in, preferred_element_type=jnp.float32
    )
    logsum = row_peak + jnp.log(row_total)
    pair_keep = key_keep[:, None] & key_keep[None, :]
    head_top = jnp.max(jnp.where(pair_keep[None], raw_scores, very_negative), axis=(1, 2))
    flat_rows = mixed_rows.astype(jnp.bfloat16).reshape(mixed_rows.shape[0], -1)
    return (flat_rows, logsum, head_top)


def attend_backward(inputs):
    queries, keys_in, values_in, key_keep, logsum, upstream = inputs
    raw_scores, masked = score_block(queries, keys_in, key_keep)
    soft_probs = jnp.exp(masked - logsum)
    probs_low = soft_probs.astype(jnp.bfloat16)
    value_grad = jnp.einsum("hqk,qhd->khd", probs_low, upstream, preferred_element_type=jnp.float32)
    prob_grad = jnp.einsum("qhd,khd->hqk", upstream, values_in, preferred_element_type=jnp.float32)
    inner_sum = jnp.sum(soft_probs * prob_grad, axis=-1, keepdims=True)
    score_grad = (soft_probs * (prob_grad - inner_sum)).astype(jnp.bfloat16)
    score_scale = HD ** (-0.5)
    query_grad = (
        jnp.einsum("hqk,khd->qhd", score_grad, keys_in, preferred_element_type=jnp.float32)
        * score_scale
    )
    key_grad = (
        jnp.einsum("hqk,qhd->khd", score_grad, queries, preferred_element_type=jnp.float32)
        * score_scale
    )
    stacked = jnp.stack([query_grad, key_grad, value_grad], axis=1)
    return stacked.astype(jnp.bfloat16).reshape(stacked.shape[0], 3, -1)


def by_head_local(
    tokens,
    filled,
    out_grad,
    norm1_gain,
    norm1_bias,
    qkv_weight,
    qv_bias,
    out_weight,
    out_bias,
    norm2_gain,
    norm2_bias,
    up_weight,
    up_bias,
    down_weight,
    down_bias,
    clip_threshold,
):
    gathered = (
        lax.all_gather(norm1_gain, "dp", axis=0, tiled=True),
        lax.all_gather(norm1_bias, "dp", axis=0, tiled=True),
        lax.all_gather(qkv_weight, "dp", axis=0, tiled=True),
        lax.all_gather(qv_bias, "dp", axis=0, tiled=True),
        lax.all_gather(out_weight, "dp", axis=0, tiled=True),
        lax.all_gather(out_bias, "dp", axis=0, tiled=True),
        lax.all_gather(norm2_gain, "dp", axis=0, tiled=True),
        lax.all_gather(norm2_bias, "dp", axis=0, tiled=True),
        lax.all_gather(up_weight, "dp", axis=0, tiled=True),
        lax.all_gather(up_bias, "dp", axis=0, tiled=True),
        lax.all_gather(down_weight, "dp", axis=0, tiled=True),
        lax.all_gather(down_bias, "dp", axis=0, tiled=True),
    )
    (
        gain_one,
        shift_one,
        w_qkv,
        b_qv,
        w_out,
        b_out,
        gain_two,
        shift_two,
        w_up,
        b_up,
        w_down,
        b_down,
    ) = gathered
    images, local_rows, model_width = tokens.shape
    groups = lax.axis_size("seq")
    group_width = model_width // groups
    local_heads = group_width // HD
    length = local_rows * groups
    row_count = images * local_rows
    tokens_flat = tokens.astype(jnp.float32).reshape(row_count, model_width)
    gain_one_f = gain_one.astype(jnp.float32)
    shift_one_f = shift_one.astype(jnp.float32)
    gain_two_f = gain_two.astype(jnp.float32)
    shift_two_f = shift_two.astype(jnp.float32)
    hidden_one = norm_apply(tokens_flat, gain_one_f, shift_one_f).astype(jnp.bfloat16)
    bias_float = b_qv.astype(jnp.float32)
    qkv_bias = jnp.concatenate(
        [bias_float[:model_width], jnp.zeros((model_width,), jnp.float32), bias_float[model_width:]]
    )
    projected = (jnp.dot(hidden_one, w_qkv, preferred_element_type=jnp.float32) + qkv_bias).astype(
        jnp.bfloat16
    )
    key_flags = lax.all_gather(filled, "seq", axis=1, tiled=True)
    keep_all = key_flags > 0
    by_heads = lax.all_to_all(
        projected.reshape(images, local_rows, 3, groups, group_width),
        "seq",
        split_axis=3,
        concat_axis=1,
        tiled=True,
    )
    by_heads = by_heads.reshape(images, length, 3, local_heads, HD)
    queries = by_heads[:, :, 0]
    keys_all = by_heads[:, :, 1]
    values_all = by_heads[:, :, 2]
    attended, logsums, tops = lax.map(attend_forward, (queries, keys_all, values_all, keep_all))
    local_peak = jnp.max(tops, axis=0)
    peak_vector = lax.dynamic_update_slice(
        jnp.full((H,), very_negative, jnp.float32),
        local_peak,
        (lax.axis_index("seq") * local_heads,),
    )
    head_max = lax.pmax(peak_vector, ("dp", "seq"))
    back_rows = lax.all_to_all(
        attended.reshape(images, groups, local_rows, group_width),
        "seq",
        split_axis=1,
        concat_axis=3,
        tiled=True,
    )
    attn_rows = back_rows.reshape(row_count, model_width)
    branch = jnp.dot(attn_rows, w_out, preferred_element_type=jnp.float32) + b_out.astype(
        jnp.float32
    )
    middle = tokens_flat + branch
    hidden_two = norm_apply(middle, gain_two_f, shift_two_f).astype(jnp.bfloat16)
    pre_act = jnp.dot(hidden_two, w_up, preferred_element_type=jnp.float32) + b_up.astype(
        jnp.float32
    )
    activated = exact_gelu(pre_act).astype(jnp.bfloat16)
    block_rows = middle + (
        jnp.dot(activated, w_down, preferred_element_type=jnp.float32) + b_down.astype(jnp.float32)
    )
    block_out = block_rows.astype(jnp.bfloat16).reshape(tokens.shape)
    gain_one_b, w_qkv_b, w_out_b, gain_two_b, w_up_b, w_down_b = (
        lax.all_gather(norm1_gain, "dp", axis=0, tiled=True),
        lax.all_gather(qkv_weight, "dp", axis=0, tiled=True),
        lax.all_gather(out_weight, "dp", axis=0, tiled=True),
        lax.all_gather(norm2_gain, "dp", axis=0, tiled=True),
        lax.all_gather(up_weight, "dp", axis=0, tiled=True),
        lax.all_gather(down_weight, "dp", axis=0, tiled=True),
    )
    upstream = out_grad.reshape(row_count, model_width)
    upstream_f = upstream.astype(jnp.float32)
    d_bias_down = jnp.sum(upstream_f, axis=0)
    d_down = first_dot(activated, upstream)
    act_grad = last_dot(upstream, w_down_b)
    gelu_out, gelu_pull = jax.vjp(exact_gelu, pre_act)
    pre_grad = gelu_pull(act_grad)[0].astype(jnp.bfloat16)
    d_bias_up = column_sum(pre_grad)
    d_up = first_dot(hidden_two, pre_grad)
    hidden_two_grad = last_dot(pre_grad, w_up_b)
    norm_out_two, pull_two = jax.vjp(
        norm_apply, middle, gain_two_b.astype(jnp.float32), shift_two_f
    )
    mid_norm_grad, d_gain_two, d_shift_two = pull_two(hidden_two_grad)
    middle_grad = upstream_f + mid_norm_grad
    branch_grad = middle_grad.astype(jnp.bfloat16)
    d_bias_out = column_sum(branch_grad)
    d_out = first_dot(attn_rows, branch_grad)
    attn_grad = last_dot(branch_grad, w_out_b).astype(jnp.bfloat16)
    grad_heads = lax.all_to_all(
        attn_grad.reshape(images, local_rows, groups, group_width),
        "seq",
        split_axis=2,
        concat_axis=1,
        tiled=True,
    )
    grad_heads = grad_heads.reshape(images, length, local_heads, HD)
    head_grads = lax.map(
        attend_backward, (queries, keys_all, values_all, keep_all, logsums, grad_heads)
    )
    token_grads = lax.all_to_all(
        head_grads.reshape(images, groups, local_rows, 3, group_width),
        "seq",
        split_axis=1,
        concat_axis=4,
        tiled=True,
    )
    token_grads = token_grads.reshape(row_count, 3 * model_width)
    d_qkv = first_dot(hidden_one, token_grads)
    bias_sums = column_sum(token_grads)
    d_bias_qv = jnp.concatenate([bias_sums[:model_width], bias_sums[2 * model_width :]])
    first_grad = last_dot(token_grads, w_qkv_b)
    norm_out_one, pull_one = jax.vjp(
        norm_apply, tokens_flat, gain_one_b.astype(jnp.float32), shift_one_f
    )
    in_norm_grad, d_gain_one, d_shift_one = pull_one(first_grad)
    tokens_grad = (middle_grad + in_norm_grad).astype(jnp.bfloat16).reshape(tokens.shape)
    terms = (
        d_gain_one,
        d_shift_one,
        d_qkv,
        d_bias_qv,
        d_out,
        d_bias_out,
        d_gain_two,
        d_shift_two,
        d_up,
        d_bias_up,
        d_down,
        d_bias_down,
    )
    data_shards = (
        lax.psum_scatter(
            terms[0].astype(jnp.bfloat16), "dp", scatter_dimension=0, tiled=True
        ).astype(jnp.float32),
        lax.psum_scatter(
            terms[1].astype(jnp.bfloat16), "dp", scatter_dimension=0, tiled=True
        ).astype(jnp.float32),
        lax.psum_scatter(
            terms[2].astype(jnp.bfloat16), "dp", scatter_dimension=0, tiled=True
        ).astype(jnp.float32),
        lax.psum_scatter(
            terms[3].astype(jnp.bfloat16), "dp", scatter_dimension=0, tiled=True
        ).astype(jnp.float32),
        lax.psum_scatter(
            terms[4].astype(jnp.bfloat16), "dp", scatter_dimension=0, tiled=True
        ).astype(jnp.float32),
        lax.psum_scatter(
            terms[5].astype(jnp.bfloat16), "dp", scatter_dimension=0, tiled=True
        ).astype(jnp.float32),
        lax.psum_scatter(
            terms[6].astype(jnp.bfloat16), "dp", scatter_dimension=0, tiled=True
        ).astype(jnp.float32),
        lax.psum_scatter(
            terms[7].astype(jnp.bfloat16), "dp", scatter_dimension=0, tiled=True
        ).astype(jnp.float32),
        lax.psum_scatter(
            terms[8].astype(jnp.bfloat16), "dp", scatter_dimension=0, tiled=True
        ).astype(jnp.float32),
        lax.psum_scatter(
            terms[9].astype(jnp.bfloat16), "dp", scatter_dimension=0, tiled=True
        ).astype(jnp.float32),
        lax.psum_scatter(
            terms[10].astype(jnp.bfloat16), "dp", scatter_dimension=0, tiled=True
        ).astype(jnp.float32),
        lax.psum_scatter(
            terms[11].astype(jnp.bfloat16), "dp", scatter_dimension=0, tiled=True
        ).astype(jnp.float32),
    )
    shards = (
        lax.psum(data_shards[0].astype(jnp.bfloat16), "seq").astype(jnp.float32),
        lax.psum(data_shards[1].astype(jnp.bfloat16), "seq").astype(jnp.float32),
        lax.psum(data_shards[2].astype(jnp.bfloat16), "seq").astype(jnp.float32),
        lax.psum(data_shards[3].astype(jnp.bfloat16), "seq").astype(jnp.float32),
        lax.psum(data_shards[4].astype(jnp.bfloat16), "seq").astype(jnp.float32),
        lax.psum(data_shards[5].astype(jnp.bfloat16), "seq").astype(jnp.float32),
        lax.psum(data_shards[6].astype(jnp.bfloat16), "seq").astype(jnp.float32),
        lax.psum(data_shards[7].astype(jnp.bfloat16), "seq").astype(jnp.float32),
        lax.psum(data_shards[8].astype(jnp.bfloat16), "seq").astype(jnp.float32),
        lax.psum(data_shards[9].astype(jnp.bfloat16), "seq").astype(jnp.float32),
        lax.psum(data_shards[10].astype(jnp.bfloat16), "seq").astype(jnp.float32),
        lax.psum(data_shards[11].astype(jnp.bfloat16), "seq").astype(jnp.float32),
    )
    limit = clip_threshold.astype(jnp.float32)
    root_factor = jnp.sqrt(limit / jnp.maximum(head_max, limit))
    head_cols = jnp.repeat(root_factor, HD)
    weight_scale = jnp.concatenate([head_cols, head_cols, jnp.ones((model_width,), jnp.float32)])
    clipped_weight = (qkv_weight.astype(jnp.float32) * weight_scale[None, :]).astype(jnp.bfloat16)
    bias_count = qv_bias.shape[0]
    bias_scale = jnp.concatenate([head_cols, jnp.ones((model_width,), jnp.float32)])
    shard_scale = lax.dynamic_slice_in_dim(
        bias_scale, lax.axis_index("dp") * bias_count, bias_count
    )
    clipped_bias = (qv_bias.astype(jnp.float32) * shard_scale).astype(jnp.bfloat16)
    return (
        block_out,
        tokens_grad,
        shards[0],
        shards[1],
        shards[2],
        shards[3],
        shards[4],
        shards[5],
        shards[6],
        shards[7],
        shards[8],
        shards[9],
        shards[10],
        shards[11],
        clipped_weight,
        clipped_bias,
        head_max,
    )


MESH = pl.DeviceIdType.MESH
BF = jnp.bfloat16
F32 = jnp.float32
SMALL = (128, 128, 256, 128, 128, 128, 512, 128)


def flip(d, m):
    y = lax.rem(lax.div(d, 4) + m // 4, 2)
    x = lax.rem(lax.rem(lax.div(d, 2), 2) + (m // 2) % 2, 2)
    k = lax.rem(lax.rem(d, 2) + m % 2, 2)
    return 4 * y + 2 * x + k


def flip_traced(d, m):
    y = lax.rem(lax.div(d, 4) + lax.div(m, 4), 2)
    x = lax.rem(lax.rem(lax.div(d, 2), 2) + lax.rem(lax.div(m, 2), 2), 2)
    k = lax.rem(lax.rem(d, 2) + lax.rem(m, 2), 2)
    return 4 * y + 2 * x + k


def dot_nn(a, b):
    return lax.dot_general(a, b, (((1,), (0,)), ((), ())), preferred_element_type=F32)


def dot_nt(a, b):
    return lax.dot_general(a, b, (((1,), (1,)), ((), ())), preferred_element_type=F32)


def dot_tn(a, b):
    return lax.dot_general(a, b, (((0,), (0,)), ((), ())), preferred_element_type=F32)


def rows_of(block, size, start=0, count=None):
    count = size if count is None else count
    step = math.gcd(size, start) if start else size
    return pl.ds(pl.multiple_of(block * size + start, step), count)


def normalized(v):
    center = jnp.mean(v, axis=-1, keepdims=True)
    centered = v - center
    spread = jnp.mean(centered * centered, axis=-1, keepdims=True)
    scale = lax.rsqrt(spread + epsilon)
    return centered * scale, scale


def half_masks():
    lane = lax.broadcasted_iota(jnp.int32, (1, 2 * HD), 1)
    low = jnp.where(lane < HD, 1.0, 0.0)
    return low.astype(BF), (1.0 - low).astype(BF), lane < HD


def add_rows(target, other, rows, step=64):
    @pl.loop(0, rows // step)
    def _(i):
        r = rows_of(i, step)
        target[r, :] = target[r, :] + other[r, :]


def front_kernel(
    tok_in, grad_in, wq_in, wo_in, wu_in, wd_in, small_in, flag_in,
    tok_h, h1_h, qkv_h, gx_h, go_h, ga_h, h2_h, gu_h, att_h, atto_h, first_h, fx_h, fy_h,
    wq_h, wo_h, wu_h, wd_h, vec_o, dbup_o, bup_o, top_o, mask_o,
    wq, wo, wu, wd, tok, grad, h1, qkv, att, x1, h2, dh, fil, small, col, slp, ust, bias,
    dst, first, mine, flags,
    own_s, own_r, rel_s, rel_r, fwd_s, fwd_r, tok_s, tok_r, att_s, att_r, fil_s, fil_r,
    sm_s, sm_r, dn_s, dn_r, fs_s, fs_r, loc, stg, hout, wsv, fin,
):
    d, s = lax.axis_index("dp"), lax.axis_index("seq")
    images, part, width = tok_in.shape
    length = images * part
    pair_count = width // (2 * HD)
    weights = ((wq_in, wq), (wo_in, wo), (wu_in, wu), (wd_in, wd))
    sib, xn, yn, dn = flip(d, 1), flip(d, 2), flip(d, 4), flip(d, 6)

    barrier = pltpu.get_barrier_semaphore()
    for m in range(1, 8):
        pl.semaphore_signal(barrier, inc=1, device_id=(flip(d, m), s), device_id_type=MESH)
    for j in range(1, images):
        pl.semaphore_signal(
            barrier, inc=1, device_id=(d, lax.rem(s + j, images)), device_id_type=MESH
        )
    pl.semaphore_wait(barrier, 7 + images - 1)

    def send(src, dst, ss, rs, to_dp, to_seq):
        return pltpu.make_async_remote_copy(
            src_ref=src, dst_ref=dst, send_sem=ss, recv_sem=rs,
            device_id=(to_dp, to_seq), device_id_type=MESH,
        )

    def exchange(src, dst, ss, rs, rows):
        copies = []
        for j in range(1, images):
            to = lax.rem(s + j, images)
            copies.append(send(src.at[to], dst.at[rows], ss.at[j - 1], rs.at[j - 1], d, to))
        return copies

    my_rows = rows_of(s, part)
    sm_copies = [
        send(mine, small.at[d], sm_s.at[m - 1], sm_r.at[m - 1], flip(d, m), s)
        for m in range(1, 8)
    ]
    fil_copies = exchange(flags, fil, fil_s, fil_r, s)
    tok_copies = exchange(tok_in, tok, tok_s.at[0], tok_r.at[0], my_rows)
    grad_copies = exchange(grad_in, grad, tok_s.at[1], tok_r.at[1], my_rows)

    def own(w, which=range(5)):
        src, dst = weights[w]
        size = src.shape[0]
        half = size // 2
        def piece(way, to, h):
            return send(
                src.at[pl.ds(h * half, half)], dst.at[rows_of(d, size, h * half, half)],
                own_s.at[w, way, h], own_r.at[w, way, h], to, s,
            )
        return [
            piece(0, xn, 0), piece(1, yn, 1), piece(0, xn, 1), piece(1, yn, 0),
            send(src, dst.at[rows_of(d, size)], own_s.at[w, 2, 0], own_r.at[w, 2, 0], sib, s),
        ]

    def relays(w):
        dst = weights[w][1]
        size = weights[w][0].shape[0]
        half = size // 2
        lower, upper = rows_of(xn, size, 0, half), rows_of(yn, size, half, half)
        return [
            send(dst.at[lower], dst.at[lower], rel_s.at[w, 0], rel_r.at[w, 0], yn, s),
            send(dst.at[upper], dst.at[upper], rel_s.at[w, 1], rel_r.at[w, 1], xn, s),
        ]

    def forwards(w):
        dst = weights[w][1]
        size = weights[w][0].shape[0]
        return [
            send(dst.at[rows_of(b, size)], dst.at[rows_of(b, size)],
                 fwd_s.at[w, i], fwd_r.at[w, i], sib, s)
            for i, b in enumerate((xn, yn, dn))
        ]

    def start_own(w):
        for copy in own(w):
            copy.start()

    def on_halves(w):
        held, relay = own(w), relays(w)
        held[0].wait_recv()
        relay[0].start()
        held[1].wait_recv()
        relay[1].start()

    def on_rest(w):
        held, forward = own(w), forwards(w)
        held[2].wait_recv()
        forward[0].start()
        held[3].wait_recv()
        forward[1].start()

    def on_first(w):
        on_halves(w)
        on_rest(w)

    def on_diag(w):
        relay = relays(w)
        relay[0].wait_recv()
        relay[1].wait_recv()
        forwards(w)[2].start()

    def on_sib(w):
        own(w)[4].wait_recv()
        for copy in forwards(w):
            copy.wait_recv()

    def drain(w):
        for copy in own(w) + relays(w) + forwards(w):
            copy.wait_send()

    def keep_own(w):
        src, dst = weights[w]
        return pltpu.make_async_copy(src, dst.at[rows_of(d, src.shape[0])], loc.at[w])

    for copy in tok_copies:
        copy.start()
    start_own(0)
    mine[...] = small_in[...].astype(F32)
    flags[...] = jnp.zeros_like(flags)
    held = jnp.where(flag_in[...] > 0, 1.0, 0.0)
    for place in range(images):
        @pl.when(s == place)
        def _():
            for image in range(images):
                flags[image, :, place * part : (place + 1) * part] = jnp.broadcast_to(
                    held[image : image + 1, :], (8, part)
                )
    for copy in sm_copies + fil_copies:
        copy.start()
    start_own(1)
    locals_ = [keep_own(w) for w in range(4)]
    locals_ += [
        pltpu.make_async_copy(tok_in.at[s], tok.at[my_rows], loc.at[4]),
        pltpu.make_async_copy(grad_in.at[s], grad.at[my_rows], loc.at[5]),
        pltpu.make_async_copy(flags.at[s], fil.at[s], loc.at[6]),
        pltpu.make_async_copy(mine, small.at[d], loc.at[7]),
    ]
    for copy in locals_:
        copy.start()

    on_first(0)
    start_own(2)

    for copy in sm_copies + fil_copies:
        copy.wait_recv()
    for copy in locals_:
        copy.wait()

    starts = [sum(SMALL[:i]) for i in range(len(SMALL))]

    def vector(i, first=0, last=8):
        return jnp.concatenate(
            [small[b, :, starts[i] : starts[i] + SMALL[i]] for b in range(first, last)], axis=1
        )

    mask = fil[0] + fil[1] + fil[2] + fil[3]
    mask_o[...] = mask
    col[...] = jnp.transpose(mask)

    for copy in tok_copies:
        copy.wait_recv()
    for copy in grad_copies:
        copy.start()

    block = 128
    gain1, shift1 = vector(0), vector(1)

    @pl.loop(0, length // block)
    def _(i):
        r = rows_of(i, block)
        xh, _ = normalized(tok[r, :].astype(F32))
        h1[r, :] = (xh * gain1 + shift1).astype(BF)

    on_diag(0)
    on_first(1)
    on_sib(0)

    tile = 512
    qkv_bias = jnp.concatenate(
        [vector(2, 0, 4), jnp.zeros((1, width), F32), vector(2, 4, 8)], axis=1
    )
    bias[pl.ds(0, 1), :] = qkv_bias[:, :width]
    bias[pl.ds(1, 1), :] = qkv_bias[:, width : 2 * width]
    bias[pl.ds(2, 1), :] = qkv_bias[:, 2 * width :]

    for third in range(3):
        @pl.loop(0, width // tile)
        def _(n):
            c = pl.ds(pl.multiple_of(n * tile, tile), tile)
            cw = pl.ds(pl.multiple_of(third * width + n * tile, tile), tile)
            value = dot_nn(h1[...], wq[:, cw]) + bias[pl.ds(third, 1), c]
            qkv[:, cw] = value.astype(BF)

    saves = [
        pltpu.make_async_copy(tok, tok_h, hout.at[0]),
        pltpu.make_async_copy(h1, h1_h, hout.at[1]),
        pltpu.make_async_copy(qkv, qkv_h, hout.at[2]),
        pltpu.make_async_copy(wq, wq_h, hout.at[3]),
        pltpu.make_async_copy(wo, wo_h, hout.at[4]),
        pltpu.make_async_copy(wu, wu_h, hout.at[5]),
        None,
        pltpu.make_async_copy(att, att_h, hout.at[7]),
        pltpu.make_async_copy(first, first_h, hout.at[8]),
        pltpu.make_async_copy(h2, h2_h, hout.at[9]),
    ]
    for copy in saves[:4]:
        copy.start()

    low, high, low_lane = half_masks()
    pad = (mask[0:1, :] - 1.0) * 1e30
    pad2 = jnp.concatenate([pad, pad], axis=1)
    chunk = length // 2

    def attend(p, carry):
        c = pl.ds(pl.multiple_of(p * 2 * HD, 2 * HD), 2 * HD)
        ck = pl.ds(pl.multiple_of(width + p * 2 * HD, 2 * HD), 2 * HD)
        cv = pl.ds(pl.multiple_of(2 * width + p * 2 * HD, 2 * HD), 2 * HD)
        k, v = qkv[:, ck], qkv[:, cv]
        k2 = jnp.concatenate([k * low, k * high], axis=0)
        v2 = jnp.concatenate([v * low, v * high], axis=0)
        best = [jnp.full((1, 1), very_negative, F32)] * 2
        for j in range(2):
            r = pl.ds(j * chunk, chunk)
            q = qkv[r, c] * jnp.asarray(HD ** (-0.5), BF)
            scores = dot_nt(q, k2) + pad2
            probs = []
            for side in range(2):
                part_s = scores[:, side * length : (side + 1) * length]
                peak = jnp.max(part_s, axis=1, keepdims=True)
                e = jnp.exp(part_s - peak)
                total = jnp.sum(e, axis=1, keepdims=True)
                probs.append((e * (1.0 / total)).astype(BF))
                held = jnp.where(col[r, 0:1] > 0.5, peak, very_negative)
                best[side] = jnp.maximum(best[side], jnp.max(held, axis=0, keepdims=True))
            att[r, c] = dot_nn(jnp.concatenate(probs, axis=1), v2).astype(BF)
        top_o[pl.ds(p, 1), :] = jnp.where(
            low_lane, jnp.broadcast_to(best[0], (1, 2 * HD)), jnp.broadcast_to(best[1], (1, 2 * HD))
        )
        return carry

    def give_back(part_of):
        wide = width // 2
        cols = pl.ds(part_of * wide, wide)
        copies = []
        for j in range(1, images):
            to = lax.rem(s + j, images)
            copies.append(
                send(att.at[rows_of(to, part), cols], atto_h.at[s, :, cols],
                     att_s.at[part_of, j - 1], att_r.at[part_of, j - 1], d, to)
            )
        return copies

    lax.fori_loop(0, pair_count // 2, attend, 0)
    back_copies = give_back(0)
    for copy in back_copies:
        copy.start()
    on_first(2)
    start_own(3)
    lax.fori_loop(pair_count // 2, pair_count, attend, 0)
    back_copies += give_back(1)
    for copy in back_copies[images - 1 :]:
        copy.start()
    keep_att = pltpu.make_async_copy(att.at[my_rows], atto_h.at[s], hout.at[10])
    keep_att.start()
    saves[7].start()
    on_diag(1)
    on_sib(1)
    saves[4].start()

    gain2, shift2, b_out, b_down = vector(4), vector(5), vector(3), vector(7)

    @pl.loop(0, length // block)
    def _(i):
        r = rows_of(i, block)
        mid = tok[r, :].astype(F32) + dot_nn(att[r, :], wo[...]) + b_out
        x1[r, :] = mid
        xh, _ = normalized(mid)
        h2[r, :] = (xh * gain2 + shift2).astype(BF)

    saves[9].start()
    bup_o[...] = vector(6)
    dh[...] = jnp.zeros_like(dh)
    for copy in grad_copies:
        copy.wait_recv()

    def add_grad(i, acc):
        return acc + jnp.sum(grad[rows_of(i, block), :].astype(F32), axis=0, keepdims=True)

    grad_sum = lax.fori_loop(0, length // block, add_grad, jnp.zeros((1, width), F32))

    on_diag(2)
    on_sib(2)
    saves[5].start()

    ff_block = wd_in.shape[0]

    half_rows = ff_block // 2

    def activation(b):
        cols = pl.ds(pl.multiple_of(b * ff_block, ff_block), ff_block)
        u = dot_nn(h2[...], wu[:, cols]) + bup_o[:, cols]
        phi = 0.5 * (1.0 + lax.erf(u * (0.5**0.5)))
        slope = phi + u * (jnp.exp(-0.5 * u * u) * (1.0 / math.sqrt(2.0 * math.pi)))
        slp[:, cols] = slope.astype(BF)
        return (u * phi).astype(BF)

    def down_send(mi):
        return send(dst.at[1], first.at[mi], dn_s.at[mi], dn_r.at[mi], sib, s)

    def down(j, carry):
        m = lax.rem(6 * (j + 1), 8)
        mi = lax.div(m, 2)

        @pl.when(j > 0)
        def _():
            down_send(lax.div(lax.rem(6 * j, 8), 2)).wait_send()

        @pl.when(j == 2)
        def _():
            on_halves(3)

        for slot in (1, 0):
            a = activation(flip_traced(d, m + slot))
            dst[slot] = dot_tn(a, grad[...]).astype(BF)
            if slot:
                down_send(mi).start()
        down_send(mi).wait_recv()
        add_rows(first.at[mi], dst.at[0], ff_block)
        return carry

    lax.fori_loop(0, 4, down, 0)
    down_send(0).wait_send()
    saves[8].start()

    def first_stage(n):
        quarter = half_rows // 2
        lower, upper = pl.ds(0, quarter), pl.ds(quarter, quarter)
        m, rows, to_ref, to = (
            (6, lower, fx_h.at[1], xn), (6, upper, fy_h.at[1], yn),
            (2, lower, fx_h.at[0], xn), (4, upper, fy_h.at[0], yn),
        )[n]
        return send(first.at[m // 2, rows], to_ref, fs_s.at[n], fs_r.at[n], to, s)

    def stage_copy(slot, b):
        cols = pl.ds(pl.multiple_of(b * ff_block, ff_block), ff_block)
        return pltpu.make_async_copy(ust.at[slot], gu_h.at[:, cols], stg.at[slot])

    def save_down(i):
        rows = rows_of(flip_traced(d, i), ff_block)
        return pltpu.make_async_copy(wd.at[rows], wd_h.at[rows], wsv.at[i])

    def mlp(i, carry):
        b = flip_traced(d, i)
        slot = lax.rem(i, 2)

        @pl.when(i == 1)
        def _():
            own(3)[4].wait_recv()

        @pl.when(i == 2)
        def _():
            on_rest(3)
            for n in range(4):
                first_stage(n).start()

        for at, which in ((3, 0), (5, 1), (7, 2)):
            @pl.when(i == at)
            def _():
                forwards(3)[which].wait_recv()

        @pl.when(i == 6)
        def _():
            on_diag(3)

        cols = pl.ds(pl.multiple_of(b * ff_block, ff_block), ff_block)
        rows = rows_of(b, ff_block)
        save_down(i).start()
        gu = (dot_nt(grad[...], wd[rows, :]) * slp[:, cols].astype(F32)).astype(BF)
        dh[...] += dot_nt(gu, wu[:, cols])

        @pl.when(i >= 2)
        def _():
            stage_copy(slot, b).wait()

        dbup_o[:, cols] = jnp.sum(gu.astype(F32), axis=0, keepdims=True)
        ust[slot] = gu
        stage_copy(slot, b).start()
        return carry

    lax.fori_loop(0, 8, mlp, 0)
    for n in (0, 9):
        saves[n].wait()

    zero = jnp.zeros((1, width), F32)

    def finals(i):
        r = rows_of(i, block)
        return [
            pltpu.make_async_copy(dh.at[r], gx_h.at[r], fin.at[0, i]),
            pltpu.make_async_copy(tok.at[r], go_h.at[r], fin.at[1, i]),
            pltpu.make_async_copy(h2.at[r], ga_h.at[r], fin.at[2, i]),
        ]

    def norm_back(i, acc):
        r = rows_of(i, block)
        g = dh[r, :]
        xh, scale = normalized(x1[r, :])
        gg = g * gain2
        inner = gg - jnp.mean(gg, axis=1, keepdims=True)
        inner = inner - xh * jnp.mean(gg * xh, axis=1, keepdims=True)
        total = grad[r, :].astype(F32) + scale * inner
        dh[r, :] = total
        low_total = total.astype(BF)
        h2[r, :] = low_total
        tok[r, :] = dot_nt(low_total, wo[...]).astype(BF)
        for copy in finals(i):
            copy.start()
        return (
            acc[0] + jnp.sum(g * xh, axis=0, keepdims=True),
            acc[1] + jnp.sum(g, axis=0, keepdims=True),
            acc[2] + jnp.sum(low_total.astype(F32), axis=0, keepdims=True),
        )

    sums = lax.fori_loop(0, length // block, norm_back, (zero, zero, zero))
    for n, row in enumerate((sums[0], sums[1], sums[2], grad_sum)):
        vec_o[pl.ds(n, 1), :] = row
    for n, row in enumerate((gain1, gain2, shift2, b_out, b_down)):
        vec_o[pl.ds(8 + n, 1), :] = row
    for slot in range(2):
        stage_copy(slot, d).wait()
    for n in range(4):
        first_stage(n).wait()
    for n in (1, 2, 3, 4, 5, 7, 8):
        saves[n].wait()
    for n in range(8):
        save_down(n).wait()
    keep_att.wait()
    for w in range(4):
        drain(w)
    for copy in sm_copies + fil_copies + tok_copies + grad_copies + back_copies:
        copy.wait_send()
    for copy in back_copies:
        copy.wait_recv()
    for i in range(length // block):
        for copy in finals(i):
            copy.wait()


def front(tokens, out_grad, filled_rows, qkv_weight, out_weight, up_weight, down_weight, small):
    images, part, width = tokens.shape
    length = images * part
    shards = lax.axis_size("dp")
    ff = up_weight.shape[1]
    wide = qkv_weight.shape[1]
    shape = jax.ShapeDtypeStruct
    any_spec = pl.BlockSpec(memory_space=pl.ANY)
    vmem_spec = pl.BlockSpec(memory_space=pltpu.VMEM)
    dma = pltpu.SemaphoreType.DMA
    vm = pltpu.VMEM
    return pl.pallas_call(
        front_kernel,
        name="front",
        out_shape=(
            shape((length, width), BF),
            shape((length, width), BF),
            shape((length, wide), BF),
            shape((length, width), F32),
            shape((length, width), BF),
            shape((length, width), BF),
            shape((length, width), BF),
            shape((length, ff), BF),
            shape((length, width), BF),
            shape((images, part, width), BF),
            shape((4, ff // 8, width), BF),
            shape((2, ff // 32, width), BF),
            shape((2, ff // 32, width), BF),
            shape((width, wide), BF),
            shape((width, width), BF),
            shape((width, ff), BF),
            shape((ff, width), BF),
            shape((16, width), F32),
            shape((1, ff), F32),
            shape((1, ff), F32),
            shape((8, 2 * HD), F32),
            shape((8, length), F32),
        ),
        in_specs=[any_spec] * 6 + [vmem_spec] * 2,
        out_specs=[any_spec] * 17 + [vmem_spec] * 5,
        scratch_shapes=[
            vm((width, wide), BF), vm((width, width), BF), vm((width, ff), BF), vm((ff, width), BF),
            vm((length, width), BF), vm((length, width), BF), vm((length, width), BF),
            vm((length, wide), BF), vm((length, width), BF), vm((length, width), F32),
            vm((length, width), BF), vm((length, width), F32),
            vm((images, 8, length), F32), vm((shards, 1, sum(SMALL)), F32),
            vm((length, 8), F32), vm((length, ff), BF),
            vm((2, length, down_weight.shape[0]), BF), vm((8, width), F32),
            vm((2, ff // 8, width), BF), vm((4, ff // 8, width), BF), vm((1, sum(SMALL)), F32),
            vm((images, 8, length), F32),
            dma((4, 3, 2)), dma((4, 3, 2)), dma((4, 2)), dma((4, 2)), dma((4, 3)), dma((4, 3)),
            dma((2, images - 1)), dma((2, images - 1)), dma((2, images - 1)), dma((2, images - 1)),
            dma((images - 1,)), dma((images - 1,)), dma((7,)), dma((7,)),
            dma((4,)), dma((4,)), dma((4,)), dma((4,)), dma((8,)), dma((2,)), dma((14,)), dma((8,)),
            dma((3, length // 128)),
        ],
        compiler_params=pltpu.CompilerParams(
            collective_id=0, has_side_effects=True, vmem_limit_bytes=63 << 20
        ),
    )(tokens, out_grad, qkv_weight, out_weight, up_weight, down_weight, small, filled_rows)


def back_kernel(*refs):
    (
        qkv_in, go_in, h1_in, gx_in, tok_in, ga_in, h2_in, gu_in, att_in, atto_in, first_in,
        fx_in, fy_in, mine_in, wq_in, wo_in, wu_in, wd_in,
        mask_in, vec_in, dbup_in, bup_in, top_in,
        out_h, tg_h, dwq_h, dwo_h, dwu_h, dwd_h, small_o, top_o,
        qkv, go, ht, gbuf, buf, dh, wqg, pq, gp, colm, dst, own_u, ust, stg_o, ast, gxs,
        psm, rsm, zsm, rtop, ztop,
    ) = refs[:52]
    refs = refs[52:]
    count = 11
    recv0, recv1x, recv1y, recv2, za, zb = [refs[i * count : (i + 1) * count] for i in range(6)]
    (
        s0_s, s0_r, u0_s, u0_r, s1_s, s1_r, s2_s, s2_r, z_s, z_r, ex_s, ex_r, sm_s, sm_r,
        zs_s, zs_r, tp_s, tp_r, tz_s, tz_r, asem, wsem, osem, lsem, gsem,
    ) = refs[6 * count :]
    d, s = lax.axis_index("dp"), lax.axis_index("seq")
    length, width = go.shape
    images, part = mine_in.shape[0], mine_in.shape[1]
    sib, xn, yn = flip(d, 1), flip(d, 2), flip(d, 4)
    group_cols = gp.shape[1] // 3
    groups = width // group_cols
    ff_block = dst.shape[1]
    shard = width // 8
    block = 128
    tile = 512

    barrier = pltpu.get_barrier_semaphore()
    for m in range(1, 8):
        pl.semaphore_signal(barrier, inc=1, device_id=(flip(d, m), s), device_id_type=MESH)
    for j in range(1, images):
        pl.semaphore_signal(
            barrier, inc=1, device_id=(d, lax.rem(s + j, images)), device_id_type=MESH
        )

    def load(src, dst_ref, n):
        return pltpu.make_async_copy(src, dst_ref, lsem.at[n])

    def send(src, dst_ref, ss, rs, to_dp, to_seq):
        return pltpu.make_async_remote_copy(
            src_ref=src, dst_ref=dst_ref, send_sem=ss, recv_sem=rs,
            device_id=(to_dp, to_seq), device_id_type=MESH,
        )

    down_rows, up_cols = recv0[0].shape[1], recv0[2].shape[2]
    size = [down_rows] * 2 + [shard] * 9

    def s1(i, n):
        half = size[i] // 2
        lower, upper = pl.ds(0, half), pl.ds(half, half)
        m, part_rows, to_ref, to = (
            (6, lower, recv1x[i].at[1], xn), (6, upper, recv1y[i].at[1], yn),
            (2, lower, recv1x[i].at[0], xn), (4, upper, recv1y[i].at[0], yn),
        )[n]
        return send(recv0[i].at[m // 2, part_rows], to_ref, s1_s.at[i, n], s1_r.at[i, n], to, s)

    def s2(i, n):
        half = size[i] // 2
        if n == 0:
            return send(recv1x[i].at[1], recv2[i].at[pl.ds(0, half)],
                        s2_s.at[i, 0], s2_r.at[i, 0], yn, s)
        return send(recv1y[i].at[1], recv2[i].at[pl.ds(half, half)],
                    s2_s.at[i, 1], s2_r.at[i, 1], xn, s)

    mate = s + 1 - 2 * lax.rem(s, 2)
    across = 3 - s
    is_mid = jnp.logical_or(s == 1, s == 2)
    is_end = jnp.logical_or(s == 0, s == 3)

    def to_mid(i):
        return send(recv2[i], za[i], z_s.at[i, 0], z_r.at[i, 0], d, mate)

    def cross(i):
        return send(za[i], zb[i], z_s.at[i, 1], z_r.at[i, 1], d, across)

    def to_end(i):
        return send(zb[i], za[i], z_s.at[i, 2], z_r.at[i, 2], d, mate)

    def outputs(i, src):
        if i < 2:
            return [pltpu.make_async_copy(src, dwd_h.at[pl.ds(i * down_rows, down_rows)],
                                          osem.at[i, 0])]
        if i < 6:
            return [pltpu.make_async_copy(src, dwu_h.at[:, pl.ds((i - 2) * up_cols, up_cols)],
                                          osem.at[i, 0])]
        if i == 6:
            return [pltpu.make_async_copy(src, dwo_h, osem.at[i, 0])]
        return [
            pltpu.make_async_copy(
                src.at[:, pl.ds(third * group_cols, group_cols)],
                dwq_h.at[:, pl.ds(third * width + (i - 7) * group_cols, group_cols)],
                osem.at[i, third],
            )
            for third in range(3)
        ]

    def step1(i):
        for n in range(4):
            s1(i, n).start()

    def arrived(i, n):
        if i:
            s1(i, n).wait_recv()
        elif n == 0:
            for copy in ready_first:
                copy.wait()

    def step2(i):
        half = size[i] // 2
        arrived(i, 0)
        add_rows(recv1x[i].at[1], recv0[i].at[2, pl.ds(0, half)], half)
        s2(i, 0).start()
        arrived(i, 1)
        add_rows(recv1y[i].at[1], recv0[i].at[1, pl.ds(half, half)], half)
        s2(i, 1).start()
        arrived(i, 2)
        add_rows(recv1x[i].at[0], recv0[i].at[0, pl.ds(0, half)], half)
        arrived(i, 3)
        add_rows(recv1y[i].at[0], recv0[i].at[0, pl.ds(half, half)], half)

    def step3(i):
        half = size[i] // 2
        s2(i, 0).wait_recv()
        add_rows(recv2[i].at[pl.ds(0, half)], recv1x[i].at[0], half)
        s2(i, 1).wait_recv()
        add_rows(recv2[i].at[pl.ds(half, half)], recv1y[i].at[0], half)

        @pl.when(is_end)
        def _():
            to_mid(i).start()

    def step4(i):
        @pl.when(is_mid)
        def _():
            to_mid(i).wait_recv()
            add_rows(za[i], recv2[i], size[i])
            cross(i).start()

    def step5(i):
        @pl.when(is_mid)
        def _():
            cross(i).wait_recv()
            add_rows(zb[i], za[i], size[i])
            to_end(i).start()
            for copy in outputs(i, zb[i]):
                copy.start()

    def step6(i):
        @pl.when(is_end)
        def _():
            to_end(i).wait_recv()
            for copy in outputs(i, za[i]):
                copy.start()

    def drain(i):
        for n in range(4 if i else 0):
            s1(i, n).wait_send()
        for n in range(2):
            s2(i, n).wait_send()

        @pl.when(is_end)
        def _():
            to_mid(i).wait_send()
            for copy in outputs(i, za[i]):
                copy.wait()

        @pl.when(is_mid)
        def _():
            cross(i).wait_send()
            to_end(i).wait_send()
            for copy in outputs(i, zb[i]):
                copy.wait()

    def cols_of(b, n=ff_block):
        return pl.ds(pl.multiple_of(b * n, n), n)

    def gu_load(slot, b):
        return pltpu.make_async_copy(gu_in.at[:, cols_of(b)], ast.at[slot], asem.at[slot])

    lower_rows, upper_rows = pl.ds(0, down_rows), pl.ds(down_rows, down_rows)
    ready_first = [
        load(fx_in, recv1x[0], 11 + 2 * images), load(fy_in, recv1y[0], 12 + 2 * images),
        load(first_in.at[:, lower_rows], recv0[0], 13 + 2 * images),
    ]
    ready_second = load(first_in.at[:, upper_rows], recv0[1], 0)
    ready_second.start()
    for copy in ready_first:
        copy.start()
    load_h2 = load(h2_in, buf, 1)
    load_h2.start()
    load_qkv = load(qkv_in, qkv, 2)
    load_qkv.start()
    load_go = load(go_in, go, 3)
    load_go.start()

    def weight_group(g):
        return [
            pltpu.make_async_copy(
                wq_in.at[:, pl.ds(third * width + g * group_cols, group_cols)],
                wqg.at[g % 2, :, pl.ds(third * group_cols, group_cols)],
                wsem.at[g % 2, third],
            )
            for third in range(3)
        ]

    for copy in weight_group(0):
        copy.start()
    pl.semaphore_wait(barrier, 7 + images - 1)
    top_copies = [
        send(top_in, rtop.at[d], tp_s.at[m - 1], tp_r.at[m - 1], flip(d, m), s)
        for m in range(1, 8)
    ]
    for copy in top_copies:
        copy.start()
    gu_load(0, 0).start()
    load_ga = load(ga_in, gbuf, 4)
    load_ga.start()
    dh[...] = jnp.zeros_like(dh)
    colm[...] = jnp.transpose((mask_in[...] - 1.0) * 1e30)
    ready_second.wait()

    def turned(src):
        @pl.loop(0, 8)
        def _(m):
            at = pl.ds(pl.multiple_of(flip_traced(d, m) * shard, shard), shard)
            ht[rows_of(m, shard), :] = jnp.transpose(src[:, at])

    load_att = load(att_in, buf, 5)
    load_h1 = load(h1_in, buf, 6)
    load_tok = load(tok_in, gbuf, 7)

    def turn1():
        load_h2.wait()
        turned(buf)
        load_att.start()

    def split_store(value, keep, give, cols_keep, cols_give):
        for m in range(8):
            piece = value[m * shard : (m + 1) * shard].astype(BF)
            if m % 2 == 0:
                keep[m // 2, :, cols_keep] = piece
            else:
                give[m // 2, :, cols_give] = piece

    blocks = up_cols // tile

    def up_send(i, n):
        return send(ust.at[n], recv0[2 + i].at[:, :, cols_of(n, tile)],
                    u0_s.at[i, n], u0_r.at[i, n], sib, s)

    def up(i):
        if i:
            for n in range(blocks):
                up_send(i - 1, n).wait_send()

        def body(n, carry):
            b = i * blocks + n
            slot = lax.rem(b, 2)
            gu_load(slot, b).wait()

            @pl.when(b + 1 < 4 * blocks)
            def _():
                gu_load(1 - slot, b + 1).start()

            value = dot_nn(ht[...], ast[slot])
            split_store(value, own_u.at[i % 2], ust.at[n], cols_of(n, tile), slice(None))
            up_send(i, n).start()
            return carry

        lax.fori_loop(0, blocks, body, 0)

    def add_up(i):
        for n in range(blocks):
            up_send(i, n).wait_recv()
        for m in (6, 2, 4, 0):
            add_rows(recv0[2 + i].at[m // 2], own_u.at[i % 2, m // 2], shard)

    def out_send(n):
        return send(ust.at[n], recv0[6].at[:, :, pl.ds(n * tile, tile)],
                    s0_s.at[0, n], s0_r.at[0, n], sib, s)

    def out():
        load_ga.wait()
        load_att.wait()
        turned(buf)
        load_h1.start()
        for n in range(blocks):
            up_send(3, n).wait_send()
        for n in range(width // tile):
            value = dot_nn(ht[...], gbuf[:, pl.ds(n * tile, tile)])
            split_store(value, stg_o, ust.at[n], pl.ds(n * tile, tile), slice(None))
            out_send(n).start()
        load_tok.start()

    def turn3():
        load_h1.wait()
        turned(buf)

    def add_out():
        for n in range(width // tile):
            out_send(n).wait_recv()
            out_send(n).wait_send()
        for m in (6, 2, 4, 0):
            add_rows(recv0[6].at[m // 2], stg_o.at[m // 2], shard)

    low, high, low_lane = half_masks()
    scale = HD ** (-0.5)
    pair = 2 * HD
    per_group = group_cols // pair
    cuts = ((0, 256), (256, length - 256)) if length > 256 else ((0, length),)
    def attention(g):
        if g == 0:
            load_qkv.wait()
            load_go.wait()
        if g + 1 < groups:
            for copy in weight_group(g + 1):
                copy.start()

        def body(n, carry):
            p = g * per_group + n
            c = pl.ds(pl.multiple_of(p * pair, pair), pair)
            ck = pl.ds(pl.multiple_of(width + p * pair, pair), pair)
            cv = pl.ds(pl.multiple_of(2 * width + p * pair, pair), pair)
            k, v = qkv[:, ck], qkv[:, cv]
            k2 = jnp.concatenate([k * low, k * high], axis=0)
            v2 = jnp.concatenate([v * low, v * high], axis=0)
            gk = jnp.zeros((2 * length, pair), F32)
            gv = jnp.zeros((2 * length, pair), F32)
            at_q = pl.ds(pl.multiple_of(n * pair, pair), pair)
            at_k = pl.ds(pl.multiple_of(group_cols + n * pair, pair), pair)
            at_v = pl.ds(pl.multiple_of(2 * group_cols + n * pair, pair), pair)
            for first, wide in cuts:
                r = pl.ds(first, wide)
                q = qkv[r, c] * jnp.asarray(scale, BF)
                g_rows = go[r, c]
                scores = dot_nt(k2, q)
                dprob = dot_nt(v2, g_rows)
                low_probs, low_grads = [], []
                for side in range(2):
                    rows = slice(side * length, (side + 1) * length)
                    part_s = scores[rows] + colm[:, 0:1]
                    e = jnp.exp(part_s - jnp.max(part_s, axis=0, keepdims=True))
                    probs = e * (1.0 / jnp.sum(e, axis=0, keepdims=True))
                    weighted = probs * dprob[rows]
                    inner = jnp.sum(weighted, axis=0, keepdims=True)
                    low_probs.append(probs.astype(BF))
                    low_grads.append((weighted - probs * inner).astype(BF))
                low_p = jnp.concatenate(low_probs, axis=0)
                low_g = jnp.concatenate(low_grads, axis=0)
                gv = gv + dot_nn(low_p, g_rows)
                gk = gk + dot_nn(low_g, q)
                gp[r, at_q] = (dot_tn(low_g, k2) * scale).astype(BF)
            gp[:, at_k] = jnp.where(low_lane, gk[:length], gk[length:]).astype(BF)
            gp[:, at_v] = jnp.where(low_lane, gv[:length], gv[length:]).astype(BF)
            return carry

        lax.fori_loop(0, per_group, body, 0)

    bias_rows = []

    def q_send(g):
        return send(pq.at[g % 2, 1], recv0[7 + g], s0_s.at[1 + g, 0], s0_r.at[1 + g, 0], sib, s)

    def group(g):
        if g >= 2:
            q_send(g - 2).wait_send()
        bias_rows.append(jnp.sum(gp[...].astype(F32), axis=0, keepdims=True))
        for third in range(3):
            cols = pl.ds(third * group_cols, group_cols)
            value = dot_nn(ht[...], gp[:, cols])
            split_store(value, pq.at[g % 2, 0], pq.at[g % 2, 1], cols, cols)
        q_send(g).start()
        for copy in weight_group(g):
            copy.wait()
        for first in range(0, width, tile):
            dh[:, pl.ds(first, tile)] += dot_nt(gp[...], wqg[g % 2, pl.ds(first, tile), :])

    def add_q(g):
        q_send(g).wait_recv()
        for m in (6, 2, 4, 0):
            add_rows(recv0[7 + g].at[m // 2], pq.at[g % 2, 0, m // 2], shard)

    gain1 = vec_in[pl.ds(8, 1), :]
    zero = jnp.zeros((1, width), F32)

    def gx_load(slot, i):
        return pltpu.make_async_copy(gx_in.at[rows_of(i, block)], gxs.at[slot], gsem.at[slot])

    def norm_back(i, acc):
        slot = lax.rem(i, 2)
        gx_load(slot, i).wait()

        @pl.when(i + 1 < length // block)
        def _():
            gx_load(1 - slot, i + 1).start()

        r = rows_of(i, block)
        g = dh[r, :]
        xh, spread = normalized(gbuf[r, :].astype(F32))
        gg = g * gain1
        inner = gg - jnp.mean(gg, axis=1, keepdims=True)
        inner = inner - xh * jnp.mean(gg * xh, axis=1, keepdims=True)
        go[r, :] = (gxs[slot] + spread * inner).astype(BF)
        return (
            acc[0] + jnp.sum(g * xh, axis=0, keepdims=True),
            acc[1] + jnp.sum(g, axis=0, keepdims=True),
        )

    late = {}
    tg_copies = []
    for j in range(1, images):
        to = lax.rem(s + j, images)
        tg_copies.append(
            send(go.at[rows_of(to, part)], tg_h.at[s], ex_s.at[j - 1], ex_r.at[j - 1], d, to)
        )
    own_tg = load(go.at[rows_of(s, part)], tg_h.at[s], 8)

    own_loads = []
    for j in range(images):
        rows = pl.ds(j * part, part)
        own_loads.append(load(mine_in.at[j], qkv.at[rows, pl.ds(0, width)], 9 + j))
        own_loads.append(load(atto_in.at[j], qkv.at[rows, pl.ds(width, width)], 9 + images + j))
    own_loads.append(load(wo_in.at[pl.ds(0, tile)], dst.at[0], 9 + 2 * images))
    own_loads.append(load(wo_in.at[pl.ds(tile, tile)], dst.at[1], 10 + 2 * images))

    def norm1():
        for copy in own_loads:
            copy.start()
        load_tok.wait()
        gx_load(0, 0).start()
        late["norm"] = lax.fori_loop(0, length // block, norm_back, (zero, zero))

    def tg():
        for copy in tg_copies:
            copy.start()
        own_tg.start()

    sm_copies = [
        send(psm.at[flip(d, m)], rsm.at[m - 1], sm_s.at[m - 1], sm_r.at[m - 1], flip(d, m), s)
        for m in range(1, 8)
    ]
    top_z, sm_z = [], []
    for j in range(1, images):
        to = lax.rem(s + j, images)
        top_z.append(send(ztop.at[s], ztop.at[s], tz_s.at[j - 1], tz_r.at[j - 1], d, to))
        sm_z.append(send(zsm.at[s], zsm.at[s], zs_s.at[j - 1], zs_r.at[j - 1], d, to))

    def smalls():
        d_gain1, d_shift1 = late["norm"]
        q_sum = jnp.concatenate([row[:, :group_cols] for row in bias_rows], axis=1)
        v_sum = jnp.concatenate([row[:, 2 * group_cols :] for row in bias_rows], axis=1)
        pieces = (
            d_gain1, d_shift1, jnp.concatenate([q_sum, v_sum], axis=1), vec_in[pl.ds(2, 1), :],
            vec_in[pl.ds(0, 1), :], vec_in[pl.ds(1, 1), :], dbup_in[...], vec_in[pl.ds(3, 1), :],
        )
        for b in range(8):
            psm[b] = jnp.concatenate(
                [piece[:, b * n : (b + 1) * n] for piece, n in zip(pieces, SMALL)], axis=1
            )
        for copy in sm_copies:
            copy.start()
        for copy in top_copies:
            copy.wait_recv()
        rtop[d] = top_in[...]
        best = rtop[0]
        for b in range(1, 8):
            best = jnp.maximum(best, rtop[b])
        ztop[s] = best
        for copy in top_z:
            copy.start()

    def smalls_z():
        for copy in sm_copies:
            copy.wait_recv()
        mine = psm[d]
        for m in range(7):
            mine = mine + rsm[m]
        zsm[s] = mine
        for copy in sm_z:
            copy.start()

    gain2, shift2 = vec_in[pl.ds(9, 1), :], vec_in[pl.ds(10, 1), :]
    b_out, b_down = vec_in[pl.ds(11, 1), :], vec_in[pl.ds(12, 1), :]

    def owners():
        for copy in own_loads:
            copy.wait()

        @pl.loop(0, length // block)
        def _(i):
            r = rows_of(i, block)
            mid = qkv[r, 0:width].astype(F32) + b_out
            mid = mid + dot_nn(qkv[r, width : width + tile], dst[0])
            mid = mid + dot_nn(qkv[r, width + tile : 2 * width], dst[1])
            xh, _ = normalized(mid)
            dh[r, :] = mid + b_down
            qkv[r, 2 * width :] = (xh * gain2 + shift2).astype(BF)

        for copy in ff_loads(0, 0):
            copy.start()

    def ff_loads(slot, b):
        return (
            pltpu.make_async_copy(wu_in.at[:, cols_of(b)], wqg.at[slot, :, pl.ds(0, ff_block)],
                                  wsem.at[slot, 0]),
            pltpu.make_async_copy(wd_in.at[rows_of(b, ff_block)], dst.at[slot],
                                  wsem.at[slot, 1]),
        )

    def feed_block(b, carry):
        slot = lax.rem(b, 2)
        for copy in ff_loads(slot, b):
            copy.wait()

        @pl.when(b < 7)
        def _():
            for copy in ff_loads(1 - slot, b + 1):
                copy.start()

        u = dot_nn(qkv[:, 2 * width :], wqg[slot, :, 0:ff_block]) + bup_in[:, cols_of(b)]
        a = (u * (0.5 * (1.0 + lax.erf(u * (0.5**0.5))))).astype(BF)
        dh[...] += dot_nn(a, dst[slot])
        return carry

    keep_out = load(buf, out_h, 1)

    def feed(n):
        lax.fori_loop(2 * n, 2 * n + 2, feed_block, 0)
        if n == 1:
            smalls_z()
        if n == 3:
            buf[...] = dh[...].astype(BF)
            keep_out.start()

    step2(0)
    turn1()
    step1(1)
    up(0)
    up(1)
    step3(0)
    add_up(0)
    add_up(1)
    step1(2)
    up(2)
    up(3)
    out()
    step2(1)
    step4(0)
    turn3()
    step1(3)
    attention(0)
    step2(2)
    step3(1)
    group(0)
    add_q(0)
    add_up(2)
    step2(3)
    step1(7)
    step1(4)
    attention(1)
    step4(1)
    step3(3)
    step5(0)
    add_out()
    group(1)
    step3(2)
    step2(7)
    step1(6)
    attention(2)
    step4(3)
    step5(1)
    step2(4)
    step3(7)
    group(2)
    step4(2)
    step2(6)
    add_up(3)
    add_q(2)
    add_q(1)
    step5(3)
    step4(7)
    step1(5)
    step6(0)
    step3(6)
    step1(9)
    attention(3)
    step4(6)
    step5(2)
    step3(4)
    step2(5)
    group(3)
    step1(8)
    step5(7)
    step4(4)
    step5(6)
    add_q(3)
    step3(5)
    step2(8)
    step2(9)
    step4(5)
    step1(10)
    step5(4)
    step3(8)
    step4(8)
    step3(9)
    step5(5)
    step6(7)
    step4(9)
    step2(10)
    step5(8)
    step3(10)
    step4(10)
    norm1()
    step6(1)
    tg()
    owners()
    step5(9)
    step6(6)
    feed(0)
    step6(4)
    smalls()
    feed(1)
    feed(2)
    step5(10)
    step6(3)
    step6(8)
    feed(3)
    step6(9)
    step6(10)
    step6(5)
    step6(2)

    for copy in top_z + sm_z:
        copy.wait_recv()
    top_o[...] = jnp.maximum(jnp.maximum(ztop[0], ztop[1]), jnp.maximum(ztop[2], ztop[3]))
    small_o[...] = (zsm[0] + zsm[1]) + (zsm[2] + zsm[3])
    for g in range(groups - 2, groups):
        q_send(g).wait_send()
    for i in range(count):
        drain(i)
    for copy in top_copies + top_z + sm_copies + sm_z + tg_copies:
        copy.wait_send()
    for copy in tg_copies:
        copy.wait_recv()
    own_tg.wait()
    keep_out.wait()


def back(tokens, saved, vecs):
    images, part, width = tokens.shape
    (
        tok, h1, qkv, gx, go, ga, h2, gu, att, atto, first, fx, fy, wq, wo, wu, wd,
    ) = saved
    vec, dbup, bup, tops, mask = vecs
    length = images * part
    wide, ff = wq.shape[1], wu.shape[1]
    shard = width // 8
    shape = jax.ShapeDtypeStruct
    any_spec = pl.BlockSpec(memory_space=pl.ANY)
    vmem_spec = pl.BlockSpec(memory_space=pltpu.VMEM)
    dma = pltpu.SemaphoreType.DMA
    vm = pltpu.VMEM
    group_cols = 256
    groups = width // group_cols
    sizes = [(ff // 16, width)] * 2 + [(shard, ff // 4)] * 4 + [(shard, width)]
    sizes += [(shard, 3 * group_cols)] * groups
    count = len(sizes)
    halves = [vm((2, r // 2, c), BF) for r, c in sizes]
    whole = [vm((r, c), BF) for r, c in sizes]
    z_peers = images - 1
    small = sum(SMALL)
    return pl.pallas_call(
        back_kernel,
        name="back",
        out_shape=(
            shape((length, width), BF),
            shape((images, part, width), BF),
            shape((shard, wide), BF),
            shape((shard, width), BF),
            shape((shard, ff), BF),
            shape((ff // 8, width), BF),
            shape((1, small), F32),
            shape((8, 2 * HD), F32),
        ),
        in_specs=[any_spec] * 18 + [vmem_spec] * 5,
        out_specs=[any_spec] * 6 + [vmem_spec] * 2,
        scratch_shapes=[
            vm((length, wide), BF), vm((length, width), BF), vm((width, length), BF),
            vm((length, width), BF), vm((length, width), BF), vm((length, width), F32),
            vm((2, width, 3 * group_cols), BF), vm((2, 2, 4, shard, 3 * group_cols), BF),
            vm((length, 3 * group_cols), BF), vm((length, 8), F32),
            vm((2, ff // 8, width), BF), vm((2, 4, shard, ff // 4), BF), vm((2, 4, shard, 512), BF),
            vm((4, shard, width), BF), vm((2, length, ff // 8), BF), vm((2, 128, width), F32),
            vm((8, 1, small), F32), vm((7, 1, small), F32),
            vm((images, 1, small), F32), vm((8, 8, 2 * HD), F32), vm((images, 8, 2 * HD), F32),
            *[vm((4, r, c), BF) for r, c in sizes], *halves, *halves, *whole, *whole, *whole,
            dma((5, 2)), dma((5, 2)), dma((4, 2)), dma((4, 2)), dma((count, 4)),
            dma((count, 4)), dma((count, 2)), dma((count, 2)), dma((count, 3)), dma((count, 3)),
            dma((z_peers,)), dma((z_peers,)), dma((7,)), dma((7,)),
            dma((z_peers,)), dma((z_peers,)), dma((7,)), dma((7,)),
            dma((z_peers,)), dma((z_peers,)), dma((2,)), dma((2, 3)), dma((count, 3)),
            dma((14 + 2 * images,)), dma((2,)),
        ],
        compiler_params=pltpu.CompilerParams(
            collective_id=1, has_side_effects=True, vmem_limit_bytes=63 << 20
        ),
    )(
        qkv, go, h1, gx, tok, ga, h2, gu, att, atto, first, fx, fy, tokens, wq, wo, wu, wd,
        mask, vec, dbup, bup, tops,
    )


def finish_kernel(
    limit_in, top_in, out_in, tg_in, dwq_in, dwo_in, dwu_in, dwd_in, w_in, small_in,
    out_o, tg_o, dwq_o, dwo_o, dwu_o, dwd_o, w_o, *small_o
):
    out_o[...] = out_in[...]
    tg_o[...] = tg_in[...]
    for src, to in ((dwq_in, dwq_o), (dwo_in, dwo_o), (dwu_in, dwu_o), (dwd_in, dwd_o)):
        to[...] = src[...].astype(F32)
    limit = jnp.full((1, 1), limit_in[0], jnp.int32).astype(F32)
    root = jnp.sqrt(limit / jnp.maximum(top_in[...], limit))
    row = jnp.concatenate([root[p : p + 1, :] for p in range(root.shape[0])], axis=1)
    width = row.shape[1]
    for third in range(3):
        c = slice(third * width, (third + 1) * width)
        if third < 2:
            w_o[:, c] = (w_in[:, c].astype(F32) * row).astype(BF)
        else:
            w_o[:, c] = w_in[:, c]
    start = 0
    for to in small_o:
        n = to.shape[1]
        to[...] = small_in[:, start : start + n]
        start += n


def finish(limit, top, out, tg, dwq, dwo, dwu, dwd, weight, small):
    steps = 2
    parts = (out, tg, dwq, dwo, dwu, dwd, weight)
    specs = [pl.BlockSpec((p.shape[0] // steps, p.shape[1]), lambda i: (i, 0)) for p in parts]

    def fixed(shape):
        return pl.BlockSpec(shape, lambda i: (0, 0))

    shape = jax.ShapeDtypeStruct
    kinds = (BF, BF, F32, F32, F32, F32, BF)
    return pl.pallas_call(
        finish_kernel,
        name="finish",
        grid=(steps,),
        out_shape=[shape(p.shape, kind) for p, kind in zip(parts, kinds)]
        + [shape((1, n), F32) for n in SMALL],
        in_specs=[pl.BlockSpec(memory_space=pltpu.SMEM), fixed(top.shape)]
        + specs + [fixed(small.shape)],
        out_specs=specs + [fixed((1, n)) for n in SMALL],
        compiler_params=pltpu.CompilerParams(vmem_limit_bytes=63 << 20),
    )(limit, top, out, tg, dwq, dwo, dwu, dwd, weight, small)


def by_image_local(
    tokens,
    filled,
    out_grad,
    norm1_gain,
    norm1_bias,
    qkv_weight,
    qv_bias,
    out_weight,
    out_bias,
    norm2_gain,
    norm2_bias,
    up_weight,
    up_bias,
    down_weight,
    down_bias,
    clip_threshold,
):
    images, local_rows, model_width = tokens.shape
    length = local_rows * images
    small, start = jnp.zeros((sum(SMALL),), BF), 0
    for piece in (
        norm1_gain, norm1_bias, qv_bias, out_bias, norm2_gain, norm2_bias, up_bias, down_bias
    ):
        count = piece.shape[0]
        small = small + jnp.pad(piece, (start, sum(SMALL) - start - count))
        start += count
    small = small[None]
    made = front(tokens, out_grad, filled, qkv_weight, out_weight, up_weight, down_weight, small)
    block_out, tokens_grad, g_qkv, g_out, g_up, g_down, mine, top = back(
        tokens, made[:17], made[17:]
    )
    (
        block_out, tokens_grad, g_qkv, g_out, g_up, g_down, clipped_weight, *small_out
    ) = finish(
        clip_threshold[None], top, block_out, tokens_grad.reshape(length, model_width),
        g_qkv, g_out, g_up, g_down, qkv_weight, mine,
    )
    s_gain_one, s_shift_one, s_qv, s_out, s_gain_two, s_shift_two, s_up, s_down = [
        piece.reshape(-1) for piece in small_out
    ]
    block_out = block_out.reshape(tokens.shape)
    tokens_grad = tokens_grad.reshape(tokens.shape)
    head_max = top[:, ::HD].reshape(-1)
    limit = clip_threshold.astype(F32)
    root_factor = jnp.sqrt(limit / jnp.maximum(head_max, limit))
    head_cols = jnp.repeat(root_factor, HD)
    ones = jnp.ones((model_width,), F32)
    bias_count = qv_bias.shape[0]
    bias_scale = jnp.concatenate([head_cols, ones])
    shard_scale = lax.dynamic_slice_in_dim(
        bias_scale, lax.axis_index("dp") * bias_count, bias_count
    )
    clipped_bias = (qv_bias.astype(F32) * shard_scale).astype(BF)
    return (
        block_out,
        tokens_grad,
        s_gain_one,
        s_shift_one,
        g_qkv,
        s_qv,
        g_out,
        s_out,
        s_gain_two,
        s_shift_two,
        g_up,
        s_up,
        g_down,
        s_down,
        clipped_weight,
        clipped_bias,
        head_max,
    )


def local(*args):
    if args[0].shape[0] == lax.axis_size("seq") == 4 and lax.axis_size("dp") == 8:
        return by_image_local(*args)
    return by_head_local(*args)


def solution(mesh):
    return jax.shard_map(
        local,
        mesh=mesh,
        in_specs=(
            P("dp", "seq", None),
            P("dp", "seq"),
            P("dp", "seq", None),
            P("dp"),
            P("dp"),
            P("dp", None),
            P("dp"),
            P("dp", None),
            P("dp"),
            P("dp"),
            P("dp"),
            P("dp", None),
            P("dp"),
            P("dp", None),
            P("dp"),
            P(),
        ),
        out_specs=(
            P("dp", "seq", None),
            P("dp", "seq", None),
            P("dp"),
            P("dp"),
            P("dp", None),
            P("dp"),
            P("dp", None),
            P("dp"),
            P("dp"),
            P("dp"),
            P("dp", None),
            P("dp"),
            P("dp", None),
            P("dp"),
            P("dp", None),
            P("dp"),
            P(),
        ),
        check_vma=False,
    )
```
